32 devices in a mesh: wide: 8 (over z, x), narrow: 4 (over y, core).
Axes of the slice: x: 2, y: 2, z: 4, core: 2. Of those that a mesh axis runs over, the one named last changes fastest.
Arguments:
- tokens: bfloat16 [4096, 1024], P('wide'), may hold values from -6 to 6
- cotangent: bfloat16 [4096, 1024], P('wide'), may hold values from -6 to 6
- seq_spans: int32 [3], replicated, may hold values from 1 to 5, as said below
- w_query: bfloat16 [1024, 1024], P(('wide', 'narrow')), may hold values from -0.1875 to 0.1875
- w_key: bfloat16 [1024, 1024], P(('wide', 'narrow')), may hold values from -0.1875 to 0.1875
- w_value: bfloat16 [1024, 1024], P(('wide', 'narrow')), may hold values from -0.1875 to 0.1875
- conv_kernel: bfloat16 [4, 3072], P(None, ('wide', 'narrow')), may hold values from -3 to 3
- persistent: bfloat16 [2, 16, 1024], P(None, None, ('wide', 'narrow')), may hold values from -6 to 6
- norm_gain: bfloat16 [1024], P(('wide', 'narrow')), may hold values from 0.5 to 1.5
- rate_proj: bfloat16 [1024, 3], P(('wide', 'narrow')), may hold values from -5 to 5
- out_gate: bfloat16 [1024, 1024], P('wide', 'narrow'), may hold values from -0.1875 to 0.1875
- out_proj: bfloat16 [1024, 1024], P('narrow', 'wide'), may hold values from -0.5 to 0.5
- memory_in: bfloat16 [1024, 4096], P('wide', 'narrow'), may hold values from -0.1875 to 0.1875
- memory_out: bfloat16 [4096, 1024], P('narrow', 'wide'), may hold values from -0.1875 to 0.1875
- ffn_gain: bfloat16 [1024], P(('wide', 'narrow')), may hold values from 0.5 to 1.5
- ffn_gate: bfloat16 [1024, 4096], P('wide', 'narrow'), may hold values from -0.1875 to 0.1875
- ffn_up: bfloat16 [1024, 4096], P('wide', 'narrow'), may hold values from -0.1875 to 0.1875
- ffn_down: bfloat16 [4096, 1024], P('narrow', 'wide'), may hold values from -0.1875 to 0.1875
Outputs:
- output: bfloat16 [4096, 1024], P('wide')
- tokens_grad: float32 [4096, 1024], P('wide')
- query_grad: float32 [1024, 1024], P('wide', 'narrow')
- key_grad: float32 [1024, 1024], P('wide', 'narrow')
- value_grad: float32 [1024, 1024], P('wide', 'narrow')
- kernel_grad: float32 [4, 3072], P(None, ('wide', 'narrow'))
- persistent_grad: float32 [2, 16, 1024], P(None, None, ('wide', 'narrow'))
- norm_grad: float32 [1024], P(('wide', 'narrow'))
- rate_grad: float32 [1024, 3], P(('wide', 'narrow'))
- out_gate_grad: float32 [1024, 1024], P('wide', 'narrow')
- out_proj_grad: float32 [1024, 1024], P('narrow', 'wide')
- memory_in_grad: float32 [1024, 4096], P('wide', 'narrow')
- memory_out_grad: float32 [4096, 1024], P('narrow', 'wide')
- ffn_gain_grad: float32 [1024], P(('wide', 'narrow'))
- ffn_gate_grad: float32 [1024, 4096], P('wide', 'narrow')
- ffn_up_grad: float32 [1024, 4096], P('wide', 'narrow')
- ffn_down_grad: float32 [4096, 1024], P('narrow', 'wide')
The draws below stay inside these ranges and needn't reach their ends.
Inputs may be any that keep to these rules, and one draw needn't show every extreme that they name: `seq_spans`: the sequences fill all 4096 tokens, one has exactly 5 spans, and the span that holds token 2048 never begins a sequence.
All inputs are finite; a program needn't handle non-finite values.
Results may differ from the reference program's by a relative error of at most 0.025.
Values may be sent and summed in bfloat16 or wider, within the bound.
A program may use at most 256 MiB of HBM per device.

```python
import math
import jax
import jax.numpy as jnp
from jax import lax

D = 1024
HEADS = 16
HEAD = 64
MEM = 4096
FF = 4096
PERS = 16
CH = 512
KER = 4
MAXCH = 5
NSEQ = 3
TOKENS = 4096
N_WIDE = 8


def draw_once(key):
    longest = jax.random.randint(jax.random.fold_in(key, 7), (), 0, NSEQ)
    seq_index = jnp.arange(NSEQ, dtype=jnp.int32)
    counts = jnp.where(seq_index == longest, MAXCH, 1).astype(jnp.int32)
    spare_spans = N_WIDE - MAXCH - (NSEQ - 1)

    def place_one(step_number, current):
        picked = jax.random.randint(jax.random.fold_in(key, 100 + step_number), (), 0, NSEQ)
        has_room = (current < MAXCH) & (seq_index != longest)
        fallback = jnp.argmax(has_room.astype(jnp.int32)).astype(jnp.int32)
        target = jnp.where(has_room[picked], picked, fallback)
        return current + (seq_index == target).astype(jnp.int32)
    return lax.fori_loop(0, spare_spans, place_one, counts)


def covering_layout():
    seq_index = jnp.arange(NSEQ, dtype=jnp.int32)
    before = NSEQ // 2
    after = NSEQ - 1 - before
    start_span = min(N_WIDE // 2 - 1, before * MAXCH, N_WIDE - MAXCH - after)
    rest_spans = N_WIDE - start_span - MAXCH
    before_counts = 1 + jnp.clip(start_span - before - (MAXCH - 1) * seq_index, 0, MAXCH - 1)
    after_index = seq_index - before - 1
    after_counts = 1 + jnp.clip(rest_spans - after - (MAXCH - 1) * after_index, 0, MAXCH - 1)
    counts = jnp.where(seq_index < before, before_counts, jnp.where(seq_index == before, MAXCH, after_counts))
    return counts.astype(jnp.int32)


def draw_seq_spans(key, part):
    candidates = jax.vmap(lambda number: draw_once(jax.random.fold_in(key, 1000 + number)))(jnp.arange(16, dtype=jnp.int32))
    stacked = jnp.concatenate([candidates, covering_layout()[None, :]], 0)
    starts = jnp.cumsum(stacked, axis=1) - stacked
    usable = jnp.all(starts != N_WIDE // 2, axis=1).astype(jnp.int32)
    chosen = jnp.argmax(usable).astype(jnp.int32)
    return stacked[chosen]


def level_of(stream_key, shape, shards, low, high):
    loudness, own = 1.0, jax.random.fold_in(stream_key, 6)
    for dim, blocks in shards:
        heights = jnp.exp(jax.random.uniform(jax.random.fold_in(own, dim), (blocks,), jnp.float32, low / len(shards), high / len(shards)))
        loudness = loudness * jnp.repeat(heights, shape[dim] // blocks).reshape([-1 if axis == dim else 1 for axis in range(len(shape))])
    return loudness


def normal_values(own_key, shape, scale, reach, split=(), held_as=jnp.bfloat16):
    level = level_of(own_key, shape, split, -0.22, 0.18) if split else 1.0
    values = jax.random.normal(own_key, shape, jnp.float32) * scale * level
    return jnp.minimum(jnp.maximum(values, -reach), reach).astype(held_as)


def setup_inputs(seed: int = 0) -> dict:
    arg_keys = jax.random.split(jax.random.key(seed), 19)
    return {
        "tokens": normal_values(arg_keys[0], (TOKENS, D), 1.0, 6.0, ((0, 8),)),
        "cotangent": normal_values(arg_keys[1], (TOKENS, D), 1.0, 6.0, ((0, 8),)),
        "seq_spans": draw_seq_spans(jax.random.fold_in(arg_keys[18], 71), 0),
        "w_query": normal_values(arg_keys[3], (D, D), D ** -0.5, 0.1875, ((0, 32),)),
        "w_key": normal_values(arg_keys[4], (D, D), D ** -0.5, 0.1875, ((0, 32),)),
        "w_value": normal_values(arg_keys[5], (D, D), D ** -0.5, 0.1875, ((0, 32),)),
        "conv_kernel": normal_values(arg_keys[6], (KER, 3 * D), 0.5, 3.0, ((1, 32),)),
        "persistent": normal_values(arg_keys[7], (2, PERS, D), 1.0, 6.0, ((2, 32),)),
        "norm_gain": jnp.clip(1.0 + 0.1 * jax.random.normal(arg_keys[8], (D,), jnp.float32), 0.5, 1.5).astype(jnp.bfloat16),
        "rate_proj": normal_values(arg_keys[9], (D, 3), 1.0, 5.0, ((0, 32),)),
        "out_gate": normal_values(arg_keys[10], (D, D), D ** -0.5, 0.1875, ((0, 8), (1, 4))),
        "out_proj": normal_values(arg_keys[11], (D, D), (D // 8) ** -0.5, 0.5, ((0, 4), (1, 8))),
        "memory_in": normal_values(arg_keys[12], (D, MEM), D ** -0.5, 0.1875, ((0, 8), (1, 4))),
        "memory_out": normal_values(arg_keys[13], (MEM, D), (MEM // 4) ** -0.5, 0.1875, ((0, 4), (1, 8))),
        "ffn_gain": jnp.clip(1.0 + 0.1 * jax.random.normal(arg_keys[14], (D,), jnp.float32), 0.5, 1.5).astype(jnp.bfloat16),
        "ffn_gate": normal_values(arg_keys[15], (D, FF), D ** -0.5, 0.1875, ((0, 8), (1, 4))),
        "ffn_up": normal_values(arg_keys[16], (D, FF), D ** -0.5, 0.1875, ((0, 8), (1, 4))),
        "ffn_down": normal_values(arg_keys[17], (FF, D), (FF // 4) ** -0.5, 0.1875, ((0, 4), (1, 8))),
    }


@jax.custom_vjp
def low(v):
    return lax.optimization_barrier(v.astype(jnp.bfloat16)).astype(jnp.float32)

@jax.custom_vjp
def low_back(v):
    return v

def low_keep(v):
    return (low(v), None)

def low_pass(kept, grad):
    return (grad,)

def back_keep(v):
    return (v, None)

def back_low(kept, grad):
    return (low(grad),)
low.defvjp(low_keep, low_pass)
low_back.defvjp(back_keep, back_low)
decay_top = 0.2
moment_top = 0.9
learn_top = 0.1
eps_norm = 1e-05
eps_head = 1e-06
masked_score = -1e+30

def matmul(left_side, right_side):
    return jnp.dot(left_side, right_side, precision=lax.Precision.HIGHEST, preferred_element_type=jnp.float32)

def rms_norm(values, gain_row):
    return values * lax.rsqrt(lax.optimization_barrier(jnp.mean(values * values, axis=-1, keepdims=True)) + eps_norm) * gain_row

def head_norm(values):
    shaped = values.reshape(values.shape[:-1] + (HEADS, HEAD))
    shaped = shaped * lax.rsqrt(lax.optimization_barrier(jnp.sum(shaped * shaped, axis=-1, keepdims=True)) + eps_head)
    return shaped.reshape(values.shape)

def silu_slope(values):
    sigmoid_val = jax.nn.sigmoid(values)
    return sigmoid_val * (1.0 + values * (1.0 - sigmoid_val))

def attend_block(query_rows, key_rows, value_rows, recalled, persist_keys, persist_values):
    recall_keys = low(head_norm(recalled))
    recall_values = low(recalled)
    keys_all = jnp.concatenate([persist_keys, recall_keys, key_rows], 0)
    values_all = jnp.concatenate([persist_values, recall_values, value_rows], 0)
    key_count = keys_all.shape[0]
    query_heads = query_rows.reshape(CH, HEADS, HEAD)
    key_heads = keys_all.reshape(key_count, HEADS, HEAD)
    value_heads = values_all.reshape(key_count, HEADS, HEAD)
    raw_scores = jnp.einsum('thd,jhd->htj', query_heads, key_heads, precision=lax.Precision.HIGHEST)
    scores = low_back(math.sqrt(HEAD) * raw_scores)
    row_index = lax.broadcasted_iota(jnp.int32, (CH, key_count), 0)
    col_index = lax.broadcasted_iota(jnp.int32, (CH, key_count), 1)
    allowed = (col_index < PERS + CH) | (col_index - PERS - CH <= row_index)
    scores = jnp.where(allowed[None], scores, masked_score)
    row_top = lax.optimization_barrier(jnp.max(scores, axis=-1, keepdims=True))
    exponent = jnp.exp(scores - row_top)
    weights = low(exponent / lax.optimization_barrier(jnp.sum(exponent, axis=-1, keepdims=True)))
    attended = low_back(jnp.einsum('htj,jhd->thd', weights, value_heads, precision=lax.Precision.HIGHEST))
    return attended.reshape(CH, D)

def memory_chain(query_low, key_low, value_act, gate_rows, span_first, first_init, second_init):

    def advance(carry, slices):
        state_first, state_second, moment_first, moment_second = carry
        query_rows, key_rows, value_rows, gate_row, is_start = slices
        state_first = jnp.where(is_start, first_init, state_first)
        state_second = jnp.where(is_start, second_init, state_second)
        moment_first = jnp.where(is_start, 0.0, moment_first)
        moment_second = jnp.where(is_start, 0.0, moment_second)
        first_low = low(state_first)
        second_low = low(state_second)
        query_hidden = low(jax.nn.silu(low_back(matmul(query_rows, first_low))))
        recalled = low_back(matmul(query_hidden, second_low))
        key_pre = low_back(matmul(key_rows, first_low))
        key_hidden = low(jax.nn.silu(key_pre))
        error_low = low((low_back(matmul(key_hidden, second_low)) - value_rows) / CH)
        grad_second = low_back(matmul(key_hidden.T, error_low))
        hidden_grad = low_back(matmul(error_low, second_low.T))
        slope_low = low(hidden_grad * silu_slope(key_pre))
        grad_first = low_back(matmul(key_rows.T, slope_low))
        moment_first = gate_row[1] * moment_first - gate_row[2] * grad_first
        moment_second = gate_row[1] * moment_second - gate_row[2] * grad_second
        state_first = (1.0 - gate_row[0]) * state_first + moment_first
        state_second = (1.0 - gate_row[0]) * state_second + moment_second
        return ((state_first, state_second, moment_first, moment_second), recalled)
    slices = (query_low.reshape(N_WIDE, CH, D), key_low.reshape(N_WIDE, CH, D), value_act.reshape(N_WIDE, CH, D), gate_rows, span_first)
    start_state = (first_init, second_init, jnp.zeros_like(first_init), jnp.zeros_like(second_init))
    scan_out = lax.scan(jax.checkpoint(advance), start_state, slices)
    return scan_out[1].reshape(N_WIDE * CH, D)

def forward(tokens, w_query, w_key, w_value, conv_kernel, persistent, norm_gain, rate_proj, out_gate, out_proj, memory_in, memory_out, ffn_gain, ffn_gate, ffn_up, ffn_down, seq_spans):
    normed = rms_norm(tokens, norm_gain)
    normed_low = low(normed)
    projected = low_back(matmul(normed_low, jnp.concatenate([w_query, w_key, w_value], 1)))
    seq_ends = jnp.cumsum(seq_spans)
    seq_starts = seq_ends - seq_spans
    span_first = jnp.any(seq_starts[None, :] == jnp.arange(N_WIDE, dtype=jnp.int32)[:, None], axis=1)
    row_index = jnp.arange(N_WIDE * CH, dtype=jnp.int32)
    row_first = jnp.repeat(span_first, CH)
    mixed_conv = conv_kernel[0] * projected
    for offset in range(1, KER):
        moved = jnp.concatenate([jnp.zeros((offset, 3 * D), jnp.float32), projected[:-offset]], 0)
        valid = jnp.logical_not(row_first & (row_index % CH < offset))
        mixed_conv = mixed_conv + conv_kernel[offset] * jnp.where(valid[:, None], moved, 0.0)
    activated = jax.nn.silu(mixed_conv)
    query_low = low(head_norm(activated[:, :D]))
    key_low = low(head_norm(activated[:, D:2 * D]))
    value_act = activated[:, 2 * D:]
    value_low = low(value_act)
    span_mean = lax.optimization_barrier(jnp.mean(normed.reshape(N_WIDE, CH, D), axis=1))
    gate_scale = jnp.array([decay_top, moment_top, learn_top], jnp.float32)
    gate_rows = jax.nn.sigmoid(matmul(span_mean, rate_proj)) * gate_scale
    recalled = memory_chain(query_low, key_low, value_act, gate_rows, span_first, memory_in, memory_out)
    persist_keys = low(head_norm(persistent[0]))
    persist_values = low(persistent[1])

    def attend_one(slices):
        return attend_block(slices[0], slices[1], slices[2], slices[3], persist_keys, persist_values)
    blocks = (query_low.reshape(N_WIDE, CH, D), key_low.reshape(N_WIDE, CH, D), value_low.reshape(N_WIDE, CH, D), recalled.reshape(N_WIDE, CH, D))
    attended = lax.map(jax.checkpoint(attend_one), blocks).reshape(N_WIDE * CH, D)
    gate_pre = low_back(matmul(normed_low, out_gate))
    gated = low(attended * jax.nn.sigmoid(gate_pre))
    middle = tokens + low_back(matmul(gated, out_proj))
    normed_two = low(rms_norm(middle, ffn_gain))
    gate_val = low_back(matmul(normed_two, ffn_gate))
    up_val = low_back(matmul(normed_two, ffn_up))
    hidden = low(jax.nn.silu(gate_val) * up_val)
    return middle + matmul(hidden, ffn_down)

def reference(tokens, cotangent, seq_spans, w_query, w_key, w_value, conv_kernel, persistent, norm_gain, rate_proj, out_gate, out_proj, memory_in, memory_out, ffn_gain, ffn_gate, ffn_up, ffn_down):
    floats = tuple((array_in.astype(jnp.float32) for array_in in (tokens, w_query, w_key, w_value, conv_kernel, persistent, norm_gain, rate_proj, out_gate, out_proj, memory_in, memory_out, ffn_gain, ffn_gate, ffn_up, ffn_down)))

    def wrapped(*params):
        return forward(*params, seq_spans)
    result, pullback = jax.vjp(wrapped, *floats)
    grads = pullback(cotangent.astype(jnp.float32))
    return (result.astype(jnp.bfloat16), grads[0], grads[1], grads[2], grads[3], grads[4], grads[5], grads[6], grads[7], grads[8], grads[9], grads[10], grads[11], grads[12], grads[13], grads[14], grads[15])
```

```python
import math

import jax
import jax.numpy as jnp
from jax import lax
from jax.experimental import pallas as pl
from jax.experimental.pallas import tpu as pltpu
from jax.sharding import PartitionSpec as P

HEAD = 64
LANE_WIDE = 4
MESH = pl.DeviceIdType.MESH
ANY = pl.BlockSpec(memory_space=pl.ANY)
bf16 = jnp.bfloat16
f32 = jnp.float32

decay_top = 0.2
moment_top = 0.9
learn_top = 0.1
eps_norm = 1e-05
eps_head = 1e-06
masked_score = -1e30


def remote(src, dst, send, recv, device):
    return pltpu.make_async_remote_copy(
        src_ref=src, dst_ref=dst, send_sem=send, recv_sem=recv, device_id=device, device_id_type=MESH
    )


def exchange(arrays, axes, ident):
    wide, narrow = lax.axis_size("wide"), lax.axis_size("narrow")
    peers = {"all": wide * narrow, "wide": wide, "narrow": narrow}[axes]
    picks = [pick for _, pick in arrays]
    operands = [array for array, _ in arrays]
    chunks = [a.shape if pick is None else a.shape[1:] for a, pick in arrays]
    count = len(arrays)

    def kernel(*refs):
        ins, outs, holds = refs[:count], refs[count : 2 * count], refs[2 * count : 3 * count]
        send_sem, recv_sem, local_sem = refs[3 * count :]
        my_wide, my_narrow = lax.axis_index("wide"), lax.axis_index("narrow")
        me = {"all": my_wide * narrow + my_narrow, "wide": my_wide, "narrow": my_narrow}[axes]

        def place(step):
            target = lax.rem(me + step, peers)
            if axes == "all":
                return lax.div(target, narrow), lax.rem(target, narrow)
            return (target, my_narrow) if axes == "wide" else (my_wide, target)

        barrier = pltpu.get_barrier_semaphore()

        def greet(step, carry):
            pl.semaphore_signal(barrier, inc=1, device_id=place(step), device_id_type=MESH)
            return carry

        lax.fori_loop(1, peers, greet, 0)

        def chunk(index, where):
            return ins[index] if picks[index] is None else ins[index].at[picks[index](*where)]

        own = [
            pltpu.make_async_copy(chunk(i, (my_wide, my_narrow)), holds[i], local_sem.at[i]) for i in range(count)
        ]
        for copy in own:
            copy.start()
        pl.semaphore_wait(barrier, peers - 1)

        def send(step, carry):
            where = place(step)
            for i in range(count):
                remote(chunk(i, where), outs[i].at[me], send_sem.at[i], recv_sem.at[i], where).start()
            return carry

        lax.fori_loop(1, peers, send, 0)
        for i in range(count):
            own[i].wait()
            back = pltpu.make_async_copy(holds[i], outs[i].at[me], local_sem.at[i])
            back.start()
            back.wait()
        for i in range(count):
            others = outs[i].at[pl.ds(0, peers - 1)]
            whole = remote(others, others, send_sem.at[i], recv_sem.at[i], place(1))
            whole.wait_send()
            whole.wait_recv()

    return pl.pallas_call(
        kernel,
        out_shape=[jax.ShapeDtypeStruct((peers,) + tuple(c), a.dtype) for a, c in zip(operands, chunks)],
        in_specs=[ANY] * count,
        out_specs=[ANY] * count,
        scratch_shapes=[pltpu.VMEM(tuple(c), a.dtype) for a, c in zip(operands, chunks)]
        + [pltpu.SemaphoreType.DMA((count,))] * 3,
        compiler_params=pltpu.CompilerParams(collective_id=ident, has_side_effects=True),
        name=f"exchange_{ident}",
    )(*operands)


def gather_all(arrays, ident):
    wide, narrow = lax.axis_size("wide"), lax.axis_size("narrow")
    zs = 4 if wide % 4 == 0 else 1
    xs, ys = wide // zs, narrow // 2
    count = len(arrays)
    rows = arrays[0].shape[0]
    half = rows // 2

    def kernel(*refs):
        ins, outs = refs[:count], refs[count : 2 * count]
        hold, local_sem, sent, got, sent_pair, got_pair = refs[2 * count :]
        my_wide, my_narrow = lax.axis_index("wide"), lax.axis_index("narrow")
        mz, mx = lax.div(my_wide, xs), lax.rem(my_wide, xs)
        my, mc = lax.div(my_narrow, 2), lax.rem(my_narrow, 2)

        def dev(z, x, y, c):
            return (z * xs + x, 2 * y + c)

        barrier = pltpu.get_barrier_semaphore()
        friends = [dev(lax.rem(mz + s, zs), mx, my, mc) for s in range(1, zs)]
        friends += [dev(mz, lax.rem(mx + s, xs), my, mc) for s in range(1, xs)]
        friends += [dev(mz, mx, lax.rem(my + s, ys), mc) for s in range(1, ys)]
        friends += [dev(mz, mx, my, 1 - mc)]
        for friend in friends:
            pl.semaphore_signal(barrier, inc=1, device_id=friend, device_id_type=MESH)
        own = [pltpu.make_async_copy(ins[i], hold.at[i], local_sem.at[i]) for i in range(count)]
        for copy in own:
            copy.start()
        pl.semaphore_wait(barrier, len(friends))

        waits = []
        number = [0]

        def piece(i, z, x, y, c, h):
            return outs[i].at[z * xs + x, 2 * y + c, pl.ds(h * half, half)]

        def spot(z, x, y):
            return (z * xs + x) * ys + y

        def push(i, z, x, y, h, target, src=None):
            here = piece(i, z, x, y, mc, h)
            copy = remote(
                here if src is None else src, here, sent.at[number[0]], got.at[i, spot(z, x, y), h], target
            )
            number[0] += 1
            copy.start()
            waits.append(copy)

        def arrived(i, z, x, y, h):
            here = piece(i, z, x, y, mc, h)
            remote(here, here, sent.at[0], got.at[i, spot(z, x, y), h], dev(mz, mx, my, 1 - mc)).wait_recv()

        pairs = []

        def to_partner(i, z, x, y, h, src=None):
            here = piece(i, z, x, y, mc, h)
            copy = remote(
                here if src is None else src,
                here,
                sent_pair.at[len(pairs)],
                got_pair.at[i, spot(z, x, y), h],
                dev(mz, mx, my, 1 - mc),
            )
            copy.start()
            pairs.append(copy)

        def first_fan(i, z, src=(None, None)):
            for s in range(1, ys):
                push(i, z, mx, my, 0, dev(mz, mx, lax.rem(my + s, ys), mc), src[0])
            for s in range(1, xs):
                push(i, z, mx, my, 1, dev(mz, lax.rem(mx + s, xs), my, mc), src[1])
            for s in range(1, xs):
                push(i, z, mx, my, 0, dev(mz, lax.rem(mx + s, xs), my, mc), src[0])
            for s in range(1, ys):
                push(i, z, mx, my, 1, dev(mz, mx, lax.rem(my + s, ys), mc), src[1])
            for h in (0, 1):
                to_partner(i, z, mx, my, h, src[h])

        for i in range(count):
            for s in range(1, zs):
                for h in (0, 1):
                    push(i, mz, mx, my, h, dev(lax.rem(mz + s, zs), mx, my, mc), ins[i].at[pl.ds(h * half, half)])
            first_fan(i, mz, (ins[i].at[pl.ds(0, half)], ins[i].at[pl.ds(half, half)]))
        for i in range(count):
            for s in range(1, zs):
                z = lax.rem(mz + zs - s, zs)
                for h in (0, 1):
                    arrived(i, z, mx, my, h)
                first_fan(i, z)
        for i in range(count):
            for s in range(zs):
                z = lax.rem(mz + zs - s, zs)
                for r in range(1, ys):
                    y = lax.rem(my + r, ys)
                    arrived(i, z, mx, y, 0)
                    for q in range(1, xs):
                        push(i, z, mx, y, 0, dev(mz, lax.rem(mx + q, xs), my, mc))
                    to_partner(i, z, mx, y, 0)
                for r in range(1, xs):
                    x = lax.rem(mx + r, xs)
                    arrived(i, z, x, my, 1)
                    for q in range(1, ys):
                        push(i, z, x, my, 1, dev(mz, mx, lax.rem(my + q, ys), mc))
                    to_partner(i, z, x, my, 1)
        for i in range(count):
            own[i].wait()
            back = pltpu.make_async_copy(hold.at[i], outs[i].at[my_wide, my_narrow], local_sem.at[i])
            back.start()
            back.wait()
        for i in range(count):
            for s in range(zs):
                z = lax.rem(mz + zs - s, zs)
                for q in range(1, xs):
                    x = lax.rem(mx + q, xs)
                    arrived(i, z, x, my, 0)
                    to_partner(i, z, x, my, 0)
                    for r in range(1, ys):
                        y = lax.rem(my + r, ys)
                        arrived(i, z, x, y, 0)
                        to_partner(i, z, x, y, 0)
                for r in range(1, ys):
                    y = lax.rem(my + r, ys)
                    arrived(i, z, mx, y, 1)
                    to_partner(i, z, mx, y, 1)
                    for q in range(1, xs):
                        x = lax.rem(mx + q, xs)
                        arrived(i, z, x, y, 1)
                        to_partner(i, z, x, y, 1)
        for copy in waits + pairs:
            copy.wait_send()
        for i in range(count):
            for z in range(zs):
                for x in range(xs):
                    for y in range(ys):
                        for h in (0, 1):
                            there = piece(i, z, x, y, 1 - mc, h)
                            remote(
                                there, there, sent.at[0], got_pair.at[i, spot(z, x, y), h], dev(mz, mx, my, 1 - mc)
                            ).wait_recv()

    chips = zs * xs * ys
    sends = count * (2 * (zs - 1) + zs * 2 * (xs - 1 + ys - 1) + 2 * zs * (xs - 1) * (ys - 1))
    return pl.pallas_call(
        kernel,
        out_shape=[jax.ShapeDtypeStruct((wide, narrow) + a.shape, a.dtype) for a in arrays],
        in_specs=[ANY] * count,
        out_specs=[ANY] * count,
        scratch_shapes=[
            pltpu.VMEM((count,) + arrays[0].shape, arrays[0].dtype),
            pltpu.SemaphoreType.DMA((count,)),
            pltpu.SemaphoreType.DMA((sends,)),
            pltpu.SemaphoreType.DMA((count, chips, 2)),
            pltpu.SemaphoreType.DMA((count * chips * 2,)),
            pltpu.SemaphoreType.DMA((count, chips, 2)),
        ],
        compiler_params=pltpu.CompilerParams(collective_id=ident, has_side_effects=True),
        name=f"gather_{ident}",
    )(*arrays)


def matmul(left_side, right_side):
    return jnp.dot(left_side, right_side, preferred_element_type=jnp.float32)


def inner_left(left_side, right_side):
    return lax.dot_general(left_side, right_side, (((0,), (0,)), ((), ())), preferred_element_type=jnp.float32)


def inner_right(left_side, right_side):
    return lax.dot_general(left_side, right_side, (((1,), (1,)), ((), ())), preferred_element_type=jnp.float32)


def silu_slope(values):
    sigmoid_val = jax.nn.sigmoid(values)
    return sigmoid_val * (1.0 + values * (1.0 - sigmoid_val))


def silu_curve(values):
    sigmoid_val = jax.nn.sigmoid(values)
    return sigmoid_val * (1.0 - sigmoid_val) * (2.0 + values * (1.0 - 2.0 * sigmoid_val))


class Lane:
    def __init__(self):
        narrow = lax.axis_size("narrow")
        self.ys = narrow // 2
        self.chips = LANE_WIDE * self.ys
        wide_pos, narrow_pos = lax.axis_index("wide"), lax.axis_index("narrow")
        self.base = lax.div(wide_pos, LANE_WIDE) * LANE_WIDE
        self.colour = lax.rem(narrow_pos, 2)
        self.chip = lax.rem(wide_pos, LANE_WIDE) * self.ys + lax.div(narrow_pos, 2)
        self.partner = (wide_pos, narrow_pos + 1 - 2 * self.colour)

    def other(self, step):
        return lax.rem(self.chip + step, self.chips)

    def device(self, chip):
        return self.base + lax.div(chip, self.ys), 2 * lax.rem(chip, self.ys) + self.colour

    def greet(self):
        barrier = pltpu.get_barrier_semaphore()
        for step in range(1, self.chips):
            pl.semaphore_signal(barrier, inc=1, device_id=self.device(self.other(step)), device_id_type=MESH)
        pl.semaphore_signal(barrier, inc=1, device_id=self.partner, device_id_type=MESH)
        pl.semaphore_wait(barrier, self.chips)


class Scatter:
    def __init__(self, lane, part, pair, half, got, sems):
        self.lane, self.part, self.pair, self.half, self.got = lane, part, pair, half, got
        self.pair_send, self.pair_recv, self.send, self.recv = sems

    @staticmethod
    def scratch(chips, rows, width):
        return [
            pltpu.VMEM((2, chips, rows, width), bf16),
            pltpu.VMEM((chips, rows, width), bf16),
            pltpu.VMEM((chips, rows, width), bf16),
            pltpu.VMEM((chips, rows, width), bf16),
            pltpu.SemaphoreType.DMA((1,)),
            pltpu.SemaphoreType.DMA((1,)),
            pltpu.SemaphoreType.DMA((chips,)),
            pltpu.SemaphoreType.DMA((chips,)),
        ]

    @classmethod
    def of(cls, lane, refs):
        return cls(lane, *refs[:4], refs[4:8])

    def pair_copy(self):
        return remote(
            self.part.at[1 - self.lane.colour],
            self.pair,
            self.pair_send.at[0],
            self.pair_recv.at[0],
            self.lane.partner,
        )

    def start_pair(self):
        self.pair_copy().start()

    def take_pair(self):
        self.pair_copy().wait()
        self.half[...] = (
            self.part[self.lane.colour].astype(f32) + self.pair[...].astype(f32)
        ).astype(bf16)

    def copy_to(self, step):
        chip = self.lane.other(step)
        return remote(
            self.half.at[chip],
            self.got.at[self.lane.chip],
            self.send.at[step],
            self.recv.at[self.lane.chip],
            self.lane.device(chip),
        )

    def start_sends(self):
        for step in range(1, self.lane.chips):
            self.copy_to(step).start()

    def total(self):
        result = self.half[self.lane.chip].astype(f32)
        for step in range(1, self.lane.chips):
            chip = self.lane.other(step)
            remote(
                self.got.at[chip], self.got.at[chip], self.send.at[step], self.recv.at[chip], self.lane.device(chip)
            ).wait_recv()
            result = result + self.got[chip].astype(f32)
        return result

    def wait_sends(self):
        for step in range(1, self.lane.chips):
            self.copy_to(step).wait_send()


class Spread:
    def __init__(self, lane, whole, sems):
        self.lane, self.whole = lane, whole
        self.send, self.recv, self.pair_send, self.pair_recv = sems

    @staticmethod
    def scratch(chips, rows, width):
        return [pltpu.VMEM((2, chips, rows, width), bf16)] + [pltpu.SemaphoreType.DMA((chips,))] * 4

    @classmethod
    def of(cls, lane, refs):
        return cls(lane, refs[0], refs[1:5])

    def mine(self):
        return self.whole.at[self.lane.colour, self.lane.chip]

    def copy_to(self, step):
        return remote(
            self.mine(),
            self.mine(),
            self.send.at[step],
            self.recv.at[self.lane.chip],
            self.lane.device(self.lane.other(step)),
        )

    def pair_copy(self, chip, colour):
        place = self.whole.at[colour, chip]
        return remote(place, place, self.pair_send.at[chip], self.pair_recv.at[chip], self.lane.partner)

    def run(self):
        lane = self.lane
        for step in range(1, lane.chips):
            self.copy_to(step).start()
        self.pair_copy(lane.chip, lane.colour).start()
        for step in range(1, lane.chips):
            chip = lane.other(step)
            place = self.whole.at[lane.colour, chip]
            remote(place, place, self.send.at[step], self.recv.at[chip], lane.device(chip)).wait_recv()
            self.pair_copy(chip, lane.colour).start()
        for chip in range(lane.chips):
            self.pair_copy(chip, 1 - lane.colour).wait_recv()
        for step in range(1, lane.chips):
            self.copy_to(step).wait_send()
        for chip in range(lane.chips):
            self.pair_copy(chip, lane.colour).wait_send()


def chain_forward(keys, queries, values, gates, first_init, second_init, ident):
    turns, blocks, span, block = keys.shape
    width, hidden = first_init.shape
    rows = values.shape[1]
    chips = LANE_WIDE * (lax.axis_size("narrow") // 2)
    n_scatter = len(Scatter.scratch(1, 8, 128))
    n_spread = len(Spread.scratch(1, 8, 128))

    def kernel(*refs):
        keys_hbm, queries_hbm, values_hbm, gates_ref, first_hbm, second_hbm = refs[:6]
        recalled_hbm, s1_hbm, s2_hbm, m1_hbm, m2_hbm, g1_hbm, g2_hbm, err_hbm, small_hbm = refs[6:15]
        rest = refs[15:]
        kbuf, qbuf, vbuf, i1, i2, s1, s2, m1, m2, g1, g2, low1, low2, small, khid, rec = rest[:16]
        in_sem, out_sem, init_sem = rest[16:19]
        rest = rest[19:]
        lane = Lane()
        lookup = Scatter.of(lane, rest[:n_scatter])
        recall = Scatter.of(lane, rest[n_scatter : 2 * n_scatter])
        error = Spread.of(lane, rest[2 * n_scatter :])

        def loads(turn, slot):
            return [
                pltpu.make_async_copy(keys_hbm.at[turn], kbuf.at[slot], in_sem.at[slot, 0]),
                pltpu.make_async_copy(queries_hbm.at[turn], qbuf.at[slot], in_sem.at[slot, 1]),
                pltpu.make_async_copy(values_hbm.at[turn], vbuf.at[slot], in_sem.at[slot, 2]),
            ]

        def state_saves(turn):
            return [
                pltpu.make_async_copy(source, target.at[turn], out_sem.at[i])
                for i, (source, target) in enumerate(((s1, s1_hbm), (s2, s2_hbm), (m1, m1_hbm), (m2, m2_hbm)))
            ]

        def other_saves(turn):
            return [
                pltpu.make_async_copy(source, target.at[turn], out_sem.at[4 + i])
                for i, (source, target) in enumerate(
                    ((g1, g1_hbm), (g2, g2_hbm), (error.whole, err_hbm), (small, small_hbm))
                )
            ]

        def rec_save(turn):
            return pltpu.make_async_copy(rec, recalled_hbm.at[turn], out_sem.at[8])

        inits = [
            pltpu.make_async_copy(first_hbm, i1, init_sem.at[0]),
            pltpu.make_async_copy(second_hbm, i2, init_sem.at[1]),
        ]
        for copy in inits + loads(0, 0):
            copy.start()
        lane.greet()
        for copy in inits:
            copy.wait()
        low1[...] = i1[...]
        low2[...] = i2[...]
        s1[...] = i1[...].astype(f32)
        s2[...] = i2[...].astype(f32)
        m1[...] = jnp.zeros_like(m1)
        m2[...] = jnp.zeros_like(m2)

        def finish_recall(turn):
            rec[...] = recall.total().astype(bf16)
            recall.wait_sends()
            rec_save(turn).start()

        def lookup_blocks(buf, slot):
            total = matmul(buf[slot, 0], low1[pl.ds(0, block), :])
            for b in range(1, blocks):
                total = total + matmul(buf[slot, b], low1[pl.ds(b * block, block), :])
            return total

        def turn_body(turn, carry):
            slot = lax.rem(turn, 2)

            @pl.when(turn + 1 < turns)
            def _():
                for copy in loads(turn + 1, 1 - slot):
                    copy.start()

            for copy in state_saves(turn):
                copy.start()
            for copy in loads(turn, slot):
                copy.wait()
            key_pre = lookup_blocks(kbuf, slot)
            small[0] = key_pre
            khid[...] = (key_pre * jax.nn.sigmoid(key_pre)).astype(bf16)
            lookup.part[...] = matmul(khid[...], low2[...]).astype(bf16).reshape(2, chips, rows, width)
            lookup.start_pair()

            @pl.when(turn > 0)
            def _():
                finish_recall(turn - 1)

            query_pre = lookup_blocks(qbuf, slot)
            small[1] = query_pre
            query_hidden = (query_pre * jax.nn.sigmoid(query_pre)).astype(bf16)
            recall.part[...] = matmul(query_hidden, low2[...]).astype(bf16).reshape(2, chips, rows, width)
            recall.start_pair()

            lookup.take_pair()
            lookup.start_sends()
            recall.take_pair()
            total = lookup.total()
            error.whole[lane.colour, lane.chip] = ((total - vbuf[slot].astype(f32)) / span).astype(bf16)
            error.run()
            lookup.wait_sends()
            recall.start_sends()

            err = error.whole[...].reshape(span, width)
            g2[...] = inner_left(khid[...], err)
            hidden_grad = inner_right(err, low2[...])
            small[2] = hidden_grad
            slope = (hidden_grad * silu_slope(small[0])).astype(bf16)
            for b in range(blocks):
                g1[pl.ds(b * block, block), :] = inner_left(kbuf[slot, b], slope)
            saves = other_saves(turn)
            for copy in saves:
                copy.start()
            decay, moment, rate, reset = (gates_ref[turn, i] for i in range(4))
            for copy in state_saves(turn):
                copy.wait()
            for s, m, g, init, low in ((s1, m1, g1, i1, low1), (s2, m2, g2, i2, low2)):
                moment_new = moment * m[...] - rate * g[...]
                state_new = (1.0 - decay) * s[...] + moment_new
                state_new = reset * init[...].astype(f32) + (1.0 - reset) * state_new
                m[...] = (1.0 - reset) * moment_new
                s[...] = state_new
                low[...] = state_new.astype(bf16)
            for copy in saves:
                copy.wait()

            @pl.when(turn > 0)
            def _():
                rec_save(turn - 1).wait()

            return carry

        lax.fori_loop(0, turns, turn_body, 0)
        finish_recall(turns - 1)
        rec_save(turns - 1).wait()

    state = [(width, hidden), (hidden, width)]
    out_shape = (
        [jax.ShapeDtypeStruct((turns, rows, width), bf16)]
        + [jax.ShapeDtypeStruct((turns,) + s, f32) for s in state * 3]
        + [
            jax.ShapeDtypeStruct((turns, 2, chips, rows, width), bf16),
            jax.ShapeDtypeStruct((turns, 3, span, hidden), f32),
        ]
    )
    scratch = (
        [pltpu.VMEM((2, blocks, span, block), bf16)] * 2
        + [pltpu.VMEM((2, rows, width), bf16)]
        + [pltpu.VMEM(s, bf16) for s in state]
        + [pltpu.VMEM(s, f32) for s in state * 3]
        + [pltpu.VMEM(s, bf16) for s in state]
        + [
            pltpu.VMEM((3, span, hidden), f32),
            pltpu.VMEM((span, hidden), bf16),
            pltpu.VMEM((rows, width), bf16),
            pltpu.SemaphoreType.DMA((2, 3)),
            pltpu.SemaphoreType.DMA((9,)),
            pltpu.SemaphoreType.DMA((2,)),
        ]
        + Scatter.scratch(chips, rows, width) * 2
        + Spread.scratch(chips, rows, width)
    )
    return pl.pallas_call(
        kernel,
        out_shape=out_shape,
        in_specs=[ANY] * 3 + [pl.BlockSpec(memory_space=pltpu.SMEM)] + [ANY] * 2,
        out_specs=[ANY] * len(out_shape),
        scratch_shapes=scratch,
        compiler_params=pltpu.CompilerParams(
            collective_id=ident, has_side_effects=True, vmem_limit_bytes=60 * 1024 * 1024
        ),
        cost_estimate=pl.CostEstimate(
            flops=turns * 7 * 2 * span * width * hidden, bytes_accessed=turns * 12 * 2**20, transcendentals=0
        ),
        name="chain_forward",
    )(keys, queries, values, gates, first_init, second_init)


def chain_backward(keys, queries, recall_grads, saved, gates, ident):
    s1_all, s2_all, m1_all, m2_all, g1_all, g2_all, err_all, small_all = saved
    turns, blocks, span, block = keys.shape
    width, hidden = s1_all.shape[1:]
    chips, rows = err_all.shape[2:4]
    n_scatter = len(Scatter.scratch(1, 8, 128))

    def kernel(*refs):
        ins, gates_ref = refs[:11], refs[11]
        qcot_hbm, kcot_hbm, vcot_hbm, sums1_ref, sums2_ref, mg1_hbm, mg2_hbm = refs[12:19]
        rest = refs[19:]
        bufs, rest = rest[:11], rest[11:]
        kbuf, qbuf, rbuf, s1, s2, m1, m2, g1, g2, errs, small = bufs
        cf, cs, cmf, cms, w1, w2, a1, a2, c1, c2, low1, low2, dh, khid, qpl, qhid, sg, qsave, ksave, vsave = rest[:20]
        in_sem, out_sem, end_sem = rest[20:23]
        rest = rest[23:]
        lane = Lane()
        lookup = Scatter.of(lane, rest[:n_scatter])
        qstream = Scatter.of(lane, rest[n_scatter : 2 * n_scatter])
        kstream = Scatter.of(lane, rest[2 * n_scatter : 3 * n_scatter])
        spread = Spread.of(lane, rest[3 * n_scatter :])

        def loads(turn, slot):
            return [
                pltpu.make_async_copy(source.at[turn], target.at[slot], in_sem.at[slot, i])
                for i, (source, target) in enumerate(zip(ins, bufs))
            ]

        for copy in loads(turns - 1, 0):
            copy.start()
        lane.greet()
        for ref in (cf, cs, cmf, cms, a1, a2):
            ref[...] = jnp.zeros_like(ref)

        def qout(turn):
            return pltpu.make_async_copy(qsave, qcot_hbm.at[turn], out_sem.at[0])

        def kout(turn):
            return pltpu.make_async_copy(ksave, kcot_hbm.at[turn], out_sem.at[1])

        def vout(turn):
            return pltpu.make_async_copy(vsave, vcot_hbm.at[turn], out_sem.at[2])

        def finish(stream, save, out):
            save[...] = stream.total().astype(bf16)
            stream.wait_sends()
            out.start()

        def body(step, carry):
            turn = turns - 1 - step
            slot = lax.rem(step, 2)

            @pl.when(step + 1 < turns)
            def _():
                for copy in loads(turn - 1, 1 - slot):
                    copy.start()

            for copy in loads(turn, slot):
                copy.wait()
            decay, moment, rate, reset = (gates_ref[turn, i] for i in range(4))
            c1[...] = (-rate * (cmf[...] + cf[...])).astype(bf16)
            c2[...] = (-rate * (cms[...] + cs[...])).astype(bf16)
            low1[...] = s1[slot].astype(bf16)
            low2[...] = s2[slot].astype(bf16)
            slope_grad = matmul(kbuf[slot, 0], c1[pl.ds(0, block), :])
            for b in range(1, blocks):
                slope_grad = slope_grad + matmul(kbuf[slot, b], c1[pl.ds(b * block, block), :])
            sg[...] = slope_grad
            key_pre = small[slot, 0]
            khid[...] = (key_pre * jax.nn.sigmoid(key_pre)).astype(bf16)
            dh[...] = (slope_grad * silu_slope(key_pre)).astype(bf16)
            lookup.part[...] = (
                (matmul(khid[...], c2[...]) + matmul(dh[...], low2[...])).astype(bf16).reshape(2, chips, rows, width)
            )
            lookup.start_pair()

            @pl.when(step > 0)
            def _():
                finish(qstream, qsave, qout(turn + 1))

            @pl.when(step > 1)
            def _():
                finish(kstream, ksave, kout(turn + 2))

            @pl.when(step > 0)
            def _():
                kstream.take_pair()

            query_pre = small[slot, 1]
            back = inner_right(rbuf[slot, 0], low2[:, pl.ds(0, block)])
            for b in range(1, blocks):
                back = back + inner_right(rbuf[slot, b], low2[:, pl.ds(b * block, block)])
            qpl[...] = (back * silu_slope(query_pre)).astype(bf16)
            qhid[...] = (query_pre * jax.nn.sigmoid(query_pre)).astype(bf16)
            qstream.part[...] = inner_right(qpl[...], low1[...]).astype(bf16).reshape(2, chips, rows, width)
            qstream.start_pair()
            lookup.take_pair()
            lookup.start_sends()
            qstream.take_pair()
            for b in range(blocks):
                w1[pl.ds(b * block, block), :] = inner_left(qbuf[slot, b], qpl[...])
                w2[:, pl.ds(b * block, block)] = inner_left(qhid[...], rbuf[slot, b])

            def sums(first_a, first_b, second_a, second_b, row):
                sums1_ref[turn, pl.ds(row, 1), :] = jnp.sum(first_a * first_b, axis=0, keepdims=True)
                sums2_ref[turn, pl.ds(row, 1), :] = jnp.sum(second_a * second_b, axis=0, keepdims=True)

            sums(cf[...], s1[slot], cs[...], s2[slot], 0)
            sums(cmf[...] + cf[...], m1[slot], cms[...] + cs[...], m2[slot], 1)
            sums(cmf[...] + cf[...], g1[slot], cms[...] + cs[...], g2[slot], 2)
            total = lookup.total()
            mine = (total / span).astype(bf16)
            spread.whole[lane.colour, lane.chip] = mine

            @pl.when(step > 0)
            def _():
                vout(turn + 1).wait()
                qout(turn + 1).wait()

            @pl.when(step > 1)
            def _():
                kout(turn + 2).wait()

            vsave[...] = mine
            vout(turn).start()
            spread.run()
            lookup.wait_sends()
            qstream.start_sends()

            @pl.when(step > 0)
            def _():
                kstream.start_sends()

            out = spread.whole[...].reshape(span, width)
            err = errs[slot].reshape(span, width)
            hidden_back = inner_right(err, c2[...]) + inner_right(out, low2[...])
            key_pre = small[slot, 0]
            hidden_grad = small[slot, 2]
            slope = silu_slope(key_pre)
            kpl = (hidden_back * slope + sg[...] * hidden_grad * silu_curve(key_pre)).astype(bf16)
            slope_low = (hidden_grad * slope).astype(bf16)
            kstream.part[...] = (
                (inner_right(kpl, low1[...]) + inner_right(slope_low, c1[...]))
                .astype(bf16)
                .reshape(2, chips, rows, width)
            )
            kstream.start_pair()
            for b in range(blocks):
                w1[pl.ds(b * block, block), :] += inner_left(kbuf[slot, b], kpl)
            w2[...] += inner_left(dh[...], err) + inner_left(khid[...], out)
            for c, m, w, acc in ((cf, cmf, w1, a1), (cs, cms, w2, a2)):
                both = m[...] + c[...]
                grad = (1.0 - decay) * c[...] + w[...]
                acc[...] += reset * grad
                c[...] = (1.0 - reset) * grad
                m[...] = (1.0 - reset) * (moment * both)
            return carry

        lax.fori_loop(0, turns, body, 0)
        finish(qstream, qsave, qout(0))
        if turns > 1:
            finish(kstream, ksave, kout(1))
            kout(1).wait()
        kstream.take_pair()
        tail = Scatter(
            lane,
            kstream.part,
            kstream.pair,
            kstream.half,
            lookup.got,
            (kstream.pair_send, kstream.pair_recv, lookup.send, lookup.recv),
        )
        tail.start_sends()
        finish(tail, ksave, kout(0))
        ends = [
            pltpu.make_async_copy(a1, mg1_hbm, end_sem.at[0]),
            pltpu.make_async_copy(a2, mg2_hbm, end_sem.at[1]),
        ]
        for copy in ends:
            copy.start()
        for copy in ends + [qout(0), kout(0), vout(0)]:
            copy.wait()

    state = [(width, hidden), (hidden, width)]
    buffers = (
        [((blocks, span, block), bf16)] * 3
        + [(s, f32) for s in state * 3]
        + [((2, chips, rows, width), bf16), ((3, span, hidden), f32)]
    )
    out_shape = (
        [jax.ShapeDtypeStruct((turns, rows, width), bf16)] * 3
        + [jax.ShapeDtypeStruct((turns, 8, hidden), f32), jax.ShapeDtypeStruct((turns, 8, width), f32)]
        + [jax.ShapeDtypeStruct(s, f32) for s in state]
    )
    scratch = (
        [pltpu.VMEM((2,) + s, t) for s, t in buffers]
        + [pltpu.VMEM(s, f32) for s in state * 4]
        + [pltpu.VMEM(s, bf16) for s in state * 2]
        + [pltpu.VMEM((span, hidden), bf16)] * 4
        + [pltpu.VMEM((span, hidden), f32)]
        + [pltpu.VMEM((rows, width), bf16)] * 3
        + [
            pltpu.SemaphoreType.DMA((2, 11)),
            pltpu.SemaphoreType.DMA((3,)),
            pltpu.SemaphoreType.DMA((2,)),
        ]
        + Scatter.scratch(chips, rows, width) * 3
        + Spread.scratch(chips, rows, width)
    )
    vmem = pl.BlockSpec(memory_space=pltpu.VMEM)
    return pl.pallas_call(
        kernel,
        out_shape=out_shape,
        in_specs=[ANY] * 11 + [pl.BlockSpec(memory_space=pltpu.SMEM)],
        out_specs=[ANY] * 3 + [vmem] * 2 + [ANY] * 2,
        scratch_shapes=scratch,
        compiler_params=pltpu.CompilerParams(
            collective_id=ident, has_side_effects=True, vmem_limit_bytes=62 * 1024 * 1024
        ),
        cost_estimate=pl.CostEstimate(
            flops=turns * 14 * 2 * span * width * hidden, bytes_accessed=turns * 16 * 2**20, transcendentals=0
        ),
        name="chain_backward",
    )(keys, queries, recall_grads, s1_all, s2_all, m1_all, m2_all, g1_all, g2_all, err_all, small_all, gates)


def from_behind(value, axis, steps):
    count = lax.axis_size(axis)
    first, last = (max(0, -steps), min(count, count - steps))
    return lax.ppermute(value, axis, [(source, source + steps) for source in range(first, last)])


def split_heads(values, head_size):
    return values.reshape(values.shape[:-1] + (values.shape[-1] // head_size, head_size))


def head_norm(values, head_size):
    shaped = split_heads(values, head_size)
    factor = lax.rsqrt(jnp.sum(shaped * shaped, axis=-1, keepdims=True) + eps_head)
    return (shaped * factor).reshape(values.shape)


def head_norm_back(values, upstream, head_size):
    shaped = split_heads(values, head_size)
    grad_shaped = split_heads(upstream, head_size)
    factor = lax.rsqrt(jnp.sum(shaped * shaped, axis=-1, keepdims=True) + eps_head)
    normed = shaped * factor
    inner_sum = jnp.sum(normed * grad_shaped, axis=-1, keepdims=True)
    return (factor * (grad_shaped - normed * inner_sum)).reshape(values.shape)


def rms_back(scaled, factor, upstream):
    return factor * (upstream - scaled * jnp.mean(upstream * scaled, axis=-1, keepdims=True))


def body(
    tokens,
    cotangent,
    seq_spans,
    w_query,
    w_key,
    w_value,
    conv_kernel,
    persistent,
    norm_gain,
    rate_proj,
    out_gate,
    out_proj,
    memory_in,
    memory_out,
    ffn_gain,
    ffn_gate,
    ffn_up,
    ffn_down,
):
    wide, narrow = lax.axis_size("wide"), lax.axis_size("narrow")
    devices = wide * narrow
    wide_pos, narrow_pos = lax.axis_index("wide"), lax.axis_index("narrow")
    span, width = tokens.shape
    taps = conv_kernel.shape[0]
    persist_count = persistent.shape[1]
    local_width = out_gate.shape[1]
    own_rows = span // narrow
    lanes = wide // LANE_WIDE
    chips = LANE_WIDE * narrow // 2
    shards = 2 * chips
    shard_rows = span // shards
    hidden = memory_in.shape[1] // LANE_WIDE
    score_scale = math.sqrt(HEAD)

    def shard_of(tw, tn):
        return lax.rem(tn, 2) * chips + lax.rem(tw, LANE_WIDE) * (narrow // 2) + lax.div(tn, 2)

    long_turns = min(6, wide * 5 // 8)
    turns = max(long_turns, wide - long_turns)
    seq_ends = jnp.cumsum(seq_spans)
    seq_starts = seq_ends - seq_spans
    long_start = seq_starts[jnp.argmax(seq_spans)]
    order = jnp.arange(wide, dtype=jnp.int32)
    span_first = jnp.any(seq_starts[None, :] == order[:, None], axis=1)
    is_first = span_first[wide_pos]
    in_long = (order >= long_start) & (order < long_start + long_turns)
    lane_of = jnp.where(in_long, 0, 1)
    turn_of = jnp.where(in_long, order - long_start, jnp.where(order < long_start, order, order - long_turns))
    lane_pos = wide_pos // LANE_WIDE
    turn_order = jnp.arange(turns, dtype=jnp.int32)
    rest_order = jnp.where(turn_order < long_start, turn_order, turn_order + long_turns)
    lane_spans = jnp.clip(jnp.where(lane_pos == 0, long_start + turn_order, rest_order), 0, wide - 1)
    lane_count = jnp.where(lane_pos == 0, long_turns, jnp.where(lane_pos == 1, wide - long_turns, 0))
    lane_valid = turn_order < lane_count
    lane_first = span_first[lane_spans] | ~lane_valid

    ffn_gate_cols = lax.all_gather(ffn_gate, "wide", axis=0, tiled=True)
    ffn_up_cols = lax.all_gather(ffn_up, "wide", axis=0, tiled=True)
    ffn_down_rows = lax.all_gather(ffn_down, "wide", axis=1, tiled=True)
    smalls = [conv_kernel, persistent, norm_gain, ffn_gain, rate_proj]
    small_sizes = [a.size for a in smalls]
    packed = jnp.concatenate([a.reshape(-1) for a in smalls])
    padded = -(-packed.size // 2048) * 2048
    packed = jnp.pad(packed, (0, padded - packed.size)).reshape(-1, 128)

    def by_narrow(a):
        return a.reshape(a.shape[0], narrow, local_width).transpose(1, 0, 2)

    small_all, wq, wk, wv = exchange(
        [(packed, None)] + [(by_narrow(a), lambda tw, tn: tn) for a in (w_query, w_key, w_value)], "all", 1
    )
    memory_cols = memory_in.reshape(memory_in.shape[0], LANE_WIDE, hidden).transpose(1, 0, 2)
    memory_rows = memory_out.reshape(LANE_WIDE, hidden, memory_out.shape[1])
    gate_all, proj_all, first_all, second_all = exchange(
        [
            (out_gate, None),
            (out_proj, None),
            (memory_cols, lambda tw, tn: lax.rem(tw, LANE_WIDE)),
            (memory_rows, lambda tw, tn: lax.rem(tw, LANE_WIDE)),
        ],
        "wide",
        2,
    )
    gate_cols = gate_all.reshape(width, local_width)
    proj_rows = proj_all.transpose(1, 0, 2).reshape(local_width, width)
    first_init = first_all.reshape(width, hidden)
    second_init = second_all.transpose(1, 0, 2).reshape(hidden, width)
    small_all = small_all.reshape(devices, padded)
    pieces, at = [], 0
    for a, size in zip(smalls, small_sizes):
        pieces.append(small_all[:, at : at + size].reshape((devices,) + a.shape))
        at += size
    kernel_all = pieces[0].transpose(1, 0, 2).reshape(taps, 3, width)
    persist_all = pieces[1].transpose(1, 2, 0, 3).reshape(2, persist_count, width)
    gain_one = pieces[2].reshape(width).astype(f32)
    gain_two = pieces[3].reshape(width).astype(f32)
    rate_f = pieces[4].reshape(width, 3).astype(f32)
    col_offset = narrow_pos * local_width

    def own_cols(values, axis):
        return lax.dynamic_slice_in_dim(values, col_offset, local_width, axis)

    def own_part(values):
        return lax.dynamic_slice_in_dim(values, narrow_pos * own_rows, own_rows, 0)

    kernel_f = own_cols(kernel_all, 2).reshape(taps, 3 * local_width).astype(f32)
    persist_f = own_cols(persist_all, 2).astype(f32)
    qkv_weights = jnp.concatenate([a.reshape(width, local_width) for a in (wq, wk, wv)], 1)

    inputs_f = tokens.astype(f32)
    first_factor = lax.rsqrt(jnp.mean(inputs_f * inputs_f, axis=-1, keepdims=True) + eps_norm)
    first_scaled = inputs_f * first_factor
    normed = first_scaled * gain_one
    normed_low = normed.astype(bf16)
    projected = matmul(normed_low, qkv_weights)
    tail_rows = from_behind(projected[span - taps + 1 :].astype(bf16), "wide", 1).astype(f32)
    extended = jnp.concatenate([jnp.where(is_first, 0.0, tail_rows), projected], 0)
    mixed_conv = kernel_f[0] * projected
    for offset in range(1, taps):
        start_row = taps - 1 - offset
        mixed_conv = mixed_conv + kernel_f[offset] * extended[start_row : start_row + span]
    activated = jax.nn.silu(mixed_conv)
    query_act = activated[:, :local_width]
    key_act = activated[:, local_width : 2 * local_width]
    query_low = head_norm(query_act, HEAD).astype(bf16)
    key_low = head_norm(key_act, HEAD).astype(bf16)
    value_low = activated[:, 2 * local_width :].astype(bf16)
    span_mean = jnp.mean(normed, axis=0)
    gate_scale = jnp.array([decay_top, moment_top, learn_top], f32)
    gate_sig = jax.nn.sigmoid(jnp.sum(span_mean[:, None] * rate_f, axis=0))
    gate_tile = jnp.broadcast_to(jnp.pad(gate_sig * gate_scale, (0, 125))[None], (8, 128))

    key_all, query_all = gather_all([key_low, query_low], 3)
    value_all, gate_got = exchange(
        [(value_low.reshape(shards, shard_rows, local_width), shard_of), (gate_tile, None)], "all", 4
    )
    value_all = value_all.reshape(wide, narrow, shard_rows, local_width).transpose(0, 2, 1, 3)
    value_all = value_all.reshape(wide, shard_rows, width)
    gate_rows = gate_got[::narrow, 0, :3]
    lane_gates = gate_rows[lane_spans]
    first_f = lane_first.astype(f32)
    next_first = jnp.concatenate([first_f[1:], jnp.ones((1,), f32)])
    keys_lane = key_all[lane_spans]
    queries_lane = query_all[lane_spans]
    chain = chain_forward(
        keys_lane,
        queries_lane,
        value_all[lane_spans],
        jnp.concatenate([lane_gates, next_first[:, None]], 1),
        first_init,
        second_init,
        5,
    )
    recalled_lane, saved = chain[0], chain[1:]

    def by_span(lane_rows):
        spans = lane_rows[turn_of]
        return spans.reshape(wide, shard_rows, narrow, local_width).transpose(0, 2, 1, 3)

    def from_lane(got):
        got = got.reshape(lanes, LANE_WIDE, narrow // 2, 2, shard_rows, local_width)
        own = lax.dynamic_index_in_dim(got, lane_of[wide_pos], 0, keepdims=False)
        return own.transpose(2, 0, 1, 3, 4).reshape(span, local_width)

    recalled_got = exchange(
        [
            (
                by_span(recalled_lane).reshape(devices, shard_rows, local_width),
                lambda tw, tn: tw * narrow + tn,
            )
        ],
        "all",
        6,
    )[0]
    recall_low = from_lane(recalled_got)
    recall_own = recall_low.astype(f32)

    keys_all = jnp.concatenate(
        [head_norm(persist_f[0], HEAD).astype(bf16), head_norm(recall_own, HEAD).astype(bf16), key_low], 0
    )
    values_all = jnp.concatenate([persist_f[1].astype(bf16), recall_low, value_low], 0)
    query_heads = split_heads(query_low, HEAD)
    key_heads = split_heads(keys_all, HEAD)
    value_heads = split_heads(values_all, HEAD)
    key_total = keys_all.shape[0]
    row_index = lax.broadcasted_iota(jnp.int32, (span, key_total), 0)
    col_index = lax.broadcasted_iota(jnp.int32, (span, key_total), 1)
    allowed = (col_index < persist_count + span) | (col_index - persist_count - span <= row_index)

    def score_block():
        raw_scores = (
            jnp.einsum("thd,jhd->htj", query_heads, key_heads, preferred_element_type=f32) * score_scale
        )
        return jnp.where(allowed[None], raw_scores, masked_score)

    scores = score_block()
    row_top = jnp.max(scores, axis=-1, keepdims=True)
    exponent = jnp.exp(scores - row_top)
    total_sum = jnp.sum(exponent, axis=-1, keepdims=True)
    log_total = row_top + jnp.log(total_sum)
    weights_low = (exponent / total_sum).astype(bf16)
    attended = jnp.einsum("htj,jhd->thd", weights_low, value_heads, preferred_element_type=f32).reshape(
        span, local_width
    )
    gate_pre = matmul(normed_low, gate_cols)
    gate_sigmoid = jax.nn.sigmoid(gate_pre)
    gated_low = (attended * gate_sigmoid).astype(bf16)

    def rows_of(parts, ident):
        got = exchange(
            [(a.astype(bf16).reshape(narrow, own_rows, width), lambda tw, tn: tn) for a in parts], "narrow", ident
        )
        return [jnp.sum(a.astype(f32), axis=0) for a in got]

    def all_rows(parts, ident):
        got = exchange([(a, None) for a in parts], "narrow", ident)
        return [a.reshape(span, width) for a in got]

    inputs_own = own_part(inputs_f)
    middle = inputs_own + rows_of([matmul(gated_low, proj_rows)], 7)[0]
    second_factor = lax.rsqrt(jnp.mean(middle * middle, axis=-1, keepdims=True) + eps_norm)
    second_scaled = middle * second_factor
    normed_two = all_rows([(second_scaled * gain_two).astype(bf16)], 8)[0]
    gate_val = matmul(normed_two, ffn_gate_cols)
    up_val = matmul(normed_two, ffn_up_cols)
    gate_silu = jax.nn.silu(gate_val)
    hidden_ffn = (gate_silu * up_val).astype(bf16)
    ffn_part = matmul(hidden_ffn, ffn_down_rows)
    down_grad = inner_left(cotangent, hidden_ffn)
    hidden_grad_ffn = inner_right(cotangent, ffn_down_rows)
    gate_sig_ffn = jax.nn.sigmoid(gate_val)
    gate_grad_low = (
        hidden_grad_ffn * up_val * gate_sig_ffn * (1.0 + gate_val * (1.0 - gate_sig_ffn))
    ).astype(bf16)
    up_grad_low = (hidden_grad_ffn * gate_silu).astype(bf16)
    ffn_gate_grad = inner_left(normed_two, gate_grad_low)
    ffn_up_grad = inner_left(normed_two, up_grad_low)
    normed_two_part = inner_right(gate_grad_low, ffn_gate_cols) + inner_right(up_grad_low, ffn_up_cols)

    def scatter_wide(grad):
        return lax.psum_scatter(grad.astype(bf16), "wide", scatter_dimension=0, tiled=True).astype(f32)

    ffn_gate_out, ffn_up_out, ffn_down_out = [scatter_wide(a) for a in (ffn_gate_grad, ffn_up_grad, down_grad)]
    ffn_rows, normed_two_grad = rows_of([ffn_part, normed_two_part], 9)
    output_own = (middle + ffn_rows).astype(bf16)
    gain_two_part = jnp.sum(normed_two_grad * second_scaled, axis=0)
    upstream = own_part(cotangent).astype(f32)
    middle_grad = upstream + rms_back(second_scaled, second_factor, normed_two_grad * gain_two)
    branch_low, output = all_rows([middle_grad.astype(bf16), output_own], 10)

    gated_grad = inner_right(branch_low, proj_rows)
    attended_grad_low = (gated_grad * gate_sigmoid).astype(bf16)
    gate_pre_low = (gated_grad * attended * gate_sigmoid * (1.0 - gate_sigmoid)).astype(bf16)
    proj_grad = inner_left(branch_low, gated_low)

    weights_again = jnp.exp(score_block() - log_total)
    grad_heads = split_heads(attended_grad_low, HEAD)
    weight_grad = jnp.einsum("thd,jhd->htj", grad_heads, value_heads, preferred_element_type=f32)
    row_delta = jnp.sum(weights_again * weight_grad, axis=-1, keepdims=True)
    score_grad_low = (weights_again * (weight_grad - row_delta)).astype(bf16)
    query_att = (
        score_scale * jnp.einsum("htj,jhd->thd", score_grad_low, key_heads, preferred_element_type=f32)
    ).reshape(span, local_width)
    keys_grad = (
        score_scale * jnp.einsum("htj,thd->jhd", score_grad_low, query_heads, preferred_element_type=f32)
    ).reshape(key_total, local_width)
    values_grad = jnp.einsum(
        "htj,thd->jhd", weights_again.astype(bf16), grad_heads, preferred_element_type=f32
    ).reshape(key_total, local_width)
    recall_end = persist_count + span
    persist_part = jnp.stack(
        [head_norm_back(persist_f[0], keys_grad[:persist_count], HEAD), values_grad[:persist_count]]
    )
    recall_grad_low = (
        head_norm_back(recall_own, keys_grad[persist_count:recall_end], HEAD)
        + values_grad[persist_count:recall_end]
    ).astype(bf16)

    recall_all = gather_all([recall_grad_low], 11)[0]
    recall_lane = jnp.where(lane_valid[:, None, None, None], recall_all[lane_spans], jnp.zeros((), bf16))
    qcot, kcot, vcot, sums1, sums2, first_grad, second_grad = chain_backward(
        keys_lane,
        queries_lane,
        recall_lane,
        saved,
        jnp.concatenate([lane_gates, first_f[:, None]], 1),
        12,
    )
    lane_sums = jnp.sum(sums1[:, :3], axis=2) + jnp.sum(sums2[:, :3], axis=2)
    span_sums = jnp.where((lane_of == lane_pos)[:, None], lane_sums[turn_of], 0.0)
    sums_tile = jnp.pad(span_sums, ((0, 0), (0, 125)))
    cots = jnp.stack([by_span(a) for a in (qcot, kcot, vcot)], 2)
    cots_got, sums_got = exchange(
        [
            (cots.reshape(devices, 3, shard_rows, local_width), lambda tw, tn: tw * narrow + tn),
            (sums_tile, None),
        ],
        "all",
        13,
    )
    query_mem, key_mem, value_mem = [from_lane(cots_got[:, i]).astype(f32) for i in range(3)]
    gate_sums = jnp.sum(sums_got[:, :, :3], axis=0)[wide_pos] * jnp.array([-1.0, 1.0, -1.0], f32)
    first_got, second_got = exchange(
        [
            (first_grad.astype(bf16).reshape(wide, width // wide, hidden), lambda tw, tn: tw),
            (
                second_grad.astype(bf16).reshape(hidden, wide, width // wide).transpose(1, 0, 2),
                lambda tw, tn: tw,
            ),
        ],
        "wide",
        14,
    )

    def over_lanes(got):
        return jnp.sum(got.reshape((lanes, LANE_WIDE) + got.shape[1:]).astype(f32), axis=0)

    first_out = over_lanes(first_got).transpose(1, 0, 2).reshape(width // wide, LANE_WIDE * hidden)
    second_out = over_lanes(second_got).reshape(LANE_WIDE * hidden, width // wide)

    logit_grad = gate_sums * gate_scale * gate_sig * (1.0 - gate_sig)
    rate_part = span_mean[:, None] * logit_grad[None, :]
    gate_row = jnp.sum(rate_f * logit_grad[None, :], axis=1)[None, :] / span
    act_grad = jnp.concatenate(
        [
            head_norm_back(query_act, query_mem + query_att, HEAD),
            head_norm_back(key_act, key_mem + keys_grad[recall_end:], HEAD),
            values_grad[recall_end:] - value_mem,
        ],
        1,
    )
    conv_grad = act_grad * silu_slope(mixed_conv)
    kernel_rows = []
    extended_grad = jnp.zeros_like(extended)
    for offset in range(taps):
        start_row = taps - 1 - offset
        kernel_rows.append(jnp.sum(conv_grad * extended[start_row : start_row + span], axis=0))
        extended_grad = extended_grad + jnp.pad(kernel_f[offset] * conv_grad, ((start_row, offset), (0, 0)))
    tail_back = from_behind(
        jnp.where(is_first, 0.0, extended_grad[: taps - 1]).astype(bf16), "wide", -1
    ).astype(f32)
    projected_grad = extended_grad[taps - 1 :] + jnp.pad(tail_back, ((span - taps + 1, 0), (0, 0)))
    projected_low = projected_grad.astype(bf16)
    normed_part = inner_right(projected_low, qkv_weights) + inner_right(gate_pre_low, gate_cols)
    normed_grad = rows_of([normed_part], 15)[0] + gate_row
    scaled_own = own_part(first_scaled)
    gain_one_part = jnp.sum(normed_grad * scaled_own, axis=0)
    tokens_own = middle_grad + rms_back(scaled_own, own_part(first_factor), normed_grad * gain_one)
    tokens_grad = all_rows([tokens_own.astype(bf16)], 16)[0].astype(f32)
    weight_grads = inner_left(normed_low, jnp.concatenate([projected_low, gate_pre_low], 1))
    weight_out = scatter_wide(weight_grads)
    proj_out = scatter_wide(proj_grad)

    def place_cols(piece, axis):
        full = piece.shape[:axis] + (width,) + piece.shape[axis + 1 :]
        return lax.dynamic_update_slice_in_dim(jnp.zeros(full, f32), piece, col_offset, axis)

    kernel_full = place_cols(jnp.stack(kernel_rows).reshape(taps, 3, local_width), 2).reshape(taps, 3 * width)
    persist_full = place_cols(persist_part, 2)
    rate_part = jnp.where(narrow_pos == 0, rate_part, 0.0)
    chunks = [
        kernel_full.reshape(taps, devices, -1).transpose(1, 0, 2),
        persist_full.reshape(2, persist_count, devices, -1).transpose(2, 0, 1, 3),
        gain_one_part.reshape(devices, -1),
        gain_two_part.reshape(devices, -1),
        rate_part.reshape(devices, -1, 3),
    ]
    flat = jnp.concatenate([a.reshape(devices, -1) for a in chunks], 1)
    flat_size = -(-flat.shape[1] // 1024) * 1024
    flat = jnp.pad(flat, ((0, 0), (0, flat_size - flat.shape[1]))).reshape(devices, -1, 128)
    flat_got = exchange([(flat, lambda tw, tn: tw * narrow + tn)], "all", 17)[0]
    flat_sum = jnp.sum(flat_got, axis=0).reshape(-1)
    small_outs, at = [], 0
    for a in chunks:
        size = a.size // devices
        small_outs.append(flat_sum[at : at + size].reshape(a.shape[1:]))
        at += size
    kernel_grad, persist_grad, norm_grad, ffn_gain_grad, rate_grad = small_outs
    return (
        output,
        tokens_grad,
        weight_out[:, :local_width],
        weight_out[:, local_width : 2 * local_width],
        weight_out[:, 2 * local_width : 3 * local_width],
        kernel_grad,
        persist_grad,
        norm_grad,
        rate_grad,
        weight_out[:, 3 * local_width :],
        proj_out.T,
        first_out,
        second_out,
        ffn_gain_grad,
        ffn_gate_out,
        ffn_up_out,
        ffn_down_out.T,
    )


def solution(mesh):
    rows, both, square, turned = P("wide", None), P(("wide", "narrow"), None), P("wide", "narrow"), P("narrow", "wide")
    flat, taps, heads = P(("wide", "narrow")), P(None, ("wide", "narrow")), P(None, None, ("wide", "narrow"))
    return jax.shard_map(
        body,
        mesh=mesh,
        in_specs=(rows, rows, P(), both, both, both, taps, heads, flat, both)
        + (square, turned, square, turned, flat, square, square, turned),
        out_specs=(rows, rows, square, square, square, taps, heads, flat, both)
        + (square, turned, square, turned, flat, square, square, turned),
        check_vma=False,
    )
```

```python
import math

import jax
import jax.numpy as jnp
from jax import lax
from jax.experimental import pallas as pl
from jax.experimental.pallas import tpu as pltpu
from jax.sharding import PartitionSpec as P

HEAD = 64
LANE_WIDE = 4
MESH = pl.DeviceIdType.MESH
ANY = pl.BlockSpec(memory_space=pl.ANY)
bf16 = jnp.bfloat16
f32 = jnp.float32

decay_top = 0.2
moment_top = 0.9
learn_top = 0.1
eps_norm = 1e-05
eps_head = 1e-06
masked_score = -1e30


def remote(src, dst, send, recv, device):
    return pltpu.make_async_remote_copy(
        src_ref=src, dst_ref=dst, send_sem=send, recv_sem=recv, device_id=device, device_id_type=MESH
    )


def exchange(arrays, axes, ident):
    wide, narrow = lax.axis_size("wide"), lax.axis_size("narrow")
    peers = {"all": wide * narrow, "wide": wide, "narrow": narrow}[axes]
    picks = [pick for _, pick in arrays]
    operands = [array for array, _ in arrays]
    chunks = [a.shape if pick is None else a.shape[1:] for a, pick in arrays]
    count = len(arrays)

    def kernel(*refs):
        ins, outs, holds = refs[:count], refs[count : 2 * count], refs[2 * count : 3 * count]
        send_sem, recv_sem, local_sem = refs[3 * count :]
        my_wide, my_narrow = lax.axis_index("wide"), lax.axis_index("narrow")
        me = {"all": my_wide * narrow + my_narrow, "wide": my_wide, "narrow": my_narrow}[axes]

        def place(step):
            target = lax.rem(me + step, peers)
            if axes == "all":
                return lax.div(target, narrow), lax.rem(target, narrow)
            return (target, my_narrow) if axes == "wide" else (my_wide, target)

        barrier = pltpu.get_barrier_semaphore()

        def greet(step, carry):
            pl.semaphore_signal(barrier, inc=1, device_id=place(step), device_id_type=MESH)
            return carry

        lax.fori_loop(1, peers, greet, 0)

        def chunk(index, where):
            return ins[index] if picks[index] is None else ins[index].at[picks[index](*where)]

        own = [
            pltpu.make_async_copy(chunk(i, (my_wide, my_narrow)), holds[i], local_sem.at[i]) for i in range(count)
        ]
        for copy in own:
            copy.start()
        pl.semaphore_wait(barrier, peers - 1)

        def send(step, carry):
            where = place(step)
            for i in range(count):
                remote(chunk(i, where), outs[i].at[me], send_sem.at[i], recv_sem.at[i], where).start()
            return carry

        lax.fori_loop(1, peers, send, 0)
        for i in range(count):
            own[i].wait()
            back = pltpu.make_async_copy(holds[i], outs[i].at[me], local_sem.at[i])
            back.start()
            back.wait()
        for i in range(count):
            others = outs[i].at[pl.ds(0, peers - 1)]
            whole = remote(others, others, send_sem.at[i], recv_sem.at[i], place(1))
            whole.wait_send()
            whole.wait_recv()

    return pl.pallas_call(
        kernel,
        out_shape=[jax.ShapeDtypeStruct((peers,) + tuple(c), a.dtype) for a, c in zip(operands, chunks)],
        in_specs=[ANY] * count,
        out_specs=[ANY] * count,
        scratch_shapes=[pltpu.VMEM(tuple(c), a.dtype) for a, c in zip(operands, chunks)]
        + [pltpu.SemaphoreType.DMA((count,))] * 3,
        compiler_params=pltpu.CompilerParams(collective_id=ident, has_side_effects=True),
        name=f"exchange_{ident}",
    )(*operands)


class Grid:
    def __init__(self):
        wide, narrow = lax.axis_size("wide"), lax.axis_size("narrow")
        self.zs = 4 if wide % 4 == 0 else 1
        self.xs, self.ys = wide // self.zs, narrow // 2
        self.wide, self.narrow = lax.axis_index("wide"), lax.axis_index("narrow")
        self.z, self.x = lax.div(self.wide, self.xs), lax.rem(self.wide, self.xs)
        self.y, self.c = lax.div(self.narrow, 2), lax.rem(self.narrow, 2)
        self.partner = self.device(self.z, self.x, self.y, 1 - self.c)

    def device(self, z, x, y, c):
        return z * self.xs + x, 2 * y + c

    def z_others(self):
        if self.zs != 4:
            return [lax.rem(self.z + s, self.zs) for s in range(1, self.zs)]
        near = self.z + 1 - 2 * lax.div(self.z + 3, 4)
        far = 3 - 3 * lax.div(self.z, 2)
        return [near, 6 - self.z - near - far, far]

    def x_others(self):
        return [lax.rem(self.x + s, self.xs) for s in range(1, self.xs)]

    def y_others(self):
        return [lax.rem(self.y + s, self.ys) for s in range(1, self.ys)]

    def greet_all(self):
        wide, narrow = lax.axis_size("wide"), lax.axis_size("narrow")
        devices = wide * narrow
        me = self.wide * narrow + self.narrow
        barrier = pltpu.get_barrier_semaphore()

        def greet(step, carry):
            target = lax.rem(me + step, devices)
            where = lax.div(target, narrow), lax.rem(target, narrow)
            pl.semaphore_signal(barrier, inc=1, device_id=where, device_id_type=MESH)
            return carry

        lax.fori_loop(1, devices, greet, 0)
        return lambda: pl.semaphore_wait(barrier, devices - 1)


class Gather:
    def __init__(self, grid, source, whole, sems):
        self.grid, self.source, self.whole = grid, source, whole
        self.sent, self.got, self.sent_pair, self.got_pair = sems
        self.rows = whole.shape[2]
        self.pushes, self.pairs = 0, 0

    @staticmethod
    def counts():
        zs = 4 if lax.axis_size("wide") % 4 == 0 else 1
        xs, ys = lax.axis_size("wide") // zs, lax.axis_size("narrow") // 2
        sends = 2 * (zs - 1) + zs * 2 * (xs - 1 + ys - 1) + 2 * zs * (xs - 1) * (ys - 1)
        return zs * xs * ys, sends, 2 * zs * xs * ys

    @classmethod
    def scratch(cls):
        chips, sends, pairs = cls.counts()
        return [
            pltpu.SemaphoreType.DMA((sends,)),
            pltpu.SemaphoreType.DMA((chips, 2)),
            pltpu.SemaphoreType.DMA((pairs,)),
            pltpu.SemaphoreType.DMA((chips, 2)),
        ]

    def half(self, ref, h):
        return ref.at[pl.ds(h * (self.rows // 2), self.rows // 2)]

    def piece(self, z, x, y, c, h):
        wide, narrow = self.grid.device(z, x, y, c)
        return self.half(self.whole.at[wide, narrow], h)

    def spot(self, z, x, y):
        return (z * self.grid.xs + x) * self.grid.ys + y

    def push(self, z, x, y, h, target, own):
        here = self.piece(z, x, y, self.grid.c, h)
        copy = remote(
            self.half(self.source, h) if own else here,
            here,
            self.sent.at[self.pushes],
            self.got.at[self.spot(z, x, y), h],
            target,
        )
        self.pushes += 1
        copy.start()

    def to_partner(self, z, x, y, h, own=False):
        here = self.piece(z, x, y, self.grid.c, h)
        copy = remote(
            self.half(self.source, h) if own else here,
            here,
            self.sent_pair.at[self.pairs],
            self.got_pair.at[self.spot(z, x, y), h],
            self.grid.partner,
        )
        self.pairs += 1
        copy.start()

    def arrived(self, z, x, y, h):
        here = self.piece(z, x, y, self.grid.c, h)
        remote(here, here, self.sent.at[0], self.got.at[self.spot(z, x, y), h], self.grid.partner).wait_recv()

    def fan(self, z, own=False):
        g = self.grid
        to_y = [g.device(g.z, g.x, y, g.c) for y in g.y_others()]
        to_x = [g.device(g.z, x, g.y, g.c) for x in g.x_others()]
        for h, targets in ((0, to_y), (1, to_x), (0, to_x), (1, to_y)):
            for target in targets:
                self.push(z, g.x, g.y, h, target, own)
        for h in (0, 1):
            self.to_partner(z, g.x, g.y, h, own)

    def begin(self):
        g = self.grid
        for z in g.z_others():
            for h in (0, 1):
                self.push(g.z, g.x, g.y, h, g.device(z, g.x, g.y, g.c), True)
        self.fan(g.z, True)

    def level(self, number):
        return ([self.grid.z] + self.grid.z_others())[number]

    def along_z(self, number):
        g, z = self.grid, self.level(number)
        for h in (0, 1):
            self.arrived(z, g.x, g.y, h)
        self.fan(z)

    def across(self, number):
        g, z = self.grid, self.level(number)
        for y in g.y_others():
            self.arrived(z, g.x, y, 0)
            for x in g.x_others():
                self.push(z, g.x, y, 0, g.device(g.z, x, g.y, g.c), False)
            self.to_partner(z, g.x, y, 0)
        for x in g.x_others():
            self.arrived(z, x, g.y, 1)
            for y in g.y_others():
                self.push(z, x, g.y, 1, g.device(g.z, g.x, y, g.c), False)
            self.to_partner(z, x, g.y, 1)

    def last(self, number):
        g, z = self.grid, self.level(number)
        for x in g.x_others():
            self.arrived(z, x, g.y, 0)
            self.to_partner(z, x, g.y, 0)
            for y in g.y_others():
                self.arrived(z, x, y, 0)
                self.to_partner(z, x, y, 0)
        for y in g.y_others():
            self.arrived(z, g.x, y, 1)
            self.to_partner(z, g.x, y, 1)
            for x in g.x_others():
                self.arrived(z, x, y, 1)
                self.to_partner(z, x, y, 1)

    def middle(self):
        for number in range(1, self.grid.zs):
            self.along_z(number)
            self.across(number - 1)
            if number > 1:
                self.last(number - 2)
        self.across(self.grid.zs - 1)
        for number in range(max(0, self.grid.zs - 2), self.grid.zs):
            self.last(number)

    def finish(self):
        g = self.grid
        here = self.piece(g.z, g.x, g.y, g.c, 0)
        _, sends, pairs = self.counts()
        for sems, number in ((self.sent, sends), (self.sent_pair, pairs)):
            for i in range(number):
                remote(here, here, sems.at[i], self.got.at[0, 0], g.partner).wait_send()
        for z in range(g.zs):
            for x in range(g.xs):
                for y in range(g.ys):
                    for h in (0, 1):
                        there = self.piece(z, x, y, 1 - g.c, h)
                        remote(
                            there, there, self.sent.at[0], self.got_pair.at[self.spot(z, x, y), h], g.partner
                        ).wait_recv()


def send_parameters(smalls, weights, blocks, ident):
    wide, narrow = lax.axis_size("wide"), lax.axis_size("narrow")
    devices = wide * narrow
    count = len(blocks)

    def kernel(*refs):
        smalls_ref, weights_ref = refs[:2]
        block_refs, refs = refs[2 : 2 + count], refs[2 + count :]
        smalls_out, weights_out = refs[:2]
        block_outs, refs = refs[2 : 2 + count], refs[2 + count :]
        hold_small, hold_weight, refs = refs[0], refs[1], refs[2:]
        hold_blocks, refs = refs[:count], refs[count:]
        local_sem, all_send, all_recv, near_send, near_recv, z_send, z_recv, x_send, x_recv, b_send, b_recv = refs
        g = Grid()
        me = g.wide * narrow + g.narrow
        wait_all = g.greet_all()
        own = [
            (smalls_ref, hold_small, smalls_out.at[me]),
            (weights_ref.at[g.narrow], hold_weight, weights_out.at[g.wide, g.narrow]),
        ] + [
            (block_refs[i].at[lax.rem(g.wide, LANE_WIDE)], hold_blocks[i], block_outs[i].at[g.wide])
            for i in range(count)
        ]
        into = [pltpu.make_async_copy(a, b, local_sem.at[i]) for i, (a, b, _) in enumerate(own)]
        back = [pltpu.make_async_copy(b, c, local_sem.at[i]) for i, (_, b, c) in enumerate(own)]
        for copy in into:
            copy.start()
        wait_all()
        near = []
        for s in range(1, narrow):
            target = lax.rem(g.narrow + s, narrow)
            copy = remote(
                weights_ref.at[target],
                weights_out.at[g.wide, g.narrow],
                near_send.at[s],
                near_recv.at[g.narrow],
                (g.wide, target),
            )
            copy.start()
            near.append(copy)

        def send_small(step, carry):
            target = lax.rem(me + step, devices)
            remote(
                smalls_ref,
                smalls_out.at[me],
                all_send.at[0],
                all_recv.at[0],
                (lax.div(target, narrow), lax.rem(target, narrow)),
            ).start()
            return carry

        lax.fori_loop(1, devices, send_small, 0)
        for copy in into:
            copy.wait()
        for copy in back:
            copy.start()
        for copy in back:
            copy.wait()
        for s in range(1, narrow):
            source = lax.rem(g.narrow + s, narrow)
            there = weights_out.at[g.wide, source]
            remote(there, there, near_send.at[s], near_recv.at[source], g.partner).wait_recv()

        def row(z, x):
            return weights_out.at[z * g.xs + x]

        sends = []

        def push(z, target, send, recv):
            copy = remote(row(z, g.x), row(z, g.x), send, recv, target)
            copy.start()
            sends.append(copy)

        for i, z in enumerate(g.z_others()):
            push(g.z, g.device(z, g.x, g.y, g.c), z_send.at[i], z_recv.at[g.z])
        for i, x in enumerate(g.x_others()):
            push(g.z, g.device(g.z, x, g.y, g.c), x_send.at[0, i], x_recv.at[g.z, g.x])
        for s in range(1, wide):
            target = lax.rem(g.wide + s, wide)
            for i in range(count):
                copy = remote(
                    block_refs[i].at[lax.rem(target, LANE_WIDE)],
                    block_outs[i].at[g.wide],
                    b_send.at[i, s],
                    b_recv.at[i, g.wide],
                    (target, g.narrow),
                )
                copy.start()
                sends.append(copy)
        for j, z in enumerate(g.z_others()):
            remote(row(z, g.x), row(z, g.x), z_send.at[0], z_recv.at[z], g.partner).wait_recv()
            for i, x in enumerate(g.x_others()):
                push(z, g.device(g.z, x, g.y, g.c), x_send.at[1 + j, i], x_recv.at[z, g.x])
        for x in g.x_others():
            for z in [g.z] + g.z_others():
                remote(row(z, x), row(z, x), z_send.at[0], x_recv.at[z, x], g.partner).wait_recv()
        for s in range(1, wide):
            source = lax.rem(g.wide + s, wide)
            for i in range(count):
                there = block_outs[i].at[source]
                remote(there, there, z_send.at[0], b_recv.at[i, source], g.partner).wait_recv()
        for copy in near + sends:
            copy.wait_send()
        others = smalls_out.at[pl.ds(0, devices - 1)]
        whole = remote(others, others, all_send.at[0], all_recv.at[0], g.partner)
        whole.wait_send()
        whole.wait_recv()

    zs = 4 if wide % 4 == 0 else 1
    xs = wide // zs
    sem = pltpu.SemaphoreType.DMA
    return pl.pallas_call(
        kernel,
        out_shape=[
            jax.ShapeDtypeStruct((devices,) + smalls.shape, smalls.dtype),
            jax.ShapeDtypeStruct((wide, narrow) + weights.shape[1:], weights.dtype),
        ]
        + [jax.ShapeDtypeStruct((wide,) + b.shape[1:], b.dtype) for b in blocks],
        in_specs=[ANY] * (2 + count),
        out_specs=[ANY] * (2 + count),
        scratch_shapes=[pltpu.VMEM(smalls.shape, smalls.dtype), pltpu.VMEM(weights.shape[1:], weights.dtype)]
        + [pltpu.VMEM(b.shape[1:], b.dtype) for b in blocks]
        + [sem((2 + count,)), sem((1,)), sem((1,)), sem((narrow,)), sem((narrow,)), sem((zs,)), sem((zs,))]
        + [sem((zs, xs)), sem((zs, xs)), sem((count, wide)), sem((count, wide))],
        compiler_params=pltpu.CompilerParams(collective_id=ident, has_side_effects=True),
        name="send_parameters",
    )(smalls, weights, *blocks)


def rows_to_lanes(rows, chunks, pick, tile, ident):
    wide, narrow = lax.axis_size("wide"), lax.axis_size("narrow")
    devices = wide * narrow

    def kernel(rows_ref, chunks_ref, tile_ref, rows_out, chunks_out, tile_out, *refs):
        hold_rows, hold_chunk, hold_tile, local_sem, send, recv = refs[:6]
        g = Grid()
        me = g.wide * narrow + g.narrow
        wait_all = g.greet_all()
        own = [
            (rows_ref, hold_rows, rows_out.at[g.wide, g.narrow]),
            (chunks_ref.at[pick(g.wide, g.narrow)], hold_chunk, chunks_out.at[me]),
            (tile_ref, hold_tile, tile_out.at[me]),
        ]
        into = [pltpu.make_async_copy(a, b, local_sem.at[i]) for i, (a, b, _) in enumerate(own)]
        back = [pltpu.make_async_copy(b, c, local_sem.at[i]) for i, (_, b, c) in enumerate(own)]
        for copy in into:
            copy.start()
        wait_all()
        gather = Gather(g, rows_ref, rows_out, refs[6:])
        gather.begin()

        def send_chunks(step, carry):
            target = lax.rem(me + step, devices)
            where = lax.div(target, narrow), lax.rem(target, narrow)
            remote(chunks_ref.at[pick(*where)], chunks_out.at[me], send.at[0], recv.at[0], where).start()
            remote(tile_ref, tile_out.at[me], send.at[1], recv.at[1], where).start()
            return carry

        lax.fori_loop(1, devices, send_chunks, 0)
        for copy in into:
            copy.wait()
        for copy in back:
            copy.start()
        gather.middle()
        for copy in back:
            copy.wait()
        for i, out in enumerate((chunks_out, tile_out)):
            others = out.at[pl.ds(0, devices - 1)]
            whole = remote(others, others, send.at[i], recv.at[i], g.partner)
            whole.wait_send()
            whole.wait_recv()
        gather.finish()

    return pl.pallas_call(
        kernel,
        out_shape=[
            jax.ShapeDtypeStruct((wide, narrow) + rows.shape, rows.dtype),
            jax.ShapeDtypeStruct((devices,) + chunks.shape[1:], chunks.dtype),
            jax.ShapeDtypeStruct((devices,) + tile.shape, tile.dtype),
        ],
        in_specs=[ANY] * 3,
        out_specs=[ANY] * 3,
        scratch_shapes=[
            pltpu.VMEM(rows.shape, rows.dtype),
            pltpu.VMEM(chunks.shape[1:], chunks.dtype),
            pltpu.VMEM(tile.shape, tile.dtype),
            pltpu.SemaphoreType.DMA((3,)),
            pltpu.SemaphoreType.DMA((2,)),
            pltpu.SemaphoreType.DMA((2,)),
        ]
        + Gather.scratch(),
        compiler_params=pltpu.CompilerParams(collective_id=ident, has_side_effects=True),
        name="rows_to_lanes",
    )(rows, chunks, tile)


def narrow_step(parts, extras, work, spread_count, locals_like, ident):
    narrow, rows, width = parts[0].shape
    ys = narrow // 2
    count, extra_count, local_count = len(parts), len(extras), len(locals_like)
    parts = [p.reshape(ys, 2, rows, width) for p in parts]

    def kernel(*refs):
        part_refs, refs = refs[:count], refs[count:]
        extra_refs, refs = refs[:extra_count], refs[extra_count:]
        spread_refs, refs = refs[:spread_count], refs[spread_count:]
        local_refs, refs = refs[:local_count], refs[local_count:]
        mine, pair, half, got, rowbuf, refs = refs[0], refs[1], refs[2], refs[3], refs[4], refs[5:]
        load_sem, pair_send, pair_recv, y_send, y_recv, s_send, s_recv, p_send, p_recv, own_sem = refs
        g = Grid()
        barrier = pltpu.get_barrier_semaphore()
        friends = [g.device(g.z, g.x, y, g.c) for y in g.y_others()] + [g.partner]
        for friend in friends:
            pl.semaphore_signal(barrier, inc=1, device_id=friend, device_id_type=MESH)
        loads = [
            pltpu.make_async_copy(part_refs[i].at[:, g.c], mine.at[i], load_sem.at[i]) for i in range(count)
        ]
        for copy in loads:
            copy.start()
        pl.semaphore_wait(barrier, len(friends))
        pairs = [
            remote(part_refs[i].at[:, 1 - g.c], pair.at[i], pair_send.at[i], pair_recv.at[i], g.partner)
            for i in range(count)
        ]
        for copy in pairs:
            copy.start()
        sends = []
        for i in range(count):
            loads[i].wait()
            pairs[i].wait_recv()
            half[i] = (mine[i].astype(f32) + pair[i].astype(f32)).astype(bf16)
            for s, y in enumerate(g.y_others()):
                copy = remote(
                    half.at[i, y], got.at[i, g.y], y_send.at[i, s], y_recv.at[i, g.y], g.device(g.z, g.x, y, g.c)
                )
                copy.start()
                sends.append(copy)
        totals = []
        for i in range(count):
            total = half[i, g.y].astype(f32)
            for y in g.y_others():
                remote(got.at[i, y], got.at[i, y], y_send.at[i, 0], y_recv.at[i, y], g.partner).wait_recv()
                total = total + got[i, y].astype(f32)
            totals.append(total)
        spreads, locals_out = work(totals, [ref[...] for ref in extra_refs])
        for ref, value in zip(local_refs, locals_out):
            ref[...] = value
        own = []
        for i, value in enumerate(spreads):
            rowbuf[i] = value
            for s, y in enumerate(g.y_others()):
                copy = remote(
                    rowbuf.at[i],
                    spread_refs[i].at[g.narrow],
                    s_send.at[i, s],
                    s_recv.at[i, g.y],
                    g.device(g.z, g.x, y, g.c),
                )
                copy.start()
                sends.append(copy)
            copy = remote(
                rowbuf.at[i], spread_refs[i].at[g.narrow], p_send.at[i, g.y], p_recv.at[i, g.y], g.partner
            )
            copy.start()
            sends.append(copy)
            copy = pltpu.make_async_copy(rowbuf.at[i], spread_refs[i].at[g.narrow], own_sem.at[i])
            copy.start()
            own.append(copy)
        for i in range(spread_count):
            for y in g.y_others():
                there = spread_refs[i].at[2 * y + g.c]
                remote(there, there, s_send.at[i, 0], s_recv.at[i, y], g.partner).wait_recv()
                copy = remote(there, there, p_send.at[i, y], p_recv.at[i, y], g.partner)
                copy.start()
                sends.append(copy)
        for i in range(spread_count):
            for y in range(ys):
                there = spread_refs[i].at[2 * y + 1 - g.c]
                remote(there, there, s_send.at[i, 0], p_recv.at[i, y], g.partner).wait_recv()
        for copy in pairs + sends:
            copy.wait_send()
        for copy in own:
            copy.wait()

    sem = pltpu.SemaphoreType.DMA
    vmem = pl.BlockSpec(memory_space=pltpu.VMEM)
    return pl.pallas_call(
        kernel,
        out_shape=[jax.ShapeDtypeStruct((narrow, rows, width), bf16)] * spread_count
        + [jax.ShapeDtypeStruct(shape, dtype) for shape, dtype in locals_like],
        in_specs=[ANY] * count + [vmem] * extra_count,
        out_specs=[ANY] * spread_count + [vmem] * local_count,
        scratch_shapes=[pltpu.VMEM((count, ys, rows, width), bf16)] * 4
        + [pltpu.VMEM((spread_count, rows, width), bf16)]
        + [sem((count,))] * 3
        + [sem((count, ys))] * 2
        + [sem((spread_count, ys))] * 4
        + [sem((spread_count,))],
        compiler_params=pltpu.CompilerParams(collective_id=ident, has_side_effects=True),
        name=f"narrow_step_{ident}",
    )(*parts, *extras)


def matmul(left_side, right_side):
    return jnp.dot(left_side, right_side, preferred_element_type=jnp.float32)


def inner_left(left_side, right_side):
    return lax.dot_general(left_side, right_side, (((0,), (0,)), ((), ())), preferred_element_type=jnp.float32)


def inner_right(left_side, right_side):
    return lax.dot_general(left_side, right_side, (((1,), (1,)), ((), ())), preferred_element_type=jnp.float32)


def silu_slope(values):
    sigmoid_val = jax.nn.sigmoid(values)
    return sigmoid_val * (1.0 + values * (1.0 - sigmoid_val))


def silu_curve(values):
    sigmoid_val = jax.nn.sigmoid(values)
    return sigmoid_val * (1.0 - sigmoid_val) * (2.0 + values * (1.0 - 2.0 * sigmoid_val))


class Lane:
    def __init__(self):
        narrow = lax.axis_size("narrow")
        self.ys = narrow // 2
        self.chips = LANE_WIDE * self.ys
        wide_pos, narrow_pos = lax.axis_index("wide"), lax.axis_index("narrow")
        self.base = lax.div(wide_pos, LANE_WIDE) * LANE_WIDE
        self.colour = lax.rem(narrow_pos, 2)
        self.chip = lax.rem(wide_pos, LANE_WIDE) * self.ys + lax.div(narrow_pos, 2)
        self.partner = (wide_pos, narrow_pos + 1 - 2 * self.colour)

    def other(self, step):
        return lax.rem(self.chip + step, self.chips)

    def device(self, chip):
        return self.base + lax.div(chip, self.ys), 2 * lax.rem(chip, self.ys) + self.colour

    def greet(self):
        barrier = pltpu.get_barrier_semaphore()
        for step in range(1, self.chips):
            pl.semaphore_signal(barrier, inc=1, device_id=self.device(self.other(step)), device_id_type=MESH)
        pl.semaphore_signal(barrier, inc=1, device_id=self.partner, device_id_type=MESH)
        pl.semaphore_wait(barrier, self.chips)


class Scatter:
    def __init__(self, lane, part, pair, half, got, sems):
        self.lane, self.part, self.pair, self.half, self.got = lane, part, pair, half, got
        self.pair_send, self.pair_recv, self.send, self.recv = sems

    @staticmethod
    def scratch(chips, rows, width):
        return [
            pltpu.VMEM((2, chips, rows, width), bf16),
            pltpu.VMEM((chips, rows, width), bf16),
            pltpu.VMEM((chips, rows, width), bf16),
            pltpu.VMEM((chips, rows, width), bf16),
            pltpu.SemaphoreType.DMA((1,)),
            pltpu.SemaphoreType.DMA((1,)),
            pltpu.SemaphoreType.DMA((chips,)),
            pltpu.SemaphoreType.DMA((chips,)),
        ]

    @classmethod
    def of(cls, lane, refs):
        return cls(lane, *refs[:4], refs[4:8])

    def pair_copy(self):
        return remote(
            self.part.at[1 - self.lane.colour],
            self.pair,
            self.pair_send.at[0],
            self.pair_recv.at[0],
            self.lane.partner,
        )

    def start_pair(self):
        self.pair_copy().start()

    def take_pair(self):
        self.pair_copy().wait()
        self.half[...] = (
            self.part[self.lane.colour].astype(f32) + self.pair[...].astype(f32)
        ).astype(bf16)
        self.got[self.lane.chip] = self.half[self.lane.chip]

    def copy_to(self, step):
        chip = self.lane.other(step)
        return remote(
            self.half.at[chip],
            self.got.at[self.lane.chip],
            self.send.at[step],
            self.recv.at[self.lane.chip],
            self.lane.device(chip),
        )

    def start_sends(self):
        for step in range(1, self.lane.chips):
            self.copy_to(step).start()

    def total(self):
        result = self.got[self.lane.chip].astype(f32)
        for step in range(1, self.lane.chips):
            chip = self.lane.other(step)
            remote(
                self.got.at[chip], self.got.at[chip], self.send.at[step], self.recv.at[chip], self.lane.device(chip)
            ).wait_recv()
            result = result + self.got[chip].astype(f32)
        return result

    def wait_sends(self):
        for step in range(1, self.lane.chips):
            self.copy_to(step).wait_send()


class Spread:
    def __init__(self, lane, whole, sems):
        self.lane, self.whole = lane, whole
        self.send, self.recv, self.pair_send, self.pair_recv = sems

    @staticmethod
    def scratch(chips, rows, width):
        return [pltpu.VMEM((2, chips, rows, width), bf16)] + [pltpu.SemaphoreType.DMA((chips,))] * 4

    @classmethod
    def of(cls, lane, refs):
        return cls(lane, refs[0], refs[1:5])

    def mine(self):
        return self.whole.at[self.lane.colour, self.lane.chip]

    def copy_to(self, step):
        return remote(
            self.mine(),
            self.mine(),
            self.send.at[step],
            self.recv.at[self.lane.chip],
            self.lane.device(self.lane.other(step)),
        )

    def pair_copy(self, chip, colour):
        place = self.whole.at[colour, chip]
        return remote(place, place, self.pair_send.at[chip], self.pair_recv.at[chip], self.lane.partner)

    def run(self):
        lane = self.lane
        for step in range(1, lane.chips):
            self.copy_to(step).start()
        self.pair_copy(lane.chip, lane.colour).start()
        for step in range(1, lane.chips):
            chip = lane.other(step)
            place = self.whole.at[lane.colour, chip]
            remote(place, place, self.send.at[step], self.recv.at[chip], lane.device(chip)).wait_recv()
            self.pair_copy(chip, lane.colour).start()
        for chip in range(lane.chips):
            self.pair_copy(chip, 1 - lane.colour).wait_recv()
        for step in range(1, lane.chips):
            self.copy_to(step).wait_send()
        for chip in range(lane.chips):
            self.pair_copy(chip, lane.colour).wait_send()


def chain_forward(keys, key_index, values, queries, spans, gates, first_init, second_init, ident):
    wide = lax.axis_size("wide")
    blocks, span, block = keys.shape[1:]
    width, hidden = first_init.shape
    rows = values.shape[1]
    turns = spans.shape[0]
    key_turns = turns - 1
    per_turn = 3 if turns <= 5 else 1
    first_left = per_turn * (key_turns - 3)
    slots = 3
    stream_keys = keys.shape[0] == turns
    chips = LANE_WIDE * (lax.axis_size("narrow") // 2)
    n_scatter = len(Scatter.scratch(1, 8, 128))

    def kernel(*refs):
        keys_hbm, values_hbm, own_hbm, index_ref, spans_ref, gates_ref, first_hbm, second_hbm = refs[:8]
        recalled_hbm, low1_hbm, low2_hbm, m1_hbm, m2_hbm, g1_hbm, g2_hbm = refs[8:15]
        err_hbm, pre_hbm, qpre_hbm, klane_hbm, qlane_hbm = refs[15:20]
        rest = refs[20:]
        kall, qall, vall, kcur, qcur, i1, i2, s1, s2, m1, m2, low1, low2, mb1, mb2, gb1, gb2 = rest[:17]
        pre, qpre, khid, rec, qpart, qpair, qhalf, qgot, own_hold = rest[17:26]
        in_sem, out_sem, q_sem, q_pair_send, q_pair_recv, q_send, q_recv = rest[26:33]
        rest = rest[33:]
        lane = Lane()
        grid = Grid()
        lookup = Scatter.of(lane, rest[:n_scatter])
        error = Spread.of(lane, rest[n_scatter : n_scatter + 5])
        gather = Gather(grid, own_hbm, qall, rest[n_scatter + 5 :])

        def recall(q, slot):
            sems = q_pair_send.at[pl.ds(q, 1)], q_pair_recv.at[pl.ds(q, 1)], q_send.at[q], q_recv.at[q]
            return Scatter(lane, qpart.at[slot], qpair.at[q], qhalf.at[slot], qgot.at[q], sems)

        def state_saves(turn):
            return [
                pltpu.make_async_copy(source, target.at[turn], out_sem.at[i])
                for i, (source, target) in enumerate(((mb1, m1_hbm), (mb2, m2_hbm), (kcur, klane_hbm)))
            ]

        def other_saves(turn):
            return [
                pltpu.make_async_copy(source, target.at[turn], out_sem.at[3 + i])
                for i, (source, target) in enumerate(
                    ((gb1, g1_hbm), (gb2, g2_hbm), (error.whole, err_hbm), (pre, pre_hbm))
                )
            ]

        def query_saves(q, slot):
            return [
                pltpu.make_async_copy(source.at[slot], target.at[q], q_sem.at[slot, i])
                for i, (source, target) in enumerate(((qcur, qlane_hbm), (qpre, qpre_hbm)))
            ]

        inputs = [
            pltpu.make_async_copy(source, target, in_sem.at[i])
            for i, (source, target) in enumerate(
                ((first_hbm, i1), (second_hbm, i2), (keys_hbm, kall), (values_hbm, vall), (own_hbm, own_hold))
            )
            if not (stream_keys and i == 2)
        ]
        for copy in inputs:
            copy.start()
        grid.greet_all()()
        gather.begin()
        for copy in inputs:
            copy.wait()
        own_store = pltpu.make_async_copy(own_hold, qall.at[grid.wide, grid.narrow], in_sem.at[4])
        own_store.start()
        low1[0] = i1[...]
        low2[0] = i2[...]
        s1[...] = i1[...].astype(f32)
        s2[...] = i2[...].astype(f32)
        for ref in (m1, m2, mb1, mb2):
            ref[...] = jnp.zeros_like(ref)
        own_store.wait()

        def lookup_blocks(buf, first):
            total = matmul(buf[0], first[pl.ds(0, block), :])
            for b in range(1, blocks):
                total = total + matmul(buf[b], first[pl.ds(b * block, block), :])
            return total

        def ask(q, slot, waits):
            def settle():
                recall(q - slots, slot).wait_sends()
                for copy in query_saves(q - slots, slot):
                    copy.wait()

            if waits is True:
                settle()
            elif waits is not False:
                pl.when(waits)(settle)
            index = spans_ref[q]
            for b in range(blocks):
                qcur[slot, b] = qall[index, b]
            query_pre = lookup_blocks(qcur.at[slot], low1.at[q])
            qpre[slot] = query_pre
            for copy in query_saves(q, slot):
                copy.start()
            query_hidden = (query_pre * jax.nn.sigmoid(query_pre)).astype(bf16)
            qpart[slot] = matmul(query_hidden, low2[q]).astype(bf16).reshape(2, chips, rows, width)
            recall(q, slot).start_pair()

        def turn_body(turn, carry):
            index, place = spans_ref[turn], index_ref[turn]
            if stream_keys:
                one = pltpu.make_async_copy(keys_hbm.at[turn], kcur, in_sem.at[2])
                one.start()
                one.wait()
            else:
                for b in range(blocks):
                    kcur[b] = kall[place, b]
            for copy in state_saves(turn):
                copy.start()
            key_pre = lookup_blocks(kcur, low1.at[turn])
            pre[0] = key_pre
            khid[...] = (key_pre * jax.nn.sigmoid(key_pre)).astype(bf16)
            lookup.part[...] = matmul(khid[...], low2[turn]).astype(bf16).reshape(2, chips, rows, width)
            lookup.start_pair()

            @pl.when(turn == 3)
            def _():
                gather.finish()

            first = per_turn * (turn - 3)

            @pl.when(turn >= 3)
            def _():
                ask(first, lax.rem(first, slots), first >= slots)

            lookup.take_pair()
            lookup.start_sends()

            @pl.when(turn >= 3)
            def _():
                recall(first, lax.rem(first, slots)).take_pair()
                for j in range(1, per_turn):
                    ask(first + j, lax.rem(first + j, slots), first + j >= slots)

            total = lookup.total()
            target = jnp.concatenate([vall[index * blocks + b] for b in range(blocks)], axis=1)
            error.whole[lane.colour, lane.chip] = ((total - target.astype(f32)) / span).astype(bf16)
            error.run()
            lookup.wait_sends()

            @pl.when(turn >= 3)
            def _():
                recall(first, lax.rem(first, slots)).start_sends()
                for j in range(1, per_turn):
                    stream = recall(first + j, lax.rem(first + j, slots))
                    stream.take_pair()
                    stream.start_sends()

            err = error.whole[...].reshape(span, width)
            grad_second = inner_left(khid[...], err)
            hidden_grad = inner_right(err, low2[turn])
            pre[1] = hidden_grad
            slope = (hidden_grad * silu_slope(pre[0])).astype(bf16)
            decay, moment, rate, reset = (gates_ref[turn, i] for i in range(4))
            for copy in state_saves(turn):
                copy.wait()
            following = jnp.minimum(turn + 1, turns - 1)

            def update(s, m, mb, init, low, grad, place):
                moment_new = moment * m[place] - rate * grad
                state_new = (1.0 - decay) * s[place] + moment_new
                state_new = reset * init[place].astype(f32) + (1.0 - reset) * state_new
                moment_new = (1.0 - reset) * moment_new
                m[place] = moment_new
                mb[place] = moment_new.astype(bf16)
                s[place] = state_new
                low[(following,) + place] = state_new.astype(bf16)

            gb2[...] = grad_second.astype(bf16)
            update(s2, m2, mb2, i2, low2, grad_second, (slice(None), slice(None)))
            for b in range(blocks):
                grad_first = inner_left(kcur[b], slope)
                place = (pl.ds(b * block, block), slice(None))
                gb1[place] = grad_first.astype(bf16)
                update(s1, m1, mb1, i1, low1, grad_first, place)
            saves = other_saves(turn)
            for copy in saves:
                copy.start()

            @pl.when(turn == 0)
            def _():
                for number in range(1, grid.zs):
                    gather.along_z(number)
                gather.across(0)

            @pl.when(turn == 1)
            def _():
                for number in range(1, grid.zs):
                    gather.across(number)
                gather.last(0)

            @pl.when(turn == 2)
            def _():
                for number in range(1, grid.zs):
                    gather.last(number)

            for copy in saves:
                copy.wait()
            return carry

        lax.fori_loop(0, key_turns, turn_body, 0)
        ends = [
            pltpu.make_async_copy(low1, low1_hbm, out_sem.at[0]),
            pltpu.make_async_copy(low2, low2_hbm, out_sem.at[1]),
        ]
        for copy in ends:
            copy.start()
        left = list(range(first_left, turns))
        for q in left:
            ask(q, q % slots, q >= slots)
            if q > left[0]:
                stream = recall(q - 1, (q - 1) % slots)
                stream.take_pair()
                stream.start_sends()
        stream = recall(turns - 1, (turns - 1) % slots)
        stream.take_pair()
        stream.start_sends()
        for q in range(turns):
            rec[q] = recall(q, q % slots).total().astype(bf16)
        last = pltpu.make_async_copy(rec, recalled_hbm, out_sem.at[2])
        last.start()
        for q in range(turns - slots, turns):
            recall(q, q % slots).wait_sends()
        for q in range(turns - slots, turns):
            for copy in query_saves(q, q % slots):
                copy.wait()
        for copy in ends + [last]:
            copy.wait()

    state = [(width, hidden), (hidden, width)]
    out_shape = (
        [jax.ShapeDtypeStruct((turns, rows, width), bf16)]
        + [jax.ShapeDtypeStruct((turns,) + s, bf16) for s in state]
        + [jax.ShapeDtypeStruct((key_turns,) + s, bf16) for s in state * 2]
        + [
            jax.ShapeDtypeStruct((key_turns, 2, chips, rows, width), bf16),
            jax.ShapeDtypeStruct((key_turns, 2, span, hidden), f32),
            jax.ShapeDtypeStruct((turns, span, hidden), f32),
            jax.ShapeDtypeStruct((key_turns, blocks, span, block), bf16),
            jax.ShapeDtypeStruct((turns, blocks, span, block), bf16),
        ]
    )
    sem = pltpu.SemaphoreType.DMA
    scratch = (
        [pltpu.VMEM((1 if stream_keys else keys.shape[0], blocks, span, block), bf16), pltpu.VMEM((wide, blocks, span, block), bf16)]
        + [pltpu.VMEM(values.shape, bf16)]
        + [pltpu.VMEM((blocks, span, block), bf16), pltpu.VMEM((slots, blocks, span, block), bf16)]
        + [pltpu.VMEM(s, bf16) for s in state]
        + [pltpu.VMEM(s, f32) for s in state * 2]
        + [pltpu.VMEM((turns,) + s, bf16) for s in state]
        + [pltpu.VMEM(s, bf16) for s in state * 2]
        + [
            pltpu.VMEM((2, span, hidden), f32),
            pltpu.VMEM((slots, span, hidden), f32),
            pltpu.VMEM((span, hidden), bf16),
            pltpu.VMEM((turns, rows, width), bf16),
            pltpu.VMEM((slots, 2, chips, rows, width), bf16),
        ]
        + [pltpu.VMEM((n, chips, rows, width), bf16) for n in (turns, slots, turns)]
        + [pltpu.VMEM((span, block), bf16)]
        + [sem((5,)), sem((7,)), sem((slots, 2)), sem((turns,)), sem((turns,)), sem((turns, chips)), sem((turns, chips))]
        + Scatter.scratch(chips, rows, width)
        + Spread.scratch(chips, rows, width)
        + Gather.scratch()
    )
    smem = pl.BlockSpec(memory_space=pltpu.SMEM)
    return pl.pallas_call(
        kernel,
        out_shape=out_shape,
        in_specs=[ANY] * 3 + [smem] * 3 + [ANY] * 2,
        out_specs=[ANY] * len(out_shape),
        scratch_shapes=scratch,
        compiler_params=pltpu.CompilerParams(
            collective_id=ident, has_side_effects=True, vmem_limit_bytes=62 * 1024 * 1024
        ),
        cost_estimate=pl.CostEstimate(
            flops=40 * turns * 2 * span * width * hidden, bytes_accessed=turns * 40 * 2**20, transcendentals=0
        ),
        name="chain_forward",
    )(keys, values, queries, key_index, spans, gates, first_init, second_init)


def chain_backward(recall_grad, saved, spans, gates, ident):
    low1_all, low2_all, m1_all, m2_all, g1_all, g2_all, err_all, pre_all, qpre_all, keys, queries = saved
    wide = lax.axis_size("wide")
    key_turns, blocks, span, block = keys.shape
    turns = key_turns + 1
    width, hidden = low1_all.shape[1:]
    chips, rows = err_all.shape[2:4]
    n_scatter = len(Scatter.scratch(1, 8, 128))

    def kernel(*refs):
        own_hbm, q_ins, k_ins, spans_ref, gates_ref = refs[0], refs[1:5], refs[5:12], refs[12], refs[13]
        qcot_hbm, kcot_hbm, vcot_hbm, sums1_ref, sums2_ref, mg1_hbm, mg2_hbm = refs[14:21]
        rest = refs[21:]
        q_bufs, k_bufs, rest = rest[:4], rest[4:11], rest[11:]
        qbuf, low1, low2, qpre = q_bufs
        kbuf, m1, m2, g1, g2, errs, pre = k_bufs
        rall, own_hold, cf, cs, cmf, cms, w1, w2, a1, a2, c1, c2 = rest[:12]
        dh, khid, qpl, qhid, kpl, slow, sg, hk, qsave, ksave, vsave = rest[12:23]
        q_sem, k_sem, out_sem, end_sem, own_sem = rest[23:28]
        rest = rest[28:]
        lane = Lane()
        grid = Grid()
        lookup = Scatter.of(lane, rest[:n_scatter])
        qstream = Scatter.of(lane, rest[n_scatter : 2 * n_scatter])
        kstream = Scatter.of(lane, rest[2 * n_scatter : 3 * n_scatter])
        spread = Spread.of(lane, rest[3 * n_scatter : 3 * n_scatter + 5])
        gather = Gather(grid, own_hbm, rall, rest[3 * n_scatter + 5 :])

        def q_loads(turn, slot):
            return [
                pltpu.make_async_copy(source.at[turn], target.at[slot], q_sem.at[slot, i])
                for i, (source, target) in enumerate(zip(q_ins, q_bufs))
            ]

        def k_loads(turn, slot):
            return [
                pltpu.make_async_copy(source.at[turn], target.at[slot], k_sem.at[slot, i])
                for i, (source, target) in enumerate(zip(k_ins, k_bufs))
            ]

        own = pltpu.make_async_copy(own_hbm, own_hold, own_sem.at[0])
        own.start()
        grid.greet_all()()
        gather.begin()
        for copy in q_loads(turns - 1, 0) + q_loads(turns - 2, 1) + k_loads(turns - 2, 1):
            copy.start()
        own.wait()
        own_store = pltpu.make_async_copy(own_hold, rall.at[grid.wide, grid.narrow], own_sem.at[0])
        own_store.start()
        for ref in (cf, cs, cmf, cms, a1, a2):
            ref[...] = jnp.zeros_like(ref)
        gather.middle()
        own_store.wait()
        gather.finish()

        def qout(turn):
            return pltpu.make_async_copy(qsave, qcot_hbm.at[turn], out_sem.at[0])

        def kout(turn):
            return pltpu.make_async_copy(ksave, kcot_hbm.at[turn], out_sem.at[1])

        def vout(turn):
            return pltpu.make_async_copy(vsave, vcot_hbm.at[turn], out_sem.at[2])

        def finish(stream, save, out):
            save[...] = stream.total().astype(bf16)
            stream.wait_sends()
            out.start()

        def query_rows(turn, slot):
            index = spans_ref[turn]
            back = inner_right(rall[index, 0], low2[slot, :, pl.ds(0, block)])
            for b in range(1, blocks):
                back = back + inner_right(rall[index, b], low2[slot, :, pl.ds(b * block, block)])
            query_pre = qpre[slot]
            qpl[...] = (gates_ref[turn, 4] * back * silu_slope(query_pre)).astype(bf16)
            qhid[...] = (query_pre * jax.nn.sigmoid(query_pre)).astype(bf16)
            qstream.part[...] = inner_right(qpl[...], low1[slot]).astype(bf16).reshape(2, chips, rows, width)
            qstream.start_pair()

        def query_weights(turn, slot):
            index = spans_ref[turn]
            valid = gates_ref[turn, 4]
            for b in range(blocks):
                w1[pl.ds(b * block, block), :] = inner_left(qbuf[slot, b], qpl[...])
                w2[:, pl.ds(b * block, block)] = valid * inner_left(qhid[...], rall[index, b])

        def key_rows(slot):
            kstream.part[...] = (
                (inner_right(kpl[...], low1[slot]) + inner_right(slow[...], c1[slot]))
                .astype(bf16)
                .reshape(2, chips, rows, width)
            )

        for copy in q_loads(turns - 1, 0):
            copy.wait()
        query_rows(turns - 1, 0)
        query_weights(turns - 1, 0)
        reset = gates_ref[turns - 1, 3]
        for c, w, acc in ((cf, w1, a1), (cs, w2, a2)):
            acc[...] = reset * w[...]
            c[...] = (1.0 - reset) * w[...]
        qstream.take_pair()
        qstream.start_sends()

        def body(step, carry):
            turn = turns - 1 - step
            slot = lax.rem(step, 2)
            decay, moment, rate, reset = (gates_ref[turn, i] for i in range(4))
            for copy in q_loads(turn, slot) + k_loads(turn, slot):
                copy.wait()
            c1[slot] = (-rate * (cmf[...] + cf[...])).astype(bf16)
            c2[...] = (-rate * (cms[...] + cs[...])).astype(bf16)
            slope_grad = matmul(kbuf[slot, 0], c1[slot, pl.ds(0, block), :])
            for b in range(1, blocks):
                slope_grad = slope_grad + matmul(kbuf[slot, b], c1[slot, pl.ds(b * block, block), :])
            sg[...] = slope_grad
            key_pre = pre[slot, 0]
            khid[...] = (key_pre * jax.nn.sigmoid(key_pre)).astype(bf16)
            dh[...] = (slope_grad * silu_slope(key_pre)).astype(bf16)
            lookup.part[...] = (
                (matmul(khid[...], c2[...]) + matmul(dh[...], low2[slot])).astype(bf16).reshape(2, chips, rows, width)
            )
            lookup.start_pair()
            finish(qstream, qsave, qout(turn + 1))

            @pl.when(step > 2)
            def _():
                finish(kstream, ksave, kout(turn + 2))

            lookup.take_pair()
            lookup.start_sends()
            query_rows(turn, slot)

            @pl.when(step > 1)
            def _():
                key_rows(1 - slot)
                kstream.start_pair()

            @pl.when(step + 1 < turns)
            def _():
                for copy in q_loads(turn - 1, 1 - slot) + k_loads(turn - 1, 1 - slot):
                    copy.start()

            query_weights(turn, slot)
            err = errs[slot].reshape(span, width)
            hk[...] = inner_right(err, c2[...])
            w2[...] += inner_left(dh[...], err)

            def sums(first_a, first_b, second_a, second_b, row):
                sums1_ref[turn, pl.ds(row, 1), :] = jnp.sum(first_a * first_b.astype(f32), axis=0, keepdims=True)
                sums2_ref[turn, pl.ds(row, 1), :] = jnp.sum(second_a * second_b.astype(f32), axis=0, keepdims=True)

            sums(cf[...], low1[slot], cs[...], low2[slot], 0)
            sums(cmf[...] + cf[...], m1[slot], cms[...] + cs[...], m2[slot], 1)
            sums(cmf[...] + cf[...], g1[slot], cms[...] + cs[...], g2[slot], 2)
            qstream.take_pair()
            total = lookup.total()
            mine = (total / span).astype(bf16)
            spread.whole[lane.colour, lane.chip] = mine
            qout(turn + 1).wait()

            @pl.when(step > 1)
            def _():
                vout(turn + 1).wait()

            @pl.when(step > 2)
            def _():
                kout(turn + 2).wait()

            vsave[...] = mine
            vout(turn).start()
            spread.run()
            lookup.wait_sends()
            qstream.start_sends()

            @pl.when(step > 1)
            def _():
                kstream.take_pair()
                kstream.start_sends()

            out = spread.whole[...].reshape(span, width)
            hidden_back = hk[...] + inner_right(out, low2[slot])
            key_pre = pre[slot, 0]
            hidden_grad = pre[slot, 1]
            slope = silu_slope(key_pre)
            kpl[...] = (hidden_back * slope + sg[...] * hidden_grad * silu_curve(key_pre)).astype(bf16)
            slow[...] = (hidden_grad * slope).astype(bf16)

            def update(c, m, acc, grad_new, place):
                grad = (1.0 - decay) * c[place] + grad_new
                both = m[place] + c[place]
                acc[place] += reset * grad
                c[place] = (1.0 - reset) * grad
                m[place] = (1.0 - reset) * (moment * both)

            for b in range(blocks):
                place = (pl.ds(b * block, block), slice(None))
                update(cf, cmf, a1, w1[place] + inner_left(kbuf[slot, b], kpl[...]), place)
            place = (slice(None), slice(None))
            update(cs, cms, a2, w2[...] + inner_left(khid[...], out), place)
            return carry

        lax.fori_loop(1, turns, body, 0)
        tail = Scatter(
            lane,
            kstream.part,
            lookup.pair,
            lookup.half,
            lookup.got,
            (lookup.pair_send, lookup.pair_recv, lookup.send, lookup.recv),
        )
        ends = [
            pltpu.make_async_copy(a1, mg1_hbm, end_sem.at[0]),
            pltpu.make_async_copy(a2, mg2_hbm, end_sem.at[1]),
        ]
        for copy in ends:
            copy.start()
        key_rows((turns - 1) % 2)
        tail.start_pair()
        finish(qstream, qsave, qout(0))
        if turns > 2:
            finish(kstream, ksave, kout(1))
        tail.take_pair()
        tail.start_sends()
        if turns > 2:
            kout(1).wait()
        finish(tail, ksave, kout(0))
        for copy in ends + [qout(0), kout(0), vout(0)]:
            copy.wait()

    state = [(width, hidden), (hidden, width)]
    q_buffers = [((blocks, span, block), bf16)] + [(s, bf16) for s in state] + [((span, hidden), f32)]
    k_buffers = (
        [((blocks, span, block), bf16)]
        + [(s, bf16) for s in state * 2]
        + [((2, chips, rows, width), bf16), ((2, span, hidden), f32)]
    )
    out_shape = (
        [jax.ShapeDtypeStruct((turns, rows, width), bf16)]
        + [jax.ShapeDtypeStruct((key_turns, rows, width), bf16)] * 2
        + [jax.ShapeDtypeStruct((key_turns, 8, hidden), f32), jax.ShapeDtypeStruct((key_turns, 8, width), f32)]
        + [jax.ShapeDtypeStruct(s, f32) for s in state]
    )
    sem = pltpu.SemaphoreType.DMA
    scratch = (
        [pltpu.VMEM((2,) + s, t) for s, t in q_buffers + k_buffers]
        + [pltpu.VMEM((wide, blocks, span, block), bf16), pltpu.VMEM((span, block), bf16)]
        + [pltpu.VMEM(s, f32) for s in state * 4]
        + [pltpu.VMEM((2,) + state[0], bf16), pltpu.VMEM(state[1], bf16)]
        + [pltpu.VMEM((span, hidden), bf16)] * 6
        + [pltpu.VMEM((span, hidden), f32)] * 2
        + [pltpu.VMEM((rows, width), bf16)] * 3
        + [sem((2, 4)), sem((2, 7)), sem((3,)), sem((2,)), sem((1,))]
        + Scatter.scratch(chips, rows, width) * 3
        + Spread.scratch(chips, rows, width)
        + Gather.scratch()
    )
    vmem = pl.BlockSpec(memory_space=pltpu.VMEM)
    smem = pl.BlockSpec(memory_space=pltpu.SMEM)
    return pl.pallas_call(
        kernel,
        out_shape=out_shape,
        in_specs=[ANY] * 12 + [smem] * 2,
        out_specs=[ANY] * 3 + [vmem] * 2 + [ANY] * 2,
        scratch_shapes=scratch,
        compiler_params=pltpu.CompilerParams(
            collective_id=ident, has_side_effects=True, vmem_limit_bytes=62 * 1024 * 1024
        ),
        cost_estimate=pl.CostEstimate(
            flops=80 * turns * 2 * span * width * hidden, bytes_accessed=turns * 60 * 2**20, transcendentals=0
        ),
        name="chain_backward",
    )(
        recall_grad, queries, low1_all, low2_all, qpre_all, keys, m1_all, m2_all, g1_all, g2_all, err_all, pre_all,
        spans, gates,
    )


def from_behind(value, axis, steps):
    count = lax.axis_size(axis)
    first, last = (max(0, -steps), min(count, count - steps))
    return lax.ppermute(value, axis, [(source, source + steps) for source in range(first, last)])


def split_heads(values, head_size):
    return values.reshape(values.shape[:-1] + (values.shape[-1] // head_size, head_size))


def head_norm(values, head_size):
    shaped = split_heads(values, head_size)
    factor = lax.rsqrt(jnp.sum(shaped * shaped, axis=-1, keepdims=True) + eps_head)
    return (shaped * factor).reshape(values.shape)


def head_norm_back(values, upstream, head_size):
    shaped = split_heads(values, head_size)
    grad_shaped = split_heads(upstream, head_size)
    factor = lax.rsqrt(jnp.sum(shaped * shaped, axis=-1, keepdims=True) + eps_head)
    normed = shaped * factor
    inner_sum = jnp.sum(normed * grad_shaped, axis=-1, keepdims=True)
    return (factor * (grad_shaped - normed * inner_sum)).reshape(values.shape)


def rms_back(scaled, factor, upstream):
    return factor * (upstream - scaled * jnp.mean(upstream * scaled, axis=-1, keepdims=True))


def body(
    tokens,
    cotangent,
    seq_spans,
    w_query,
    w_key,
    w_value,
    conv_kernel,
    persistent,
    norm_gain,
    rate_proj,
    out_gate,
    out_proj,
    memory_in,
    memory_out,
    ffn_gain,
    ffn_gate,
    ffn_up,
    ffn_down,
):
    wide, narrow = lax.axis_size("wide"), lax.axis_size("narrow")
    devices = wide * narrow
    wide_pos, narrow_pos = lax.axis_index("wide"), lax.axis_index("narrow")
    span, width = tokens.shape
    taps = conv_kernel.shape[0]
    persist_count = persistent.shape[1]
    local_width = out_gate.shape[1]
    own_rows = span // narrow
    lanes = wide // LANE_WIDE
    chips = LANE_WIDE * narrow // 2
    shards = 2 * chips
    shard_rows = span // shards
    hidden = memory_in.shape[1] // LANE_WIDE
    score_scale = math.sqrt(HEAD)

    def shard_of(tw, tn):
        return lax.rem(tn, 2) * chips + lax.rem(tw, LANE_WIDE) * (narrow // 2) + lax.div(tn, 2)

    long_turns = min(6, wide * 5 // 8)
    turns = max(long_turns, wide - long_turns)
    seq_ends = jnp.cumsum(seq_spans)
    seq_starts = seq_ends - seq_spans
    long_start = seq_starts[jnp.argmax(seq_spans)]
    order = jnp.arange(wide, dtype=jnp.int32)
    span_first = jnp.any(seq_starts[None, :] == order[:, None], axis=1)
    is_first = span_first[wide_pos]
    in_long = (order >= long_start) & (order < long_start + long_turns)
    lane_of = jnp.where(in_long, 0, 1)
    turn_of = jnp.where(in_long, order - long_start, jnp.where(order < long_start, order, order - long_turns))
    lane_pos = wide_pos // LANE_WIDE
    turn_order = jnp.arange(turns, dtype=jnp.int32)
    rest_order = jnp.where(turn_order < long_start, turn_order, turn_order + long_turns)
    lane_spans = jnp.clip(jnp.where(lane_pos == 0, long_start + turn_order, rest_order), 0, wide - 1)
    lane_count = jnp.where(lane_pos == 0, long_turns, jnp.where(lane_pos == 1, wide - long_turns, 0))
    lane_valid = turn_order < lane_count
    lane_first = span_first[lane_spans] | ~lane_valid

    smalls = [conv_kernel, persistent, norm_gain, ffn_gain, rate_proj]
    small_sizes = [a.size for a in smalls]
    packed = jnp.concatenate([a.reshape(-1) for a in smalls])
    padded = -(-packed.size // 2048) * 2048
    packed = jnp.pad(packed, (0, padded - packed.size)).reshape(-1, 128)
    own_weights = jnp.concatenate(
        [a.reshape(a.shape[0], narrow, local_width) for a in (w_query, w_key, w_value)], 2
    ).transpose(1, 0, 2)
    memory_cols = memory_in.reshape(memory_in.shape[0], LANE_WIDE, hidden).transpose(1, 0, 2)
    memory_rows = memory_out.reshape(LANE_WIDE, hidden, memory_out.shape[1])
    small_all, weights_all, first_all, second_all = send_parameters(
        packed, own_weights, [memory_cols, memory_rows], 1
    )
    first_init = first_all.reshape(width, hidden)
    second_init = second_all.transpose(1, 0, 2).reshape(hidden, width)
    small_all = small_all.reshape(devices, padded)
    pieces, at = [], 0
    for a, size in zip(smalls, small_sizes):
        pieces.append(small_all[:, at : at + size].reshape((devices,) + a.shape))
        at += size
    kernel_all = pieces[0].transpose(1, 0, 2).reshape(taps, 3, width)
    persist_all = pieces[1].transpose(1, 2, 0, 3).reshape(2, persist_count, width)
    gain_one = pieces[2].reshape(width).astype(f32)
    gain_two = pieces[3].reshape(width).astype(f32)
    rate_f = pieces[4].reshape(width, 3).astype(f32)
    col_offset = narrow_pos * local_width

    def own_cols(values, axis):
        return lax.dynamic_slice_in_dim(values, col_offset, local_width, axis)

    def own_part(values):
        return lax.dynamic_slice_in_dim(values, narrow_pos * own_rows, own_rows, 0)

    kernel_f = own_cols(kernel_all, 2).reshape(taps, 3 * local_width).astype(f32)
    persist_f = own_cols(persist_all, 2).astype(f32)
    qkv_weights = weights_all.reshape(width, 3 * local_width)

    inputs_f = tokens.astype(f32)
    first_factor = lax.rsqrt(jnp.mean(inputs_f * inputs_f, axis=-1, keepdims=True) + eps_norm)
    first_scaled = inputs_f * first_factor
    normed = first_scaled * gain_one
    normed_low = normed.astype(bf16)
    projected = matmul(normed_low, qkv_weights)
    tail_rows = from_behind(projected[span - taps + 1 :].astype(bf16), "wide", 1).astype(f32)
    extended = jnp.concatenate([jnp.where(is_first, 0.0, tail_rows), projected], 0)
    mixed_conv = kernel_f[0] * projected
    for offset in range(1, taps):
        start_row = taps - 1 - offset
        mixed_conv = mixed_conv + kernel_f[offset] * extended[start_row : start_row + span]
    activated = jax.nn.silu(mixed_conv)
    query_act = activated[:, :local_width]
    key_act = activated[:, local_width : 2 * local_width]
    query_low = head_norm(query_act, HEAD).astype(bf16)
    key_low = head_norm(key_act, HEAD).astype(bf16)
    value_low = activated[:, 2 * local_width :].astype(bf16)
    span_mean = jnp.mean(normed, axis=0)
    gate_scale = jnp.array([decay_top, moment_top, learn_top], f32)
    gate_sig = jax.nn.sigmoid(jnp.sum(span_mean[:, None] * rate_f, axis=0))
    gate_tile = jnp.broadcast_to(jnp.pad(gate_sig * gate_scale, (0, 125))[None], (8, 128))

    key_all, value_got, gate_got = rows_to_lanes(
        key_low, value_low.reshape(shards, shard_rows, local_width), shard_of, gate_tile, 2
    )
    later = (ffn_gate, ffn_up, ffn_down, jnp.concatenate([out_gate, out_proj.T], 1))
    key_all, *later = lax.optimization_barrier((key_all,) + later)
    out_weights = lax.all_gather(later[3], "wide", axis=0, tiled=True)
    ffn_gate_cols = lax.all_gather(later[0], "wide", axis=0, tiled=True)
    ffn_up_cols = lax.all_gather(later[1], "wide", axis=0, tiled=True)
    ffn_down_rows = lax.all_gather(later[2], "wide", axis=1, tiled=True)
    gate_cols = out_weights[:, :local_width]
    proj_cols = out_weights[:, local_width:]
    gate_rows = gate_got[::narrow, 0, :3]
    lane_gates = gate_rows[lane_spans]
    first_f = lane_first.astype(f32)
    next_first = jnp.concatenate([first_f[1:], jnp.ones((1,), f32)])
    key_index = lane_spans
    if wide > 8:
        key_all, key_index = key_all[lane_spans], turn_order
    chain = chain_forward(
        key_all,
        key_index,
        value_got,
        query_low,
        lane_spans,
        jnp.concatenate([lane_gates, next_first[:, None]], 1),
        first_init,
        second_init,
        3,
    )
    recalled_lane, saved = chain[0], chain[1:]

    def by_span(lane_rows):
        spans = lane_rows[turn_of]
        return spans.reshape(wide, shard_rows, narrow, local_width).transpose(0, 2, 1, 3)

    def from_lane(got):
        got = got.reshape(lanes, LANE_WIDE, narrow // 2, 2, shard_rows, local_width)
        own = lax.dynamic_index_in_dim(got, lane_of[wide_pos], 0, keepdims=False)
        return own.transpose(2, 0, 1, 3, 4).reshape(span, local_width)

    recalled_got = exchange(
        [
            (
                by_span(recalled_lane).reshape(devices, shard_rows, local_width),
                lambda tw, tn: tw * narrow + tn,
            )
        ],
        "all",
        6,
    )[0]
    recall_low = from_lane(recalled_got)
    recall_own = recall_low.astype(f32)

    keys_all = jnp.concatenate(
        [head_norm(persist_f[0], HEAD).astype(bf16), head_norm(recall_own, HEAD).astype(bf16), key_low], 0
    )
    values_all = jnp.concatenate([persist_f[1].astype(bf16), recall_low, value_low], 0)
    query_heads = split_heads(query_low, HEAD)
    key_heads = split_heads(keys_all, HEAD)
    value_heads = split_heads(values_all, HEAD)
    key_total = keys_all.shape[0]
    row_index = lax.broadcasted_iota(jnp.int32, (span, key_total), 0)
    col_index = lax.broadcasted_iota(jnp.int32, (span, key_total), 1)
    allowed = (col_index < persist_count + span) | (col_index - persist_count - span <= row_index)

    def score_block():
        raw_scores = (
            jnp.einsum("thd,jhd->htj", query_heads, key_heads, preferred_element_type=f32) * score_scale
        )
        return jnp.where(allowed[None], raw_scores, masked_score)

    scores = score_block()
    row_top = jnp.max(scores, axis=-1, keepdims=True)
    exponent = jnp.exp(scores - row_top)
    total_sum = jnp.sum(exponent, axis=-1, keepdims=True)
    log_total = row_top + jnp.log(total_sum)
    weights_low = (exponent / total_sum).astype(bf16)
    attended = jnp.einsum("htj,jhd->thd", weights_low, value_heads, preferred_element_type=f32).reshape(
        span, local_width
    )
    gate_pre = matmul(normed_low, gate_cols)
    gate_sigmoid = jax.nn.sigmoid(gate_pre)
    gated_low = (attended * gate_sigmoid).astype(bf16)

    def by_rows(part):
        return part.astype(bf16).reshape(narrow, own_rows, width)

    tokens_own, cotangent_own = own_part(tokens), own_part(cotangent)
    rows_f32, row_f32 = ((own_rows, width), f32), ((1, width), f32)

    def scaled_of(values):
        factor = lax.rsqrt(jnp.mean(values * values, axis=-1, keepdims=True) + eps_norm)
        return values * factor, factor

    def after_branch(totals, extras):
        tokens_rows, gain = extras
        middle = tokens_rows.astype(f32) + totals[0]
        return [(scaled_of(middle)[0] * gain).astype(bf16)], [middle]

    normed_two, middle = narrow_step(
        [by_rows(inner_right(gated_low, proj_cols))],
        [tokens_own, gain_two[None]],
        after_branch,
        1,
        [rows_f32],
        7,
    )
    normed_two = normed_two.reshape(span, width)
    gate_val = matmul(normed_two, ffn_gate_cols)
    up_val = matmul(normed_two, ffn_up_cols)
    gate_silu = jax.nn.silu(gate_val)
    hidden_ffn = (gate_silu * up_val).astype(bf16)
    ffn_part = matmul(hidden_ffn, ffn_down_rows)
    down_grad = inner_left(cotangent, hidden_ffn).astype(bf16)
    hidden_grad_ffn = inner_right(cotangent, ffn_down_rows)
    gate_sig_ffn = jax.nn.sigmoid(gate_val)
    gate_grad_low = (
        hidden_grad_ffn * up_val * gate_sig_ffn * (1.0 + gate_val * (1.0 - gate_sig_ffn))
    ).astype(bf16)
    up_grad_low = (hidden_grad_ffn * gate_silu).astype(bf16)
    ffn_gate_grad = inner_left(normed_two, gate_grad_low).astype(bf16)
    ffn_up_grad = inner_left(normed_two, up_grad_low).astype(bf16)
    normed_two_part = inner_right(gate_grad_low, ffn_gate_cols) + inner_right(up_grad_low, ffn_up_cols)

    def scatter_wide(grad):
        return lax.psum_scatter(grad.astype(bf16), "wide", scatter_dimension=0, tiled=True).astype(f32)

    ffn_sums = (by_rows(ffn_part), by_rows(normed_two_part))
    ffn_sums, ffn_grads = lax.optimization_barrier((ffn_sums, (ffn_gate_grad, ffn_up_grad, down_grad)))
    ffn_gate_out, ffn_up_out, ffn_down_out = [scatter_wide(a) for a in ffn_grads]

    def after_ffn(totals, extras):
        middle_rows, cotangent_rows, gain = extras
        scaled, factor = scaled_of(middle_rows)
        grad = cotangent_rows.astype(f32) + rms_back(scaled, factor, totals[1] * gain)
        gain_part = jnp.sum(totals[1] * scaled, axis=0, keepdims=True)
        return [grad.astype(bf16), (middle_rows + totals[0]).astype(bf16)], [grad, gain_part]

    branch_low, output, middle_grad, gain_two_part = narrow_step(
        list(ffn_sums), [middle, cotangent_own, gain_two[None]], after_ffn, 2, [rows_f32, row_f32], 9
    )
    branch_low, output = branch_low.reshape(span, width), output.reshape(span, width)

    gated_grad = matmul(branch_low, proj_cols)
    attended_grad_low = (gated_grad * gate_sigmoid).astype(bf16)
    gate_pre_low = (gated_grad * attended * gate_sigmoid * (1.0 - gate_sigmoid)).astype(bf16)
    proj_grad = inner_left(branch_low, gated_low)

    weights_again = jnp.exp(score_block() - log_total)
    grad_heads = split_heads(attended_grad_low, HEAD)
    weight_grad = jnp.einsum("thd,jhd->htj", grad_heads, value_heads, preferred_element_type=f32)
    row_delta = jnp.sum(weights_again * weight_grad, axis=-1, keepdims=True)
    score_grad_low = (weights_again * (weight_grad - row_delta)).astype(bf16)
    query_att = (
        score_scale * jnp.einsum("htj,jhd->thd", score_grad_low, key_heads, preferred_element_type=f32)
    ).reshape(span, local_width)
    keys_grad = (
        score_scale * jnp.einsum("htj,thd->jhd", score_grad_low, query_heads, preferred_element_type=f32)
    ).reshape(key_total, local_width)
    values_grad = jnp.einsum(
        "htj,thd->jhd", weights_again.astype(bf16), grad_heads, preferred_element_type=f32
    ).reshape(key_total, local_width)
    recall_end = persist_count + span
    persist_part = jnp.stack(
        [head_norm_back(persist_f[0], keys_grad[:persist_count], HEAD), values_grad[:persist_count]]
    )
    recall_grad_low = (
        head_norm_back(recall_own, keys_grad[persist_count:recall_end], HEAD)
        + values_grad[persist_count:recall_end]
    ).astype(bf16)

    qcot, kcot, vcot, sums1, sums2, first_grad, second_grad = chain_backward(
        recall_grad_low,
        saved,
        lane_spans,
        jnp.concatenate([lane_gates, first_f[:, None], lane_valid.astype(f32)[:, None]], 1),
        12,
    )
    kcot, vcot = [jnp.concatenate([a, jnp.zeros_like(a[:1])], 0) for a in (kcot, vcot)]
    lane_sums = jnp.sum(sums1[:, :3], axis=2) + jnp.sum(sums2[:, :3], axis=2)
    lane_sums = jnp.pad(lane_sums, ((0, 1), (0, 0)))
    span_sums = jnp.where((lane_of == lane_pos)[:, None], lane_sums[turn_of], 0.0)
    sums_tile = jnp.pad(span_sums, ((0, 0), (0, 125)))
    cots = jnp.stack([by_span(a) for a in (qcot, kcot, vcot)], 2)
    cots_got, sums_got = exchange(
        [
            (cots.reshape(devices, 3, shard_rows, local_width), lambda tw, tn: tw * narrow + tn),
            (sums_tile, None),
        ],
        "all",
        13,
    )
    query_mem, key_mem, value_mem = [from_lane(cots_got[:, i]).astype(f32) for i in range(3)]
    gate_sums = jnp.sum(sums_got[:, :, :3], axis=0)[wide_pos] * jnp.array([-1.0, 1.0, -1.0], f32)
    first_got, second_got = exchange(
        [
            (first_grad.astype(bf16).reshape(wide, width // wide, hidden), lambda tw, tn: tw),
            (
                second_grad.astype(bf16).reshape(hidden, wide, width // wide).transpose(1, 0, 2),
                lambda tw, tn: tw,
            ),
        ],
        "wide",
        14,
    )

    def over_lanes(got):
        return jnp.sum(got.reshape((lanes, LANE_WIDE) + got.shape[1:]).astype(f32), axis=0)

    first_out = over_lanes(first_got).transpose(1, 0, 2).reshape(width // wide, LANE_WIDE * hidden)
    second_out = over_lanes(second_got).reshape(LANE_WIDE * hidden, width // wide)

    logit_grad = gate_sums * gate_scale * gate_sig * (1.0 - gate_sig)
    rate_part = span_mean[:, None] * logit_grad[None, :]
    gate_row = jnp.sum(rate_f * logit_grad[None, :], axis=1)[None, :] / span
    act_grad = jnp.concatenate(
        [
            head_norm_back(query_act, query_mem + query_att, HEAD),
            head_norm_back(key_act, key_mem + keys_grad[recall_end:], HEAD),
            values_grad[recall_end:] - value_mem,
        ],
        1,
    )
    conv_grad = act_grad * silu_slope(mixed_conv)
    kernel_rows = []
    extended_grad = jnp.zeros_like(extended)
    for offset in range(taps):
        start_row = taps - 1 - offset
        kernel_rows.append(jnp.sum(conv_grad * extended[start_row : start_row + span], axis=0))
        extended_grad = extended_grad + jnp.pad(kernel_f[offset] * conv_grad, ((start_row, offset), (0, 0)))
    tail_back = from_behind(
        jnp.where(is_first, 0.0, extended_grad[: taps - 1]).astype(bf16), "wide", -1
    ).astype(f32)
    projected_grad = extended_grad[taps - 1 :] + jnp.pad(tail_back, ((span - taps + 1, 0), (0, 0)))
    projected_low = projected_grad.astype(bf16)
    normed_part = inner_right(projected_low, qkv_weights) + inner_right(gate_pre_low, gate_cols)

    def after_all(totals, extras):
        tokens_rows, grad_rows, gain, row = extras
        scaled, factor = scaled_of(tokens_rows.astype(f32))
        normed_grad = totals[0] + row
        gain_part = jnp.sum(normed_grad * scaled, axis=0, keepdims=True)
        return [(grad_rows + rms_back(scaled, factor, normed_grad * gain)).astype(bf16)], [gain_part]

    tokens_grad, gain_one_part = narrow_step(
        [by_rows(normed_part)], [tokens_own, middle_grad, gain_one[None], gate_row], after_all, 1, [row_f32], 15
    )
    tokens_grad = tokens_grad.reshape(span, width).astype(f32)
    weight_grads = inner_left(normed_low, jnp.concatenate([projected_low, gate_pre_low], 1))
    weight_out = scatter_wide(weight_grads)
    proj_out = scatter_wide(proj_grad)

    def place_cols(piece, axis):
        full = piece.shape[:axis] + (width,) + piece.shape[axis + 1 :]
        return lax.dynamic_update_slice_in_dim(jnp.zeros(full, f32), piece, col_offset, axis)

    kernel_full = place_cols(jnp.stack(kernel_rows).reshape(taps, 3, local_width), 2).reshape(taps, 3 * width)
    persist_full = place_cols(persist_part, 2)
    rate_part = jnp.where(narrow_pos == 0, rate_part, 0.0)
    chunks = [
        kernel_full.reshape(taps, devices, -1).transpose(1, 0, 2),
        persist_full.reshape(2, persist_count, devices, -1).transpose(2, 0, 1, 3),
        gain_one_part.reshape(devices, -1),
        gain_two_part.reshape(devices, -1),
        rate_part.reshape(devices, -1, 3),
    ]
    flat = jnp.concatenate([a.reshape(devices, -1) for a in chunks], 1)
    flat_size = -(-flat.shape[1] // 1024) * 1024
    flat = jnp.pad(flat, ((0, 0), (0, flat_size - flat.shape[1]))).reshape(devices, -1, 128)
    flat_got = exchange([(flat, lambda tw, tn: tw * narrow + tn)], "all", 17)[0]
    flat_sum = jnp.sum(flat_got, axis=0).reshape(-1)
    small_outs, at = [], 0
    for a in chunks:
        size = a.size // devices
        small_outs.append(flat_sum[at : at + size].reshape(a.shape[1:]))
        at += size
    kernel_grad, persist_grad, norm_grad, ffn_gain_grad, rate_grad = small_outs
    return (
        output,
        tokens_grad,
        weight_out[:, :local_width],
        weight_out[:, local_width : 2 * local_width],
        weight_out[:, 2 * local_width : 3 * local_width],
        kernel_grad,
        persist_grad,
        norm_grad,
        rate_grad,
        weight_out[:, 3 * local_width :],
        proj_out.T,
        first_out,
        second_out,
        ffn_gain_grad,
        ffn_gate_out,
        ffn_up_out,
        ffn_down_out.T,
    )


def solution(mesh):
    rows, both, square, turned = P("wide", None), P(("wide", "narrow"), None), P("wide", "narrow"), P("narrow", "wide")
    flat, taps, heads = P(("wide", "narrow")), P(None, ("wide", "narrow")), P(None, None, ("wide", "narrow"))
    return jax.shard_map(
        body,
        mesh=mesh,
        in_specs=(rows, rows, P(), both, both, both, taps, heads, flat, both)
        + (square, turned, square, turned, flat, square, square, turned),
        out_specs=(rows, rows, square, square, square, taps, heads, flat, both)
        + (square, turned, square, turned, flat, square, square, turned),
        check_vma=False,
    )
```

```python
import math

import jax
import jax.numpy as jnp
from jax import lax
from jax.experimental import pallas as pl
from jax.experimental.pallas import tpu as pltpu
from jax.sharding import PartitionSpec as P

HEAD = 64
LANE_WIDE = 4
MESH = pl.DeviceIdType.MESH
ANY = pl.BlockSpec(memory_space=pl.ANY)
bf16 = jnp.bfloat16
f32 = jnp.float32

decay_top = 0.2
moment_top = 0.9
learn_top = 0.1
eps_norm = 1e-05
eps_head = 1e-06
masked_score = -1e30


def remote(src, dst, send, recv, device):
    return pltpu.make_async_remote_copy(
        src_ref=src, dst_ref=dst, send_sem=send, recv_sem=recv, device_id=device, device_id_type=MESH
    )


class Grid:
    def __init__(self):
        wide, narrow = lax.axis_size("wide"), lax.axis_size("narrow")
        self.zs = 4 if wide % 4 == 0 else 1
        self.xs, self.ys = wide // self.zs, narrow // 2
        self.wide, self.narrow = lax.axis_index("wide"), lax.axis_index("narrow")
        self.z, self.x = lax.div(self.wide, self.xs), lax.rem(self.wide, self.xs)
        self.y, self.c = lax.div(self.narrow, 2), lax.rem(self.narrow, 2)
        self.partner = self.device(self.z, self.x, self.y, 1 - self.c)

    def device(self, z, x, y, c):
        return z * self.xs + x, 2 * y + c

    def z_others(self):
        if self.zs != 4:
            return [lax.rem(self.z + s, self.zs) for s in range(1, self.zs)]
        near = self.z + 1 - 2 * lax.div(self.z + 3, 4)
        far = 3 - 3 * lax.div(self.z, 2)
        return [near, 6 - self.z - near - far, far]

    def x_others(self):
        return [lax.rem(self.x + s, self.xs) for s in range(1, self.xs)]

    def y_others(self):
        return [lax.rem(self.y + s, self.ys) for s in range(1, self.ys)]

    def greet_all(self):
        wide, narrow = lax.axis_size("wide"), lax.axis_size("narrow")
        devices = wide * narrow
        me = self.wide * narrow + self.narrow
        barrier = pltpu.get_barrier_semaphore()

        def greet(step, carry):
            target = lax.rem(me + step, devices)
            where = lax.div(target, narrow), lax.rem(target, narrow)
            pl.semaphore_signal(barrier, inc=1, device_id=where, device_id_type=MESH)
            return carry

        lax.fori_loop(1, devices, greet, 0)
        return lambda: pl.semaphore_wait(barrier, devices - 1)


class Gather:
    def __init__(self, grid, source, whole, sems):
        self.grid, self.source, self.whole = grid, source, whole
        self.sent, self.got, self.sent_pair, self.got_pair = sems
        self.rows = whole.shape[2]
        self.pushes, self.pairs = 0, 0

    @staticmethod
    def counts():
        zs = 4 if lax.axis_size("wide") % 4 == 0 else 1
        xs, ys = lax.axis_size("wide") // zs, lax.axis_size("narrow") // 2
        sends = 2 * (zs - 1) + zs * 2 * (xs - 1 + ys - 1) + 2 * zs * (xs - 1) * (ys - 1)
        return zs * xs * ys, sends, 2 * zs * xs * ys

    @classmethod
    def scratch(cls):
        chips, sends, pairs = cls.counts()
        return [
            pltpu.SemaphoreType.DMA((sends,)),
            pltpu.SemaphoreType.DMA((chips, 2)),
            pltpu.SemaphoreType.DMA((pairs,)),
            pltpu.SemaphoreType.DMA((chips, 2)),
        ]

    def half(self, ref, h):
        return ref.at[pl.ds(h * (self.rows // 2), self.rows // 2)]

    def piece(self, z, x, y, c, h):
        wide, narrow = self.grid.device(z, x, y, c)
        return self.half(self.whole.at[wide, narrow], h)

    def spot(self, z, x, y):
        return (z * self.grid.xs + x) * self.grid.ys + y

    def push(self, z, x, y, h, target, own):
        here = self.piece(z, x, y, self.grid.c, h)
        copy = remote(
            self.half(self.source, h) if own else here,
            here,
            self.sent.at[self.pushes],
            self.got.at[self.spot(z, x, y), h],
            target,
        )
        self.pushes += 1
        copy.start()

    def to_partner(self, z, x, y, h, own=False):
        here = self.piece(z, x, y, self.grid.c, h)
        copy = remote(
            self.half(self.source, h) if own else here,
            here,
            self.sent_pair.at[self.pairs],
            self.got_pair.at[self.spot(z, x, y), h],
            self.grid.partner,
        )
        self.pairs += 1
        copy.start()

    def arrived(self, z, x, y, h):
        here = self.piece(z, x, y, self.grid.c, h)
        remote(here, here, self.sent.at[0], self.got.at[self.spot(z, x, y), h], self.grid.partner).wait_recv()

    def fan(self, z, own=False):
        g = self.grid
        to_y = [g.device(g.z, g.x, y, g.c) for y in g.y_others()]
        to_x = [g.device(g.z, x, g.y, g.c) for x in g.x_others()]
        for h, targets in ((0, to_y), (1, to_x), (0, to_x), (1, to_y)):
            for target in targets:
                self.push(z, g.x, g.y, h, target, own)
        for h in (0, 1):
            self.to_partner(z, g.x, g.y, h, own)

    def begin(self):
        g = self.grid
        for z in g.z_others():
            for h in (0, 1):
                self.push(g.z, g.x, g.y, h, g.device(z, g.x, g.y, g.c), True)
        self.fan(g.z, True)

    def level(self, number):
        return ([self.grid.z] + self.grid.z_others())[number]

    def along_z(self, number):
        g, z = self.grid, self.level(number)
        for h in (0, 1):
            self.arrived(z, g.x, g.y, h)
        self.fan(z)

    def across(self, number):
        g, z = self.grid, self.level(number)
        for y in g.y_others():
            self.arrived(z, g.x, y, 0)
            for x in g.x_others():
                self.push(z, g.x, y, 0, g.device(g.z, x, g.y, g.c), False)
            self.to_partner(z, g.x, y, 0)
        for x in g.x_others():
            self.arrived(z, x, g.y, 1)
            for y in g.y_others():
                self.push(z, x, g.y, 1, g.device(g.z, g.x, y, g.c), False)
            self.to_partner(z, x, g.y, 1)

    def last(self, number):
        g, z = self.grid, self.level(number)
        for x in g.x_others():
            self.arrived(z, x, g.y, 0)
            self.to_partner(z, x, g.y, 0)
            for y in g.y_others():
                self.arrived(z, x, y, 0)
                self.to_partner(z, x, y, 0)
        for y in g.y_others():
            self.arrived(z, g.x, y, 1)
            self.to_partner(z, g.x, y, 1)
            for x in g.x_others():
                self.arrived(z, x, y, 1)
                self.to_partner(z, x, y, 1)

    def middle(self):
        for number in range(1, self.grid.zs):
            self.along_z(number)
            self.across(number - 1)
            if number > 1:
                self.last(number - 2)
        self.across(self.grid.zs - 1)
        for number in range(max(0, self.grid.zs - 2), self.grid.zs):
            self.last(number)

    def finish(self):
        g = self.grid
        here = self.piece(g.z, g.x, g.y, g.c, 0)
        _, sends, pairs = self.counts()
        for sems, number in ((self.sent, sends), (self.sent_pair, pairs)):
            for i in range(number):
                remote(here, here, sems.at[i], self.got.at[0, 0], g.partner).wait_send()
        for z in range(g.zs):
            for x in range(g.xs):
                for y in range(g.ys):
                    for h in (0, 1):
                        there = self.piece(z, x, y, 1 - g.c, h)
                        remote(
                            there, there, self.sent.at[0], self.got_pair.at[self.spot(z, x, y), h], g.partner
                        ).wait_recv()


def send_parameters(smalls, weights, blocks, ident):
    wide, narrow = lax.axis_size("wide"), lax.axis_size("narrow")
    devices = wide * narrow
    count = len(blocks)

    def kernel(*refs):
        smalls_ref, weights_ref = refs[:2]
        block_refs, refs = refs[2 : 2 + count], refs[2 + count :]
        smalls_out, weights_out = refs[:2]
        block_outs, refs = refs[2 : 2 + count], refs[2 + count :]
        hold_small, hold_weight, refs = refs[0], refs[1], refs[2:]
        hold_blocks, refs = refs[:count], refs[count:]
        local_sem, all_send, all_recv, near_send, near_recv, z_send, z_recv, x_send, x_recv, b_send, b_recv = refs
        g = Grid()
        me = g.wide * narrow + g.narrow
        wait_all = g.greet_all()
        own = [
            (smalls_ref, hold_small, smalls_out.at[me]),
            (weights_ref.at[g.narrow], hold_weight, weights_out.at[g.wide, g.narrow]),
        ] + [
            (block_refs[i].at[lax.rem(g.wide, LANE_WIDE)], hold_blocks[i], block_outs[i].at[g.wide])
            for i in range(count)
        ]
        into = [pltpu.make_async_copy(a, b, local_sem.at[i]) for i, (a, b, _) in enumerate(own)]
        back = [pltpu.make_async_copy(b, c, local_sem.at[i]) for i, (_, b, c) in enumerate(own)]
        for copy in into:
            copy.start()
        wait_all()
        near = []
        for s in range(1, narrow):
            target = lax.rem(g.narrow + s, narrow)
            copy = remote(
                weights_ref.at[target],
                weights_out.at[g.wide, g.narrow],
                near_send.at[s],
                near_recv.at[g.narrow],
                (g.wide, target),
            )
            copy.start()
            near.append(copy)

        def send_small(step, carry):
            target = lax.rem(me + step, devices)
            remote(
                smalls_ref,
                smalls_out.at[me],
                all_send.at[0],
                all_recv.at[0],
                (lax.div(target, narrow), lax.rem(target, narrow)),
            ).start()
            return carry

        lax.fori_loop(1, devices, send_small, 0)
        for copy in into:
            copy.wait()
        for copy in back:
            copy.start()
        for copy in back:
            copy.wait()
        for s in range(1, narrow):
            source = lax.rem(g.narrow + s, narrow)
            there = weights_out.at[g.wide, source]
            remote(there, there, near_send.at[s], near_recv.at[source], g.partner).wait_recv()

        def row(z, x):
            return weights_out.at[z * g.xs + x]

        sends = []

        def push(z, target, send, recv):
            copy = remote(row(z, g.x), row(z, g.x), send, recv, target)
            copy.start()
            sends.append(copy)

        for i, z in enumerate(g.z_others()):
            push(g.z, g.device(z, g.x, g.y, g.c), z_send.at[i], z_recv.at[g.z])
        for i, x in enumerate(g.x_others()):
            push(g.z, g.device(g.z, x, g.y, g.c), x_send.at[0, i], x_recv.at[g.z, g.x])
        for s in range(1, wide):
            target = lax.rem(g.wide + s, wide)
            for i in range(count):
                copy = remote(
                    block_refs[i].at[lax.rem(target, LANE_WIDE)],
                    block_outs[i].at[g.wide],
                    b_send.at[i, s],
                    b_recv.at[i, g.wide],
                    (target, g.narrow),
                )
                copy.start()
                sends.append(copy)
        for j, z in enumerate(g.z_others()):
            remote(row(z, g.x), row(z, g.x), z_send.at[0], z_recv.at[z], g.partner).wait_recv()
            for i, x in enumerate(g.x_others()):
                push(z, g.device(g.z, x, g.y, g.c), x_send.at[1 + j, i], x_recv.at[z, g.x])
        for x in g.x_others():
            for z in [g.z] + g.z_others():
                remote(row(z, x), row(z, x), z_send.at[0], x_recv.at[z, x], g.partner).wait_recv()
        for s in range(1, wide):
            source = lax.rem(g.wide + s, wide)
            for i in range(count):
                there = block_outs[i].at[source]
                remote(there, there, z_send.at[0], b_recv.at[i, source], g.partner).wait_recv()
        for copy in near + sends:
            copy.wait_send()
        others = smalls_out.at[pl.ds(0, devices - 1)]
        whole = remote(others, others, all_send.at[0], all_recv.at[0], g.partner)
        whole.wait_send()
        whole.wait_recv()

    zs = 4 if wide % 4 == 0 else 1
    xs = wide // zs
    sem = pltpu.SemaphoreType.DMA
    return pl.pallas_call(
        kernel,
        out_shape=[
            jax.ShapeDtypeStruct((devices,) + smalls.shape, smalls.dtype),
            jax.ShapeDtypeStruct((wide, narrow) + weights.shape[1:], weights.dtype),
        ]
        + [jax.ShapeDtypeStruct((wide,) + b.shape[1:], b.dtype) for b in blocks],
        in_specs=[ANY] * (2 + count),
        out_specs=[ANY] * (2 + count),
        scratch_shapes=[pltpu.VMEM(smalls.shape, smalls.dtype), pltpu.VMEM(weights.shape[1:], weights.dtype)]
        + [pltpu.VMEM(b.shape[1:], b.dtype) for b in blocks]
        + [sem((2 + count,)), sem((1,)), sem((1,)), sem((narrow,)), sem((narrow,)), sem((zs,)), sem((zs,))]
        + [sem((zs, xs)), sem((zs, xs)), sem((count, wide)), sem((count, wide))],
        compiler_params=pltpu.CompilerParams(collective_id=ident, has_side_effects=True),
        name="send_parameters",
    )(smalls, weights, *blocks)


def rows_to_lanes(rows, chunks, pick, tile, ident):
    wide, narrow = lax.axis_size("wide"), lax.axis_size("narrow")
    devices = wide * narrow

    def kernel(rows_ref, chunks_ref, tile_ref, rows_out, chunks_out, tile_out, *refs):
        hold_rows, hold_chunk, hold_tile, local_sem, send, recv = refs[:6]
        g = Grid()
        me = g.wide * narrow + g.narrow
        wait_all = g.greet_all()
        own = [
            (rows_ref, hold_rows, rows_out.at[g.wide, g.narrow]),
            (chunks_ref.at[pick(g.wide, g.narrow)], hold_chunk, chunks_out.at[me]),
            (tile_ref, hold_tile, tile_out.at[me]),
        ]
        into = [pltpu.make_async_copy(a, b, local_sem.at[i]) for i, (a, b, _) in enumerate(own)]
        back = [pltpu.make_async_copy(b, c, local_sem.at[i]) for i, (_, b, c) in enumerate(own)]
        for copy in into:
            copy.start()
        wait_all()
        gather = Gather(g, rows_ref, rows_out, refs[6:])
        gather.begin()

        def send_chunks(step, carry):
            target = lax.rem(me + step, devices)
            where = lax.div(target, narrow), lax.rem(target, narrow)
            remote(chunks_ref.at[pick(*where)], chunks_out.at[me], send.at[0], recv.at[0], where).start()
            remote(tile_ref, tile_out.at[me], send.at[1], recv.at[1], where).start()
            return carry

        lax.fori_loop(1, devices, send_chunks, 0)
        for copy in into:
            copy.wait()
        for copy in back:
            copy.start()
        gather.middle()
        for copy in back:
            copy.wait()
        for i, out in enumerate((chunks_out, tile_out)):
            others = out.at[pl.ds(0, devices - 1)]
            whole = remote(others, others, send.at[i], recv.at[i], g.partner)
            whole.wait_send()
            whole.wait_recv()
        gather.finish()

    return pl.pallas_call(
        kernel,
        out_shape=[
            jax.ShapeDtypeStruct((wide, narrow) + rows.shape, rows.dtype),
            jax.ShapeDtypeStruct((devices,) + chunks.shape[1:], chunks.dtype),
            jax.ShapeDtypeStruct((devices,) + tile.shape, tile.dtype),
        ],
        in_specs=[ANY] * 3,
        out_specs=[ANY] * 3,
        scratch_shapes=[
            pltpu.VMEM(rows.shape, rows.dtype),
            pltpu.VMEM(chunks.shape[1:], chunks.dtype),
            pltpu.VMEM(tile.shape, tile.dtype),
            pltpu.SemaphoreType.DMA((3,)),
            pltpu.SemaphoreType.DMA((2,)),
            pltpu.SemaphoreType.DMA((2,)),
        ]
        + Gather.scratch(),
        compiler_params=pltpu.CompilerParams(collective_id=ident, has_side_effects=True),
        name="rows_to_lanes",
    )(rows, chunks, tile)


def narrow_step(parts, extras, work, spread_count, locals_like, ident):
    narrow, rows, width = parts[0].shape
    ys = narrow // 2
    count, extra_count, local_count = len(parts), len(extras), len(locals_like)
    parts = [p.reshape(ys, 2, rows, width) for p in parts]

    def kernel(*refs):
        part_refs, refs = refs[:count], refs[count:]
        extra_refs, refs = refs[:extra_count], refs[extra_count:]
        spread_refs, refs = refs[:spread_count], refs[spread_count:]
        local_refs, refs = refs[:local_count], refs[local_count:]
        mine, pair, half, got, rowbuf, refs = refs[0], refs[1], refs[2], refs[3], refs[4], refs[5:]
        load_sem, pair_send, pair_recv, y_send, y_recv, s_send, s_recv, p_send, p_recv, own_sem = refs
        g = Grid()
        barrier = pltpu.get_barrier_semaphore()
        friends = [g.device(g.z, g.x, y, g.c) for y in g.y_others()] + [g.partner]
        for friend in friends:
            pl.semaphore_signal(barrier, inc=1, device_id=friend, device_id_type=MESH)
        loads = [
            pltpu.make_async_copy(part_refs[i].at[:, g.c], mine.at[i], load_sem.at[i]) for i in range(count)
        ]
        for copy in loads:
            copy.start()
        pl.semaphore_wait(barrier, len(friends))
        pairs = [
            remote(part_refs[i].at[:, 1 - g.c], pair.at[i], pair_send.at[i], pair_recv.at[i], g.partner)
            for i in range(count)
        ]
        for copy in pairs:
            copy.start()
        sends = []
        for i in range(count):
            loads[i].wait()
            pairs[i].wait_recv()
            half[i] = (mine[i].astype(f32) + pair[i].astype(f32)).astype(bf16)
            for s, y in enumerate(g.y_others()):
                copy = remote(
                    half.at[i, y], got.at[i, g.y], y_send.at[i, s], y_recv.at[i, g.y], g.device(g.z, g.x, y, g.c)
                )
                copy.start()
                sends.append(copy)
        totals = []
        for i in range(count):
            total = half[i, g.y].astype(f32)
            for y in g.y_others():
                remote(got.at[i, y], got.at[i, y], y_send.at[i, 0], y_recv.at[i, y], g.partner).wait_recv()
                total = total + got[i, y].astype(f32)
            totals.append(total)
        spreads, locals_out = work(totals, [ref[...] for ref in extra_refs])
        for ref, value in zip(local_refs, locals_out):
            ref[...] = value
        own = []
        for i, value in enumerate(spreads):
            rowbuf[i] = value
            for s, y in enumerate(g.y_others()):
                copy = remote(
                    rowbuf.at[i],
                    spread_refs[i].at[g.narrow],
                    s_send.at[i, s],
                    s_recv.at[i, g.y],
                    g.device(g.z, g.x, y, g.c),
                )
                copy.start()
                sends.append(copy)
            copy = remote(
                rowbuf.at[i], spread_refs[i].at[g.narrow], p_send.at[i, g.y], p_recv.at[i, g.y], g.partner
            )
            copy.start()
            sends.append(copy)
            copy = pltpu.make_async_copy(rowbuf.at[i], spread_refs[i].at[g.narrow], own_sem.at[i])
            copy.start()
            own.append(copy)
        for i in range(spread_count):
            for y in g.y_others():
                there = spread_refs[i].at[2 * y + g.c]
                remote(there, there, s_send.at[i, 0], s_recv.at[i, y], g.partner).wait_recv()
                copy = remote(there, there, p_send.at[i, y], p_recv.at[i, y], g.partner)
                copy.start()
                sends.append(copy)
        for i in range(spread_count):
            for y in range(ys):
                there = spread_refs[i].at[2 * y + 1 - g.c]
                remote(there, there, s_send.at[i, 0], p_recv.at[i, y], g.partner).wait_recv()
        for copy in pairs + sends:
            copy.wait_send()
        for copy in own:
            copy.wait()

    sem = pltpu.SemaphoreType.DMA
    vmem = pl.BlockSpec(memory_space=pltpu.VMEM)
    return pl.pallas_call(
        kernel,
        out_shape=[jax.ShapeDtypeStruct((narrow, rows, width), bf16)] * spread_count
        + [jax.ShapeDtypeStruct(shape, dtype) for shape, dtype in locals_like],
        in_specs=[ANY] * count + [vmem] * extra_count,
        out_specs=[ANY] * spread_count + [vmem] * local_count,
        scratch_shapes=[pltpu.VMEM((count, ys, rows, width), bf16)] * 4
        + [pltpu.VMEM((spread_count, rows, width), bf16)]
        + [sem((count,))] * 3
        + [sem((count, ys))] * 2
        + [sem((spread_count, ys))] * 4
        + [sem((spread_count,))],
        compiler_params=pltpu.CompilerParams(collective_id=ident, has_side_effects=True),
        name=f"narrow_step_{ident}",
    )(*parts, *extras)


def last_step(part, extras, work, grads, chunks, flat, ident):
    narrow, rows, width = part.shape
    wide = lax.axis_size("wide")
    devices = wide * narrow
    ys = narrow // 2
    zs = 4 if wide % 4 == 0 else 1
    xs = wide // zs
    lanes = wide // LANE_WIDE
    extra_count = len(extras)
    part = part.reshape(ys, 2, rows, width)
    own_grad = grads.shape[1:]
    grads = grads.reshape((zs, xs) + own_grad)
    first_shape, second_shape, flat_shape = chunks[0].shape[1:], chunks[1].shape[1:], flat.shape[1:]

    def kernel(*refs):
        part_ref, grads_ref, first_ref, second_ref, flat_ref = refs[:5]
        extra_refs, refs = refs[5 : 5 + extra_count], refs[5 + extra_count :]
        spread_ref, grads_out, first_out, second_out, flat_out, row_out, refs = refs[:6] + (refs[6:],)
        mine, pair, half, got, rowbuf, rowtile, rowgot, refs = refs[:7] + (refs[7:],)
        gown, gx, ghalf, gz, fgot, sgot, flatgot, refs = refs[:7] + (refs[7:],)
        load_sem, pair_sem, y_send, y_recv, s_send, s_recv, p_send, p_recv, refs = refs[:8] + (refs[8:],)
        gx_send, gx_recv, gz_send, gz_recv, c_send, c_recv, all_send, all_recv = refs
        g = Grid()
        me = g.wide * narrow + g.narrow
        wait_all = g.greet_all()
        loads = [
            pltpu.make_async_copy(part_ref.at[:, g.c], mine, load_sem.at[0]),
            pltpu.make_async_copy(grads_ref.at[:, g.x], gown, load_sem.at[1]),
            pltpu.make_async_copy(first_ref.at[g.wide], fgot.at[g.wide], load_sem.at[2]),
            pltpu.make_async_copy(second_ref.at[g.wide], sgot.at[g.wide], load_sem.at[3]),
            pltpu.make_async_copy(flat_ref.at[me], flatgot.at[me], load_sem.at[4]),
        ]
        for copy in loads:
            copy.start()
        wait_all()
        pair_copy = remote(part_ref.at[:, 1 - g.c], pair, pair_sem.at[0], pair_sem.at[1], g.partner)
        pair_copy.start()
        sends = []
        order = g.z_others()[::-1] + [g.z]
        for z in order:
            for i, x in enumerate(g.x_others()):
                copy = remote(
                    grads_ref.at[z, x],
                    gx.at[g.x, z],
                    gx_send.at[i, z],
                    gx_recv.at[g.x, z],
                    g.device(g.z, x, g.y, g.c),
                )
                copy.start()
                sends.append(copy)
        for s in range(1, wide):
            target = lax.rem(g.wide + s, wide)
            for i, (source, place) in enumerate(((first_ref, fgot), (second_ref, sgot))):
                copy = remote(
                    source.at[target],
                    place.at[g.wide],
                    c_send.at[i, s],
                    c_recv.at[i, g.wide],
                    (target, g.narrow),
                )
                copy.start()
                sends.append(copy)

        def send_flat(step, carry):
            target = lax.rem(me + step, devices)
            where = lax.div(target, narrow), lax.rem(target, narrow)
            remote(flat_ref.at[target], flatgot.at[me], all_send.at[0], all_recv.at[0], where).start()
            return carry

        lax.fori_loop(1, devices, send_flat, 0)
        loads[0].wait()
        pair_copy.wait()
        half[...] = (mine[...].astype(f32) + pair[...].astype(f32)).astype(bf16)
        for s, y in enumerate(g.y_others()):
            copy = remote(half.at[y], got.at[g.y], y_send.at[s], y_recv.at[g.y], g.device(g.z, g.x, y, g.c))
            copy.start()
            sends.append(copy)
        for copy in loads[1:]:
            copy.wait()

        def grad_along_z(z):
            total = gown[z].astype(f32)
            for x in g.x_others():
                place = gx.at[x, z]
                remote(place, place, gx_send.at[0, 0], gx_recv.at[x, z], g.partner).wait_recv()
                total = total + gx[x, z].astype(f32)
            ghalf[z] = total.astype(bf16)

        for i, z in enumerate(order[:-1]):
            grad_along_z(z)
            copy = remote(
                ghalf.at[z], gz.at[g.z], gz_send.at[i], gz_recv.at[g.z], g.device(z, g.x, g.y, g.c)
            )
            copy.start()
            sends.append(copy)
            if i == 0:
                total = half[g.y].astype(f32)
                for y in g.y_others():
                    remote(got.at[y], got.at[y], y_send.at[0], y_recv.at[y], g.partner).wait_recv()
                    total = total + got[y].astype(f32)
                spreads, locals_out = work([total], [ref[...] for ref in extra_refs])
                rowbuf[...] = spreads[0]
                for j in range(8):
                    rowtile[pl.ds(j, 1), :] = locals_out[0][:, j * width // 8 : (j + 1) * width // 8]
                for s, y in enumerate(g.y_others()):
                    copy = remote(
                        rowbuf,
                        spread_ref.at[g.narrow],
                        s_send.at[s],
                        s_recv.at[g.y],
                        g.device(g.z, g.x, y, g.c),
                    )
                    copy.start()
                    sends.append(copy)
                copy = remote(rowbuf, spread_ref.at[g.narrow], p_send.at[g.y], p_recv.at[g.y], g.partner)
                copy.start()
                sends.append(copy)
                own = pltpu.make_async_copy(rowbuf, spread_ref.at[g.narrow], load_sem.at[0])
                own.start()

                def send_row(step, carry):
                    target = lax.rem(me + step, devices)
                    where = lax.div(target, narrow), lax.rem(target, narrow)
                    remote(rowtile, rowgot.at[me], all_send.at[1], all_recv.at[1], where).start()
                    return carry

                lax.fori_loop(1, devices, send_row, 0)
                rowgot[me] = rowtile[...]
        for y in g.y_others():
            there = spread_ref.at[2 * y + g.c]
            remote(there, there, s_send.at[0], s_recv.at[y], g.partner).wait_recv()
            copy = remote(there, there, p_send.at[y], p_recv.at[y], g.partner)
            copy.start()
            sends.append(copy)
        grad_along_z(g.z)
        for s in range(1, wide):
            source = lax.rem(g.wide + s, wide)
            for i, place in enumerate((fgot, sgot)):
                there = place.at[source]
                remote(there, there, c_send.at[i, 0], c_recv.at[i, source], g.partner).wait_recv()
        for p in range(LANE_WIDE):
            first_sum, second_sum = fgot[p].astype(f32), sgot[p].astype(f32)
            for lane in range(1, lanes):
                first_sum = first_sum + fgot[lane * LANE_WIDE + p].astype(f32)
                second_sum = second_sum + sgot[lane * LANE_WIDE + p].astype(f32)
            first_out[:, p * first_shape[1] : (p + 1) * first_shape[1]] = first_sum
            second_out[p * second_shape[0] : (p + 1) * second_shape[0], :] = second_sum
        total = ghalf[g.z].astype(f32)
        for z in order[:-1]:
            place = gz.at[z]
            remote(place, place, gz_send.at[0], gz_recv.at[z], g.partner).wait_recv()
            total = total + gz[z].astype(f32)
        grads_out[...] = total
        for i, place in enumerate((flatgot, rowgot)):
            others = place.at[pl.ds(0, devices - 1)]
            whole = remote(others, others, all_send.at[i], all_recv.at[i], g.partner)
            whole.wait_send()
            whole.wait_recv()
        flat_out[...] = jnp.sum(flatgot[...], axis=0)
        row_out[...] = jnp.sum(rowgot[...], axis=0)
        for y in range(ys):
            there = spread_ref.at[2 * y + 1 - g.c]
            remote(there, there, s_send.at[0], p_recv.at[y], g.partner).wait_recv()
        for copy in sends:
            copy.wait_send()
        own.wait()

    sem = pltpu.SemaphoreType.DMA
    vmem = pl.BlockSpec(memory_space=pltpu.VMEM)
    return pl.pallas_call(
        kernel,
        out_shape=[
            jax.ShapeDtypeStruct((narrow, rows, width), bf16),
            jax.ShapeDtypeStruct(own_grad, f32),
            jax.ShapeDtypeStruct((first_shape[0], LANE_WIDE * first_shape[1]), f32),
            jax.ShapeDtypeStruct((LANE_WIDE * second_shape[0], second_shape[1]), f32),
            jax.ShapeDtypeStruct(flat_shape, f32),
            jax.ShapeDtypeStruct((8, width // 8), f32),
        ],
        in_specs=[ANY] * 5 + [vmem] * extra_count,
        out_specs=[ANY] + [vmem] * 5,
        scratch_shapes=[pltpu.VMEM((ys, rows, width), bf16)] * 4
        + [pltpu.VMEM((rows, width), bf16)]
        + [pltpu.VMEM((8, width // 8), f32), pltpu.VMEM((devices, 8, width // 8), f32)]
        + [
            pltpu.VMEM((zs,) + own_grad, bf16),
            pltpu.VMEM((xs, zs) + own_grad, bf16),
            pltpu.VMEM((zs,) + own_grad, bf16),
            pltpu.VMEM((zs,) + own_grad, bf16),
            pltpu.VMEM((wide,) + first_shape, bf16),
            pltpu.VMEM((wide,) + second_shape, bf16),
            pltpu.VMEM((devices,) + flat_shape, f32),
        ]
        + [sem((5,)), sem((2,))]
        + [sem((ys,))] * 6
        + [sem((xs, zs))] * 2
        + [sem((zs,))] * 2
        + [sem((2, wide))] * 2
        + [sem((2,))] * 2,
        compiler_params=pltpu.CompilerParams(
            collective_id=ident, has_side_effects=True, vmem_limit_bytes=48 * 1024 * 1024
        ),
        name="last_step",
    )(part, grads, chunks[0], chunks[1], flat, *extras)


def matmul(left_side, right_side):
    return jnp.dot(left_side, right_side, preferred_element_type=jnp.float32)


def inner_left(left_side, right_side):
    return lax.dot_general(left_side, right_side, (((0,), (0,)), ((), ())), preferred_element_type=jnp.float32)


def inner_right(left_side, right_side):
    return lax.dot_general(left_side, right_side, (((1,), (1,)), ((), ())), preferred_element_type=jnp.float32)


def silu_slope(values):
    sigmoid_val = jax.nn.sigmoid(values)
    return sigmoid_val * (1.0 + values * (1.0 - sigmoid_val))


def silu_curve(values):
    sigmoid_val = jax.nn.sigmoid(values)
    return sigmoid_val * (1.0 - sigmoid_val) * (2.0 + values * (1.0 - 2.0 * sigmoid_val))


class Lane:
    def __init__(self):
        narrow = lax.axis_size("narrow")
        self.ys = narrow // 2
        self.chips = LANE_WIDE * self.ys
        wide_pos, narrow_pos = lax.axis_index("wide"), lax.axis_index("narrow")
        self.base = lax.div(wide_pos, LANE_WIDE) * LANE_WIDE
        self.colour = lax.rem(narrow_pos, 2)
        self.chip = lax.rem(wide_pos, LANE_WIDE) * self.ys + lax.div(narrow_pos, 2)
        self.partner = (wide_pos, narrow_pos + 1 - 2 * self.colour)

    def other(self, step):
        return lax.rem(self.chip + step, self.chips)

    def device(self, chip):
        return self.base + lax.div(chip, self.ys), 2 * lax.rem(chip, self.ys) + self.colour

    def greet(self):
        barrier = pltpu.get_barrier_semaphore()
        for step in range(1, self.chips):
            pl.semaphore_signal(barrier, inc=1, device_id=self.device(self.other(step)), device_id_type=MESH)
        pl.semaphore_signal(barrier, inc=1, device_id=self.partner, device_id_type=MESH)
        pl.semaphore_wait(barrier, self.chips)


class Scatter:
    def __init__(self, lane, part, pair, half, got, sems):
        self.lane, self.part, self.pair, self.half, self.got = lane, part, pair, half, got
        self.pair_send, self.pair_recv, self.send, self.recv = sems

    @staticmethod
    def scratch(chips, rows, width):
        return [
            pltpu.VMEM((2, chips, rows, width), bf16),
            pltpu.VMEM((chips, rows, width), bf16),
            pltpu.VMEM((chips, rows, width), bf16),
            pltpu.VMEM((chips, rows, width), bf16),
            pltpu.SemaphoreType.DMA((1,)),
            pltpu.SemaphoreType.DMA((1,)),
            pltpu.SemaphoreType.DMA((chips,)),
            pltpu.SemaphoreType.DMA((chips,)),
        ]

    @classmethod
    def of(cls, lane, refs):
        return cls(lane, *refs[:4], refs[4:8])

    def pair_copy(self):
        return remote(
            self.part.at[1 - self.lane.colour],
            self.pair,
            self.pair_send.at[0],
            self.pair_recv.at[0],
            self.lane.partner,
        )

    def start_pair(self):
        self.pair_copy().start()

    def take_pair(self):
        self.pair_copy().wait()
        self.half[...] = (
            self.part[self.lane.colour].astype(f32) + self.pair[...].astype(f32)
        ).astype(bf16)
        self.got[self.lane.chip] = self.half[self.lane.chip]

    def copy_to(self, step):
        chip = self.lane.other(step)
        return remote(
            self.half.at[chip],
            self.got.at[self.lane.chip],
            self.send.at[step],
            self.recv.at[self.lane.chip],
            self.lane.device(chip),
        )

    def start_sends(self):
        for step in range(1, self.lane.chips):
            self.copy_to(step).start()

    def total(self):
        result = self.got[self.lane.chip].astype(f32)
        for step in range(1, self.lane.chips):
            chip = self.lane.other(step)
            remote(
                self.got.at[chip], self.got.at[chip], self.send.at[step], self.recv.at[chip], self.lane.device(chip)
            ).wait_recv()
            result = result + self.got[chip].astype(f32)
        return result

    def wait_sends(self):
        for step in range(1, self.lane.chips):
            self.copy_to(step).wait_send()


class Spread:
    def __init__(self, lane, whole, sems):
        self.lane, self.whole = lane, whole
        self.send, self.recv, self.pair_send, self.pair_recv = sems

    @staticmethod
    def scratch(chips, rows, width):
        return [pltpu.VMEM((2, chips, rows, width), bf16)] + [pltpu.SemaphoreType.DMA((chips,))] * 4

    @classmethod
    def of(cls, lane, refs):
        return cls(lane, refs[0], refs[1:5])

    def mine(self):
        return self.whole.at[self.lane.colour, self.lane.chip]

    def copy_to(self, step):
        return remote(
            self.mine(),
            self.mine(),
            self.send.at[step],
            self.recv.at[self.lane.chip],
            self.lane.device(self.lane.other(step)),
        )

    def pair_copy(self, chip, colour):
        place = self.whole.at[colour, chip]
        return remote(place, place, self.pair_send.at[chip], self.pair_recv.at[chip], self.lane.partner)

    def run(self):
        lane = self.lane
        for step in range(1, lane.chips):
            self.copy_to(step).start()
        self.pair_copy(lane.chip, lane.colour).start()
        for step in range(1, lane.chips):
            chip = lane.other(step)
            place = self.whole.at[lane.colour, chip]
            remote(place, place, self.send.at[step], self.recv.at[chip], lane.device(chip)).wait_recv()
            self.pair_copy(chip, lane.colour).start()
        for chip in range(lane.chips):
            self.pair_copy(chip, 1 - lane.colour).wait_recv()
        for step in range(1, lane.chips):
            self.copy_to(step).wait_send()
        for chip in range(lane.chips):
            self.pair_copy(chip, lane.colour).wait_send()


class Plan:
    def __init__(self, spans_ref, gates_ref, count):
        self.wide = lax.axis_size("wide")
        self.long = min(6, self.wide * 5 // 8)
        self.gates = gates_ref
        lengths = [spans_ref[i] for i in range(count)]
        self.starts, at = [], 0
        for length in lengths:
            self.starts.append(at)
            at = at + length
        longest, self.start = lengths[0], 0
        for i in range(1, count):
            more = lengths[i] > longest
            longest = jnp.where(more, lengths[i], longest)
            self.start = jnp.where(more, self.starts[i], self.start)
        self.lane = lax.div(lax.axis_index("wide"), LANE_WIDE)

    def span(self, turn):
        rest = jnp.where(turn < self.start, turn, turn + self.long)
        return jnp.clip(jnp.where(self.lane == 0, self.start + turn, rest), 0, self.wide - 1)

    def valid(self, turn):
        count = jnp.where(self.lane == 0, self.long, jnp.where(self.lane == 1, self.wide - self.long, 0))
        return jnp.where(turn < count, 1.0, 0.0)

    def first(self, turn):
        span = self.span(turn)
        found = jnp.where(span == self.starts[0], 1.0, 0.0)
        for start in self.starts[1:]:
            found = jnp.maximum(found, jnp.where(span == start, 1.0, 0.0))
        return jnp.maximum(found, 1.0 - self.valid(turn))

    def rates(self, turn):
        span = self.span(turn)
        return self.gates[span, 0], self.gates[span, 1], self.gates[span, 2]

    def lane_of(self, span):
        inside = (span >= self.start) & (span < self.start + self.long)
        return jnp.where(inside, 0, 1)

    def turn_of(self, span):
        inside = (span >= self.start) & (span < self.start + self.long)
        outside = jnp.where(span < self.start, span, span - self.long)
        return jnp.where(inside, span - self.start, outside)


class Deliver:
    def __init__(self, grid, plan, chips, out, got, sems):
        self.grid, self.plan, self.chips, self.out, self.got = grid, plan, chips, out, got
        self.send, self.recv = sems
        self.wide, self.narrow = lax.axis_size("wide"), lax.axis_size("narrow")
        self.me = grid.wide * self.narrow + grid.narrow

    @staticmethod
    def scratch(kinds, rows, block):
        devices = lax.axis_size("wide") * lax.axis_size("narrow")
        return [pltpu.VMEM((devices, kinds, rows, block), bf16)] * 2 + [pltpu.SemaphoreType.DMA((1,))] * 2

    def start(self, kinds):
        block = self.out.shape[3]
        for span in range(self.wide):
            turn = self.plan.turn_of(span)
            for i, kind in enumerate(kinds):
                lane_rows = kind[turn]
                for n in range(self.narrow):
                    self.out[span * self.narrow + n, i] = lane_rows[:, n * block : (n + 1) * block]

        def push(step, carry):
            target = lax.rem(self.me + step, self.wide * self.narrow)
            where = lax.div(target, self.narrow), lax.rem(target, self.narrow)
            remote(self.out.at[target], self.got.at[self.me], self.send.at[0], self.recv.at[0], where).start()
            return carry

        lax.fori_loop(1, self.wide * self.narrow, push, 0)
        self.got[self.me] = self.out[self.me]

    def finish(self, result):
        others = self.got.at[pl.ds(0, self.wide * self.narrow - 1)]
        whole = remote(others, others, self.send.at[0], self.recv.at[0], self.grid.partner)
        whole.wait_send()
        whole.wait_recv()
        base = self.plan.lane_of(self.grid.wide) * LANE_WIDE
        ys = self.narrow // 2
        for p in range(LANE_WIDE):
            for y in range(ys):
                for colour in range(2):
                    source = (base + p) * self.narrow + 2 * y + colour
                    for i in range(result.shape[0]):
                        result[i, colour, p * ys + y] = self.got[source, i]


def chain_forward(keys, values, queries, lengths, gates, turns, first_init, second_init, ident):
    wide = lax.axis_size("wide")
    blocks, span, block = keys.shape[1:]
    width, hidden = first_init.shape
    rows = values.shape[1]
    sequences = lengths.shape[0]
    key_turns = turns - 1
    per_turn = 3 if turns <= 5 else 1
    first_left = per_turn * (key_turns - 3)
    slots = 3
    stream_keys = keys.shape[0] == turns
    chips = LANE_WIDE * (lax.axis_size("narrow") // 2)
    n_scatter = len(Scatter.scratch(1, 8, 128))

    def kernel(*refs):
        keys_hbm, values_hbm, own_hbm, lengths_ref, gates_ref, first_hbm, second_hbm = refs[:7]
        recalled_hbm, low1_hbm, low2_hbm, m1_hbm, m2_hbm, g1_hbm, g2_hbm = refs[7:14]
        err_hbm, pre_hbm, qpre_hbm, klane_hbm, qlane_hbm = refs[14:19]
        rest = refs[19:]
        kall, qall, vall, kcur, qcur, i1, i2, s1, s2, m1, m2, low1, low2, mb1, mb2, gb1, gb2 = rest[:17]
        pre, qpre, khid, rec, qpart, qpair, qhalf, qgot, own_hold = rest[17:26]
        in_sem, out_sem, q_sem, q_pair_send, q_pair_recv, q_send, q_recv = rest[26:33]
        rest = rest[33:]
        lane = Lane()
        grid = Grid()
        plan = Plan(lengths_ref, gates_ref, sequences)
        lookup = Scatter.of(lane, rest[:n_scatter])
        error = Spread.of(lane, rest[n_scatter : n_scatter + 5])
        gather = Gather(grid, own_hbm, qall, rest[n_scatter + 5 : n_scatter + 9])
        deliver = Deliver(grid, plan, chips, *rest[n_scatter + 9 : n_scatter + 11], rest[n_scatter + 11 : n_scatter + 13])
        result = rest[n_scatter + 13]

        def recall(q, slot):
            sems = q_pair_send.at[pl.ds(q, 1)], q_pair_recv.at[pl.ds(q, 1)], q_send.at[q], q_recv.at[q]
            return Scatter(lane, qpart.at[slot], qpair.at[q], qhalf.at[slot], qgot.at[q], sems)

        def state_saves(turn):
            return [
                pltpu.make_async_copy(source, target.at[turn], out_sem.at[i])
                for i, (source, target) in enumerate(((mb1, m1_hbm), (mb2, m2_hbm), (kcur, klane_hbm)))
            ]

        def other_saves(turn):
            return [
                pltpu.make_async_copy(source, target.at[turn], out_sem.at[3 + i])
                for i, (source, target) in enumerate(
                    ((gb1, g1_hbm), (gb2, g2_hbm), (error.whole, err_hbm), (pre, pre_hbm))
                )
            ]

        def query_saves(q, slot):
            return [
                pltpu.make_async_copy(source.at[slot], target.at[q], q_sem.at[slot, i])
                for i, (source, target) in enumerate(((qcur, qlane_hbm), (qpre, qpre_hbm)))
            ]

        inputs = [
            pltpu.make_async_copy(source, target, in_sem.at[i])
            for i, (source, target) in enumerate(
                ((first_hbm, i1), (second_hbm, i2), (keys_hbm, kall), (values_hbm, vall), (own_hbm, own_hold))
            )
            if not (stream_keys and i == 2)
        ]
        for copy in inputs:
            copy.start()
        grid.greet_all()()
        gather.begin()
        for copy in inputs:
            copy.wait()
        own_store = pltpu.make_async_copy(own_hold, qall.at[grid.wide, grid.narrow], in_sem.at[4])
        own_store.start()
        low1[0] = i1[...]
        low2[0] = i2[...]
        s1[...] = i1[...].astype(f32)
        s2[...] = i2[...].astype(f32)
        for ref in (m1, m2, mb1, mb2):
            ref[...] = jnp.zeros_like(ref)
        own_store.wait()

        def lookup_blocks(buf, first):
            total = matmul(buf[0], first[pl.ds(0, block), :])
            for b in range(1, blocks):
                total = total + matmul(buf[b], first[pl.ds(b * block, block), :])
            return total

        def ask(q, slot, waits):
            def settle():
                recall(q - slots, slot).wait_sends()
                for copy in query_saves(q - slots, slot):
                    copy.wait()

            if waits is True:
                settle()
            elif waits is not False:
                pl.when(waits)(settle)
            index = plan.span(q)
            for b in range(blocks):
                qcur[slot, b] = qall[index, b]
            query_pre = lookup_blocks(qcur.at[slot], low1.at[q])
            qpre[slot] = query_pre
            for copy in query_saves(q, slot):
                copy.start()
            query_hidden = (query_pre * jax.nn.sigmoid(query_pre)).astype(bf16)
            qpart[slot] = matmul(query_hidden, low2[q]).astype(bf16).reshape(2, chips, rows, width)
            recall(q, slot).start_pair()

        def turn_body(turn, carry):
            index = plan.span(turn)
            if stream_keys:
                one = pltpu.make_async_copy(keys_hbm.at[turn], kcur, in_sem.at[2])
                one.start()
                one.wait()
            else:
                for b in range(blocks):
                    kcur[b] = kall[index, b]
            for copy in state_saves(turn):
                copy.start()
            key_pre = lookup_blocks(kcur, low1.at[turn])
            pre[0] = key_pre
            khid[...] = (key_pre * jax.nn.sigmoid(key_pre)).astype(bf16)
            lookup.part[...] = matmul(khid[...], low2[turn]).astype(bf16).reshape(2, chips, rows, width)
            lookup.start_pair()

            @pl.when(turn == 3)
            def _():
                gather.finish()

            first = per_turn * (turn - 3)

            @pl.when(turn >= 3)
            def _():
                ask(first, lax.rem(first, slots), first >= slots)

            lookup.take_pair()
            lookup.start_sends()

            @pl.when(turn >= 3)
            def _():
                recall(first, lax.rem(first, slots)).take_pair()
                for j in range(1, per_turn):
                    ask(first + j, lax.rem(first + j, slots), first + j >= slots)

            total = lookup.total()
            target = jnp.concatenate([vall[index * blocks + b] for b in range(blocks)], axis=1)
            error.whole[lane.colour, lane.chip] = ((total - target.astype(f32)) / span).astype(bf16)
            error.run()
            lookup.wait_sends()

            @pl.when(turn >= 3)
            def _():
                recall(first, lax.rem(first, slots)).start_sends()
                for j in range(1, per_turn):
                    stream = recall(first + j, lax.rem(first + j, slots))
                    stream.take_pair()
                    stream.start_sends()

            err = error.whole[...].reshape(span, width)
            grad_second = inner_left(khid[...], err)
            hidden_grad = inner_right(err, low2[turn])
            pre[1] = hidden_grad
            slope = (hidden_grad * silu_slope(pre[0])).astype(bf16)
            decay, moment, rate = plan.rates(turn)
            reset = plan.first(turn + 1)
            for copy in state_saves(turn):
                copy.wait()
            following = jnp.minimum(turn + 1, turns - 1)

            def update(s, m, mb, init, low, grad, place):
                moment_new = moment * m[place] - rate * grad
                state_new = (1.0 - decay) * s[place] + moment_new
                state_new = reset * init[place].astype(f32) + (1.0 - reset) * state_new
                moment_new = (1.0 - reset) * moment_new
                m[place] = moment_new
                mb[place] = moment_new.astype(bf16)
                s[place] = state_new
                low[(following,) + place] = state_new.astype(bf16)

            gb2[...] = grad_second.astype(bf16)
            update(s2, m2, mb2, i2, low2, grad_second, (slice(None), slice(None)))
            for b in range(blocks):
                grad_first = inner_left(kcur[b], slope)
                place = (pl.ds(b * block, block), slice(None))
                gb1[place] = grad_first.astype(bf16)
                update(s1, m1, mb1, i1, low1, grad_first, place)
            saves = other_saves(turn)
            for copy in saves:
                copy.start()

            @pl.when(turn == 0)
            def _():
                for number in range(1, grid.zs):
                    gather.along_z(number)
                gather.across(0)

            @pl.when(turn == 1)
            def _():
                for number in range(1, grid.zs):
                    gather.across(number)
                gather.last(0)

            @pl.when(turn == 2)
            def _():
                for number in range(1, grid.zs):
                    gather.last(number)

            for copy in saves:
                copy.wait()
            return carry

        lax.fori_loop(0, key_turns, turn_body, 0)
        ends = [
            pltpu.make_async_copy(low1, low1_hbm, out_sem.at[0]),
            pltpu.make_async_copy(low2, low2_hbm, out_sem.at[1]),
        ]
        for copy in ends:
            copy.start()
        left = list(range(first_left, turns))
        for q in left:
            ask(q, q % slots, q >= slots)
            if q > left[0]:
                stream = recall(q - 1, (q - 1) % slots)
                stream.take_pair()
                stream.start_sends()
        stream = recall(turns - 1, (turns - 1) % slots)
        stream.take_pair()
        stream.start_sends()
        for q in range(turns):
            rec[q] = recall(q, q % slots).total().astype(bf16)
        deliver.start([rec])
        for q in range(turns - slots, turns):
            recall(q, q % slots).wait_sends()
        for q in range(turns - slots, turns):
            for copy in query_saves(q, q % slots):
                copy.wait()
        deliver.finish(result)
        last = pltpu.make_async_copy(result.at[0], recalled_hbm, out_sem.at[2])
        last.start()
        for copy in ends + [last]:
            copy.wait()

    state = [(width, hidden), (hidden, width)]
    out_shape = (
        [jax.ShapeDtypeStruct((2, chips, rows, block), bf16)]
        + [jax.ShapeDtypeStruct((turns,) + s, bf16) for s in state]
        + [jax.ShapeDtypeStruct((key_turns,) + s, bf16) for s in state * 2]
        + [
            jax.ShapeDtypeStruct((key_turns, 2, chips, rows, width), bf16),
            jax.ShapeDtypeStruct((key_turns, 2, span, hidden), f32),
            jax.ShapeDtypeStruct((turns, span, hidden), f32),
            jax.ShapeDtypeStruct((key_turns, blocks, span, block), bf16),
            jax.ShapeDtypeStruct((turns, blocks, span, block), bf16),
        ]
    )
    sem = pltpu.SemaphoreType.DMA
    scratch = (
        [pltpu.VMEM((1 if stream_keys else keys.shape[0], blocks, span, block), bf16), pltpu.VMEM((wide, blocks, span, block), bf16)]
        + [pltpu.VMEM(values.shape, bf16)]
        + [pltpu.VMEM((blocks, span, block), bf16), pltpu.VMEM((slots, blocks, span, block), bf16)]
        + [pltpu.VMEM(s, bf16) for s in state]
        + [pltpu.VMEM(s, f32) for s in state * 2]
        + [pltpu.VMEM((turns,) + s, bf16) for s in state]
        + [pltpu.VMEM(s, bf16) for s in state * 2]
        + [
            pltpu.VMEM((2, span, hidden), f32),
            pltpu.VMEM((slots, span, hidden), f32),
            pltpu.VMEM((span, hidden), bf16),
            pltpu.VMEM((turns, rows, width), bf16),
            pltpu.VMEM((slots, 2, chips, rows, width), bf16),
        ]
        + [pltpu.VMEM((n, chips, rows, width), bf16) for n in (turns, slots, turns)]
        + [pltpu.VMEM((span, block), bf16)]
        + [sem((5,)), sem((7,)), sem((slots, 2)), sem((turns,)), sem((turns,)), sem((turns, chips)), sem((turns, chips))]
        + Scatter.scratch(chips, rows, width)
        + Spread.scratch(chips, rows, width)
        + Gather.scratch()
        + Deliver.scratch(1, rows, block)
        + [pltpu.VMEM((1, 2, chips, rows, block), bf16)]
    )
    smem = pl.BlockSpec(memory_space=pltpu.SMEM)
    return pl.pallas_call(
        kernel,
        out_shape=out_shape,
        in_specs=[ANY] * 3 + [smem] * 2 + [ANY] * 2,
        out_specs=[ANY] * len(out_shape),
        scratch_shapes=scratch,
        compiler_params=pltpu.CompilerParams(
            collective_id=ident, has_side_effects=True, vmem_limit_bytes=62 * 1024 * 1024
        ),
        cost_estimate=pl.CostEstimate(
            flops=40 * turns * 2 * span * width * hidden, bytes_accessed=turns * 40 * 2**20, transcendentals=0
        ),
        name="chain_forward",
    )(keys, values, queries, lengths, gates, first_init, second_init)


def chain_backward(recall_grad, saved, lengths, gates, ident):
    low1_all, low2_all, m1_all, m2_all, g1_all, g2_all, err_all, pre_all, qpre_all, keys, queries = saved
    wide = lax.axis_size("wide")
    devices = wide * lax.axis_size("narrow")
    key_turns, blocks, span, block = keys.shape
    turns = key_turns + 1
    width, hidden = low1_all.shape[1:]
    chips, rows = err_all.shape[2:4]
    n_scatter = len(Scatter.scratch(1, 8, 128))

    def kernel(*refs):
        own_hbm, q_ins, k_ins, lengths_ref, gates_ref = refs[0], refs[1:5], refs[5:12], refs[12], refs[13]
        cots_hbm, sums_out, mg1_hbm, mg2_hbm = refs[14:18]
        rest = refs[18:]
        q_bufs, k_bufs, rest = rest[:4], rest[4:11], rest[11:]
        qbuf, low1, low2, qpre = q_bufs
        kbuf, m1, m2, g1, g2, errs, pre = k_bufs
        rall, own_hold, cf, cs, cmf, cms, w1, w2, a1, a2, c1, c2 = rest[:12]
        dh, khid, qpl, qhid, kpl, slow, sg, hk, qcots, kcots, vcots, sumrows, tile, mb1, mb2, result = rest[12:28]
        q_sem, k_sem, end_sem, own_sem, tile_send, tile_recv = rest[28:34]
        rest = rest[34:]
        lane = Lane()
        grid = Grid()
        plan = Plan(lengths_ref, gates_ref, lengths.shape[0])
        lookup = Scatter.of(lane, rest[:n_scatter])
        qstream = Scatter.of(lane, rest[n_scatter : 2 * n_scatter])
        kstream = Scatter.of(lane, rest[2 * n_scatter : 3 * n_scatter])
        spread = Spread.of(lane, rest[3 * n_scatter : 3 * n_scatter + 5])
        gather = Gather(grid, own_hbm, rall, rest[3 * n_scatter + 5 : 3 * n_scatter + 9])
        rest = rest[3 * n_scatter + 9 :]
        deliver = Deliver(grid, plan, chips, *rest[:2], rest[2:4])

        def q_loads(turn, slot):
            return [
                pltpu.make_async_copy(source.at[turn], target.at[slot], q_sem.at[slot, i])
                for i, (source, target) in enumerate(zip(q_ins, q_bufs))
            ]

        def k_loads(turn, slot):
            return [
                pltpu.make_async_copy(source.at[turn], target.at[slot], k_sem.at[slot, i])
                for i, (source, target) in enumerate(zip(k_ins, k_bufs))
            ]

        own = pltpu.make_async_copy(own_hbm, own_hold, own_sem.at[0])
        own.start()
        grid.greet_all()()
        gather.begin()
        for copy in q_loads(turns - 1, 0) + q_loads(turns - 2, 1) + k_loads(turns - 2, 1):
            copy.start()
        own.wait()
        own_store = pltpu.make_async_copy(own_hold, rall.at[grid.wide, grid.narrow], own_sem.at[0])
        own_store.start()
        for ref in (cf, cs, cmf, cms, a1, a2):
            ref[...] = jnp.zeros_like(ref)
        gather.middle()
        own_store.wait()
        gather.finish()

        kcots[turns - 1] = jnp.zeros((rows, width), bf16)
        vcots[turns - 1] = jnp.zeros((rows, width), bf16)
        sumrows[turns - 1] = jnp.zeros((8, 128), f32)

        def finish(stream, save, turn):
            save[turn] = stream.total().astype(bf16)
            stream.wait_sends()

        def query_rows(turn, slot):
            index = plan.span(turn)
            back = inner_right(rall[index, 0], low2[slot, :, pl.ds(0, block)])
            for b in range(1, blocks):
                back = back + inner_right(rall[index, b], low2[slot, :, pl.ds(b * block, block)])
            query_pre = qpre[slot]
            qpl[...] = (plan.valid(turn) * back * silu_slope(query_pre)).astype(bf16)
            qhid[...] = (query_pre * jax.nn.sigmoid(query_pre)).astype(bf16)
            qstream.part[...] = inner_right(qpl[...], low1[slot]).astype(bf16).reshape(2, chips, rows, width)
            qstream.start_pair()

        def query_weights(turn, slot):
            index = plan.span(turn)
            valid = plan.valid(turn)
            for b in range(blocks):
                w1[pl.ds(b * block, block), :] = inner_left(qbuf[slot, b], qpl[...])
                w2[:, pl.ds(b * block, block)] = valid * inner_left(qhid[...], rall[index, b])

        def key_rows(slot):
            kstream.part[...] = (
                (inner_right(kpl[...], low1[slot]) + inner_right(slow[...], c1[slot]))
                .astype(bf16)
                .reshape(2, chips, rows, width)
            )

        for copy in q_loads(turns - 1, 0):
            copy.wait()
        query_rows(turns - 1, 0)
        query_weights(turns - 1, 0)
        reset = plan.first(turns - 1)
        for c, w, acc in ((cf, w1, a1), (cs, w2, a2)):
            acc[...] = reset * w[...]
            c[...] = (1.0 - reset) * w[...]
        qstream.take_pair()
        qstream.start_sends()

        def body(step, carry):
            turn = turns - 1 - step
            slot = lax.rem(step, 2)
            decay, moment, rate = plan.rates(turn)
            reset = plan.first(turn)
            for copy in q_loads(turn, slot) + k_loads(turn, slot):
                copy.wait()
            c1[slot] = (-rate * (cmf[...] + cf[...])).astype(bf16)
            c2[...] = (-rate * (cms[...] + cs[...])).astype(bf16)
            slope_grad = matmul(kbuf[slot, 0], c1[slot, pl.ds(0, block), :])
            for b in range(1, blocks):
                slope_grad = slope_grad + matmul(kbuf[slot, b], c1[slot, pl.ds(b * block, block), :])
            sg[...] = slope_grad
            key_pre = pre[slot, 0]
            khid[...] = (key_pre * jax.nn.sigmoid(key_pre)).astype(bf16)
            dh[...] = (slope_grad * silu_slope(key_pre)).astype(bf16)
            lookup.part[...] = (
                (matmul(khid[...], c2[...]) + matmul(dh[...], low2[slot])).astype(bf16).reshape(2, chips, rows, width)
            )
            lookup.start_pair()
            finish(qstream, qcots, turn + 1)

            @pl.when(step > 2)
            def _():
                finish(kstream, kcots, turn + 2)

            lookup.take_pair()
            lookup.start_sends()
            query_rows(turn, slot)

            @pl.when(step > 1)
            def _():
                key_rows(1 - slot)
                kstream.start_pair()

            @pl.when(step + 1 < turns)
            def _():
                for copy in q_loads(turn - 1, 1 - slot) + k_loads(turn - 1, 1 - slot):
                    copy.start()

            query_weights(turn, slot)
            err = errs[slot].reshape(span, width)
            hk[...] = inner_right(err, c2[...])
            w2[...] += inner_left(dh[...], err)

            def whole_sum(first_a, first_b, second_a, second_b):
                first = jnp.sum(first_a * first_b.astype(f32), axis=0, keepdims=True)
                second = jnp.sum(second_a * second_b.astype(f32), axis=0, keepdims=True)
                return jnp.sum(first, axis=1, keepdims=True) + jnp.sum(second, axis=1, keepdims=True)

            kinds = (
                whole_sum(cf[...], low1[slot], cs[...], low2[slot]),
                whole_sum(cmf[...] + cf[...], m1[slot], cms[...] + cs[...], m2[slot]),
                whole_sum(cmf[...] + cf[...], g1[slot], cms[...] + cs[...], g2[slot]),
            )
            column = lax.broadcasted_iota(jnp.int32, (8, 128), 1)
            sumrow = jnp.zeros((8, 128), f32)
            for i, kind in enumerate(kinds):
                sumrow = jnp.where(column == i, kind, sumrow)
            sumrows[turn] = sumrow
            qstream.take_pair()
            total = lookup.total()
            mine = (total / span).astype(bf16)
            spread.whole[lane.colour, lane.chip] = mine
            vcots[turn] = mine
            spread.run()
            lookup.wait_sends()
            qstream.start_sends()

            @pl.when(step > 1)
            def _():
                kstream.take_pair()
                kstream.start_sends()

            out = spread.whole[...].reshape(span, width)
            hidden_back = hk[...] + inner_right(out, low2[slot])
            key_pre = pre[slot, 0]
            hidden_grad = pre[slot, 1]
            slope = silu_slope(key_pre)
            kpl[...] = (hidden_back * slope + sg[...] * hidden_grad * silu_curve(key_pre)).astype(bf16)
            slow[...] = (hidden_grad * slope).astype(bf16)

            def update(c, m, acc, grad_new, place):
                grad = (1.0 - decay) * c[place] + grad_new
                both = m[place] + c[place]
                acc[place] += reset * grad
                c[place] = (1.0 - reset) * grad
                m[place] = (1.0 - reset) * (moment * both)

            for b in range(blocks):
                place = (pl.ds(b * block, block), slice(None))
                update(cf, cmf, a1, w1[place] + inner_left(kbuf[slot, b], kpl[...]), place)
            place = (slice(None), slice(None))
            update(cs, cms, a2, w2[...] + inner_left(khid[...], out), place)
            return carry

        lax.fori_loop(1, turns, body, 0)
        tail = Scatter(
            lane,
            kstream.part,
            lookup.pair,
            lookup.half,
            lookup.got,
            (lookup.pair_send, lookup.pair_recv, lookup.send, lookup.recv),
        )
        key_rows((turns - 1) % 2)
        tail.start_pair()
        mb1[...] = a1[...].astype(bf16).reshape(mb1.shape)
        for owner in range(wide):
            mb2[owner] = a2[:, owner * (width // wide) : (owner + 1) * (width // wide)].astype(bf16)
        ends = [
            pltpu.make_async_copy(mb1, mg1_hbm, end_sem.at[0]),
            pltpu.make_async_copy(mb2, mg2_hbm, end_sem.at[1]),
        ]
        for copy in ends:
            copy.start()
        for span_number in range(wide):
            here = jnp.where(plan.lane_of(span_number) == plan.lane, 1.0, 0.0)
            tile[pl.ds(span_number, 1), :] = here * sumrows[plan.turn_of(span_number)][:1]

        def send_tile(step, carry):
            target = lax.rem(deliver.me + step, devices)
            where = lax.div(target, blocks), lax.rem(target, blocks)
            remote(tile, sums_out.at[deliver.me], tile_send.at[0], tile_recv.at[0], where).start()
            return carry

        lax.fori_loop(1, devices, send_tile, 0)
        sums_out[deliver.me] = tile[...]
        finish(qstream, qcots, 0)
        if turns > 2:
            finish(kstream, kcots, 1)
        tail.take_pair()
        tail.start_sends()
        finish(tail, kcots, 0)
        deliver.start([qcots, kcots, vcots])
        others = sums_out.at[pl.ds(0, devices - 1)]
        tiles = remote(others, others, tile_send.at[0], tile_recv.at[0], grid.partner)
        tiles.wait_send()
        tiles.wait_recv()
        deliver.finish(result)
        ends.append(pltpu.make_async_copy(result, cots_hbm, end_sem.at[2]))
        ends[2].start()
        for copy in ends:
            copy.wait()

    state = [(width, hidden), (hidden, width)]
    q_buffers = [((blocks, span, block), bf16)] + [(s, bf16) for s in state] + [((span, hidden), f32)]
    k_buffers = (
        [((blocks, span, block), bf16)]
        + [(s, bf16) for s in state * 2]
        + [((2, chips, rows, width), bf16), ((2, span, hidden), f32)]
    )
    by_owner = [(wide, width // wide, hidden), (wide, hidden, width // wide)]
    out_shape = [
        jax.ShapeDtypeStruct((3, 2, chips, rows, block), bf16),
        jax.ShapeDtypeStruct((devices, wide, 128), f32),
    ] + [jax.ShapeDtypeStruct(s, bf16) for s in by_owner]
    sem = pltpu.SemaphoreType.DMA
    scratch = (
        [pltpu.VMEM((2,) + s, t) for s, t in q_buffers + k_buffers]
        + [pltpu.VMEM((wide, blocks, span, block), bf16), pltpu.VMEM((span, block), bf16)]
        + [pltpu.VMEM(s, f32) for s in state * 4]
        + [pltpu.VMEM((2,) + state[0], bf16), pltpu.VMEM(state[1], bf16)]
        + [pltpu.VMEM((span, hidden), bf16)] * 6
        + [pltpu.VMEM((span, hidden), f32)] * 2
        + [pltpu.VMEM((turns, rows, width), bf16)] * 3
        + [pltpu.VMEM((turns, 8, 128), f32), pltpu.VMEM((wide, 128), f32)]
        + [pltpu.VMEM(s, bf16) for s in by_owner]
        + [pltpu.VMEM((3, 2, chips, rows, block), bf16)]
        + [sem((2, 4)), sem((2, 7)), sem((3,)), sem((1,)), sem((1,)), sem((1,))]
        + Scatter.scratch(chips, rows, width) * 3
        + Spread.scratch(chips, rows, width)
        + Gather.scratch()
        + Deliver.scratch(3, rows, block)
    )
    vmem = pl.BlockSpec(memory_space=pltpu.VMEM)
    smem = pl.BlockSpec(memory_space=pltpu.SMEM)
    return pl.pallas_call(
        kernel,
        out_shape=out_shape,
        in_specs=[ANY] * 12 + [smem] * 2,
        out_specs=[ANY, vmem, ANY, ANY],
        scratch_shapes=scratch,
        compiler_params=pltpu.CompilerParams(
            collective_id=ident, has_side_effects=True, vmem_limit_bytes=62 * 1024 * 1024
        ),
        cost_estimate=pl.CostEstimate(
            flops=80 * turns * 2 * span * width * hidden, bytes_accessed=turns * 60 * 2**20, transcendentals=0
        ),
        name="chain_backward",
    )(
        recall_grad, queries, low1_all, low2_all, qpre_all, keys, m1_all, m2_all, g1_all, g2_all, err_all, pre_all,
        lengths, gates,
    )


def from_behind(value, axis, steps):
    count = lax.axis_size(axis)
    first, last = (max(0, -steps), min(count, count - steps))
    return lax.ppermute(value, axis, [(source, source + steps) for source in range(first, last)])


def split_heads(values, head_size):
    return values.reshape(values.shape[:-1] + (values.shape[-1] // head_size, head_size))


def head_norm(values, head_size):
    shaped = split_heads(values, head_size)
    factor = lax.rsqrt(jnp.sum(shaped * shaped, axis=-1, keepdims=True) + eps_head)
    return (shaped * factor).reshape(values.shape)


def head_norm_back(values, upstream, head_size):
    shaped = split_heads(values, head_size)
    grad_shaped = split_heads(upstream, head_size)
    factor = lax.rsqrt(jnp.sum(shaped * shaped, axis=-1, keepdims=True) + eps_head)
    normed = shaped * factor
    inner_sum = jnp.sum(normed * grad_shaped, axis=-1, keepdims=True)
    return (factor * (grad_shaped - normed * inner_sum)).reshape(values.shape)


def rms_back(scaled, factor, upstream):
    return factor * (upstream - scaled * jnp.mean(upstream * scaled, axis=-1, keepdims=True))


def body(
    tokens,
    cotangent,
    seq_spans,
    w_query,
    w_key,
    w_value,
    conv_kernel,
    persistent,
    norm_gain,
    rate_proj,
    out_gate,
    out_proj,
    memory_in,
    memory_out,
    ffn_gain,
    ffn_gate,
    ffn_up,
    ffn_down,
):
    wide, narrow = lax.axis_size("wide"), lax.axis_size("narrow")
    devices = wide * narrow
    wide_pos, narrow_pos = lax.axis_index("wide"), lax.axis_index("narrow")
    span, width = tokens.shape
    taps = conv_kernel.shape[0]
    persist_count = persistent.shape[1]
    local_width = out_gate.shape[1]
    own_rows = span // narrow
    lanes = wide // LANE_WIDE
    chips = LANE_WIDE * narrow // 2
    shards = 2 * chips
    shard_rows = span // shards
    hidden = memory_in.shape[1] // LANE_WIDE
    score_scale = math.sqrt(HEAD)

    def shard_of(tw, tn):
        return lax.rem(tn, 2) * chips + lax.rem(tw, LANE_WIDE) * (narrow // 2) + lax.div(tn, 2)

    long_turns = min(6, wide * 5 // 8)
    turns = max(long_turns, wide - long_turns)
    is_first = False
    start = 0
    for i in range(seq_spans.shape[0]):
        is_first = is_first | (wide_pos == start)
        start = start + seq_spans[i]

    smalls = [conv_kernel, persistent, norm_gain, ffn_gain, rate_proj]
    small_sizes = [a.size for a in smalls]
    packed = jnp.concatenate([a.reshape(-1) for a in smalls])
    padded = -(-packed.size // 2048) * 2048
    packed = jnp.pad(packed, (0, padded - packed.size)).reshape(-1, 128)
    own_weights = jnp.concatenate(
        [a.reshape(a.shape[0], narrow, local_width) for a in (w_query, w_key, w_value)], 2
    ).transpose(1, 0, 2)
    memory_cols = memory_in.reshape(memory_in.shape[0], LANE_WIDE, hidden).transpose(1, 0, 2)
    memory_rows = memory_out.reshape(LANE_WIDE, hidden, memory_out.shape[1])
    small_all, weights_all, first_all, second_all = send_parameters(
        packed, own_weights, [memory_cols, memory_rows], 1
    )
    first_init = first_all.reshape(width, hidden)
    second_init = second_all.transpose(1, 0, 2).reshape(hidden, width)
    small_all = small_all.reshape(devices, padded)
    pieces, at = [], 0
    for a, size in zip(smalls, small_sizes):
        pieces.append(small_all[:, at : at + size].reshape((devices,) + a.shape))
        at += size
    kernel_all = pieces[0].transpose(1, 0, 2).reshape(taps, 3, width)
    persist_all = pieces[1].transpose(1, 2, 0, 3).reshape(2, persist_count, width)
    gain_one = pieces[2].reshape(width).astype(f32)
    gain_two = pieces[3].reshape(width).astype(f32)
    rate_f = pieces[4].reshape(width, 3).astype(f32)
    col_offset = narrow_pos * local_width

    def own_cols(values, axis):
        return lax.dynamic_slice_in_dim(values, col_offset, local_width, axis)

    def own_part(values):
        return lax.dynamic_slice_in_dim(values, narrow_pos * own_rows, own_rows, 0)

    kernel_f = own_cols(kernel_all, 2).reshape(taps, 3 * local_width).astype(f32)
    persist_f = own_cols(persist_all, 2).astype(f32)
    qkv_weights = weights_all.reshape(width, 3 * local_width)

    inputs_f = tokens.astype(f32)
    first_factor = lax.rsqrt(jnp.mean(inputs_f * inputs_f, axis=-1, keepdims=True) + eps_norm)
    first_scaled = inputs_f * first_factor
    normed = first_scaled * gain_one
    normed_low = normed.astype(bf16)
    projected = matmul(normed_low, qkv_weights)
    tail_rows = from_behind(projected[span - taps + 1 :].astype(bf16), "wide", 1).astype(f32)
    extended = jnp.concatenate([jnp.where(is_first, 0.0, tail_rows), projected], 0)
    mixed_conv = kernel_f[0] * projected
    for offset in range(1, taps):
        start_row = taps - 1 - offset
        mixed_conv = mixed_conv + kernel_f[offset] * extended[start_row : start_row + span]
    activated = jax.nn.silu(mixed_conv)
    query_act = activated[:, :local_width]
    key_act = activated[:, local_width : 2 * local_width]
    query_low = head_norm(query_act, HEAD).astype(bf16)
    key_low = head_norm(key_act, HEAD).astype(bf16)
    value_low = activated[:, 2 * local_width :].astype(bf16)
    span_mean = jnp.mean(normed, axis=0)
    gate_scale = jnp.array([decay_top, moment_top, learn_top], f32)
    gate_sig = jax.nn.sigmoid(jnp.sum(span_mean[:, None] * rate_f, axis=0))
    gate_tile = jnp.broadcast_to(jnp.pad(gate_sig * gate_scale, (0, 125))[None], (8, 128))

    key_all, value_got, gate_got = rows_to_lanes(
        key_low, value_low.reshape(shards, shard_rows, local_width), shard_of, gate_tile, 2
    )
    later = (ffn_gate, ffn_up, ffn_down, jnp.concatenate([out_gate, out_proj.T], 1))
    key_all, *later = lax.optimization_barrier((key_all,) + later)
    out_weights = lax.all_gather(later[3], "wide", axis=0, tiled=True)
    ffn_gate_cols = lax.all_gather(later[0], "wide", axis=0, tiled=True)
    ffn_up_cols = lax.all_gather(later[1], "wide", axis=0, tiled=True)
    ffn_down_rows = lax.all_gather(later[2], "wide", axis=1, tiled=True)
    gate_cols = out_weights[:, :local_width]
    proj_cols = out_weights[:, local_width:]
    gate_rows = gate_got[::narrow, 0, :3]
    if wide > 8:
        long_start = (jnp.cumsum(seq_spans) - seq_spans)[jnp.argmax(seq_spans)]
        turn_order = jnp.arange(turns, dtype=jnp.int32)
        rest_order = jnp.where(turn_order < long_start, turn_order, turn_order + long_turns)
        lane_spans = jnp.where(wide_pos // LANE_WIDE == 0, long_start + turn_order, rest_order)
        key_all = key_all[jnp.clip(lane_spans, 0, wide - 1)]
    chain = chain_forward(
        key_all, value_got, query_low, seq_spans, gate_rows, turns, first_init, second_init, 3
    )
    recall_low, saved = chain[0].reshape(span, local_width), chain[1:]
    recall_own = recall_low.astype(f32)

    keys_all = jnp.concatenate(
        [head_norm(persist_f[0], HEAD).astype(bf16), head_norm(recall_own, HEAD).astype(bf16), key_low], 0
    )
    values_all = jnp.concatenate([persist_f[1].astype(bf16), recall_low, value_low], 0)
    query_heads = split_heads(query_low, HEAD)
    key_heads = split_heads(keys_all, HEAD)
    value_heads = split_heads(values_all, HEAD)
    key_total = keys_all.shape[0]
    row_index = lax.broadcasted_iota(jnp.int32, (span, key_total), 0)
    col_index = lax.broadcasted_iota(jnp.int32, (span, key_total), 1)
    allowed = (col_index < persist_count + span) | (col_index - persist_count - span <= row_index)

    def score_block():
        raw_scores = (
            jnp.einsum("thd,jhd->htj", query_heads, key_heads, preferred_element_type=f32) * score_scale
        )
        return jnp.where(allowed[None], raw_scores, masked_score)

    scores = score_block()
    row_top = jnp.max(scores, axis=-1, keepdims=True)
    exponent = jnp.exp(scores - row_top)
    total_sum = jnp.sum(exponent, axis=-1, keepdims=True)
    log_total = row_top + jnp.log(total_sum)
    weights_low = (exponent / total_sum).astype(bf16)
    attended = jnp.einsum("htj,jhd->thd", weights_low, value_heads, preferred_element_type=f32).reshape(
        span, local_width
    )
    gate_pre = matmul(normed_low, gate_cols)
    gate_sigmoid = jax.nn.sigmoid(gate_pre)
    gated_low = (attended * gate_sigmoid).astype(bf16)

    def by_rows(part):
        return part.astype(bf16).reshape(narrow, own_rows, width)

    tokens_own, cotangent_own = own_part(tokens), own_part(cotangent)
    rows_f32, row_f32 = ((own_rows, width), f32), ((1, width), f32)

    def scaled_of(values):
        factor = lax.rsqrt(jnp.mean(values * values, axis=-1, keepdims=True) + eps_norm)
        return values * factor, factor

    def after_branch(totals, extras):
        tokens_rows, gain = extras
        middle = tokens_rows.astype(f32) + totals[0]
        return [(scaled_of(middle)[0] * gain).astype(bf16)], [middle]

    normed_two, middle = narrow_step(
        [by_rows(inner_right(gated_low, proj_cols))],
        [tokens_own, gain_two[None]],
        after_branch,
        1,
        [rows_f32],
        7,
    )
    normed_two = normed_two.reshape(span, width)
    gate_val = matmul(normed_two, ffn_gate_cols)
    up_val = matmul(normed_two, ffn_up_cols)
    gate_silu = jax.nn.silu(gate_val)
    hidden_ffn = (gate_silu * up_val).astype(bf16)
    ffn_part = matmul(hidden_ffn, ffn_down_rows)
    down_grad = inner_left(cotangent, hidden_ffn).astype(bf16)
    hidden_grad_ffn = inner_right(cotangent, ffn_down_rows)
    gate_sig_ffn = jax.nn.sigmoid(gate_val)
    gate_grad_low = (
        hidden_grad_ffn * up_val * gate_sig_ffn * (1.0 + gate_val * (1.0 - gate_sig_ffn))
    ).astype(bf16)
    up_grad_low = (hidden_grad_ffn * gate_silu).astype(bf16)
    ffn_gate_grad = inner_left(normed_two, gate_grad_low).astype(bf16)
    ffn_up_grad = inner_left(normed_two, up_grad_low).astype(bf16)
    normed_two_part = inner_right(gate_grad_low, ffn_gate_cols) + inner_right(up_grad_low, ffn_up_cols)

    def scatter_wide(grad):
        return lax.psum_scatter(grad.astype(bf16), "wide", scatter_dimension=0, tiled=True).astype(f32)

    ffn_sums = (by_rows(ffn_part), by_rows(normed_two_part))
    ffn_sums, ffn_grads = lax.optimization_barrier((ffn_sums, (ffn_gate_grad, ffn_up_grad, down_grad)))
    ffn_gate_out, ffn_up_out, ffn_down_out = [scatter_wide(a) for a in ffn_grads]

    def after_ffn(totals, extras):
        middle_rows, cotangent_rows, gain = extras
        scaled, factor = scaled_of(middle_rows)
        grad = cotangent_rows.astype(f32) + rms_back(scaled, factor, totals[1] * gain)
        gain_part = jnp.sum(totals[1] * scaled, axis=0, keepdims=True)
        return [grad.astype(bf16), (middle_rows + totals[0]).astype(bf16)], [grad, gain_part]

    branch_low, output, middle_grad, gain_two_part = narrow_step(
        list(ffn_sums), [middle, cotangent_own, gain_two[None]], after_ffn, 2, [rows_f32, row_f32], 9
    )
    branch_low, output = branch_low.reshape(span, width), output.reshape(span, width)

    gated_grad = matmul(branch_low, proj_cols)
    attended_grad_low = (gated_grad * gate_sigmoid).astype(bf16)
    gate_pre_low = (gated_grad * attended * gate_sigmoid * (1.0 - gate_sigmoid)).astype(bf16)
    early_grads = jnp.concatenate([inner_left(normed_low, gate_pre_low), inner_left(branch_low, gated_low)], 1)
    early_out = scatter_wide(early_grads)

    weights_again = jnp.exp(score_block() - log_total)
    grad_heads = split_heads(attended_grad_low, HEAD)
    weight_grad = jnp.einsum("thd,jhd->htj", grad_heads, value_heads, preferred_element_type=f32)
    row_delta = jnp.sum(weights_again * weight_grad, axis=-1, keepdims=True)
    score_grad_low = (weights_again * (weight_grad - row_delta)).astype(bf16)
    query_att = (
        score_scale * jnp.einsum("htj,jhd->thd", score_grad_low, key_heads, preferred_element_type=f32)
    ).reshape(span, local_width)
    keys_grad = (
        score_scale * jnp.einsum("htj,thd->jhd", score_grad_low, query_heads, preferred_element_type=f32)
    ).reshape(key_total, local_width)
    values_grad = jnp.einsum(
        "htj,thd->jhd", weights_again.astype(bf16), grad_heads, preferred_element_type=f32
    ).reshape(key_total, local_width)
    recall_end = persist_count + span
    persist_part = jnp.stack(
        [head_norm_back(persist_f[0], keys_grad[:persist_count], HEAD), values_grad[:persist_count]]
    )
    recall_grad_low = (
        head_norm_back(recall_own, keys_grad[persist_count:recall_end], HEAD)
        + values_grad[persist_count:recall_end]
    ).astype(bf16)

    cots, sums_got, first_chunks, second_chunks = chain_backward(recall_grad_low, saved, seq_spans, gate_rows, 12)
    query_mem, key_mem, value_mem = [cots[i].reshape(span, local_width).astype(f32) for i in range(3)]
    gate_sums = jnp.sum(sums_got[:, :, :3], axis=0)[wide_pos] * jnp.array([-1.0, 1.0, -1.0], f32)

    logit_grad = gate_sums * gate_scale * gate_sig * (1.0 - gate_sig)
    rate_part = span_mean[:, None] * logit_grad[None, :]
    gate_row = jnp.sum(rate_f * logit_grad[None, :], axis=1)[None, :] / span
    act_grad = jnp.concatenate(
        [
            head_norm_back(query_act, query_mem + query_att, HEAD),
            head_norm_back(key_act, key_mem + keys_grad[recall_end:], HEAD),
            values_grad[recall_end:] - value_mem,
        ],
        1,
    )
    conv_grad = act_grad * silu_slope(mixed_conv)
    kernel_rows = []
    extended_grad = jnp.zeros_like(extended)
    for offset in range(taps):
        start_row = taps - 1 - offset
        kernel_rows.append(jnp.sum(conv_grad * extended[start_row : start_row + span], axis=0))
        extended_grad = extended_grad + jnp.pad(kernel_f[offset] * conv_grad, ((start_row, offset), (0, 0)))
    tail_back = from_behind(
        jnp.where(is_first, 0.0, extended_grad[: taps - 1]).astype(bf16), "wide", -1
    ).astype(f32)
    projected_grad = extended_grad[taps - 1 :] + jnp.pad(tail_back, ((span - taps + 1, 0), (0, 0)))
    projected_low = projected_grad.astype(bf16)
    normed_part = inner_right(projected_low, qkv_weights) + inner_right(gate_pre_low, gate_cols)

    def after_all(totals, extras):
        tokens_rows, grad_rows, gain, row = extras
        scaled, factor = scaled_of(tokens_rows.astype(f32))
        normed_grad = totals[0] + row
        gain_part = jnp.sum(normed_grad * scaled, axis=0, keepdims=True)
        return [(grad_rows + rms_back(scaled, factor, normed_grad * gain)).astype(bf16)], [gain_part]

    weight_grads = inner_left(normed_low, projected_low).astype(bf16)

    def place_cols(piece, axis):
        full = piece.shape[:axis] + (width,) + piece.shape[axis + 1 :]
        return lax.dynamic_update_slice_in_dim(jnp.zeros(full, f32), piece, col_offset, axis)

    kernel_full = place_cols(jnp.stack(kernel_rows).reshape(taps, 3, local_width), 2).reshape(taps, 3 * width)
    persist_full = place_cols(persist_part, 2)
    rate_part = jnp.where(narrow_pos == 0, rate_part, 0.0)
    chunks = [
        kernel_full.reshape(taps, devices, -1).transpose(1, 0, 2),
        persist_full.reshape(2, persist_count, devices, -1).transpose(2, 0, 1, 3),
        gain_two_part.reshape(devices, -1),
        rate_part.reshape(devices, -1, 3),
    ]
    flat = jnp.concatenate([a.reshape(devices, -1) for a in chunks], 1)
    flat_size = -(-flat.shape[1] // 1024) * 1024
    flat = jnp.pad(flat, ((0, 0), (0, flat_size - flat.shape[1]))).reshape(devices, -1, 128)
    tokens_grad, weight_out, first_out, second_out, flat_sum, gain_sum = last_step(
        by_rows(normed_part),
        [tokens_own, middle_grad, gain_one[None], gate_row],
        after_all,
        weight_grads.reshape(wide, width // wide, 3 * local_width),
        [first_chunks, second_chunks],
        flat,
        15,
    )
    tokens_grad = tokens_grad.reshape(span, width).astype(f32)
    flat_sum = flat_sum.reshape(-1)
    own_start = (wide_pos * narrow + narrow_pos) * (width // devices)
    norm_grad = lax.dynamic_slice_in_dim(gain_sum.reshape(-1), own_start, width // devices, 0)
    small_outs, at = [], 0
    for a in chunks:
        size = a.size // devices
        small_outs.append(flat_sum[at : at + size].reshape(a.shape[1:]))
        at += size
    kernel_grad, persist_grad, ffn_gain_grad, rate_grad = small_outs
    return (
        output,
        tokens_grad,
        weight_out[:, :local_width],
        weight_out[:, local_width : 2 * local_width],
        weight_out[:, 2 * local_width : 3 * local_width],
        kernel_grad,
        persist_grad,
        norm_grad,
        rate_grad,
        early_out[:, :local_width],
        early_out[:, local_width:].T,
        first_out,
        second_out,
        ffn_gain_grad,
        ffn_gate_out,
        ffn_up_out,
        ffn_down_out.T,
    )


def solution(mesh):
    rows, both, square, turned = P("wide", None), P(("wide", "narrow"), None), P("wide", "narrow"), P("narrow", "wide")
    flat, taps, heads = P(("wide", "narrow")), P(None, ("wide", "narrow")), P(None, None, ("wide", "narrow"))
    return jax.shard_map(
        body,
        mesh=mesh,
        in_specs=(rows, rows, P(), both, both, both, taps, heads, flat, both)
        + (square, turned, square, turned, flat, square, square, turned),
        out_specs=(rows, rows, square, square, square, taps, heads, flat, both)
        + (square, turned, square, turned, flat, square, square, turned),
        check_vma=False,
    )
```

```python
import math

import jax
import jax.numpy as jnp
from jax import lax
from jax.experimental import pallas as pl
from jax.experimental.pallas import tpu as pltpu
from jax.sharding import PartitionSpec as P

HEAD = 64
LANE_WIDE = 4
MESH = pl.DeviceIdType.MESH
ANY = pl.BlockSpec(memory_space=pl.ANY)
bf16 = jnp.bfloat16
f32 = jnp.float32

decay_top = 0.2
moment_top = 0.9
learn_top = 0.1
eps_norm = 1e-05
eps_head = 1e-06
masked_score = -1e30


def remote(src, dst, send, recv, device):
    return pltpu.make_async_remote_copy(
        src_ref=src, dst_ref=dst, send_sem=send, recv_sem=recv, device_id=device, device_id_type=MESH
    )


class Grid:
    def __init__(self):
        wide, narrow = lax.axis_size("wide"), lax.axis_size("narrow")
        self.zs = 4 if wide % 4 == 0 else 1
        self.xs, self.ys = wide // self.zs, narrow // 2
        self.wide, self.narrow = lax.axis_index("wide"), lax.axis_index("narrow")
        self.z, self.x = lax.div(self.wide, self.xs), lax.rem(self.wide, self.xs)
        self.y, self.c = lax.div(self.narrow, 2), lax.rem(self.narrow, 2)
        self.partner = self.device(self.z, self.x, self.y, 1 - self.c)

    def device(self, z, x, y, c):
        return z * self.xs + x, 2 * y + c

    def z_others(self):
        if self.zs != 4:
            return [lax.rem(self.z + s, self.zs) for s in range(1, self.zs)]
        near = self.z + 1 - 2 * lax.div(self.z + 3, 4)
        far = 3 - 3 * lax.div(self.z, 2)
        return [near, 6 - self.z - near - far, far]

    def x_others(self):
        return [lax.rem(self.x + s, self.xs) for s in range(1, self.xs)]

    def y_others(self):
        return [lax.rem(self.y + s, self.ys) for s in range(1, self.ys)]

    def greet_all(self):
        wide, narrow = lax.axis_size("wide"), lax.axis_size("narrow")
        devices = wide * narrow
        me = self.wide * narrow + self.narrow
        barrier = pltpu.get_barrier_semaphore()

        def greet(step, carry):
            target = lax.rem(me + step, devices)
            where = lax.div(target, narrow), lax.rem(target, narrow)
            pl.semaphore_signal(barrier, inc=1, device_id=where, device_id_type=MESH)
            return carry

        lax.fori_loop(1, devices, greet, 0)
        return lambda: pl.semaphore_wait(barrier, devices - 1)


class Gather:
    def __init__(self, grid, source, whole, sems):
        self.grid, self.source, self.whole = grid, source, whole
        self.sent, self.got, self.sent_pair, self.got_pair = sems
        self.rows = whole.shape[2]
        self.pushes, self.pairs = 0, 0

    @staticmethod
    def counts():
        zs = 4 if lax.axis_size("wide") % 4 == 0 else 1
        xs, ys = lax.axis_size("wide") // zs, lax.axis_size("narrow") // 2
        sends = 2 * (zs - 1) + zs * 2 * (xs - 1 + ys - 1) + 2 * zs * (xs - 1) * (ys - 1)
        return zs * xs * ys, sends, 2 * zs * xs * ys

    @classmethod
    def scratch(cls):
        chips, sends, pairs = cls.counts()
        return [
            pltpu.SemaphoreType.DMA((sends,)),
            pltpu.SemaphoreType.DMA((chips, 2)),
            pltpu.SemaphoreType.DMA((pairs,)),
            pltpu.SemaphoreType.DMA((chips, 2)),
        ]

    def half(self, ref, h):
        return ref.at[pl.ds(h * (self.rows // 2), self.rows // 2)]

    def piece(self, z, x, y, c, h):
        wide, narrow = self.grid.device(z, x, y, c)
        return self.half(self.whole.at[wide, narrow], h)

    def spot(self, z, x, y):
        return (z * self.grid.xs + x) * self.grid.ys + y

    def push(self, z, x, y, h, target, own):
        here = self.piece(z, x, y, self.grid.c, h)
        copy = remote(
            self.half(self.source, h) if own else here,
            here,
            self.sent.at[self.pushes],
            self.got.at[self.spot(z, x, y), h],
            target,
        )
        self.pushes += 1
        copy.start()

    def to_partner(self, z, x, y, h, own=False):
        here = self.piece(z, x, y, self.grid.c, h)
        copy = remote(
            self.half(self.source, h) if own else here,
            here,
            self.sent_pair.at[self.pairs],
            self.got_pair.at[self.spot(z, x, y), h],
            self.grid.partner,
        )
        self.pairs += 1
        copy.start()

    def arrived(self, z, x, y, h):
        here = self.piece(z, x, y, self.grid.c, h)
        remote(here, here, self.sent.at[0], self.got.at[self.spot(z, x, y), h], self.grid.partner).wait_recv()

    def fan(self, z, own=False):
        g = self.grid
        to_y = [g.device(g.z, g.x, y, g.c) for y in g.y_others()]
        to_x = [g.device(g.z, x, g.y, g.c) for x in g.x_others()]
        for h, targets in ((0, to_y), (1, to_x), (0, to_x), (1, to_y)):
            for target in targets:
                self.push(z, g.x, g.y, h, target, own)
        for h in (0, 1):
            self.to_partner(z, g.x, g.y, h, own)

    def begin(self):
        g = self.grid
        for z in g.z_others():
            for h in (0, 1):
                self.push(g.z, g.x, g.y, h, g.device(z, g.x, g.y, g.c), True)
        self.fan(g.z, True)

    def level(self, number):
        return ([self.grid.z] + self.grid.z_others())[number]

    def along_z(self, number):
        g, z = self.grid, self.level(number)
        for h in (0, 1):
            self.arrived(z, g.x, g.y, h)
        self.fan(z)

    def across(self, number):
        g, z = self.grid, self.level(number)
        for y in g.y_others():
            self.arrived(z, g.x, y, 0)
            for x in g.x_others():
                self.push(z, g.x, y, 0, g.device(g.z, x, g.y, g.c), False)
            self.to_partner(z, g.x, y, 0)
        for x in g.x_others():
            self.arrived(z, x, g.y, 1)
            for y in g.y_others():
                self.push(z, x, g.y, 1, g.device(g.z, g.x, y, g.c), False)
            self.to_partner(z, x, g.y, 1)

    def last(self, number):
        g, z = self.grid, self.level(number)
        for x in g.x_others():
            self.arrived(z, x, g.y, 0)
            self.to_partner(z, x, g.y, 0)
            for y in g.y_others():
                self.arrived(z, x, y, 0)
                self.to_partner(z, x, y, 0)
        for y in g.y_others():
            self.arrived(z, g.x, y, 1)
            self.to_partner(z, g.x, y, 1)
            for x in g.x_others():
                self.arrived(z, x, y, 1)
                self.to_partner(z, x, y, 1)

    def middle(self):
        for number in range(1, self.grid.zs):
            self.along_z(number)
            self.across(number - 1)
            if number > 1:
                self.last(number - 2)
        self.across(self.grid.zs - 1)
        for number in range(max(0, self.grid.zs - 2), self.grid.zs):
            self.last(number)

    def finish(self):
        g = self.grid
        here = self.piece(g.z, g.x, g.y, g.c, 0)
        _, sends, pairs = self.counts()
        for sems, number in ((self.sent, sends), (self.sent_pair, pairs)):
            for i in range(number):
                remote(here, here, sems.at[i], self.got.at[0, 0], g.partner).wait_send()
        for z in range(g.zs):
            for x in range(g.xs):
                for y in range(g.ys):
                    for h in (0, 1):
                        there = self.piece(z, x, y, 1 - g.c, h)
                        remote(
                            there, there, self.sent.at[0], self.got_pair.at[self.spot(z, x, y), h], g.partner
                        ).wait_recv()


def send_parameters(smalls, weights, blocks, ident):
    wide, narrow = lax.axis_size("wide"), lax.axis_size("narrow")
    devices = wide * narrow
    count = len(blocks)

    def kernel(*refs):
        smalls_ref, weights_ref = refs[:2]
        block_refs, refs = refs[2 : 2 + count], refs[2 + count :]
        smalls_out, weights_out = refs[:2]
        block_outs, refs = refs[2 : 2 + count], refs[2 + count :]
        hold_small, hold_weight, refs = refs[0], refs[1], refs[2:]
        hold_blocks, refs = refs[:count], refs[count:]
        local_sem, all_send, all_recv, near_send, near_recv, z_send, z_recv, x_send, x_recv, b_send, b_recv = refs
        g = Grid()
        me = g.wide * narrow + g.narrow
        wait_all = g.greet_all()
        own = [
            (smalls_ref, hold_small, smalls_out.at[me]),
            (weights_ref.at[g.narrow], hold_weight, weights_out.at[g.wide, g.narrow]),
        ] + [
            (block_refs[i].at[lax.rem(g.wide, LANE_WIDE)], hold_blocks[i], block_outs[i].at[g.wide])
            for i in range(count)
        ]
        into = [pltpu.make_async_copy(a, b, local_sem.at[i]) for i, (a, b, _) in enumerate(own)]
        back = [pltpu.make_async_copy(b, c, local_sem.at[i]) for i, (_, b, c) in enumerate(own)]
        for copy in into:
            copy.start()
        wait_all()
        near = []
        for s in range(1, narrow):
            target = lax.rem(g.narrow + s, narrow)
            copy = remote(
                weights_ref.at[target],
                weights_out.at[g.wide, g.narrow],
                near_send.at[s],
                near_recv.at[g.narrow],
                (g.wide, target),
            )
            copy.start()
            near.append(copy)

        def send_small(step, carry):
            target = lax.rem(me + step, devices)
            remote(
                smalls_ref,
                smalls_out.at[me],
                all_send.at[0],
                all_recv.at[0],
                (lax.div(target, narrow), lax.rem(target, narrow)),
            ).start()
            return carry

        lax.fori_loop(1, devices, send_small, 0)
        for copy in into:
            copy.wait()
        for copy in back:
            copy.start()
        for copy in back:
            copy.wait()
        for s in range(1, narrow):
            source = lax.rem(g.narrow + s, narrow)
            there = weights_out.at[g.wide, source]
            remote(there, there, near_send.at[s], near_recv.at[source], g.partner).wait_recv()

        def row(z, x):
            return weights_out.at[z * g.xs + x]

        sends = []

        def push(z, target, send, recv):
            copy = remote(row(z, g.x), row(z, g.x), send, recv, target)
            copy.start()
            sends.append(copy)

        for i, z in enumerate(g.z_others()):
            push(g.z, g.device(z, g.x, g.y, g.c), z_send.at[i], z_recv.at[g.z])
        for i, x in enumerate(g.x_others()):
            push(g.z, g.device(g.z, x, g.y, g.c), x_send.at[0, i], x_recv.at[g.z, g.x])
        for s in range(1, wide):
            target = lax.rem(g.wide + s, wide)
            for i in range(count):
                copy = remote(
                    block_refs[i].at[lax.rem(target, LANE_WIDE)],
                    block_outs[i].at[g.wide],
                    b_send.at[i, s],
                    b_recv.at[i, g.wide],
                    (target, g.narrow),
                )
                copy.start()
                sends.append(copy)
        for j, z in enumerate(g.z_others()):
            remote(row(z, g.x), row(z, g.x), z_send.at[0], z_recv.at[z], g.partner).wait_recv()
            for i, x in enumerate(g.x_others()):
                push(z, g.device(g.z, x, g.y, g.c), x_send.at[1 + j, i], x_recv.at[z, g.x])
        for x in g.x_others():
            for z in [g.z] + g.z_others():
                remote(row(z, x), row(z, x), z_send.at[0], x_recv.at[z, x], g.partner).wait_recv()
        for s in range(1, wide):
            source = lax.rem(g.wide + s, wide)
            for i in range(count):
                there = block_outs[i].at[source]
                remote(there, there, z_send.at[0], b_recv.at[i, source], g.partner).wait_recv()
        for copy in near + sends:
            copy.wait_send()
        others = smalls_out.at[pl.ds(0, devices - 1)]
        whole = remote(others, others, all_send.at[0], all_recv.at[0], g.partner)
        whole.wait_send()
        whole.wait_recv()

    zs = 4 if wide % 4 == 0 else 1
    xs = wide // zs
    sem = pltpu.SemaphoreType.DMA
    return pl.pallas_call(
        kernel,
        out_shape=[
            jax.ShapeDtypeStruct((devices,) + smalls.shape, smalls.dtype),
            jax.ShapeDtypeStruct((wide, narrow) + weights.shape[1:], weights.dtype),
        ]
        + [jax.ShapeDtypeStruct((wide,) + b.shape[1:], b.dtype) for b in blocks],
        in_specs=[ANY] * (2 + count),
        out_specs=[ANY] * (2 + count),
        scratch_shapes=[pltpu.VMEM(smalls.shape, smalls.dtype), pltpu.VMEM(weights.shape[1:], weights.dtype)]
        + [pltpu.VMEM(b.shape[1:], b.dtype) for b in blocks]
        + [sem((2 + count,)), sem((1,)), sem((1,)), sem((narrow,)), sem((narrow,)), sem((zs,)), sem((zs,))]
        + [sem((zs, xs)), sem((zs, xs)), sem((count, wide)), sem((count, wide))],
        compiler_params=pltpu.CompilerParams(collective_id=ident, has_side_effects=True),
        name="send_parameters",
    )(smalls, weights, *blocks)


def narrow_step(parts, extras, work, spread_count, locals_like, ident):
    narrow, rows, width = parts[0].shape
    ys = narrow // 2
    count, extra_count, local_count = len(parts), len(extras), len(locals_like)
    parts = [p.reshape(ys, 2, rows, width) for p in parts]

    def kernel(*refs):
        part_refs, refs = refs[:count], refs[count:]
        extra_refs, refs = refs[:extra_count], refs[extra_count:]
        spread_refs, refs = refs[:spread_count], refs[spread_count:]
        local_refs, refs = refs[:local_count], refs[local_count:]
        mine, pair, half, got, rowbuf, refs = refs[0], refs[1], refs[2], refs[3], refs[4], refs[5:]
        load_sem, pair_send, pair_recv, y_send, y_recv, s_send, s_recv, p_send, p_recv, own_sem = refs
        g = Grid()
        barrier = pltpu.get_barrier_semaphore()
        friends = [g.device(g.z, g.x, y, g.c) for y in g.y_others()] + [g.partner]
        for friend in friends:
            pl.semaphore_signal(barrier, inc=1, device_id=friend, device_id_type=MESH)
        loads = [
            pltpu.make_async_copy(part_refs[i].at[:, g.c], mine.at[i], load_sem.at[i]) for i in range(count)
        ]
        for copy in loads:
            copy.start()
        pl.semaphore_wait(barrier, len(friends))
        pairs = [
            remote(part_refs[i].at[:, 1 - g.c], pair.at[i], pair_send.at[i], pair_recv.at[i], g.partner)
            for i in range(count)
        ]
        for copy in pairs:
            copy.start()
        sends = []
        for i in range(count):
            loads[i].wait()
            pairs[i].wait_recv()
            half[i] = (mine[i].astype(f32) + pair[i].astype(f32)).astype(bf16)
            for s, y in enumerate(g.y_others()):
                copy = remote(
                    half.at[i, y], got.at[i, g.y], y_send.at[i, s], y_recv.at[i, g.y], g.device(g.z, g.x, y, g.c)
                )
                copy.start()
                sends.append(copy)
        totals = []
        for i in range(count):
            total = half[i, g.y].astype(f32)
            for y in g.y_others():
                remote(got.at[i, y], got.at[i, y], y_send.at[i, 0], y_recv.at[i, y], g.partner).wait_recv()
                total = total + got[i, y].astype(f32)
            totals.append(total)
        spreads, locals_out = work(totals, [ref[...] for ref in extra_refs])
        for ref, value in zip(local_refs, locals_out):
            ref[...] = value
        own = []
        for i, value in enumerate(spreads):
            rowbuf[i] = value
            for s, y in enumerate(g.y_others()):
                copy = remote(
                    rowbuf.at[i],
                    spread_refs[i].at[g.narrow],
                    s_send.at[i, s],
                    s_recv.at[i, g.y],
                    g.device(g.z, g.x, y, g.c),
                )
                copy.start()
                sends.append(copy)
            copy = remote(
                rowbuf.at[i], spread_refs[i].at[g.narrow], p_send.at[i, g.y], p_recv.at[i, g.y], g.partner
            )
            copy.start()
            sends.append(copy)
            copy = pltpu.make_async_copy(rowbuf.at[i], spread_refs[i].at[g.narrow], own_sem.at[i])
            copy.start()
            own.append(copy)
        for i in range(spread_count):
            for y in g.y_others():
                there = spread_refs[i].at[2 * y + g.c]
                remote(there, there, s_send.at[i, 0], s_recv.at[i, y], g.partner).wait_recv()
                copy = remote(there, there, p_send.at[i, y], p_recv.at[i, y], g.partner)
                copy.start()
                sends.append(copy)
        for i in range(spread_count):
            for y in range(ys):
                there = spread_refs[i].at[2 * y + 1 - g.c]
                remote(there, there, s_send.at[i, 0], p_recv.at[i, y], g.partner).wait_recv()
        for copy in pairs + sends:
            copy.wait_send()
        for copy in own:
            copy.wait()

    sem = pltpu.SemaphoreType.DMA
    vmem = pl.BlockSpec(memory_space=pltpu.VMEM)
    return pl.pallas_call(
        kernel,
        out_shape=[jax.ShapeDtypeStruct((narrow, rows, width), bf16)] * spread_count
        + [jax.ShapeDtypeStruct(shape, dtype) for shape, dtype in locals_like],
        in_specs=[ANY] * count + [vmem] * extra_count,
        out_specs=[ANY] * spread_count + [vmem] * local_count,
        scratch_shapes=[pltpu.VMEM((count, ys, rows, width), bf16)] * 4
        + [pltpu.VMEM((spread_count, rows, width), bf16)]
        + [sem((count,))] * 3
        + [sem((count, ys))] * 2
        + [sem((spread_count, ys))] * 4
        + [sem((spread_count,))],
        compiler_params=pltpu.CompilerParams(collective_id=ident, has_side_effects=True),
        name=f"narrow_step_{ident}",
    )(*parts, *extras)


def last_step(part, extras, work, grads, chunks, flat, ident):
    narrow, rows, width = part.shape
    wide = lax.axis_size("wide")
    devices = wide * narrow
    ys = narrow // 2
    zs = 4 if wide % 4 == 0 else 1
    xs = wide // zs
    lanes = wide // LANE_WIDE
    extra_count = len(extras)
    part = part.reshape(ys, 2, rows, width)
    own_grad = grads.shape[1:]
    grads = grads.reshape((zs, xs) + own_grad)
    first_shape, second_shape, flat_shape = chunks[0].shape[1:], chunks[1].shape[1:], flat.shape[1:]

    def kernel(*refs):
        part_ref, grads_ref, first_ref, second_ref, flat_ref = refs[:5]
        extra_refs, refs = refs[5 : 5 + extra_count], refs[5 + extra_count :]
        spread_ref, grads_out, first_out, second_out, flat_out, row_out, refs = refs[:6] + (refs[6:],)
        mine, pair, half, got, rowbuf, rowtile, rowgot, refs = refs[:7] + (refs[7:],)
        gown, gx, ghalf, gz, fgot, sgot, flatgot, refs = refs[:7] + (refs[7:],)
        load_sem, pair_sem, y_send, y_recv, s_send, s_recv, p_send, p_recv, refs = refs[:8] + (refs[8:],)
        gx_send, gx_recv, gz_send, gz_recv, c_send, c_recv, all_send, all_recv = refs
        g = Grid()
        me = g.wide * narrow + g.narrow
        wait_all = g.greet_all()
        loads = [
            pltpu.make_async_copy(part_ref.at[:, g.c], mine, load_sem.at[0]),
            pltpu.make_async_copy(grads_ref.at[:, g.x], gown, load_sem.at[1]),
            pltpu.make_async_copy(first_ref.at[g.wide], fgot.at[g.wide], load_sem.at[2]),
            pltpu.make_async_copy(second_ref.at[g.wide], sgot.at[g.wide], load_sem.at[3]),
            pltpu.make_async_copy(flat_ref.at[me], flatgot.at[me], load_sem.at[4]),
        ]
        for copy in loads:
            copy.start()
        wait_all()
        pair_copy = remote(part_ref.at[:, 1 - g.c], pair, pair_sem.at[0], pair_sem.at[1], g.partner)
        pair_copy.start()
        sends = []
        order = g.z_others()[::-1] + [g.z]
        for z in order:
            for i, x in enumerate(g.x_others()):
                copy = remote(
                    grads_ref.at[z, x],
                    gx.at[g.x, z],
                    gx_send.at[i, z],
                    gx_recv.at[g.x, z],
                    g.device(g.z, x, g.y, g.c),
                )
                copy.start()
                sends.append(copy)
        for s in range(1, wide):
            target = lax.rem(g.wide + s, wide)
            for i, (source, place) in enumerate(((first_ref, fgot), (second_ref, sgot))):
                copy = remote(
                    source.at[target],
                    place.at[g.wide],
                    c_send.at[i, s],
                    c_recv.at[i, g.wide],
                    (target, g.narrow),
                )
                copy.start()
                sends.append(copy)

        def send_flat(step, carry):
            target = lax.rem(me + step, devices)
            where = lax.div(target, narrow), lax.rem(target, narrow)
            remote(flat_ref.at[target], flatgot.at[me], all_send.at[0], all_recv.at[0], where).start()
            return carry

        lax.fori_loop(1, devices, send_flat, 0)
        loads[0].wait()
        pair_copy.wait()
        half[...] = (mine[...].astype(f32) + pair[...].astype(f32)).astype(bf16)
        for s, y in enumerate(g.y_others()):
            copy = remote(half.at[y], got.at[g.y], y_send.at[s], y_recv.at[g.y], g.device(g.z, g.x, y, g.c))
            copy.start()
            sends.append(copy)
        for copy in loads[1:]:
            copy.wait()

        def grad_along_z(z):
            total = gown[z].astype(f32)
            for x in g.x_others():
                place = gx.at[x, z]
                remote(place, place, gx_send.at[0, 0], gx_recv.at[x, z], g.partner).wait_recv()
                total = total + gx[x, z].astype(f32)
            ghalf[z] = total.astype(bf16)

        for i, z in enumerate(order[:-1]):
            grad_along_z(z)
            copy = remote(
                ghalf.at[z], gz.at[g.z], gz_send.at[i], gz_recv.at[g.z], g.device(z, g.x, g.y, g.c)
            )
            copy.start()
            sends.append(copy)
            if i == 0:
                total = half[g.y].astype(f32)
                for y in g.y_others():
                    remote(got.at[y], got.at[y], y_send.at[0], y_recv.at[y], g.partner).wait_recv()
                    total = total + got[y].astype(f32)
                spreads, locals_out = work([total], [ref[...] for ref in extra_refs])
                rowbuf[...] = spreads[0]
                for j in range(8):
                    rowtile[pl.ds(j, 1), :] = locals_out[0][:, j * width // 8 : (j + 1) * width // 8]
                for s, y in enumerate(g.y_others()):
                    copy = remote(
                        rowbuf,
                        spread_ref.at[g.narrow],
                        s_send.at[s],
                        s_recv.at[g.y],
                        g.device(g.z, g.x, y, g.c),
                    )
                    copy.start()
                    sends.append(copy)
                copy = remote(rowbuf, spread_ref.at[g.narrow], p_send.at[g.y], p_recv.at[g.y], g.partner)
                copy.start()
                sends.append(copy)
                own = pltpu.make_async_copy(rowbuf, spread_ref.at[g.narrow], load_sem.at[0])
                own.start()

                def send_row(step, carry):
                    target = lax.rem(me + step, devices)
                    where = lax.div(target, narrow), lax.rem(target, narrow)
                    remote(rowtile, rowgot.at[me], all_send.at[1], all_recv.at[1], where).start()
                    return carry

                lax.fori_loop(1, devices, send_row, 0)
                rowgot[me] = rowtile[...]
        for y in g.y_others():
            there = spread_ref.at[2 * y + g.c]
            remote(there, there, s_send.at[0], s_recv.at[y], g.partner).wait_recv()
            copy = remote(there, there, p_send.at[y], p_recv.at[y], g.partner)
            copy.start()
            sends.append(copy)
        grad_along_z(g.z)
        for s in range(1, wide):
            source = lax.rem(g.wide + s, wide)
            for i, place in enumerate((fgot, sgot)):
                there = place.at[source]
                remote(there, there, c_send.at[i, 0], c_recv.at[i, source], g.partner).wait_recv()
        for p in range(LANE_WIDE):
            first_sum, second_sum = fgot[p].astype(f32), sgot[p].astype(f32)
            for lane in range(1, lanes):
                first_sum = first_sum + fgot[lane * LANE_WIDE + p].astype(f32)
                second_sum = second_sum + sgot[lane * LANE_WIDE + p].astype(f32)
            first_out[:, p * first_shape[1] : (p + 1) * first_shape[1]] = first_sum
            second_out[p * second_shape[0] : (p + 1) * second_shape[0], :] = second_sum
        total = ghalf[g.z].astype(f32)
        for z in order[:-1]:
            place = gz.at[z]
            remote(place, place, gz_send.at[0], gz_recv.at[z], g.partner).wait_recv()
            total = total + gz[z].astype(f32)
        grads_out[...] = total
        for i, place in enumerate((flatgot, rowgot)):
            others = place.at[pl.ds(0, devices - 1)]
            whole = remote(others, others, all_send.at[i], all_recv.at[i], g.partner)
            whole.wait_send()
            whole.wait_recv()
        flat_out[...] = jnp.sum(flatgot[...], axis=0)
        row_out[...] = jnp.sum(rowgot[...], axis=0)
        for y in range(ys):
            there = spread_ref.at[2 * y + 1 - g.c]
            remote(there, there, s_send.at[0], p_recv.at[y], g.partner).wait_recv()
        for copy in sends:
            copy.wait_send()
        own.wait()

    sem = pltpu.SemaphoreType.DMA
    vmem = pl.BlockSpec(memory_space=pltpu.VMEM)
    return pl.pallas_call(
        kernel,
        out_shape=[
            jax.ShapeDtypeStruct((narrow, rows, width), bf16),
            jax.ShapeDtypeStruct(own_grad, f32),
            jax.ShapeDtypeStruct((first_shape[0], LANE_WIDE * first_shape[1]), f32),
            jax.ShapeDtypeStruct((LANE_WIDE * second_shape[0], second_shape[1]), f32),
            jax.ShapeDtypeStruct(flat_shape, f32),
            jax.ShapeDtypeStruct((8, width // 8), f32),
        ],
        in_specs=[ANY] * 5 + [vmem] * extra_count,
        out_specs=[ANY] + [vmem] * 5,
        scratch_shapes=[pltpu.VMEM((ys, rows, width), bf16)] * 4
        + [pltpu.VMEM((rows, width), bf16)]
        + [pltpu.VMEM((8, width // 8), f32), pltpu.VMEM((devices, 8, width // 8), f32)]
        + [
            pltpu.VMEM((zs,) + own_grad, bf16),
            pltpu.VMEM((xs, zs) + own_grad, bf16),
            pltpu.VMEM((zs,) + own_grad, bf16),
            pltpu.VMEM((zs,) + own_grad, bf16),
            pltpu.VMEM((wide,) + first_shape, bf16),
            pltpu.VMEM((wide,) + second_shape, bf16),
            pltpu.VMEM((devices,) + flat_shape, f32),
        ]
        + [sem((5,)), sem((2,))]
        + [sem((ys,))] * 6
        + [sem((xs, zs))] * 2
        + [sem((zs,))] * 2
        + [sem((2, wide))] * 2
        + [sem((2,))] * 2,
        compiler_params=pltpu.CompilerParams(
            collective_id=ident, has_side_effects=True, vmem_limit_bytes=48 * 1024 * 1024
        ),
        name="last_step",
    )(part, grads, chunks[0], chunks[1], flat, *extras)


class Plan:
    def __init__(self, spans_ref, gates_ref, count):
        self.wide = lax.axis_size("wide")
        self.long = min(6, self.wide * 5 // 8)
        self.gates = gates_ref
        lengths = [spans_ref[i] for i in range(count)]
        self.starts, at = [], 0
        for length in lengths:
            self.starts.append(at)
            at = at + length
        longest, self.start = lengths[0], 0
        for i in range(1, count):
            more = lengths[i] > longest
            longest = jnp.where(more, lengths[i], longest)
            self.start = jnp.where(more, self.starts[i], self.start)
        self.lane = lax.div(lax.axis_index("wide"), LANE_WIDE)

    def span(self, turn):
        rest = jnp.where(turn < self.start, turn, turn + self.long)
        return jnp.clip(jnp.where(self.lane == 0, self.start + turn, rest), 0, self.wide - 1)

    def valid(self, turn):
        count = jnp.where(self.lane == 0, self.long, jnp.where(self.lane == 1, self.wide - self.long, 0))
        return jnp.where(turn < count, 1.0, 0.0)

    def first(self, turn):
        span = self.span(turn)
        found = jnp.where(span == self.starts[0], 1.0, 0.0)
        for start in self.starts[1:]:
            found = jnp.maximum(found, jnp.where(span == start, 1.0, 0.0))
        return jnp.maximum(found, 1.0 - self.valid(turn))

    def rates(self, turn):
        span = self.span(turn)
        return self.gates[span, 0], self.gates[span, 1], self.gates[span, 2]

    def lane_of(self, span):
        inside = (span >= self.start) & (span < self.start + self.long)
        return jnp.where(inside, 0, 1)

    def turn_of(self, span):
        inside = (span >= self.start) & (span < self.start + self.long)
        outside = jnp.where(span < self.start, span, span - self.long)
        return jnp.where(inside, span - self.start, outside)


def paired_lanes():
    wide = lax.axis_size("wide")
    long = min(6, wide * 5 // 8)
    return wide == 2 * LANE_WIDE and long == LANE_WIDE + 1 and lax.axis_size("narrow") == 4


class LaneGather:
    def __init__(self, grid, plan, source, whole, refs):
        self.grid, self.plan, self.source, self.whole = grid, plan, source, whole
        self.own, self.taken, self.mine = refs[:3]
        self.sent, self.got, self.sent_pair, self.got_pair, self.swap_sent, self.swap_got, self.local = refs[3:]
        self.rows = whole.shape[2]
        self.quarter = self.rows // LANE_WIDE
        third = (self.rows + self.quarter) // 3 // 16 * 16
        self.cuts = [(0, third), (third, third), (2 * third, self.rows - 2 * third)]
        self.side = lax.div(grid.wide, LANE_WIDE)
        self.spot = lax.rem(grid.wide, LANE_WIDE)
        long = plan.long
        lone = jnp.where((grid.wide >= plan.wide - long) & (grid.wide < long), 1, 0)
        self.paired = lone == 0
        self.pair = (grid.wide + long - 2 * long * self.side, grid.narrow)
        self.here = (lax.div(self.spot, 2), lax.rem(self.spot, 2), grid.y)

    @staticmethod
    def scratch(rows, cols):
        sem = pltpu.SemaphoreType.DMA
        return [
            pltpu.VMEM((rows, cols), bf16),
            pltpu.VMEM((rows, cols), bf16),
            pltpu.VMEM((rows + rows // LANE_WIDE, cols), bf16),
            sem((4, 7)),
            sem((4, 8)),
            sem((4, 8)),
            sem((4, 8)),
            sem((4,)),
            sem((4,)),
            sem((5,)),
        ]

    @staticmethod
    def shape(rows, cols):
        return (LANE_WIDE + 1, lax.axis_size("narrow"), rows, cols)

    def order(self, part):
        return ((0, 1, 2), (1, 2, 0), (2, 0, 1))[part]

    def place(self, mask):
        return [1 - v if mask >> i & 1 else v for i, v in enumerate(self.here)]

    def device(self, mask, colour):
        z, x, y = self.place(mask)
        return self.side * LANE_WIDE + 2 * z + x, 2 * y + colour

    def pieces(self, part, mask, colour):
        z, x, y = self.place(mask)
        spot, narrow = 2 * z + x, 2 * y + colour
        start, size = self.cuts[part]
        result = [(part, self.whole.at[spot, narrow, pl.ds(start, size)], self.mine.at[pl.ds(start, size)])]
        if part == 2:
            there = self.whole.at[LANE_WIDE, narrow, pl.ds(spot * self.quarter, self.quarter)]
            result.append((3, there, self.mine.at[pl.ds(self.rows, self.quarter)]))
        return result

    def push(self, part, mask, axis, number):
        for i, there, own in self.pieces(part, mask, self.grid.c):
            remote(
                there if mask else own,
                there,
                self.sent.at[i, number],
                self.got.at[i, mask | 1 << axis],
                self.device(1 << axis, self.grid.c),
            ).start()

    def to_partner(self, part, mask):
        for i, there, own in self.pieces(part, mask, self.grid.c):
            remote(
                there if mask else own,
                there,
                self.sent_pair.at[i, mask],
                self.got_pair.at[i, mask],
                self.grid.partner,
            ).start()

    def arrived(self, part, mask):
        for i, there, _ in self.pieces(part, mask, self.grid.c):
            remote(there, there, self.sent.at[i, 0], self.got.at[i, mask], self.grid.partner).wait_recv()

    def swaps(self):
        return [
            remote(
                self.source.at[pl.ds(start, size)],
                self.taken.at[pl.ds(start, size)],
                self.swap_sent.at[i],
                self.swap_got.at[i],
                self.pair,
            )
            for i, (start, size) in enumerate(self.cuts)
        ]

    def quarters(self):
        return [
            remote(
                self.source.at[pl.ds(q * self.quarter, self.quarter)],
                self.mine.at[pl.ds(self.rows, self.quarter)],
                self.swap_sent.at[q],
                self.swap_got.at[3],
                (q, self.grid.narrow),
            )
            for q in range(LANE_WIDE)
        ]

    def begin(self):
        @pl.when(self.paired)
        def _():
            for copy in self.swaps():
                copy.start()

        @pl.when(self.grid.wide == LANE_WIDE)
        def _():
            for copy in self.quarters():
                copy.start()

        pltpu.make_async_copy(self.source, self.own, self.local.at[4]).start()

        @pl.when(self.side == 1)
        def _():
            self.mine[pl.ds(self.rows, self.quarter), :] = jnp.zeros((self.quarter, self.mine.shape[1]), bf16)

    def stage_a(self):
        pltpu.make_async_copy(self.source, self.own, self.local.at[4]).wait()
        keep = self.plan.lane_of(self.grid.wide) == self.side
        for part in range(3):
            start, size = self.cuts[part]
            place = (pl.ds(start, size), slice(None))

            @pl.when(self.paired)
            def _():
                self.swaps()[part].wait_recv()
                self.mine[place] = jnp.where(keep, self.own[place], self.taken[place])

            @pl.when(jnp.logical_not(self.paired))
            def _():
                self.mine[place] = self.own[place]

            if part == 2:

                @pl.when(self.side == 0)
                def _():
                    self.quarters()[0].wait_recv()

            for number, axis in enumerate(self.order(part)):
                self.push(part, 0, axis, number)
            self.to_partner(part, 0)
            for i, there, own in self.pieces(part, 0, self.grid.c):
                pltpu.make_async_copy(own, there, self.local.at[i]).start()

    def stage_b(self):
        for part in range(3):
            a, b, c = self.order(part)
            self.arrived(part, 1 << a)
            self.push(part, 1 << a, b, 3)
            self.push(part, 1 << a, c, 4)
            self.to_partner(part, 1 << a)
            self.arrived(part, 1 << b)
            self.push(part, 1 << b, c, 5)
            self.to_partner(part, 1 << b)
        for part in range(3):
            a, b, c = self.order(part)
            self.arrived(part, 1 << a | 1 << b)
            self.push(part, 1 << a | 1 << b, c, 6)
            self.to_partner(part, 1 << a | 1 << b)

    def stage_c(self):
        for part in range(3):
            a, b, c = self.order(part)
            for mask in (1 << c, 1 << a | 1 << c, 1 << b | 1 << c, 7):
                self.arrived(part, mask)
                self.to_partner(part, mask)

    def finish(self):
        for part in range(3):
            for i, there, own in self.pieces(part, 0, self.grid.c):
                for number in range(7):
                    remote(own, there, self.sent.at[i, number], self.got.at[i, 0], self.grid.partner).wait_send()
                for mask in range(8):
                    remote(own, there, self.sent_pair.at[i, mask], self.got.at[i, 0], self.grid.partner).wait_send()
                pltpu.make_async_copy(own, there, self.local.at[i]).wait()
            for mask in range(8):
                for i, there, _ in self.pieces(part, mask, 1 - self.grid.c):
                    remote(there, there, self.sent.at[i, 0], self.got_pair.at[i, mask], self.grid.partner).wait_recv()

        @pl.when(self.paired)
        def _():
            for copy in self.swaps():
                copy.wait_send()

        @pl.when(self.grid.wide == LANE_WIDE)
        def _():
            for copy in self.quarters():
                copy.wait_send()

    def middle(self):
        self.stage_a()
        self.stage_b()
        self.stage_c()

    def index(self, turn):
        start = lax.rem(self.plan.start + turn, self.plan.long)
        return jnp.where(self.plan.lane == 0, start, jnp.minimum(turn + 1, LANE_WIDE - 1))


class SpanGather(Gather):
    def __init__(self, grid, plan, source, whole, refs):
        super().__init__(grid, source, whole, refs[1:5])
        self.plan, self.own, self.local = plan, refs[0], refs[5]

    @classmethod
    def scratch(cls, rows, cols):
        return [pltpu.VMEM((rows, cols), bf16)] + Gather.scratch() + [pltpu.SemaphoreType.DMA((1,))]

    @staticmethod
    def shape(rows, cols):
        return (lax.axis_size("wide"), lax.axis_size("narrow"), rows, cols)

    def own_copies(self):
        there = self.whole.at[self.grid.wide, self.grid.narrow]
        return (
            pltpu.make_async_copy(self.source, self.own, self.local.at[0]),
            pltpu.make_async_copy(self.own, there, self.local.at[0]),
        )

    def begin(self):
        super().begin()
        self.own_copies()[0].start()

    def stage_a(self):
        self.own_copies()[0].wait()
        self.own_copies()[1].start()
        for number in range(1, self.grid.zs):
            self.along_z(number)
        self.across(0)

    def stage_b(self):
        for number in range(1, self.grid.zs):
            self.across(number)
        self.last(0)

    def stage_c(self):
        for number in range(1, self.grid.zs):
            self.last(number)

    def finish(self):
        super().finish()
        self.own_copies()[1].wait()

    def middle(self):
        self.stage_a()
        self.stage_b()
        self.stage_c()

    def index(self, turn):
        return self.plan.span(turn)


def lane_gather():
    return LaneGather if paired_lanes() else SpanGather


def rows_to_lanes(rows, lengths, chunks, pick, tile, ident):
    wide, narrow = lax.axis_size("wide"), lax.axis_size("narrow")
    devices = wide * narrow
    kind = lane_gather()

    def kernel(rows_ref, lengths_ref, chunks_ref, tile_ref, rows_out, chunks_out, tile_out, *refs):
        hold_chunk, hold_tile, local_sem, send, recv = refs[:5]
        g = Grid()
        me = g.wide * narrow + g.narrow
        wait_all = g.greet_all()
        own = [
            (chunks_ref.at[pick(g.wide, g.narrow)], hold_chunk, chunks_out.at[me]),
            (tile_ref, hold_tile, tile_out.at[me]),
        ]
        into = [pltpu.make_async_copy(a, b, local_sem.at[i]) for i, (a, b, _) in enumerate(own)]
        back = [pltpu.make_async_copy(b, c, local_sem.at[i]) for i, (_, b, c) in enumerate(own)]
        for copy in into:
            copy.start()
        wait_all()
        gather = kind(g, Plan(lengths_ref, None, lengths.shape[0]), rows_ref, rows_out, refs[5:])
        gather.begin()

        def send_chunks(step, carry):
            target = lax.rem(me + step, devices)
            where = lax.div(target, narrow), lax.rem(target, narrow)
            remote(chunks_ref.at[pick(*where)], chunks_out.at[me], send.at[0], recv.at[0], where).start()
            remote(tile_ref, tile_out.at[me], send.at[1], recv.at[1], where).start()
            return carry

        lax.fori_loop(1, devices, send_chunks, 0)
        for copy in into:
            copy.wait()
        for copy in back:
            copy.start()
        gather.middle()
        for copy in back:
            copy.wait()
        for i, out in enumerate((chunks_out, tile_out)):
            others = out.at[pl.ds(0, devices - 1)]
            whole = remote(others, others, send.at[i], recv.at[i], g.partner)
            whole.wait_send()
            whole.wait_recv()
        gather.finish()

    return pl.pallas_call(
        kernel,
        out_shape=[
            jax.ShapeDtypeStruct(kind.shape(*rows.shape), rows.dtype),
            jax.ShapeDtypeStruct((devices,) + chunks.shape[1:], chunks.dtype),
            jax.ShapeDtypeStruct((devices,) + tile.shape, tile.dtype),
        ],
        in_specs=[ANY, pl.BlockSpec(memory_space=pltpu.SMEM), ANY, ANY],
        out_specs=[ANY] * 3,
        scratch_shapes=[
            pltpu.VMEM(chunks.shape[1:], chunks.dtype),
            pltpu.VMEM(tile.shape, tile.dtype),
            pltpu.SemaphoreType.DMA((2,)),
            pltpu.SemaphoreType.DMA((2,)),
            pltpu.SemaphoreType.DMA((2,)),
        ]
        + kind.scratch(*rows.shape),
        compiler_params=pltpu.CompilerParams(collective_id=ident, has_side_effects=True),
        name="rows_to_lanes",
    )(rows, lengths, chunks, tile)


def matmul(left_side, right_side):
    return jnp.dot(left_side, right_side, preferred_element_type=jnp.float32)


def inner_left(left_side, right_side):
    return lax.dot_general(left_side, right_side, (((0,), (0,)), ((), ())), preferred_element_type=jnp.float32)


def inner_right(left_side, right_side):
    return lax.dot_general(left_side, right_side, (((1,), (1,)), ((), ())), preferred_element_type=jnp.float32)


def silu_slope(values):
    sigmoid_val = jax.nn.sigmoid(values)
    return sigmoid_val * (1.0 + values * (1.0 - sigmoid_val))


def silu_curve(values):
    sigmoid_val = jax.nn.sigmoid(values)
    return sigmoid_val * (1.0 - sigmoid_val) * (2.0 + values * (1.0 - 2.0 * sigmoid_val))


class Lane:
    def __init__(self):
        narrow = lax.axis_size("narrow")
        self.ys = narrow // 2
        self.chips = LANE_WIDE * self.ys
        wide_pos, narrow_pos = lax.axis_index("wide"), lax.axis_index("narrow")
        self.base = lax.div(wide_pos, LANE_WIDE) * LANE_WIDE
        self.colour = lax.rem(narrow_pos, 2)
        self.chip = lax.rem(wide_pos, LANE_WIDE) * self.ys + lax.div(narrow_pos, 2)
        self.partner = (wide_pos, narrow_pos + 1 - 2 * self.colour)

    def other(self, step):
        return lax.rem(self.chip + step, self.chips)

    def device(self, chip):
        return self.base + lax.div(chip, self.ys), 2 * lax.rem(chip, self.ys) + self.colour

    def greet(self):
        barrier = pltpu.get_barrier_semaphore()
        for step in range(1, self.chips):
            pl.semaphore_signal(barrier, inc=1, device_id=self.device(self.other(step)), device_id_type=MESH)
        pl.semaphore_signal(barrier, inc=1, device_id=self.partner, device_id_type=MESH)
        pl.semaphore_wait(barrier, self.chips)


class Scatter:
    def __init__(self, lane, part, pair, half, got, sems):
        self.lane, self.part, self.pair, self.half, self.got = lane, part, pair, half, got
        self.pair_send, self.pair_recv, self.send, self.recv = sems

    @staticmethod
    def scratch(chips, rows, width):
        return [
            pltpu.VMEM((2, chips, rows, width), bf16),
            pltpu.VMEM((chips, rows, width), bf16),
            pltpu.VMEM((chips, rows, width), bf16),
            pltpu.VMEM((chips, rows, width), bf16),
            pltpu.SemaphoreType.DMA((1,)),
            pltpu.SemaphoreType.DMA((1,)),
            pltpu.SemaphoreType.DMA((chips,)),
            pltpu.SemaphoreType.DMA((chips,)),
        ]

    @classmethod
    def of(cls, lane, refs):
        return cls(lane, *refs[:4], refs[4:8])

    def pair_copy(self):
        return remote(
            self.part.at[1 - self.lane.colour],
            self.pair,
            self.pair_send.at[0],
            self.pair_recv.at[0],
            self.lane.partner,
        )

    def start_pair(self):
        self.pair_copy().start()

    def take_pair(self):
        self.pair_copy().wait()
        self.half[...] = (
            self.part[self.lane.colour].astype(f32) + self.pair[...].astype(f32)
        ).astype(bf16)
        self.got[self.lane.chip] = self.half[self.lane.chip]

    def copy_to(self, step):
        chip = self.lane.other(step)
        return remote(
            self.half.at[chip],
            self.got.at[self.lane.chip],
            self.send.at[step],
            self.recv.at[self.lane.chip],
            self.lane.device(chip),
        )

    def start_sends(self):
        for step in range(1, self.lane.chips):
            self.copy_to(step).start()

    def total(self):
        result = self.got[self.lane.chip].astype(f32)
        for step in range(1, self.lane.chips):
            chip = self.lane.other(step)
            remote(
                self.got.at[chip], self.got.at[chip], self.send.at[step], self.recv.at[chip], self.lane.device(chip)
            ).wait_recv()
            result = result + self.got[chip].astype(f32)
        return result

    def wait_sends(self):
        for step in range(1, self.lane.chips):
            self.copy_to(step).wait_send()


class Spread:
    def __init__(self, lane, whole, sems):
        self.lane, self.whole = lane, whole
        self.send, self.recv, self.pair_send, self.pair_recv = sems

    @staticmethod
    def scratch(chips, rows, width):
        return [pltpu.VMEM((2, chips, rows, width), bf16)] + [pltpu.SemaphoreType.DMA((chips,))] * 4

    @classmethod
    def of(cls, lane, refs):
        return cls(lane, refs[0], refs[1:5])

    def mine(self):
        return self.whole.at[self.lane.colour, self.lane.chip]

    def copy_to(self, step):
        return remote(
            self.mine(),
            self.mine(),
            self.send.at[step],
            self.recv.at[self.lane.chip],
            self.lane.device(self.lane.other(step)),
        )

    def pair_copy(self, chip, colour):
        place = self.whole.at[colour, chip]
        return remote(place, place, self.pair_send.at[chip], self.pair_recv.at[chip], self.lane.partner)

    def run(self):
        lane = self.lane
        for step in range(1, lane.chips):
            self.copy_to(step).start()
        self.pair_copy(lane.chip, lane.colour).start()
        for step in range(1, lane.chips):
            chip = lane.other(step)
            place = self.whole.at[lane.colour, chip]
            remote(place, place, self.send.at[step], self.recv.at[chip], lane.device(chip)).wait_recv()
            self.pair_copy(chip, lane.colour).start()
        for chip in range(lane.chips):
            self.pair_copy(chip, 1 - lane.colour).wait_recv()
        for step in range(1, lane.chips):
            self.copy_to(step).wait_send()
        for chip in range(lane.chips):
            self.pair_copy(chip, lane.colour).wait_send()


class Deliver:
    def __init__(self, grid, plan, chips, out, got, sems):
        self.grid, self.plan, self.chips, self.out, self.got = grid, plan, chips, out, got
        self.send, self.recv = sems
        self.wide, self.narrow = lax.axis_size("wide"), lax.axis_size("narrow")
        self.me = grid.wide * self.narrow + grid.narrow

    @staticmethod
    def scratch(kinds, rows, block):
        devices = lax.axis_size("wide") * lax.axis_size("narrow")
        return [pltpu.VMEM((devices, kinds, rows, block), bf16)] * 2 + [pltpu.SemaphoreType.DMA((1,))] * 2

    def start(self, kinds):
        block = self.out.shape[3]
        for span in range(self.wide):
            turn = self.plan.turn_of(span)
            for i, kind in enumerate(kinds):
                lane_rows = kind[turn]
                for n in range(self.narrow):
                    self.out[span * self.narrow + n, i] = lane_rows[:, n * block : (n + 1) * block]

        def push(step, carry):
            target = lax.rem(self.me + step, self.wide * self.narrow)
            where = lax.div(target, self.narrow), lax.rem(target, self.narrow)
            remote(self.out.at[target], self.got.at[self.me], self.send.at[0], self.recv.at[0], where).start()
            return carry

        lax.fori_loop(1, self.wide * self.narrow, push, 0)
        self.got[self.me] = self.out[self.me]

    def finish(self, result):
        others = self.got.at[pl.ds(0, self.wide * self.narrow - 1)]
        whole = remote(others, others, self.send.at[0], self.recv.at[0], self.grid.partner)
        whole.wait_send()
        whole.wait_recv()
        base = self.plan.lane_of(self.grid.wide) * LANE_WIDE
        ys = self.narrow // 2
        for p in range(LANE_WIDE):
            for y in range(ys):
                for colour in range(2):
                    source = (base + p) * self.narrow + 2 * y + colour
                    for i in range(result.shape[0]):
                        result[i, colour, p * ys + y] = self.got[source, i]


def chain_forward(keys, values, queries, lengths, gates, turns, first_init, second_init, ident):
    wide = lax.axis_size("wide")
    blocks, span, block = keys.shape[1:]
    width, hidden = first_init.shape
    rows = values.shape[1]
    sequences = lengths.shape[0]
    key_turns = turns - 1
    kind = lane_gather()
    own_rows = kind.scratch(span, block)
    per_turn, ask_from = (2, 2) if paired_lanes() else (1, 3)
    first_left = per_turn * (key_turns - ask_from)
    slots = 3
    stream_keys = not paired_lanes()
    chips = LANE_WIDE * (lax.axis_size("narrow") // 2)
    n_scatter = len(Scatter.scratch(1, 8, 128))

    def kernel(*refs):
        keys_hbm, values_hbm, own_hbm, lengths_ref, gates_ref, first_hbm, second_hbm = refs[:7]
        recalled_hbm, low1_hbm, low2_hbm, m1_hbm, m2_hbm, g1_hbm, g2_hbm = refs[7:14]
        err_hbm, pre_hbm, qpre_hbm, klane_hbm, qlane_hbm = refs[14:19]
        rest = refs[19:]
        kall, qall, vall, kcur, qcur, i1, i2, s1, s2, m1, m2, low1, low2, mb1, mb2, gb1, gb2 = rest[:17]
        pre, qpre, khid, rec, qpart, qpair, qhalf, qgot = rest[17:25]
        in_sem, out_sem, q_sem, q_pair_send, q_pair_recv, q_send, q_recv = rest[25:32]
        rest = rest[32:]
        lane = Lane()
        grid = Grid()
        plan = Plan(lengths_ref, gates_ref, sequences)
        lookup = Scatter.of(lane, rest[:n_scatter])
        error = Spread.of(lane, rest[n_scatter : n_scatter + 5])
        rest = rest[n_scatter + 5 :]
        gather = kind(grid, plan, own_hbm, qall, rest[: len(own_rows)])
        rest = rest[len(own_rows) :]
        deliver = Deliver(grid, plan, chips, *rest[:2], rest[2:4])
        result = rest[4]

        def recall(q, slot):
            sems = q_pair_send.at[pl.ds(q, 1)], q_pair_recv.at[pl.ds(q, 1)], q_send.at[q], q_recv.at[q]
            return Scatter(lane, qpart.at[slot], qpair.at[q], qhalf.at[slot], qgot.at[q], sems)

        def state_saves(turn):
            return [
                pltpu.make_async_copy(source, target.at[turn], out_sem.at[i])
                for i, (source, target) in enumerate(((mb1, m1_hbm), (mb2, m2_hbm), (kcur, klane_hbm)))
            ]

        def other_saves(turn):
            return [
                pltpu.make_async_copy(source, target.at[turn], out_sem.at[3 + i])
                for i, (source, target) in enumerate(
                    ((gb1, g1_hbm), (gb2, g2_hbm), (error.whole, err_hbm), (pre, pre_hbm))
                )
            ]

        def query_saves(q, slot):
            return [
                pltpu.make_async_copy(source.at[slot], target.at[q], q_sem.at[slot, i])
                for i, (source, target) in enumerate(((qcur, qlane_hbm), (qpre, qpre_hbm)))
            ]

        inputs = [
            pltpu.make_async_copy(source, target, in_sem.at[i])
            for i, (source, target) in enumerate(
                ((first_hbm, i1), (second_hbm, i2), (keys_hbm, kall), (values_hbm, vall))
            )
            if not (stream_keys and i == 2)
        ]
        for copy in inputs:
            copy.start()
        grid.greet_all()()
        gather.begin()
        for copy in inputs:
            copy.wait()
        low1[0] = i1[...]
        low2[0] = i2[...]
        s1[...] = i1[...].astype(f32)
        s2[...] = i2[...].astype(f32)
        for ref in (m1, m2, mb1, mb2):
            ref[...] = jnp.zeros_like(ref)

        def lookup_blocks(buf, first):
            total = matmul(buf[0], first[pl.ds(0, block), :])
            for b in range(1, blocks):
                total = total + matmul(buf[b], first[pl.ds(b * block, block), :])
            return total

        def ask(q, slot, waits):
            def settle():
                recall(q - slots, slot).wait_sends()
                for copy in query_saves(q - slots, slot):
                    copy.wait()

            if waits is True:
                settle()
            elif waits is not False:
                pl.when(waits)(settle)
            index = gather.index(q)
            for b in range(blocks):
                qcur[slot, b] = qall[index, b]
            query_pre = lookup_blocks(qcur.at[slot], low1.at[q])
            qpre[slot] = query_pre
            for copy in query_saves(q, slot):
                copy.start()
            query_hidden = (query_pre * jax.nn.sigmoid(query_pre)).astype(bf16)
            qpart[slot] = matmul(query_hidden, low2[q]).astype(bf16).reshape(2, chips, rows, width)
            recall(q, slot).start_pair()

        def turn_body(turn, carry):
            index = plan.span(turn)
            if stream_keys:
                one = pltpu.make_async_copy(keys_hbm.at[turn], kcur, in_sem.at[2])
                one.start()
                one.wait()
            else:
                for b in range(blocks):
                    kcur[b] = kall[gather.index(turn), b]
            for copy in state_saves(turn):
                copy.start()
            key_pre = lookup_blocks(kcur, low1.at[turn])
            pre[0] = key_pre
            khid[...] = (key_pre * jax.nn.sigmoid(key_pre)).astype(bf16)
            lookup.part[...] = matmul(khid[...], low2[turn]).astype(bf16).reshape(2, chips, rows, width)
            lookup.start_pair()

            @pl.when(turn == ask_from)
            def _():
                gather.finish()

            first = per_turn * (turn - ask_from)

            @pl.when(turn >= ask_from)
            def _():
                ask(first, lax.rem(first, slots), first >= slots)

            lookup.take_pair()
            lookup.start_sends()

            @pl.when(turn >= ask_from)
            def _():
                recall(first, lax.rem(first, slots)).take_pair()
                for j in range(1, per_turn):
                    ask(first + j, lax.rem(first + j, slots), first + j >= slots)

            if paired_lanes():
                pl.when(turn == 1)(gather.stage_b)

            total = lookup.total()
            target = jnp.concatenate([vall[index * blocks + b] for b in range(blocks)], axis=1)
            error.whole[lane.colour, lane.chip] = ((total - target.astype(f32)) / span).astype(bf16)
            error.run()
            lookup.wait_sends()

            @pl.when(turn >= ask_from)
            def _():
                recall(first, lax.rem(first, slots)).start_sends()
                for j in range(1, per_turn):
                    stream = recall(first + j, lax.rem(first + j, slots))
                    stream.take_pair()
                    stream.start_sends()

            if paired_lanes():
                pl.when(turn == 0)(gather.stage_a)
                pl.when(turn == 1)(gather.stage_c)

            err = error.whole[...].reshape(span, width)
            grad_second = inner_left(khid[...], err)
            hidden_grad = inner_right(err, low2[turn])
            pre[1] = hidden_grad
            slope = (hidden_grad * silu_slope(pre[0])).astype(bf16)
            decay, moment, rate = plan.rates(turn)
            reset = plan.first(turn + 1)
            for copy in state_saves(turn):
                copy.wait()
            following = jnp.minimum(turn + 1, turns - 1)

            def update(s, m, mb, init, low, grad, place):
                moment_new = moment * m[place] - rate * grad
                state_new = (1.0 - decay) * s[place] + moment_new
                state_new = reset * init[place].astype(f32) + (1.0 - reset) * state_new
                moment_new = (1.0 - reset) * moment_new
                m[place] = moment_new
                mb[place] = moment_new.astype(bf16)
                s[place] = state_new
                low[(following,) + place] = state_new.astype(bf16)

            gb2[...] = grad_second.astype(bf16)
            update(s2, m2, mb2, i2, low2, grad_second, (slice(None), slice(None)))
            for b in range(blocks):
                grad_first = inner_left(kcur[b], slope)
                place = (pl.ds(b * block, block), slice(None))
                gb1[place] = grad_first.astype(bf16)
                update(s1, m1, mb1, i1, low1, grad_first, place)
            saves = other_saves(turn)
            for copy in saves:
                copy.start()

            if not paired_lanes():
                pl.when(turn == 0)(gather.stage_a)
                pl.when(turn == 1)(gather.stage_b)
                pl.when(turn == 2)(gather.stage_c)

            for copy in saves:
                copy.wait()
            return carry

        lax.fori_loop(0, key_turns, turn_body, 0)
        ends = [
            pltpu.make_async_copy(low1, low1_hbm, out_sem.at[0]),
            pltpu.make_async_copy(low2, low2_hbm, out_sem.at[1]),
        ]
        for copy in ends:
            copy.start()
        left = list(range(first_left, turns))
        for q in left:
            ask(q, q % slots, q >= slots)
            if q > left[0]:
                stream = recall(q - 1, (q - 1) % slots)
                stream.take_pair()
                stream.start_sends()
        stream = recall(turns - 1, (turns - 1) % slots)
        stream.take_pair()
        stream.start_sends()
        for q in range(turns):
            rec[q] = recall(q, q % slots).total().astype(bf16)
        deliver.start([rec])
        for q in range(turns - slots, turns):
            recall(q, q % slots).wait_sends()
        for q in range(turns - slots, turns):
            for copy in query_saves(q, q % slots):
                copy.wait()
        deliver.finish(result)
        last = pltpu.make_async_copy(result.at[0], recalled_hbm, out_sem.at[2])
        last.start()
        for copy in ends + [last]:
            copy.wait()

    state = [(width, hidden), (hidden, width)]
    out_shape = (
        [jax.ShapeDtypeStruct((2, chips, rows, block), bf16)]
        + [jax.ShapeDtypeStruct((turns,) + s, bf16) for s in state]
        + [jax.ShapeDtypeStruct((key_turns,) + s, bf16) for s in state * 2]
        + [
            jax.ShapeDtypeStruct((key_turns, 2, chips, rows, width), bf16),
            jax.ShapeDtypeStruct((key_turns, 2, span, hidden), f32),
            jax.ShapeDtypeStruct((turns, span, hidden), f32),
            jax.ShapeDtypeStruct((key_turns, blocks, span, block), bf16),
            jax.ShapeDtypeStruct((turns, blocks, span, block), bf16),
        ]
    )
    sem = pltpu.SemaphoreType.DMA
    scratch = (
        [pltpu.VMEM((1 if stream_keys else keys.shape[0], blocks, span, block), bf16), pltpu.VMEM(kind.shape(span, block), bf16)]
        + [pltpu.VMEM(values.shape, bf16)]
        + [pltpu.VMEM((blocks, span, block), bf16), pltpu.VMEM((slots, blocks, span, block), bf16)]
        + [pltpu.VMEM(s, bf16) for s in state]
        + [pltpu.VMEM(s, f32) for s in state * 2]
        + [pltpu.VMEM((turns,) + s, bf16) for s in state]
        + [pltpu.VMEM(s, bf16) for s in state * 2]
        + [
            pltpu.VMEM((2, span, hidden), f32),
            pltpu.VMEM((slots, span, hidden), f32),
            pltpu.VMEM((span, hidden), bf16),
            pltpu.VMEM((turns, rows, width), bf16),
            pltpu.VMEM((slots, 2, chips, rows, width), bf16),
        ]
        + [pltpu.VMEM((n, chips, rows, width), bf16) for n in (turns, slots, turns)]
        + [sem((4,)), sem((7,)), sem((slots, 2)), sem((turns,)), sem((turns,)), sem((turns, chips)), sem((turns, chips))]
        + Scatter.scratch(chips, rows, width)
        + Spread.scratch(chips, rows, width)
        + own_rows
        + Deliver.scratch(1, rows, block)
        + [pltpu.VMEM((1, 2, chips, rows, block), bf16)]
    )
    smem = pl.BlockSpec(memory_space=pltpu.SMEM)
    return pl.pallas_call(
        kernel,
        out_shape=out_shape,
        in_specs=[ANY] * 3 + [smem] * 2 + [ANY] * 2,
        out_specs=[ANY] * len(out_shape),
        scratch_shapes=scratch,
        compiler_params=pltpu.CompilerParams(
            collective_id=ident, has_side_effects=True, vmem_limit_bytes=62 * 1024 * 1024
        ),
        cost_estimate=pl.CostEstimate(
            flops=40 * turns * 2 * span * width * hidden, bytes_accessed=turns * 40 * 2**20, transcendentals=0
        ),
        name="chain_forward",
    )(keys, values, queries, lengths, gates, first_init, second_init)


def chain_backward(recall_grad, saved, lengths, gates, ident):
    low1_all, low2_all, m1_all, m2_all, g1_all, g2_all, err_all, pre_all, qpre_all, keys, queries = saved
    wide = lax.axis_size("wide")
    devices = wide * lax.axis_size("narrow")
    key_turns, blocks, span, block = keys.shape
    turns = key_turns + 1
    width, hidden = low1_all.shape[1:]
    chips, rows = err_all.shape[2:4]
    n_scatter = len(Scatter.scratch(1, 8, 128))
    kind = lane_gather()
    own_rows = kind.scratch(span, block)

    def kernel(*refs):
        own_hbm, q_ins, k_ins, lengths_ref, gates_ref = refs[0], refs[1:5], refs[5:12], refs[12], refs[13]
        cots_hbm, sums_out, mg1_hbm, mg2_hbm = refs[14:18]
        rest = refs[18:]
        q_bufs, k_bufs, rest = rest[:4], rest[4:11], rest[11:]
        qbuf, low1, low2, qpre = q_bufs
        kbuf, m1, m2, g1, g2, errs, pre = k_bufs
        rall, cf, cs, cmf, cms, w1, w2, a1, a2, c1, c2 = rest[:11]
        dh, khid, qpl, qhid, kpl, slow, sg, hk, qcots, kcots, vcots, sumrows, tile, mb1, mb2, result = rest[11:27]
        q_sem, k_sem, end_sem, tile_send, tile_recv = rest[27:32]
        rest = rest[32:]
        lane = Lane()
        grid = Grid()
        plan = Plan(lengths_ref, gates_ref, lengths.shape[0])
        lookup = Scatter.of(lane, rest[:n_scatter])
        qstream = Scatter.of(lane, rest[n_scatter : 2 * n_scatter])
        kstream = Scatter.of(lane, rest[2 * n_scatter : 3 * n_scatter])
        spread = Spread.of(lane, rest[3 * n_scatter : 3 * n_scatter + 5])
        rest = rest[3 * n_scatter + 5 :]
        gather = kind(grid, plan, own_hbm, rall, rest[: len(own_rows)])
        rest = rest[len(own_rows) :]
        deliver = Deliver(grid, plan, chips, *rest[:2], rest[2:4])

        def q_loads(turn, slot):
            return [
                pltpu.make_async_copy(source.at[turn], target.at[slot], q_sem.at[slot, i])
                for i, (source, target) in enumerate(zip(q_ins, q_bufs))
            ]

        def k_loads(turn, slot):
            return [
                pltpu.make_async_copy(source.at[turn], target.at[slot], k_sem.at[slot, i])
                for i, (source, target) in enumerate(zip(k_ins, k_bufs))
            ]

        grid.greet_all()()
        gather.begin()
        for copy in q_loads(turns - 1, 0) + q_loads(turns - 2, 1) + k_loads(turns - 2, 1):
            copy.start()
        for ref in (cf, cs, cmf, cms, a1, a2):
            ref[...] = jnp.zeros_like(ref)
        gather.middle()
        gather.finish()

        kcots[turns - 1] = jnp.zeros((rows, width), bf16)
        vcots[turns - 1] = jnp.zeros((rows, width), bf16)
        sumrows[turns - 1] = jnp.zeros((8, 128), f32)

        def finish(stream, save, turn):
            save[turn] = stream.total().astype(bf16)
            stream.wait_sends()

        def query_rows(turn, slot):
            index = gather.index(turn)
            back = inner_right(rall[index, 0], low2[slot, :, pl.ds(0, block)])
            for b in range(1, blocks):
                back = back + inner_right(rall[index, b], low2[slot, :, pl.ds(b * block, block)])
            query_pre = qpre[slot]
            qpl[...] = (plan.valid(turn) * back * silu_slope(query_pre)).astype(bf16)
            qhid[...] = (query_pre * jax.nn.sigmoid(query_pre)).astype(bf16)
            qstream.part[...] = inner_right(qpl[...], low1[slot]).astype(bf16).reshape(2, chips, rows, width)
            qstream.start_pair()

        def query_weights(turn, slot):
            index = gather.index(turn)
            valid = plan.valid(turn)
            for b in range(blocks):
                w1[pl.ds(b * block, block), :] = inner_left(qbuf[slot, b], qpl[...])
                w2[:, pl.ds(b * block, block)] = valid * inner_left(qhid[...], rall[index, b])

        def key_rows(slot):
            kstream.part[...] = (
                (inner_right(kpl[...], low1[slot]) + inner_right(slow[...], c1[slot]))
                .astype(bf16)
                .reshape(2, chips, rows, width)
            )

        for copy in q_loads(turns - 1, 0):
            copy.wait()
        query_rows(turns - 1, 0)
        query_weights(turns - 1, 0)
        reset = plan.first(turns - 1)
        for c, w, acc in ((cf, w1, a1), (cs, w2, a2)):
            acc[...] = reset * w[...]
            c[...] = (1.0 - reset) * w[...]
        qstream.take_pair()
        qstream.start_sends()

        def body(step, carry):
            turn = turns - 1 - step
            slot = lax.rem(step, 2)
            decay, moment, rate = plan.rates(turn)
            reset = plan.first(turn)
            for copy in q_loads(turn, slot) + k_loads(turn, slot):
                copy.wait()
            c1[slot] = (-rate * (cmf[...] + cf[...])).astype(bf16)
            c2[...] = (-rate * (cms[...] + cs[...])).astype(bf16)
            slope_grad = matmul(kbuf[slot, 0], c1[slot, pl.ds(0, block), :])
            for b in range(1, blocks):
                slope_grad = slope_grad + matmul(kbuf[slot, b], c1[slot, pl.ds(b * block, block), :])
            sg[...] = slope_grad
            key_pre = pre[slot, 0]
            khid[...] = (key_pre * jax.nn.sigmoid(key_pre)).astype(bf16)
            dh[...] = (slope_grad * silu_slope(key_pre)).astype(bf16)
            lookup.part[...] = (
                (matmul(khid[...], c2[...]) + matmul(dh[...], low2[slot])).astype(bf16).reshape(2, chips, rows, width)
            )
            lookup.start_pair()
            finish(qstream, qcots, turn + 1)

            @pl.when(step > 2)
            def _():
                finish(kstream, kcots, turn + 2)

            lookup.take_pair()
            lookup.start_sends()
            query_rows(turn, slot)

            @pl.when(step > 1)
            def _():
                key_rows(1 - slot)
                kstream.start_pair()

            @pl.when(step + 1 < turns)
            def _():
                for copy in q_loads(turn - 1, 1 - slot) + k_loads(turn - 1, 1 - slot):
                    copy.start()

            query_weights(turn, slot)
            err = errs[slot].reshape(span, width)
            hk[...] = inner_right(err, c2[...])
            w2[...] += inner_left(dh[...], err)

            def whole_sum(first_a, first_b, second_a, second_b):
                first = jnp.sum(first_a * first_b.astype(f32), axis=0, keepdims=True)
                second = jnp.sum(second_a * second_b.astype(f32), axis=0, keepdims=True)
                return jnp.sum(first, axis=1, keepdims=True) + jnp.sum(second, axis=1, keepdims=True)

            kinds = (
                whole_sum(cf[...], low1[slot], cs[...], low2[slot]),
                whole_sum(cmf[...] + cf[...], m1[slot], cms[...] + cs[...], m2[slot]),
                whole_sum(cmf[...] + cf[...], g1[slot], cms[...] + cs[...], g2[slot]),
            )
            column = lax.broadcasted_iota(jnp.int32, (8, 128), 1)
            sumrow = jnp.zeros((8, 128), f32)
            for i, kind in enumerate(kinds):
                sumrow = jnp.where(column == i, kind, sumrow)
            sumrows[turn] = sumrow
            qstream.take_pair()
            total = lookup.total()
            mine = (total / span).astype(bf16)
            spread.whole[lane.colour, lane.chip] = mine
            vcots[turn] = mine
            spread.run()
            lookup.wait_sends()
            qstream.start_sends()

            @pl.when(step > 1)
            def _():
                kstream.take_pair()
                kstream.start_sends()

            out = spread.whole[...].reshape(span, width)
            hidden_back = hk[...] + inner_right(out, low2[slot])
            key_pre = pre[slot, 0]
            hidden_grad = pre[slot, 1]
            slope = silu_slope(key_pre)
            kpl[...] = (hidden_back * slope + sg[...] * hidden_grad * silu_curve(key_pre)).astype(bf16)
            slow[...] = (hidden_grad * slope).astype(bf16)

            def update(c, m, acc, grad_new, place):
                grad = (1.0 - decay) * c[place] + grad_new
                both = m[place] + c[place]
                acc[place] += reset * grad
                c[place] = (1.0 - reset) * grad
                m[place] = (1.0 - reset) * (moment * both)

            for b in range(blocks):
                place = (pl.ds(b * block, block), slice(None))
                update(cf, cmf, a1, w1[place] + inner_left(kbuf[slot, b], kpl[...]), place)
            place = (slice(None), slice(None))
            update(cs, cms, a2, w2[...] + inner_left(khid[...], out), place)
            return carry

        lax.fori_loop(1, turns, body, 0)
        tail = Scatter(
            lane,
            kstream.part,
            lookup.pair,
            lookup.half,
            lookup.got,
            (lookup.pair_send, lookup.pair_recv, lookup.send, lookup.recv),
        )
        key_rows((turns - 1) % 2)
        tail.start_pair()
        mb1[...] = a1[...].astype(bf16).reshape(mb1.shape)
        for owner in range(wide):
            mb2[owner] = a2[:, owner * (width // wide) : (owner + 1) * (width // wide)].astype(bf16)
        ends = [
            pltpu.make_async_copy(mb1, mg1_hbm, end_sem.at[0]),
            pltpu.make_async_copy(mb2, mg2_hbm, end_sem.at[1]),
        ]
        for copy in ends:
            copy.start()
        for span_number in range(wide):
            here = jnp.where(plan.lane_of(span_number) == plan.lane, 1.0, 0.0)
            tile[pl.ds(span_number, 1), :] = here * sumrows[plan.turn_of(span_number)][:1]

        def send_tile(step, carry):
            target = lax.rem(deliver.me + step, devices)
            where = lax.div(target, blocks), lax.rem(target, blocks)
            remote(tile, sums_out.at[deliver.me], tile_send.at[0], tile_recv.at[0], where).start()
            return carry

        lax.fori_loop(1, devices, send_tile, 0)
        sums_out[deliver.me] = tile[...]
        finish(qstream, qcots, 0)
        if turns > 2:
            finish(kstream, kcots, 1)
        tail.take_pair()
        tail.start_sends()
        finish(tail, kcots, 0)
        deliver.start([qcots, kcots, vcots])
        others = sums_out.at[pl.ds(0, devices - 1)]
        tiles = remote(others, others, tile_send.at[0], tile_recv.at[0], grid.partner)
        tiles.wait_send()
        tiles.wait_recv()
        deliver.finish(result)
        ends.append(pltpu.make_async_copy(result, cots_hbm, end_sem.at[2]))
        ends[2].start()
        for copy in ends:
            copy.wait()

    state = [(width, hidden), (hidden, width)]
    q_buffers = [((blocks, span, block), bf16)] + [(s, bf16) for s in state] + [((span, hidden), f32)]
    k_buffers = (
        [((blocks, span, block), bf16)]
        + [(s, bf16) for s in state * 2]
        + [((2, chips, rows, width), bf16), ((2, span, hidden), f32)]
    )
    by_owner = [(wide, width // wide, hidden), (wide, hidden, width // wide)]
    out_shape = [
        jax.ShapeDtypeStruct((3, 2, chips, rows, block), bf16),
        jax.ShapeDtypeStruct((devices, wide, 128), f32),
    ] + [jax.ShapeDtypeStruct(s, bf16) for s in by_owner]
    sem = pltpu.SemaphoreType.DMA
    scratch = (
        [pltpu.VMEM((2,) + s, t) for s, t in q_buffers + k_buffers]
        + [pltpu.VMEM(kind.shape(span, block), bf16)]
        + [pltpu.VMEM(s, f32) for s in state * 4]
        + [pltpu.VMEM((2,) + state[0], bf16), pltpu.VMEM(state[1], bf16)]
        + [pltpu.VMEM((span, hidden), bf16)] * 6
        + [pltpu.VMEM((span, hidden), f32)] * 2
        + [pltpu.VMEM((turns, rows, width), bf16)] * 3
        + [pltpu.VMEM((turns, 8, 128), f32), pltpu.VMEM((wide, 128), f32)]
        + [pltpu.VMEM(s, bf16) for s in by_owner]
        + [pltpu.VMEM((3, 2, chips, rows, block), bf16)]
        + [sem((2, 4)), sem((2, 7)), sem((3,)), sem((1,)), sem((1,))]
        + Scatter.scratch(chips, rows, width) * 3
        + Spread.scratch(chips, rows, width)
        + own_rows
        + Deliver.scratch(3, rows, block)
    )
    vmem = pl.BlockSpec(memory_space=pltpu.VMEM)
    smem = pl.BlockSpec(memory_space=pltpu.SMEM)
    return pl.pallas_call(
        kernel,
        out_shape=out_shape,
        in_specs=[ANY] * 12 + [smem] * 2,
        out_specs=[ANY, vmem, ANY, ANY],
        scratch_shapes=scratch,
        compiler_params=pltpu.CompilerParams(
            collective_id=ident, has_side_effects=True, vmem_limit_bytes=62 * 1024 * 1024
        ),
        cost_estimate=pl.CostEstimate(
            flops=80 * turns * 2 * span * width * hidden, bytes_accessed=turns * 60 * 2**20, transcendentals=0
        ),
        name="chain_backward",
    )(
        recall_grad, queries, low1_all, low2_all, qpre_all, keys, m1_all, m2_all, g1_all, g2_all, err_all, pre_all,
        lengths, gates,
    )


def from_behind(value, axis, steps):
    count = lax.axis_size(axis)
    first, last = (max(0, -steps), min(count, count - steps))
    return lax.ppermute(value, axis, [(source, source + steps) for source in range(first, last)])


def split_heads(values, head_size):
    return values.reshape(values.shape[:-1] + (values.shape[-1] // head_size, head_size))


def head_norm(values, head_size):
    shaped = split_heads(values, head_size)
    factor = lax.rsqrt(jnp.sum(shaped * shaped, axis=-1, keepdims=True) + eps_head)
    return (shaped * factor).reshape(values.shape)


def head_norm_back(values, upstream, head_size):
    shaped = split_heads(values, head_size)
    grad_shaped = split_heads(upstream, head_size)
    factor = lax.rsqrt(jnp.sum(shaped * shaped, axis=-1, keepdims=True) + eps_head)
    normed = shaped * factor
    inner_sum = jnp.sum(normed * grad_shaped, axis=-1, keepdims=True)
    return (factor * (grad_shaped - normed * inner_sum)).reshape(values.shape)


def rms_back(scaled, factor, upstream):
    return factor * (upstream - scaled * jnp.mean(upstream * scaled, axis=-1, keepdims=True))


def body(
    tokens,
    cotangent,
    seq_spans,
    w_query,
    w_key,
    w_value,
    conv_kernel,
    persistent,
    norm_gain,
    rate_proj,
    out_gate,
    out_proj,
    memory_in,
    memory_out,
    ffn_gain,
    ffn_gate,
    ffn_up,
    ffn_down,
):
    wide, narrow = lax.axis_size("wide"), lax.axis_size("narrow")
    devices = wide * narrow
    wide_pos, narrow_pos = lax.axis_index("wide"), lax.axis_index("narrow")
    span, width = tokens.shape
    taps = conv_kernel.shape[0]
    persist_count = persistent.shape[1]
    local_width = out_gate.shape[1]
    own_rows = span // narrow
    lanes = wide // LANE_WIDE
    chips = LANE_WIDE * narrow // 2
    shards = 2 * chips
    shard_rows = span // shards
    hidden = memory_in.shape[1] // LANE_WIDE
    score_scale = math.sqrt(HEAD)

    def shard_of(tw, tn):
        return lax.rem(tn, 2) * chips + lax.rem(tw, LANE_WIDE) * (narrow // 2) + lax.div(tn, 2)

    long_turns = min(6, wide * 5 // 8)
    turns = max(long_turns, wide - long_turns)
    is_first = False
    start = 0
    for i in range(seq_spans.shape[0]):
        is_first = is_first | (wide_pos == start)
        start = start + seq_spans[i]

    smalls = [conv_kernel, persistent, norm_gain, ffn_gain, rate_proj]
    small_sizes = [a.size for a in smalls]
    packed = jnp.concatenate([a.reshape(-1) for a in smalls])
    padded = -(-packed.size // 2048) * 2048
    packed = jnp.pad(packed, (0, padded - packed.size)).reshape(-1, 128)
    own_weights = jnp.concatenate(
        [a.reshape(a.shape[0], narrow, local_width) for a in (w_query, w_key, w_value)], 2
    ).transpose(1, 0, 2)
    memory_cols = memory_in.reshape(memory_in.shape[0], LANE_WIDE, hidden).transpose(1, 0, 2)
    memory_rows = memory_out.reshape(LANE_WIDE, hidden, memory_out.shape[1])
    small_all, weights_all, first_all, second_all = send_parameters(
        packed, own_weights, [memory_cols, memory_rows], 1
    )
    first_init = first_all.reshape(width, hidden)
    second_init = second_all.transpose(1, 0, 2).reshape(hidden, width)
    small_all = small_all.reshape(devices, padded)
    pieces, at = [], 0
    for a, size in zip(smalls, small_sizes):
        pieces.append(small_all[:, at : at + size].reshape((devices,) + a.shape))
        at += size
    kernel_all = pieces[0].transpose(1, 0, 2).reshape(taps, 3, width)
    persist_all = pieces[1].transpose(1, 2, 0, 3).reshape(2, persist_count, width)
    gain_one = pieces[2].reshape(width).astype(f32)
    gain_two = pieces[3].reshape(width).astype(f32)
    rate_f = pieces[4].reshape(width, 3).astype(f32)
    col_offset = narrow_pos * local_width

    def own_cols(values, axis):
        return lax.dynamic_slice_in_dim(values, col_offset, local_width, axis)

    def own_part(values):
        return lax.dynamic_slice_in_dim(values, narrow_pos * own_rows, own_rows, 0)

    kernel_f = own_cols(kernel_all, 2).reshape(taps, 3 * local_width).astype(f32)
    persist_f = own_cols(persist_all, 2).astype(f32)
    qkv_weights = weights_all.reshape(width, 3 * local_width)

    inputs_f = tokens.astype(f32)
    first_factor = lax.rsqrt(jnp.mean(inputs_f * inputs_f, axis=-1, keepdims=True) + eps_norm)
    first_scaled = inputs_f * first_factor
    normed = first_scaled * gain_one
    normed_low = normed.astype(bf16)
    projected = matmul(normed_low, qkv_weights)
    tail_rows = from_behind(projected[span - taps + 1 :].astype(bf16), "wide", 1).astype(f32)
    extended = jnp.concatenate([jnp.where(is_first, 0.0, tail_rows), projected], 0)
    mixed_conv = kernel_f[0] * projected
    for offset in range(1, taps):
        start_row = taps - 1 - offset
        mixed_conv = mixed_conv + kernel_f[offset] * extended[start_row : start_row + span]
    activated = jax.nn.silu(mixed_conv)
    query_act = activated[:, :local_width]
    key_act = activated[:, local_width : 2 * local_width]
    query_low = head_norm(query_act, HEAD).astype(bf16)
    key_low = head_norm(key_act, HEAD).astype(bf16)
    value_low = activated[:, 2 * local_width :].astype(bf16)
    span_mean = jnp.mean(normed, axis=0)
    gate_scale = jnp.array([decay_top, moment_top, learn_top], f32)
    gate_sig = jax.nn.sigmoid(jnp.sum(span_mean[:, None] * rate_f, axis=0))
    gate_tile = jnp.broadcast_to(jnp.pad(gate_sig * gate_scale, (0, 125))[None], (8, 128))

    key_all, value_got, gate_got = rows_to_lanes(
        key_low, seq_spans, value_low.reshape(shards, shard_rows, local_width), shard_of, gate_tile, 2
    )
    later = (ffn_gate, ffn_up, ffn_down, jnp.concatenate([out_gate, out_proj.T], 1))
    key_all, *later = lax.optimization_barrier((key_all,) + later)
    out_weights = lax.all_gather(later[3], "wide", axis=0, tiled=True)
    ffn_gate_cols = lax.all_gather(later[0], "wide", axis=0, tiled=True)
    ffn_up_cols = lax.all_gather(later[1], "wide", axis=0, tiled=True)
    ffn_down_rows = lax.all_gather(later[2], "wide", axis=1, tiled=True)
    gate_cols = out_weights[:, :local_width]
    proj_cols = out_weights[:, local_width:]
    gate_rows = gate_got[::narrow, 0, :3]
    if not paired_lanes():
        long_start = (jnp.cumsum(seq_spans) - seq_spans)[jnp.argmax(seq_spans)]
        turn_order = jnp.arange(turns, dtype=jnp.int32)
        rest_order = jnp.where(turn_order < long_start, turn_order, turn_order + long_turns)
        lane_spans = jnp.where(wide_pos // LANE_WIDE == 0, long_start + turn_order, rest_order)
        key_all = key_all[jnp.clip(lane_spans, 0, wide - 1)]
    chain = chain_forward(
        key_all, value_got, query_low, seq_spans, gate_rows, turns, first_init, second_init, 3
    )
    recall_low, saved = chain[0].reshape(span, local_width), chain[1:]
    recall_own = recall_low.astype(f32)

    keys_all = jnp.concatenate(
        [head_norm(persist_f[0], HEAD).astype(bf16), head_norm(recall_own, HEAD).astype(bf16), key_low], 0
    )
    values_all = jnp.concatenate([persist_f[1].astype(bf16), recall_low, value_low], 0)
    query_heads = split_heads(query_low, HEAD)
    key_heads = split_heads(keys_all, HEAD)
    value_heads = split_heads(values_all, HEAD)
    key_total = keys_all.shape[0]
    row_index = lax.broadcasted_iota(jnp.int32, (span, key_total), 0)
    col_index = lax.broadcasted_iota(jnp.int32, (span, key_total), 1)
    allowed = (col_index < persist_count + span) | (col_index - persist_count - span <= row_index)

    def score_block():
        raw_scores = (
            jnp.einsum("thd,jhd->htj", query_heads, key_heads, preferred_element_type=f32) * score_scale
        )
        return jnp.where(allowed[None], raw_scores, masked_score)

    scores = score_block()
    row_top = jnp.max(scores, axis=-1, keepdims=True)
    exponent = jnp.exp(scores - row_top)
    total_sum = jnp.sum(exponent, axis=-1, keepdims=True)
    log_total = row_top + jnp.log(total_sum)
    weights_low = (exponent / total_sum).astype(bf16)
    attended = jnp.einsum("htj,jhd->thd", weights_low, value_heads, preferred_element_type=f32).reshape(
        span, local_width
    )
    gate_pre = matmul(normed_low, gate_cols)
    gate_sigmoid = jax.nn.sigmoid(gate_pre)
    gated_low = (attended * gate_sigmoid).astype(bf16)

    def by_rows(part):
        return part.astype(bf16).reshape(narrow, own_rows, width)

    tokens_own, cotangent_own = own_part(tokens), own_part(cotangent)
    rows_f32, row_f32 = ((own_rows, width), f32), ((1, width), f32)

    def scaled_of(values):
        factor = lax.rsqrt(jnp.mean(values * values, axis=-1, keepdims=True) + eps_norm)
        return values * factor, factor

    def after_branch(totals, extras):
        tokens_rows, gain = extras
        middle = tokens_rows.astype(f32) + totals[0]
        return [(scaled_of(middle)[0] * gain).astype(bf16)], [middle]

    normed_two, middle = narrow_step(
        [by_rows(inner_right(gated_low, proj_cols))],
        [tokens_own, gain_two[None]],
        after_branch,
        1,
        [rows_f32],
        7,
    )
    normed_two = normed_two.reshape(span, width)
    gate_val = matmul(normed_two, ffn_gate_cols)
    up_val = matmul(normed_two, ffn_up_cols)
    gate_silu = jax.nn.silu(gate_val)
    hidden_ffn = (gate_silu * up_val).astype(bf16)
    ffn_part = matmul(hidden_ffn, ffn_down_rows)
    down_grad = inner_left(cotangent, hidden_ffn).astype(bf16)
    hidden_grad_ffn = inner_right(cotangent, ffn_down_rows)
    gate_sig_ffn = jax.nn.sigmoid(gate_val)
    gate_grad_low = (
        hidden_grad_ffn * up_val * gate_sig_ffn * (1.0 + gate_val * (1.0 - gate_sig_ffn))
    ).astype(bf16)
    up_grad_low = (hidden_grad_ffn * gate_silu).astype(bf16)
    ffn_gate_grad = inner_left(normed_two, gate_grad_low).astype(bf16)
    ffn_up_grad = inner_left(normed_two, up_grad_low).astype(bf16)
    normed_two_part = inner_right(gate_grad_low, ffn_gate_cols) + inner_right(up_grad_low, ffn_up_cols)

    def scatter_wide(grad):
        return lax.psum_scatter(grad.astype(bf16), "wide", scatter_dimension=0, tiled=True).astype(f32)

    ffn_sums = (by_rows(ffn_part), by_rows(normed_two_part))
    ffn_sums, ffn_grads = lax.optimization_barrier((ffn_sums, (ffn_gate_grad, ffn_up_grad, down_grad)))
    ffn_gate_out, ffn_up_out, ffn_down_out = [scatter_wide(a) for a in ffn_grads]

    def after_ffn(totals, extras):
        middle_rows, cotangent_rows, gain = extras
        scaled, factor = scaled_of(middle_rows)
        grad = cotangent_rows.astype(f32) + rms_back(scaled, factor, totals[1] * gain)
        gain_part = jnp.sum(totals[1] * scaled, axis=0, keepdims=True)
        return [grad.astype(bf16), (middle_rows + totals[0]).astype(bf16)], [grad, gain_part]

    branch_low, output, middle_grad, gain_two_part = narrow_step(
        list(ffn_sums), [middle, cotangent_own, gain_two[None]], after_ffn, 2, [rows_f32, row_f32], 9
    )
    branch_low, output = branch_low.reshape(span, width), output.reshape(span, width)

    gated_grad = matmul(branch_low, proj_cols)
    attended_grad_low = (gated_grad * gate_sigmoid).astype(bf16)
    gate_pre_low = (gated_grad * attended * gate_sigmoid * (1.0 - gate_sigmoid)).astype(bf16)
    early_grads = jnp.concatenate([inner_left(normed_low, gate_pre_low), inner_left(branch_low, gated_low)], 1)
    early_out = scatter_wide(early_grads)

    weights_again = jnp.exp(score_block() - log_total)
    grad_heads = split_heads(attended_grad_low, HEAD)
    weight_grad = jnp.einsum("thd,jhd->htj", grad_heads, value_heads, preferred_element_type=f32)
    row_delta = jnp.sum(weights_again * weight_grad, axis=-1, keepdims=True)
    score_grad_low = (weights_again * (weight_grad - row_delta)).astype(bf16)
    query_att = (
        score_scale * jnp.einsum("htj,jhd->thd", score_grad_low, key_heads, preferred_element_type=f32)
    ).reshape(span, local_width)
    keys_grad = (
        score_scale * jnp.einsum("htj,thd->jhd", score_grad_low, query_heads, preferred_element_type=f32)
    ).reshape(key_total, local_width)
    values_grad = jnp.einsum(
        "htj,thd->jhd", weights_again.astype(bf16), grad_heads, preferred_element_type=f32
    ).reshape(key_total, local_width)
    recall_end = persist_count + span
    persist_part = jnp.stack(
        [head_norm_back(persist_f[0], keys_grad[:persist_count], HEAD), values_grad[:persist_count]]
    )
    recall_grad_low = (
        head_norm_back(recall_own, keys_grad[persist_count:recall_end], HEAD)
        + values_grad[persist_count:recall_end]
    ).astype(bf16)

    cots, sums_got, first_chunks, second_chunks = chain_backward(recall_grad_low, saved, seq_spans, gate_rows, 12)
    query_mem, key_mem, value_mem = [cots[i].reshape(span, local_width).astype(f32) for i in range(3)]
    gate_sums = jnp.sum(sums_got[:, :, :3], axis=0)[wide_pos] * jnp.array([-1.0, 1.0, -1.0], f32)

    logit_grad = gate_sums * gate_scale * gate_sig * (1.0 - gate_sig)
    rate_part = span_mean[:, None] * logit_grad[None, :]
    gate_row = jnp.sum(rate_f * logit_grad[None, :], axis=1)[None, :] / span
    act_grad = jnp.concatenate(
        [
            head_norm_back(query_act, query_mem + query_att, HEAD),
            head_norm_back(key_act, key_mem + keys_grad[recall_end:], HEAD),
            values_grad[recall_end:] - value_mem,
        ],
        1,
    )
    conv_grad = act_grad * silu_slope(mixed_conv)
    kernel_rows = []
    extended_grad = jnp.zeros_like(extended)
    for offset in range(taps):
        start_row = taps - 1 - offset
        kernel_rows.append(jnp.sum(conv_grad * extended[start_row : start_row + span], axis=0))
        extended_grad = extended_grad + jnp.pad(kernel_f[offset] * conv_grad, ((start_row, offset), (0, 0)))
    tail_back = from_behind(
        jnp.where(is_first, 0.0, extended_grad[: taps - 1]).astype(bf16), "wide", -1
    ).astype(f32)
    projected_grad = extended_grad[taps - 1 :] + jnp.pad(tail_back, ((span - taps + 1, 0), (0, 0)))
    projected_low = projected_grad.astype(bf16)
    normed_part = inner_right(projected_low, qkv_weights) + inner_right(gate_pre_low, gate_cols)

    def after_all(totals, extras):
        tokens_rows, grad_rows, gain, row = extras
        scaled, factor = scaled_of(tokens_rows.astype(f32))
        normed_grad = totals[0] + row
        gain_part = jnp.sum(normed_grad * scaled, axis=0, keepdims=True)
        return [(grad_rows + rms_back(scaled, factor, normed_grad * gain)).astype(bf16)], [gain_part]

    weight_grads = inner_left(normed_low, projected_low).astype(bf16)

    def place_cols(piece, axis):
        full = piece.shape[:axis] + (width,) + piece.shape[axis + 1 :]
        return lax.dynamic_update_slice_in_dim(jnp.zeros(full, f32), piece, col_offset, axis)

    kernel_full = place_cols(jnp.stack(kernel_rows).reshape(taps, 3, local_width), 2).reshape(taps, 3 * width)
    persist_full = place_cols(persist_part, 2)
    rate_part = jnp.where(narrow_pos == 0, rate_part, 0.0)
    chunks = [
        kernel_full.reshape(taps, devices, -1).transpose(1, 0, 2),
        persist_full.reshape(2, persist_count, devices, -1).transpose(2, 0, 1, 3),
        gain_two_part.reshape(devices, -1),
        rate_part.reshape(devices, -1, 3),
    ]
    flat = jnp.concatenate([a.reshape(devices, -1) for a in chunks], 1)
    flat_size = -(-flat.shape[1] // 1024) * 1024
    flat = jnp.pad(flat, ((0, 0), (0, flat_size - flat.shape[1]))).reshape(devices, -1, 128)
    tokens_grad, weight_out, first_out, second_out, flat_sum, gain_sum = last_step(
        by_rows(normed_part),
        [tokens_own, middle_grad, gain_one[None], gate_row],
        after_all,
        weight_grads.reshape(wide, width // wide, 3 * local_width),
        [first_chunks, second_chunks],
        flat,
        15,
    )
    tokens_grad = tokens_grad.reshape(span, width).astype(f32)
    flat_sum = flat_sum.reshape(-1)
    own_start = (wide_pos * narrow + narrow_pos) * (width // devices)
    norm_grad = lax.dynamic_slice_in_dim(gain_sum.reshape(-1), own_start, width // devices, 0)
    small_outs, at = [], 0
    for a in chunks:
        size = a.size // devices
        small_outs.append(flat_sum[at : at + size].reshape(a.shape[1:]))
        at += size
    kernel_grad, persist_grad, ffn_gain_grad, rate_grad = small_outs
    return (
        output,
        tokens_grad,
        weight_out[:, :local_width],
        weight_out[:, local_width : 2 * local_width],
        weight_out[:, 2 * local_width : 3 * local_width],
        kernel_grad,
        persist_grad,
        norm_grad,
        rate_grad,
        early_out[:, :local_width],
        early_out[:, local_width:].T,
        first_out,
        second_out,
        ffn_gain_grad,
        ffn_gate_out,
        ffn_up_out,
        ffn_down_out.T,
    )


def solution(mesh):
    rows, both, square, turned = P("wide", None), P(("wide", "narrow"), None), P("wide", "narrow"), P("narrow", "wide")
    flat, taps, heads = P(("wide", "narrow")), P(None, ("wide", "narrow")), P(None, None, ("wide", "narrow"))
    return jax.shard_map(
        body,
        mesh=mesh,
        in_specs=(rows, rows, P(), both, both, both, taps, heads, flat, both)
        + (square, turned, square, turned, flat, square, square, turned),
        out_specs=(rows, rows, square, square, square, taps, heads, flat, both)
        + (square, turned, square, turned, flat, square, square, turned),
        check_vma=False,
    )
```

```python
import math

import jax
import jax.numpy as jnp
from jax import lax
from jax.experimental import pallas as pl
from jax.experimental.pallas import tpu as pltpu
from jax.sharding import PartitionSpec as P

HEAD = 64
LANE_WIDE = 4
MESH = pl.DeviceIdType.MESH
ANY = pl.BlockSpec(memory_space=pl.ANY)
bf16 = jnp.bfloat16
f32 = jnp.float32

decay_top = 0.2
moment_top = 0.9
learn_top = 0.1
eps_norm = 1e-05
eps_head = 1e-06
masked_score = -1e30


def remote(src, dst, send, recv, device):
    return pltpu.make_async_remote_copy(
        src_ref=src, dst_ref=dst, send_sem=send, recv_sem=recv, device_id=device, device_id_type=MESH
    )


def sigmoid(values):
    return 1.0 / (1.0 + jnp.exp(-values))
class Grid:
    def __init__(self):
        wide, narrow = lax.axis_size("wide"), lax.axis_size("narrow")
        self.zs = 4 if wide % 4 == 0 else 1
        self.xs, self.ys = wide // self.zs, narrow // 2
        self.wide, self.narrow = lax.axis_index("wide"), lax.axis_index("narrow")
        self.z, self.x = lax.div(self.wide, self.xs), lax.rem(self.wide, self.xs)
        self.y, self.c = lax.div(self.narrow, 2), lax.rem(self.narrow, 2)
        self.partner = self.device(self.z, self.x, self.y, 1 - self.c)

    def device(self, z, x, y, c):
        return z * self.xs + x, 2 * y + c

    def z_others(self):
        if self.zs != 4:
            return [lax.rem(self.z + s, self.zs) for s in range(1, self.zs)]
        near = self.z + 1 - 2 * lax.div(self.z + 3, 4)
        far = 3 - 3 * lax.div(self.z, 2)
        return [near, 6 - self.z - near - far, far]

    def x_others(self):
        return [lax.rem(self.x + s, self.xs) for s in range(1, self.xs)]

    def y_others(self):
        return [lax.rem(self.y + s, self.ys) for s in range(1, self.ys)]

    def greet_all(self):
        wide, narrow = lax.axis_size("wide"), lax.axis_size("narrow")
        devices = wide * narrow
        me = self.wide * narrow + self.narrow
        barrier = pltpu.get_barrier_semaphore()

        def greet(step, carry):
            target = lax.rem(me + step, devices)
            where = lax.div(target, narrow), lax.rem(target, narrow)
            pl.semaphore_signal(barrier, inc=1, device_id=where, device_id_type=MESH)
            return carry

        lax.fori_loop(1, devices, greet, 0)
        return lambda: pl.semaphore_wait(barrier, devices - 1)


class Gather:
    def __init__(self, grid, source, whole, sems):
        self.grid, self.source, self.whole = grid, source, whole
        self.sent, self.got, self.sent_pair, self.got_pair = sems
        self.rows = whole.shape[2]
        self.pushes, self.pairs = 0, 0

    @staticmethod
    def counts():
        zs = 4 if lax.axis_size("wide") % 4 == 0 else 1
        xs, ys = lax.axis_size("wide") // zs, lax.axis_size("narrow") // 2
        sends = 2 * (zs - 1) + zs * 2 * (xs - 1 + ys - 1) + 2 * zs * (xs - 1) * (ys - 1)
        return zs * xs * ys, sends, 2 * zs * xs * ys

    @classmethod
    def scratch(cls):
        chips, sends, pairs = cls.counts()
        return [
            pltpu.SemaphoreType.DMA((sends,)),
            pltpu.SemaphoreType.DMA((chips, 2)),
            pltpu.SemaphoreType.DMA((pairs,)),
            pltpu.SemaphoreType.DMA((chips, 2)),
        ]

    def half(self, ref, h):
        return ref.at[pl.ds(h * (self.rows // 2), self.rows // 2)]

    def piece(self, z, x, y, c, h):
        wide, narrow = self.grid.device(z, x, y, c)
        return self.half(self.whole.at[wide, narrow], h)

    def spot(self, z, x, y):
        return (z * self.grid.xs + x) * self.grid.ys + y

    def push(self, z, x, y, h, target, own):
        here = self.piece(z, x, y, self.grid.c, h)
        copy = remote(
            self.half(self.source, h) if own else here,
            here,
            self.sent.at[self.pushes],
            self.got.at[self.spot(z, x, y), h],
            target,
        )
        self.pushes += 1
        copy.start()

    def to_partner(self, z, x, y, h, own=False):
        here = self.piece(z, x, y, self.grid.c, h)
        copy = remote(
            self.half(self.source, h) if own else here,
            here,
            self.sent_pair.at[self.pairs],
            self.got_pair.at[self.spot(z, x, y), h],
            self.grid.partner,
        )
        self.pairs += 1
        copy.start()

    def arrived(self, z, x, y, h):
        here = self.piece(z, x, y, self.grid.c, h)
        remote(here, here, self.sent.at[0], self.got.at[self.spot(z, x, y), h], self.grid.partner).wait_recv()

    def fan(self, z, own=False):
        g = self.grid
        to_y = [g.device(g.z, g.x, y, g.c) for y in g.y_others()]
        to_x = [g.device(g.z, x, g.y, g.c) for x in g.x_others()]
        for h, targets in ((0, to_y), (1, to_x), (0, to_x), (1, to_y)):
            for target in targets:
                self.push(z, g.x, g.y, h, target, own)
        for h in (0, 1):
            self.to_partner(z, g.x, g.y, h, own)

    def begin(self):
        g = self.grid
        for z in g.z_others():
            for h in (0, 1):
                self.push(g.z, g.x, g.y, h, g.device(z, g.x, g.y, g.c), True)
        self.fan(g.z, True)

    def level(self, number):
        return ([self.grid.z] + self.grid.z_others())[number]

    def along_z(self, number):
        g, z = self.grid, self.level(number)
        for h in (0, 1):
            self.arrived(z, g.x, g.y, h)
        self.fan(z)

    def across(self, number):
        g, z = self.grid, self.level(number)
        for y in g.y_others():
            self.arrived(z, g.x, y, 0)
            for x in g.x_others():
                self.push(z, g.x, y, 0, g.device(g.z, x, g.y, g.c), False)
            self.to_partner(z, g.x, y, 0)
        for x in g.x_others():
            self.arrived(z, x, g.y, 1)
            for y in g.y_others():
                self.push(z, x, g.y, 1, g.device(g.z, g.x, y, g.c), False)
            self.to_partner(z, x, g.y, 1)

    def last(self, number):
        g, z = self.grid, self.level(number)
        for x in g.x_others():
            self.arrived(z, x, g.y, 0)
            self.to_partner(z, x, g.y, 0)
            for y in g.y_others():
                self.arrived(z, x, y, 0)
                self.to_partner(z, x, y, 0)
        for y in g.y_others():
            self.arrived(z, g.x, y, 1)
            self.to_partner(z, g.x, y, 1)
            for x in g.x_others():
                self.arrived(z, x, y, 1)
                self.to_partner(z, x, y, 1)

    def middle(self):
        for number in range(1, self.grid.zs):
            self.along_z(number)
            self.across(number - 1)
            if number > 1:
                self.last(number - 2)
        self.across(self.grid.zs - 1)
        for number in range(max(0, self.grid.zs - 2), self.grid.zs):
            self.last(number)

    def finish(self):
        g = self.grid
        here = self.piece(g.z, g.x, g.y, g.c, 0)
        _, sends, pairs = self.counts()
        for sems, number in ((self.sent, sends), (self.sent_pair, pairs)):
            for i in range(number):
                remote(here, here, sems.at[i], self.got.at[0, 0], g.partner).wait_send()
        for z in range(g.zs):
            for x in range(g.xs):
                for y in range(g.ys):
                    for h in (0, 1):
                        there = self.piece(z, x, y, 1 - g.c, h)
                        remote(
                            there, there, self.sent.at[0], self.got_pair.at[self.spot(z, x, y), h], g.partner
                        ).wait_recv()


def send_parameters(smalls, weights, blocks, tokens, ident):
    wide, narrow = lax.axis_size("wide"), lax.axis_size("narrow")
    devices = wide * narrow
    count = len(blocks)

    def kernel(*refs):
        smalls_ref, weights_ref = refs[:2]
        block_refs, tokens_ref, refs = refs[2 : 2 + count], refs[2 + count], refs[3 + count :]
        smalls_out, weights_out = refs[:2]
        block_outs, tail_out, refs = refs[2 : 2 + count], refs[2 + count], refs[3 + count :]
        hold_small, hold_weight, refs = refs[0], refs[1], refs[2:]
        hold_blocks, refs = refs[:count], refs[count:]
        local_sem, all_send, all_recv, near_send, near_recv, z_send, z_recv, x_send, x_recv, b_send, b_recv, t_sem = refs
        g = Grid()
        me = g.wide * narrow + g.narrow
        wait_all = g.greet_all()
        own = [
            (smalls_ref, hold_small, smalls_out.at[me]),
            (weights_ref.at[g.narrow], hold_weight, weights_out.at[g.wide, g.narrow]),
        ] + [
            (block_refs[i].at[lax.rem(g.wide, LANE_WIDE)], hold_blocks[i], block_outs[i].at[g.wide])
            for i in range(count)
        ]
        into = [pltpu.make_async_copy(a, b, local_sem.at[i]) for i, (a, b, _) in enumerate(own)]
        back = [pltpu.make_async_copy(b, c, local_sem.at[i]) for i, (_, b, c) in enumerate(own)]
        for copy in into:
            copy.start()
        wait_all()
        near = []
        for s in range(1, narrow):
            target = lax.rem(g.narrow + s, narrow)
            copy = remote(
                weights_ref.at[target],
                weights_out.at[g.wide, g.narrow],
                near_send.at[s],
                near_recv.at[g.narrow],
                (g.wide, target),
            )
            copy.start()
            near.append(copy)
        tail = remote(
            tokens_ref.at[pl.ds(tokens_ref.shape[0] - 8, 8)],
            tail_out,
            t_sem.at[0],
            t_sem.at[1],
            (lax.rem(g.wide + 1, wide), g.narrow),
        )
        tail.start()

        def send_small(step, carry):
            target = lax.rem(me + step, devices)
            remote(
                smalls_ref,
                smalls_out.at[me],
                all_send.at[0],
                all_recv.at[0],
                (lax.div(target, narrow), lax.rem(target, narrow)),
            ).start()
            return carry

        lax.fori_loop(1, devices, send_small, 0)
        for copy in into:
            copy.wait()
        for copy in back:
            copy.start()
        for copy in back:
            copy.wait()
        for s in range(1, narrow):
            source = lax.rem(g.narrow + s, narrow)
            there = weights_out.at[g.wide, source]
            remote(there, there, near_send.at[s], near_recv.at[source], g.partner).wait_recv()

        def row(z, x):
            return weights_out.at[z * g.xs + x]

        sends = []

        def push(z, target, send, recv):
            copy = remote(row(z, g.x), row(z, g.x), send, recv, target)
            copy.start()
            sends.append(copy)

        for i, z in enumerate(g.z_others()):
            push(g.z, g.device(z, g.x, g.y, g.c), z_send.at[i], z_recv.at[g.z])
        for i, x in enumerate(g.x_others()):
            push(g.z, g.device(g.z, x, g.y, g.c), x_send.at[0, i], x_recv.at[g.z, g.x])
        for j, z in enumerate(g.z_others()):
            remote(row(z, g.x), row(z, g.x), z_send.at[0], z_recv.at[z], g.partner).wait_recv()
            for i, x in enumerate(g.x_others()):
                push(z, g.device(g.z, x, g.y, g.c), x_send.at[1 + j, i], x_recv.at[z, g.x])
        for s in range(1, wide):
            target = lax.rem(g.wide + s, wide)
            for i in range(count):
                copy = remote(
                    block_refs[i].at[lax.rem(target, LANE_WIDE)],
                    block_outs[i].at[g.wide],
                    b_send.at[i, s],
                    b_recv.at[i, g.wide],
                    (target, g.narrow),
                )
                copy.start()
                sends.append(copy)
        for x in g.x_others():
            for z in [g.z] + g.z_others():
                remote(row(z, x), row(z, x), z_send.at[0], x_recv.at[z, x], g.partner).wait_recv()
        for s in range(1, wide):
            source = lax.rem(g.wide + s, wide)
            for i in range(count):
                there = block_outs[i].at[source]
                remote(there, there, z_send.at[0], b_recv.at[i, source], g.partner).wait_recv()
        for copy in near + sends:
            copy.wait_send()
        tail.wait()
        others = smalls_out.at[pl.ds(0, devices - 1)]
        whole = remote(others, others, all_send.at[0], all_recv.at[0], g.partner)
        whole.wait_send()
        whole.wait_recv()

    zs = 4 if wide % 4 == 0 else 1
    xs = wide // zs
    sem = pltpu.SemaphoreType.DMA
    return pl.pallas_call(
        kernel,
        out_shape=[
            jax.ShapeDtypeStruct((devices,) + smalls.shape, smalls.dtype),
            jax.ShapeDtypeStruct((wide, narrow) + weights.shape[1:], weights.dtype),
        ]
        + [jax.ShapeDtypeStruct((wide,) + b.shape[1:], b.dtype) for b in blocks]
        + [jax.ShapeDtypeStruct((8, tokens.shape[1]), tokens.dtype)],
        in_specs=[ANY] * (3 + count),
        out_specs=[ANY] * (3 + count),
        scratch_shapes=[pltpu.VMEM(smalls.shape, smalls.dtype), pltpu.VMEM(weights.shape[1:], weights.dtype)]
        + [pltpu.VMEM(b.shape[1:], b.dtype) for b in blocks]
        + [sem((2 + count,)), sem((1,)), sem((1,)), sem((narrow,)), sem((narrow,)), sem((zs,)), sem((zs,))]
        + [sem((zs, xs)), sem((zs, xs)), sem((count, wide)), sem((count, wide)), sem((2,))],
        compiler_params=pltpu.CompilerParams(collective_id=ident, has_side_effects=True),
        name="send_parameters",
    )(smalls, weights, *blocks, tokens)


def narrow_step(parts, extras, work, spread_count, locals_like, ident):
    narrow, rows, width = parts[0].shape
    ys = narrow // 2
    count, extra_count, local_count = len(parts), len(extras), len(locals_like)
    parts = [p.reshape(ys, 2, rows, width) for p in parts]

    def kernel(*refs):
        part_refs, refs = refs[:count], refs[count:]
        extra_refs, refs = refs[:extra_count], refs[extra_count:]
        spread_refs, refs = refs[:spread_count], refs[spread_count:]
        local_refs, refs = refs[:local_count], refs[local_count:]
        mine, pair, half, got, rowbuf, refs = refs[0], refs[1], refs[2], refs[3], refs[4], refs[5:]
        load_sem, pair_send, pair_recv, y_send, y_recv, s_send, s_recv, p_send, p_recv, own_sem = refs
        g = Grid()
        barrier = pltpu.get_barrier_semaphore()
        friends = [g.device(g.z, g.x, y, g.c) for y in g.y_others()] + [g.partner]
        for friend in friends:
            pl.semaphore_signal(barrier, inc=1, device_id=friend, device_id_type=MESH)
        loads = [
            pltpu.make_async_copy(part_refs[i].at[:, g.c], mine.at[i], load_sem.at[i]) for i in range(count)
        ]
        for copy in loads:
            copy.start()
        pl.semaphore_wait(barrier, len(friends))
        pairs = [
            remote(part_refs[i].at[:, 1 - g.c], pair.at[i], pair_send.at[i], pair_recv.at[i], g.partner)
            for i in range(count)
        ]
        for copy in pairs:
            copy.start()
        sends = []
        for i in range(count):
            loads[i].wait()
            pairs[i].wait_recv()
            mine[i] += pair[i]
            half[i] = mine[i].astype(bf16)
            for s, y in enumerate(g.y_others()):
                copy = remote(
                    half.at[i, y], got.at[i, g.y], y_send.at[i, s], y_recv.at[i, g.y], g.device(g.z, g.x, y, g.c)
                )
                copy.start()
                sends.append(copy)
        totals = []
        for i in range(count):
            total = mine[i, g.y]
            for y in g.y_others():
                remote(got.at[i, y], got.at[i, y], y_send.at[i, 0], y_recv.at[i, y], g.partner).wait_recv()
                total = total + got[i, y].astype(f32)
            totals.append(total)
        spreads, locals_out = work(totals, [ref[...] for ref in extra_refs])
        for ref, value in zip(local_refs, locals_out):
            ref[...] = value
        own = []
        for i, value in enumerate(spreads):
            rowbuf[i] = value
            for s, y in enumerate(g.y_others()):
                copy = remote(
                    rowbuf.at[i],
                    spread_refs[i].at[g.narrow],
                    s_send.at[i, s],
                    s_recv.at[i, g.y],
                    g.device(g.z, g.x, y, g.c),
                )
                copy.start()
                sends.append(copy)
            copy = remote(
                rowbuf.at[i], spread_refs[i].at[g.narrow], p_send.at[i, g.y], p_recv.at[i, g.y], g.partner
            )
            copy.start()
            sends.append(copy)
            copy = pltpu.make_async_copy(rowbuf.at[i], spread_refs[i].at[g.narrow], own_sem.at[i])
            copy.start()
            own.append(copy)
        for i in range(spread_count):
            for y in g.y_others():
                there = spread_refs[i].at[2 * y + g.c]
                remote(there, there, s_send.at[i, 0], s_recv.at[i, y], g.partner).wait_recv()
                copy = remote(there, there, p_send.at[i, y], p_recv.at[i, y], g.partner)
                copy.start()
                sends.append(copy)
        for i in range(spread_count):
            for y in range(ys):
                there = spread_refs[i].at[2 * y + 1 - g.c]
                remote(there, there, s_send.at[i, 0], p_recv.at[i, y], g.partner).wait_recv()
        for copy in pairs + sends:
            copy.wait_send()
        for copy in own:
            copy.wait()

    sem = pltpu.SemaphoreType.DMA
    vmem = pl.BlockSpec(memory_space=pltpu.VMEM)
    return pl.pallas_call(
        kernel,
        out_shape=[jax.ShapeDtypeStruct((narrow, rows, width), bf16)] * spread_count
        + [jax.ShapeDtypeStruct(shape, dtype) for shape, dtype in locals_like],
        in_specs=[ANY] * count + [vmem] * extra_count,
        out_specs=[ANY] * spread_count + [vmem] * local_count,
        scratch_shapes=[pltpu.VMEM((count, ys, rows, width), f32)] * 2
        + [pltpu.VMEM((count, ys, rows, width), bf16)] * 2
        + [pltpu.VMEM((spread_count, rows, width), bf16)]
        + [sem((count,))] * 3
        + [sem((count, ys))] * 2
        + [sem((spread_count, ys))] * 4
        + [sem((spread_count,))],
        compiler_params=pltpu.CompilerParams(collective_id=ident, has_side_effects=True),
        cost_estimate=pl.CostEstimate(flops=30 * 10**9, bytes_accessed=100 * 2**20, transcendentals=0),
        name=f"narrow_step_{ident}",
    )(*parts, *extras)


def last_step(heads, conv, lengths, gate_back, extras, work, early, chunks, flat, ident):
    span, columns = conv[0].shape
    block = columns // 3
    width = conv[3].shape[0]
    narrow = lax.axis_size("narrow")
    rows = span // narrow
    wide = lax.axis_size("wide")
    devices = wide * narrow
    ys = narrow // 2
    zs = 4 if wide % 4 == 0 else 1
    xs = wide // zs
    lanes = wide // LANE_WIDE
    extra_count = len(extras)
    own_grad, own_early = (width // wide, columns), (width // wide, early.shape[1])
    early = early.reshape((zs, xs) + own_early)
    compute = list(heads) + list(conv) + list(gate_back)
    compute_count = len(compute)
    count = 4
    first_shape, second_shape, flat_shape = chunks[0].shape[1:], chunks[1].shape[1:], flat.shape[1:]

    def kernel(*refs):
        first_ref, second_ref, flat_ref, early_ref, lengths_ref = refs[:5]
        compute_refs, refs = refs[5 : 5 + compute_count], refs[5 + compute_count :]
        extra_refs, refs = refs[:extra_count], refs[extra_count:]
        spread_ref, grads_out, first_out, second_out, flat_out, row_out, taps_out, early_out = refs[:8]
        refs = refs[8:]
        part_ref, grads_ref, conv_grad, tap_rows, halo_out, halo_in, halo_sem, taps_sem, refs = refs[:8] + (refs[8:],)
        pair, half, got, rowbuf, rowtile, rowgot, refs = refs[:6] + (refs[6:],)
        gx, ghalf, gz, fgot, sgot, flatgot, refs = refs[:6] + (refs[6:],)
        load_sem, pair_sem, y_send, y_recv, s_send, s_recv, p_send, p_recv, refs = refs[:8] + (refs[8:],)
        gx_send, gx_recv, gz_send, gz_recv, c_send, c_recv, all_send, all_recv = refs[:8]
        early_own, ex, ehalf, ez, e_sems = refs[8], refs[9], refs[10], refs[11], refs[12:16]
        g = Grid()
        me = g.wide * narrow + g.narrow
        wait_all = g.greet_all()
        plan = Plan(lengths_ref, None, lengths.shape[0])
        loads = [
            pltpu.make_async_copy(first_ref.at[g.wide], fgot.at[g.wide], load_sem.at[0]),
            pltpu.make_async_copy(second_ref.at[g.wide], sgot.at[g.wide], load_sem.at[1]),
            pltpu.make_async_copy(flat_ref.at[me], flatgot.at[me], load_sem.at[2]),
            pltpu.make_async_copy(early_ref.at[:, g.x], early_own, load_sem.at[3]),
        ]
        for copy in loads:
            copy.start()
        wait_all()
        sends = []
        order = g.z_others()[::-1] + [g.z]

        def along_x(source, place, sems):
            for z in order:
                for i, x in enumerate(g.x_others()):
                    copy = remote(
                        source.at[z, x],
                        place.at[g.x, z],
                        sems[0].at[i, z],
                        sems[1].at[g.x, z],
                        g.device(g.z, x, g.y, g.c),
                    )
                    copy.start()
                    sends.append(copy)

        def join(z, own, place, joined, sems):
            total = own.astype(f32)
            for x in g.x_others():
                there = place.at[x, z]
                remote(there, there, sems[0].at[0, 0], sems[1].at[x, z], g.partner).wait_recv()
                total = total + place[x, z].astype(f32)
            joined[z] = total.astype(bf16)

        def along_z(i, z, joined, place, sems):
            copy = remote(joined.at[z], place.at[g.z], sems[2].at[i], sems[3].at[g.z], g.device(z, g.x, g.y, g.c))
            copy.start()
            sends.append(copy)

        def whole_of(joined, place, sems):
            total = joined[g.z].astype(f32)
            for z in order[:-1]:
                there = place.at[z]
                remote(there, there, sems[2].at[0], sems[3].at[z], g.partner).wait_recv()
                total = total + place[z].astype(f32)
            return total

        g_sems = (gx_send, gx_recv, gz_send, gz_recv)
        along_x(early_ref, ex, e_sems)
        for s in range(1, wide):
            target = lax.rem(g.wide + s, wide)
            for i, (source, place) in enumerate(((first_ref, fgot), (second_ref, sgot))):
                copy = remote(
                    source.at[target],
                    place.at[g.wide],
                    c_send.at[i, s],
                    c_recv.at[i, g.wide],
                    (target, g.narrow),
                )
                copy.start()
                sends.append(copy)

        def send_flat(step, carry):
            target = lax.rem(me + step, devices)
            where = lax.div(target, narrow), lax.rem(target, narrow)
            remote(flat_ref.at[target], flatgot.at[me], all_send.at[0], all_recv.at[0], where).start()
            return carry

        lax.fori_loop(1, devices, send_flat, 0)
        qmem, kmem, vmem_ref, qatt, katt, vatt = compute_refs[:6]
        mixed_ref, ext_ref, taps_ref, weights_ref, normed_ref, gate_low, gate_cols = compute_refs[6:]
        for third, (memory, attention) in enumerate(((qmem, qatt), (kmem, katt), (vmem_ref, vatt))):
            place = pl.ds(third * block, block)
            mixed = mixed_ref[:, place]
            if third < 2:
                grad = memory[...].astype(f32) + attention[...]
                act = mixed * sigmoid(mixed)
                factor = lax.rsqrt(head_sums(act * act) + eps_head)
                normed = act * factor
                grad = factor * (grad - normed * head_sums(normed * grad))
            else:
                grad = attention[...] - memory[...].astype(f32)
            grad = grad * silu_slope(mixed)
            conv_grad[pl.ds(0, span), place] = grad
            for j in range(count):
                tap_rows[pl.ds(j, 1), place] = jnp.sum(grad * ext_ref[pl.ds(8 - j, span), place], axis=0, keepdims=True)
        begins = plan.begins(g.wide)
        halo_out[...] = jnp.where(begins, 0.0, conv_grad[pl.ds(0, 8), :])
        halo = remote(
            halo_out, halo_in, halo_sem.at[0], halo_sem.at[1], (lax.rem(g.wide + wide - 1, wide), g.narrow)
        )
        halo.start()

        def send_taps(step, carry):
            target = lax.rem(me + step, devices)
            where = lax.div(target, narrow), lax.rem(target, narrow)
            remote(tap_rows, taps_out.at[me], taps_sem.at[0], taps_sem.at[1], where).start()
            return carry

        lax.fori_loop(1, devices, send_taps, 0)
        taps_out[me] = tap_rows[...]
        for copy in loads:
            copy.wait()
        for i, z in enumerate(order):
            join(z, early_own[z], ex, ehalf, e_sems)
            if i < len(order) - 1:
                along_z(i, z, ehalf, ez, e_sems)
        halo.wait()
        conv_grad[pl.ds(span, 8), :] = halo_in[...]
        projected = taps_ref[pl.ds(0, 1), :] * conv_grad[pl.ds(0, span), :]
        for j in range(1, count):
            projected = projected + taps_ref[pl.ds(j, 1), :] * conv_grad[pl.ds(j, span), :]
        projected_low = projected.astype(bf16)
        part = inner_right(projected_low, weights_ref[...]) + inner_right(gate_low[...], gate_cols[...])
        part_ref[...] = part.reshape(ys, 2, rows, width)
        pair_copy = remote(part_ref.at[:, 1 - g.c], pair, pair_sem.at[0], pair_sem.at[1], g.partner)
        pair_copy.start()
        grads_ref[...] = inner_left(normed_ref[...], projected_low).astype(bf16).reshape((zs, xs) + own_grad)
        along_x(grads_ref, gx, g_sems)
        pair_copy.wait()
        pair[...] += part_ref[:, g.c]
        half[...] = pair[...].astype(bf16)
        for s, y in enumerate(g.y_others()):
            copy = remote(half.at[y], got.at[g.y], y_send.at[s], y_recv.at[g.y], g.device(g.z, g.x, y, g.c))
            copy.start()
            sends.append(copy)
        for i, z in enumerate(order[:-1]):
            join(z, grads_ref[z, g.x], gx, ghalf, g_sems)
            along_z(i, z, ghalf, gz, g_sems)
            if i == 0:
                total = pair[g.y]
                for y in g.y_others():
                    remote(got.at[y], got.at[y], y_send.at[0], y_recv.at[y], g.partner).wait_recv()
                    total = total + got[y].astype(f32)
                spreads, locals_out = work([total], [ref[...] for ref in extra_refs])
                rowbuf[...] = spreads[0]
                for j in range(8):
                    rowtile[pl.ds(j, 1), :] = locals_out[0][:, j * width // 8 : (j + 1) * width // 8]
                for s, y in enumerate(g.y_others()):
                    copy = remote(
                        rowbuf,
                        spread_ref.at[g.narrow],
                        s_send.at[s],
                        s_recv.at[g.y],
                        g.device(g.z, g.x, y, g.c),
                    )
                    copy.start()
                    sends.append(copy)
                copy = remote(rowbuf, spread_ref.at[g.narrow], p_send.at[g.y], p_recv.at[g.y], g.partner)
                copy.start()
                sends.append(copy)
                own = pltpu.make_async_copy(rowbuf, spread_ref.at[g.narrow], load_sem.at[0])
                own.start()

                def send_row(step, carry):
                    target = lax.rem(me + step, devices)
                    where = lax.div(target, narrow), lax.rem(target, narrow)
                    remote(rowtile, rowgot.at[me], all_send.at[1], all_recv.at[1], where).start()
                    return carry

                lax.fori_loop(1, devices, send_row, 0)
                rowgot[me] = rowtile[...]
        for y in g.y_others():
            there = spread_ref.at[2 * y + g.c]
            remote(there, there, s_send.at[0], s_recv.at[y], g.partner).wait_recv()
            copy = remote(there, there, p_send.at[y], p_recv.at[y], g.partner)
            copy.start()
            sends.append(copy)
        join(g.z, grads_ref[g.z, g.x], gx, ghalf, g_sems)
        early_out[...] = whole_of(ehalf, ez, e_sems)
        for s in range(1, wide):
            source = lax.rem(g.wide + s, wide)
            for i, place in enumerate((fgot, sgot)):
                there = place.at[source]
                remote(there, there, c_send.at[i, 0], c_recv.at[i, source], g.partner).wait_recv()
        for p in range(LANE_WIDE):
            first_sum, second_sum = fgot[p].astype(f32), sgot[p].astype(f32)
            for lane in range(1, lanes):
                first_sum = first_sum + fgot[lane * LANE_WIDE + p].astype(f32)
                second_sum = second_sum + sgot[lane * LANE_WIDE + p].astype(f32)
            first_out[:, p * first_shape[1] : (p + 1) * first_shape[1]] = first_sum
            second_out[p * second_shape[0] : (p + 1) * second_shape[0], :] = second_sum
        grads_out[...] = whole_of(ghalf, gz, g_sems)
        ends = ((flatgot, all_send.at[0], all_recv.at[0]), (rowgot, all_send.at[1], all_recv.at[1]))
        for place, send, recv in ends + ((taps_out, taps_sem.at[0], taps_sem.at[1]),):
            others = place.at[pl.ds(0, devices - 1)]
            whole = remote(others, others, send, recv, g.partner)
            whole.wait_send()
            whole.wait_recv()
        flat_out[...] = jnp.sum(flatgot[...], axis=0)
        row_out[...] = jnp.sum(rowgot[...], axis=0)
        for y in range(ys):
            there = spread_ref.at[2 * y + 1 - g.c]
            remote(there, there, s_send.at[0], p_recv.at[y], g.partner).wait_recv()
        for copy in sends:
            copy.wait_send()
        own.wait()

    sem = pltpu.SemaphoreType.DMA
    vmem = pl.BlockSpec(memory_space=pltpu.VMEM)
    return pl.pallas_call(
        kernel,
        out_shape=[
            jax.ShapeDtypeStruct((narrow, rows, width), bf16),
            jax.ShapeDtypeStruct(own_grad, f32),
            jax.ShapeDtypeStruct((first_shape[0], LANE_WIDE * first_shape[1]), f32),
            jax.ShapeDtypeStruct((LANE_WIDE * second_shape[0], second_shape[1]), f32),
            jax.ShapeDtypeStruct(flat_shape, f32),
            jax.ShapeDtypeStruct((8, width // 8), f32),
            jax.ShapeDtypeStruct((devices, count, columns), f32),
            jax.ShapeDtypeStruct(own_early, f32),
        ],
        in_specs=[ANY] * 4
        + [pl.BlockSpec(memory_space=pltpu.SMEM)]
        + [vmem] * (compute_count + extra_count),
        out_specs=[ANY] + [vmem] * 7,
        scratch_shapes=[
            pltpu.VMEM((ys, 2, rows, width), f32),
            pltpu.VMEM((zs, xs) + own_grad, bf16),
            pltpu.VMEM((span + 8, columns), f32),
            pltpu.VMEM((count, columns), f32),
            pltpu.VMEM((8, columns), f32),
            pltpu.VMEM((8, columns), f32),
            sem((2,)),
            sem((2,)),
        ]
        + [pltpu.VMEM((ys, rows, width), f32)]
        + [pltpu.VMEM((ys, rows, width), bf16)] * 2
        + [pltpu.VMEM((rows, width), bf16)]
        + [pltpu.VMEM((8, width // 8), f32), pltpu.VMEM((devices, 8, width // 8), f32)]
        + [
            pltpu.VMEM((xs, zs) + own_grad, bf16),
            pltpu.VMEM((zs,) + own_grad, bf16),
            pltpu.VMEM((zs,) + own_grad, bf16),
            pltpu.VMEM((wide,) + first_shape, bf16),
            pltpu.VMEM((wide,) + second_shape, bf16),
            pltpu.VMEM((devices,) + flat_shape, f32),
        ]
        + [sem((4,)), sem((2,))]
        + [sem((ys,))] * 6
        + [sem((xs, zs))] * 2
        + [sem((zs,))] * 2
        + [sem((2, wide))] * 2
        + [sem((2,))] * 2
        + [
            pltpu.VMEM((zs,) + own_early, bf16),
            pltpu.VMEM((xs, zs) + own_early, bf16),
            pltpu.VMEM((zs,) + own_early, bf16),
            pltpu.VMEM((zs,) + own_early, bf16),
        ]
        + [sem((xs, zs))] * 2
        + [sem((zs,))] * 2,
        compiler_params=pltpu.CompilerParams(
            collective_id=ident, has_side_effects=True, vmem_limit_bytes=60 * 1024 * 1024
        ),
        name="last_step",
    )(chunks[0], chunks[1], flat, early, lengths, *compute, *extras)


class Plan:
    def __init__(self, spans_ref, gates_ref, count):
        self.wide = lax.axis_size("wide")
        self.long = min(6, self.wide * 5 // 8)
        self.gates = gates_ref
        lengths = [spans_ref[i] for i in range(count)]
        self.starts, at = [], 0
        for length in lengths:
            self.starts.append(at)
            at = at + length
        longest, self.start = lengths[0], 0
        for i in range(1, count):
            more = lengths[i] > longest
            longest = jnp.where(more, lengths[i], longest)
            self.start = jnp.where(more, self.starts[i], self.start)
        self.lane = lax.div(lax.axis_index("wide"), LANE_WIDE)

    def span(self, turn):
        rest = jnp.where(turn < self.start, turn, turn + self.long)
        return jnp.clip(jnp.where(self.lane == 0, self.start + turn, rest), 0, self.wide - 1)

    def valid(self, turn):
        count = jnp.where(self.lane == 0, self.long, jnp.where(self.lane == 1, self.wide - self.long, 0))
        return jnp.where(turn < count, 1.0, 0.0)

    def first(self, turn):
        span = self.span(turn)
        found = jnp.where(span == self.starts[0], 1.0, 0.0)
        for start in self.starts[1:]:
            found = jnp.maximum(found, jnp.where(span == start, 1.0, 0.0))
        return jnp.maximum(found, 1.0 - self.valid(turn))

    def begins(self, span):
        found = span == self.starts[0]
        for start in self.starts[1:]:
            found = found | (span == start)
        return found

    def rates(self, turn):
        span = self.span(turn)
        return self.gates[span, 0], self.gates[span, 1], self.gates[span, 2]

    def lane_of(self, span):
        inside = (span >= self.start) & (span < self.start + self.long)
        return jnp.where(inside, 0, 1)

    def turn_of(self, span):
        inside = (span >= self.start) & (span < self.start + self.long)
        outside = jnp.where(span < self.start, span, span - self.long)
        return jnp.where(inside, span - self.start, outside)


def paired_lanes():
    wide = lax.axis_size("wide")
    long = min(6, wide * 5 // 8)
    return wide == 2 * LANE_WIDE and long == LANE_WIDE + 1 and lax.axis_size("narrow") == 4


class LaneGather:
    def __init__(self, grid, plan, source, whole, refs):
        self.grid, self.plan, self.source, self.whole = grid, plan, source, whole
        self.own, self.taken, self.mine = refs[:3]
        self.sent, self.got, self.sent_pair, self.got_pair, self.swap_sent, self.swap_got, self.local = refs[3:]
        self.rows = whole.shape[2]
        self.quarter = self.rows // LANE_WIDE
        third = (self.rows + self.quarter) // 3 // 16 * 16
        self.cuts = [(0, third), (third, third), (2 * third, self.rows - 2 * third)]
        self.side = lax.div(grid.wide, LANE_WIDE)
        self.spot = lax.rem(grid.wide, LANE_WIDE)
        long = plan.long
        lone = jnp.where((grid.wide >= plan.wide - long) & (grid.wide < long), 1, 0)
        self.paired = lone == 0
        self.pair = (grid.wide + long - 2 * long * self.side, grid.narrow)
        self.here = (lax.div(self.spot, 2), lax.rem(self.spot, 2), grid.y)

    @staticmethod
    def scratch(rows, cols):
        sem = pltpu.SemaphoreType.DMA
        return [
            pltpu.VMEM((rows, cols), bf16),
            pltpu.VMEM((rows, cols), bf16),
            pltpu.VMEM((rows + rows // LANE_WIDE, cols), bf16),
            sem((4, 7)),
            sem((4, 8)),
            sem((4, 8)),
            sem((4, 8)),
            sem((4,)),
            sem((4,)),
            sem((5,)),
        ]

    @staticmethod
    def shape(rows, cols):
        return (LANE_WIDE + 1, lax.axis_size("narrow"), rows, cols)

    def order(self, part):
        return ((0, 1, 2), (1, 2, 0), (2, 0, 1))[part]

    def place(self, mask):
        return [1 - v if mask >> i & 1 else v for i, v in enumerate(self.here)]

    def device(self, mask, colour):
        z, x, y = self.place(mask)
        return self.side * LANE_WIDE + 2 * z + x, 2 * y + colour

    def pieces(self, part, mask, colour):
        z, x, y = self.place(mask)
        spot, narrow = 2 * z + x, 2 * y + colour
        start, size = self.cuts[part]
        result = [(part, self.whole.at[spot, narrow, pl.ds(start, size)], self.mine.at[pl.ds(start, size)])]
        if part == 2:
            there = self.whole.at[LANE_WIDE, narrow, pl.ds(spot * self.quarter, self.quarter)]
            result.append((3, there, self.mine.at[pl.ds(self.rows, self.quarter)]))
        return result

    def push(self, part, mask, axis, number):
        for i, there, own in self.pieces(part, mask, self.grid.c):
            remote(
                there if mask else own,
                there,
                self.sent.at[i, number],
                self.got.at[i, mask | 1 << axis],
                self.device(1 << axis, self.grid.c),
            ).start()

    def to_partner(self, part, mask):
        for i, there, own in self.pieces(part, mask, self.grid.c):
            remote(
                there if mask else own,
                there,
                self.sent_pair.at[i, mask],
                self.got_pair.at[i, mask],
                self.grid.partner,
            ).start()

    def arrived(self, part, mask):
        for i, there, _ in self.pieces(part, mask, self.grid.c):
            remote(there, there, self.sent.at[i, 0], self.got.at[i, mask], self.grid.partner).wait_recv()

    def swaps(self):
        return [
            remote(
                self.source.at[pl.ds(start, size)],
                self.taken.at[pl.ds(start, size)],
                self.swap_sent.at[i],
                self.swap_got.at[i],
                self.pair,
            )
            for i, (start, size) in enumerate(self.cuts)
        ]

    def quarters(self):
        return [
            remote(
                self.source.at[pl.ds(q * self.quarter, self.quarter)],
                self.mine.at[pl.ds(self.rows, self.quarter)],
                self.swap_sent.at[q],
                self.swap_got.at[3],
                (q, self.grid.narrow),
            )
            for q in range(LANE_WIDE)
        ]

    def begin(self):
        @pl.when(self.paired)
        def _():
            for copy in self.swaps():
                copy.start()

        @pl.when(self.grid.wide == LANE_WIDE)
        def _():
            for copy in self.quarters():
                copy.start()

        pltpu.make_async_copy(self.source, self.own, self.local.at[4]).start()

        @pl.when(self.side == 1)
        def _():
            self.mine[pl.ds(self.rows, self.quarter), :] = jnp.zeros((self.quarter, self.mine.shape[1]), bf16)

    def stage_a(self):
        pltpu.make_async_copy(self.source, self.own, self.local.at[4]).wait()
        keep = self.plan.lane_of(self.grid.wide) == self.side
        for part in range(3):
            start, size = self.cuts[part]
            place = (pl.ds(start, size), slice(None))

            @pl.when(self.paired)
            def _():
                self.swaps()[part].wait_recv()
                self.mine[place] = jnp.where(keep, self.own[place], self.taken[place])

            @pl.when(jnp.logical_not(self.paired))
            def _():
                self.mine[place] = self.own[place]

            if part == 2:

                @pl.when(self.side == 0)
                def _():
                    self.quarters()[0].wait_recv()

            for number, axis in enumerate(self.order(part)):
                self.push(part, 0, axis, number)
            self.to_partner(part, 0)
            for i, there, own in self.pieces(part, 0, self.grid.c):
                pltpu.make_async_copy(own, there, self.local.at[i]).start()

    def stage_b(self):
        for part in range(3):
            a, b, c = self.order(part)
            self.arrived(part, 1 << a)
            self.push(part, 1 << a, b, 3)
            self.push(part, 1 << a, c, 4)
            self.to_partner(part, 1 << a)
            self.arrived(part, 1 << b)
            self.push(part, 1 << b, c, 5)
            self.to_partner(part, 1 << b)
        for part in range(3):
            a, b, c = self.order(part)
            self.arrived(part, 1 << a | 1 << b)
            self.push(part, 1 << a | 1 << b, c, 6)
            self.to_partner(part, 1 << a | 1 << b)

    def stage_c(self):
        for part in range(3):
            a, b, c = self.order(part)
            for mask in (1 << c, 1 << a | 1 << c, 1 << b | 1 << c, 7):
                self.arrived(part, mask)
                self.to_partner(part, mask)

    def finish(self):
        for part in range(3):
            for i, there, own in self.pieces(part, 0, self.grid.c):
                for number in range(7):
                    remote(own, there, self.sent.at[i, number], self.got.at[i, 0], self.grid.partner).wait_send()
                for mask in range(8):
                    remote(own, there, self.sent_pair.at[i, mask], self.got.at[i, 0], self.grid.partner).wait_send()
                pltpu.make_async_copy(own, there, self.local.at[i]).wait()
            for mask in range(8):
                for i, there, _ in self.pieces(part, mask, 1 - self.grid.c):
                    remote(there, there, self.sent.at[i, 0], self.got_pair.at[i, mask], self.grid.partner).wait_recv()

        @pl.when(self.paired)
        def _():
            for copy in self.swaps():
                copy.wait_send()

        @pl.when(self.grid.wide == LANE_WIDE)
        def _():
            for copy in self.quarters():
                copy.wait_send()

    def middle(self):
        self.stage_a()
        self.stage_b()
        self.stage_c()

    def index(self, turn):
        start = lax.rem(self.plan.start + turn, self.plan.long)
        return jnp.where(self.plan.lane == 0, start, jnp.minimum(turn + 1, LANE_WIDE - 1))


class SpanGather(Gather):
    def __init__(self, grid, plan, source, whole, refs):
        super().__init__(grid, source, whole, refs[1:5])
        self.plan, self.own, self.local = plan, refs[0], refs[5]

    @classmethod
    def scratch(cls, rows, cols):
        return [pltpu.VMEM((rows, cols), bf16)] + Gather.scratch() + [pltpu.SemaphoreType.DMA((1,))]

    @staticmethod
    def shape(rows, cols):
        return (lax.axis_size("wide"), lax.axis_size("narrow"), rows, cols)

    def own_copies(self):
        there = self.whole.at[self.grid.wide, self.grid.narrow]
        return (
            pltpu.make_async_copy(self.source, self.own, self.local.at[0]),
            pltpu.make_async_copy(self.own, there, self.local.at[0]),
        )

    def begin(self):
        super().begin()
        self.own_copies()[0].start()

    def stage_a(self):
        self.own_copies()[0].wait()
        self.own_copies()[1].start()
        for number in range(1, self.grid.zs):
            self.along_z(number)
        self.across(0)

    def stage_b(self):
        for number in range(1, self.grid.zs):
            self.across(number)
        self.last(0)

    def stage_c(self):
        for number in range(1, self.grid.zs):
            self.last(number)

    def finish(self):
        super().finish()
        self.own_copies()[1].wait()

    def middle(self):
        self.stage_a()
        self.stage_b()
        self.stage_c()

    def index(self, turn):
        return self.plan.span(turn)


def lane_gather():
    return LaneGather if paired_lanes() else SpanGather


def head_sums(values):
    width = values.shape[1]
    row = lax.broadcasted_iota(jnp.int32, (width, width), 0) // HEAD
    column = lax.broadcasted_iota(jnp.int32, (width, width), 1) // HEAD
    same = jnp.where(row == column, 1.0, 0.0)
    return jnp.dot(values, same, precision=lax.Precision.HIGHEST, preferred_element_type=f32)


def front_step(tokens, tail, gain, weights, taps, rates, lengths, pick, ident):
    span, width = tokens.shape
    block = weights.shape[1] // 3
    wide, narrow = lax.axis_size("wide"), lax.axis_size("narrow")
    devices = wide * narrow
    shards = LANE_WIDE * narrow
    shard_rows = span // shards
    kind = lane_gather()
    count = 4

    def kernel(*refs):
        tokens_ref, tail_ref, gain_ref, weights_ref, taps_ref, rates_ref, lengths_ref = refs[:7]
        keys_out, chunks_out, tile_out, key_out, query_out, value_out = refs[7:13]
        normed_out, ext_out, mixed_out, mean_out, gate_out = refs[13:18]
        tail_low, tile, send, recv = refs[18:22]
        g = Grid()
        me = g.wide * narrow + g.narrow
        plan = Plan(lengths_ref, None, lengths.shape[0])
        wait_all = g.greet_all()
        gather = kind(g, plan, key_out, keys_out, refs[22:])

        def normed_of(rows):
            values = rows.astype(f32)
            factor = lax.rsqrt(jnp.mean(values * values, axis=-1, keepdims=True) + eps_norm)
            return values * factor * gain_ref[...]

        normed = normed_of(tokens_ref[...])
        normed_out[...] = normed.astype(bf16)
        mean_out[...] = jnp.mean(normed, axis=0, keepdims=True)
        tail_low[...] = normed_of(tail_ref[...]).astype(bf16)
        begins = plan.begins(g.wide)

        def activated(third):
            columns = pl.ds(third * block, block)
            ext_out[pl.ds(0, 8), columns] = jnp.where(begins, 0.0, matmul(tail_low[...], weights_ref[:, columns]))
            ext_out[pl.ds(8, span), columns] = matmul(normed_out[...], weights_ref[:, columns])
            mixed = taps_ref[pl.ds(0, 1), columns] * ext_out[pl.ds(8, span), columns]
            for j in range(1, count):
                mixed = mixed + taps_ref[pl.ds(j, 1), columns] * ext_out[pl.ds(8 - j, span), columns]
            mixed_out[:, columns] = mixed
            return mixed * sigmoid(mixed)

        def normed_heads(values):
            return (values * lax.rsqrt(head_sums(values * values) + eps_head)).astype(bf16)

        key_out[...] = normed_heads(activated(1))
        wait_all()
        gather.begin()
        value_out[...] = activated(2).astype(bf16).reshape(shards, shard_rows, block)
        column = lax.broadcasted_iota(jnp.int32, (8, 128), 1)
        gates = jnp.zeros((8, 128), f32)
        for i in range(3):
            logit = jnp.sum(mean_out[...] * rates_ref[pl.ds(i, 1), :], axis=1, keepdims=True)
            gates = jnp.where(column == i, sigmoid(logit), gates)
        gate_out[...] = gates
        scale = jnp.where(column == 0, decay_top, jnp.where(column == 1, moment_top, learn_top))
        tile[...] = gates * scale

        def send_chunks(step, carry):
            target = lax.rem(me + step, devices)
            where = lax.div(target, narrow), lax.rem(target, narrow)
            remote(value_out.at[pick(*where)], chunks_out.at[me], send.at[0], recv.at[0], where).start()
            remote(tile, tile_out.at[me], send.at[1], recv.at[1], where).start()
            return carry

        lax.fori_loop(1, devices, send_chunks, 0)
        chunks_out[me] = value_out[pick(g.wide, g.narrow)]
        tile_out[me] = tile[...]
        query_out[...] = normed_heads(activated(0))
        gather.middle()
        for i, out in enumerate((chunks_out, tile_out)):
            others = out.at[pl.ds(0, devices - 1)]
            whole = remote(others, others, send.at[i], recv.at[i], g.partner)
            whole.wait_send()
            whole.wait_recv()
        gather.finish()

    vmem = pl.BlockSpec(memory_space=pltpu.VMEM)
    return pl.pallas_call(
        kernel,
        out_shape=[
            jax.ShapeDtypeStruct(kind.shape(span, block), bf16),
            jax.ShapeDtypeStruct((devices, shard_rows, block), bf16),
            jax.ShapeDtypeStruct((devices, 8, 128), f32),
            jax.ShapeDtypeStruct((span, block), bf16),
            jax.ShapeDtypeStruct((span, block), bf16),
            jax.ShapeDtypeStruct((shards, shard_rows, block), bf16),
            jax.ShapeDtypeStruct((span, width), bf16),
            jax.ShapeDtypeStruct((8 + span, 3 * block), f32),
            jax.ShapeDtypeStruct((span, 3 * block), f32),
            jax.ShapeDtypeStruct((1, width), f32),
            jax.ShapeDtypeStruct((8, 128), f32),
        ],
        in_specs=[vmem] * 6 + [pl.BlockSpec(memory_space=pltpu.SMEM)],
        out_specs=[ANY] + [vmem] * 10,
        scratch_shapes=[
            pltpu.VMEM((8, width), bf16),
            pltpu.VMEM((8, 128), f32),
            pltpu.SemaphoreType.DMA((2,)),
            pltpu.SemaphoreType.DMA((2,)),
        ]
        + kind.scratch(span, block),
        compiler_params=pltpu.CompilerParams(
            collective_id=ident, has_side_effects=True, vmem_limit_bytes=40 * 1024 * 1024
        ),
        name="front_step",
    )(tokens, tail, gain, weights, taps, rates, lengths)


def matmul(left_side, right_side):
    return jnp.dot(left_side, right_side, preferred_element_type=jnp.float32)


def inner_left(left_side, right_side):
    return lax.dot_general(left_side, right_side, (((0,), (0,)), ((), ())), preferred_element_type=jnp.float32)


def inner_right(left_side, right_side):
    return lax.dot_general(left_side, right_side, (((1,), (1,)), ((), ())), preferred_element_type=jnp.float32)


def silu_slope(values):
    sigmoid_val = sigmoid(values)
    return sigmoid_val * (1.0 + values * (1.0 - sigmoid_val))


def silu_curve(values):
    sigmoid_val = sigmoid(values)
    return sigmoid_val * (1.0 - sigmoid_val) * (2.0 + values * (1.0 - 2.0 * sigmoid_val))


class Lane:
    def __init__(self):
        narrow = lax.axis_size("narrow")
        self.ys = narrow // 2
        self.chips = LANE_WIDE * self.ys
        wide_pos, narrow_pos = lax.axis_index("wide"), lax.axis_index("narrow")
        self.base = lax.div(wide_pos, LANE_WIDE) * LANE_WIDE
        self.colour = lax.rem(narrow_pos, 2)
        self.chip = lax.rem(wide_pos, LANE_WIDE) * self.ys + lax.div(narrow_pos, 2)
        self.partner = (wide_pos, narrow_pos + 1 - 2 * self.colour)

    def other(self, step):
        return lax.rem(self.chip + step, self.chips)

    def device(self, chip):
        return self.base + lax.div(chip, self.ys), 2 * lax.rem(chip, self.ys) + self.colour

    def greet(self):
        barrier = pltpu.get_barrier_semaphore()
        for step in range(1, self.chips):
            pl.semaphore_signal(barrier, inc=1, device_id=self.device(self.other(step)), device_id_type=MESH)
        pl.semaphore_signal(barrier, inc=1, device_id=self.partner, device_id_type=MESH)
        pl.semaphore_wait(barrier, self.chips)


class Scatter:
    def __init__(self, lane, part, pair, half, got, sems, own=None):
        self.lane, self.part, self.pair, self.half, self.got, self.own = lane, part, pair, half, got, own
        self.pair_send, self.pair_recv, self.send, self.recv = sems

    @staticmethod
    def scratch(chips, rows, width, pair_type=f32):
        return [
            pltpu.VMEM((rows, width), f32),
            pltpu.VMEM((2, chips, rows, width), pair_type),
            pltpu.VMEM((chips, rows, width), pair_type),
            pltpu.VMEM((chips, rows, width), bf16),
            pltpu.VMEM((chips, rows, width), bf16),
            pltpu.SemaphoreType.DMA((1,)),
            pltpu.SemaphoreType.DMA((1,)),
            pltpu.SemaphoreType.DMA((chips,)),
            pltpu.SemaphoreType.DMA((chips,)),
        ]

    @classmethod
    def of(cls, lane, refs):
        return cls(lane, *refs[1:5], refs[5:9], refs[0])

    def pair_copy(self):
        return remote(
            self.part.at[1 - self.lane.colour],
            self.pair,
            self.pair_send.at[0],
            self.pair_recv.at[0],
            self.lane.partner,
        )

    def start_pair(self):
        self.pair_copy().start()

    def take_pair(self):
        self.pair_copy().wait()
        self.half[...] = (self.part[self.lane.colour].astype(f32) + self.pair[...].astype(f32)).astype(bf16)
        if self.own is None:
            self.got[self.lane.chip] = self.half[self.lane.chip]
        else:
            chip = self.lane.chip
            self.own[...] = self.part[self.lane.colour, chip].astype(f32) + self.pair[chip].astype(f32)

    def copy_to(self, step):
        chip = self.lane.other(step)
        return remote(
            self.half.at[chip],
            self.got.at[self.lane.chip],
            self.send.at[step],
            self.recv.at[self.lane.chip],
            self.lane.device(chip),
        )

    def start_sends(self):
        for step in range(1, self.lane.chips):
            self.copy_to(step).start()

    def total(self):
        result = self.got[self.lane.chip].astype(f32) if self.own is None else self.own[...]
        for step in range(1, self.lane.chips):
            chip = self.lane.other(step)
            remote(
                self.got.at[chip], self.got.at[chip], self.send.at[step], self.recv.at[chip], self.lane.device(chip)
            ).wait_recv()
            result = result + self.got[chip].astype(f32)
        return result

    def wait_sends(self):
        for step in range(1, self.lane.chips):
            self.copy_to(step).wait_send()


class Spread:
    def __init__(self, lane, whole, sems):
        self.lane, self.whole = lane, whole
        self.send, self.recv, self.pair_send, self.pair_recv = sems

    @staticmethod
    def scratch(chips, rows, width):
        return [pltpu.VMEM((2, chips, rows, width), bf16)] + [pltpu.SemaphoreType.DMA((chips,))] * 4

    @classmethod
    def of(cls, lane, refs):
        return cls(lane, refs[0], refs[1:5])

    def mine(self):
        return self.whole.at[self.lane.colour, self.lane.chip]

    def copy_to(self, step):
        return remote(
            self.mine(),
            self.mine(),
            self.send.at[step],
            self.recv.at[self.lane.chip],
            self.lane.device(self.lane.other(step)),
        )

    def pair_copy(self, chip, colour):
        place = self.whole.at[colour, chip]
        return remote(place, place, self.pair_send.at[chip], self.pair_recv.at[chip], self.lane.partner)

    def run(self):
        lane = self.lane
        for step in range(1, lane.chips):
            self.copy_to(step).start()
        self.pair_copy(lane.chip, lane.colour).start()
        for step in range(1, lane.chips):
            chip = lane.other(step)
            place = self.whole.at[lane.colour, chip]
            remote(place, place, self.send.at[step], self.recv.at[chip], lane.device(chip)).wait_recv()
            self.pair_copy(chip, lane.colour).start()
        for chip in range(lane.chips):
            self.pair_copy(chip, 1 - lane.colour).wait_recv()
        for step in range(1, lane.chips):
            self.copy_to(step).wait_send()
        for chip in range(lane.chips):
            self.pair_copy(chip, lane.colour).wait_send()


class Deliver:
    def __init__(self, grid, plan, chips, out, got, sems):
        self.grid, self.plan, self.chips, self.out, self.got = grid, plan, chips, out, got
        self.send, self.recv = sems
        self.wide, self.narrow = lax.axis_size("wide"), lax.axis_size("narrow")
        self.me = grid.wide * self.narrow + grid.narrow

    @staticmethod
    def scratch(kinds, rows, block):
        devices = lax.axis_size("wide") * lax.axis_size("narrow")
        return [pltpu.VMEM((devices, kinds, rows, block), bf16)] * 2 + [pltpu.SemaphoreType.DMA((1,))] * 2

    def start(self, kinds):
        block = self.out.shape[3]
        for span in range(self.wide):
            turn = self.plan.turn_of(span)
            for i, kind in enumerate(kinds):
                lane_rows = kind[turn]
                for n in range(self.narrow):
                    self.out[span * self.narrow + n, i] = lane_rows[:, n * block : (n + 1) * block]

        def push(step, carry):
            target = lax.rem(self.me + step, self.wide * self.narrow)
            where = lax.div(target, self.narrow), lax.rem(target, self.narrow)
            remote(self.out.at[target], self.got.at[self.me], self.send.at[0], self.recv.at[0], where).start()
            return carry

        lax.fori_loop(1, self.wide * self.narrow, push, 0)
        self.got[self.me] = self.out[self.me]

    def finish(self, result):
        others = self.got.at[pl.ds(0, self.wide * self.narrow - 1)]
        whole = remote(others, others, self.send.at[0], self.recv.at[0], self.grid.partner)
        whole.wait_send()
        whole.wait_recv()
        base = self.plan.lane_of(self.grid.wide) * LANE_WIDE
        ys = self.narrow // 2
        for p in range(LANE_WIDE):
            for y in range(ys):
                for colour in range(2):
                    source = (base + p) * self.narrow + 2 * y + colour
                    for i in range(result.shape[0]):
                        result[i, colour, p * ys + y] = self.got[source, i]


def chain_forward(keys, values, queries, lengths, gates, turns, first_init, second_init, ident):
    wide = lax.axis_size("wide")
    blocks, span, block = keys.shape[1:]
    width, hidden = first_init.shape
    rows = values.shape[1]
    sequences = lengths.shape[0]
    key_turns = turns - 1
    kind = lane_gather()
    own_rows = kind.scratch(span, block)
    per_turn, ask_from = (2, 2) if paired_lanes() else (1, 3)
    first_left = per_turn * (key_turns - ask_from)
    slots = 3
    stream_keys = not paired_lanes()
    chips = LANE_WIDE * (lax.axis_size("narrow") // 2)
    n_scatter = len(Scatter.scratch(1, 8, 128))

    def kernel(*refs):
        keys_hbm, values_hbm, own_hbm, lengths_ref, gates_ref, first_hbm, second_hbm = refs[:7]
        recalled_hbm, low1_hbm, low2_hbm, s1_hbm, s2_hbm, m1_hbm, m2_hbm, g1_hbm, g2_hbm = refs[7:16]
        err_hbm, pre_hbm, qpre_hbm, klane_hbm, qlane_hbm = refs[16:21]
        rest = refs[21:]
        kall, qall, vall, kcur, qcur, i1, i2, s1, s2, m1, m2, gb1, gb2, low1, low2 = rest[:15]
        pre, qpre, khid, rec, qpart, qpair, qhalf, qgot = rest[15:23]
        in_sem, out_sem, q_sem, q_pair_send, q_pair_recv, q_send, q_recv = rest[23:30]
        rest = rest[30:]
        lane = Lane()
        grid = Grid()
        plan = Plan(lengths_ref, gates_ref, sequences)
        lookup = Scatter.of(lane, rest[:n_scatter])
        error = Spread.of(lane, rest[n_scatter : n_scatter + 5])
        rest = rest[n_scatter + 5 :]
        gather = kind(grid, plan, own_hbm, qall, rest[: len(own_rows)])
        rest = rest[len(own_rows) :]
        deliver = Deliver(grid, plan, chips, *rest[:2], rest[2:4])
        result = rest[4]

        def recall(q, slot):
            sems = q_pair_send.at[pl.ds(q, 1)], q_pair_recv.at[pl.ds(q, 1)], q_send.at[q], q_recv.at[q]
            return Scatter(lane, qpart.at[slot], qpair.at[q], qhalf.at[slot], qgot.at[q], sems)

        def state_saves(turn):
            return [
                pltpu.make_async_copy(source, target.at[turn], out_sem.at[i])
                for i, (source, target) in enumerate(((m1, m1_hbm), (m2, m2_hbm), (kcur, klane_hbm), (s1, s1_hbm), (s2, s2_hbm)))
            ]

        def other_saves(turn):
            return [
                pltpu.make_async_copy(source, target.at[turn], out_sem.at[5 + i])
                for i, (source, target) in enumerate(
                    ((gb1, g1_hbm), (gb2, g2_hbm), (error.whole, err_hbm), (pre, pre_hbm))
                )
            ]

        def query_saves(q, slot):
            return [
                pltpu.make_async_copy(source.at[slot], target.at[q], q_sem.at[slot, i])
                for i, (source, target) in enumerate(((qcur, qlane_hbm), (qpre, qpre_hbm)))
            ]

        inputs = [
            pltpu.make_async_copy(source, target, in_sem.at[i])
            for i, (source, target) in enumerate(
                ((first_hbm, i1), (second_hbm, i2), (keys_hbm, kall), (values_hbm, vall))
            )
            if not (stream_keys and i == 2)
        ]
        for copy in inputs:
            copy.start()
        grid.greet_all()()
        gather.begin()
        for copy in inputs:
            copy.wait()
        low1[0] = i1[...]
        low2[0] = i2[...]
        s1[...] = i1[...].astype(f32)
        s2[...] = i2[...].astype(f32)
        for ref in (m1, m2):
            ref[...] = jnp.zeros_like(ref)

        def lookup_blocks(buf, first):
            total = matmul(buf[0], first[pl.ds(0, block), :])
            for b in range(1, blocks):
                total = total + matmul(buf[b], first[pl.ds(b * block, block), :])
            return total

        def ask(q, slot, waits):
            def settle():
                recall(q - slots, slot).wait_sends()
                for copy in query_saves(q - slots, slot):
                    copy.wait()

            if waits is True:
                settle()
            elif waits is not False:
                pl.when(waits)(settle)
            index = gather.index(q)
            for b in range(blocks):
                qcur[slot, b] = qall[index, b]
            query_pre = lookup_blocks(qcur.at[slot], low1.at[q])
            qpre[slot] = query_pre
            for copy in query_saves(q, slot):
                copy.start()
            query_hidden = (query_pre * sigmoid(query_pre)).astype(bf16)
            qpart[slot] = matmul(query_hidden, low2[q]).astype(bf16).reshape(2, chips, rows, width)
            recall(q, slot).start_pair()

        def turn_body(turn, carry):
            index = plan.span(turn)
            if stream_keys:
                one = pltpu.make_async_copy(keys_hbm.at[turn], kcur, in_sem.at[2])
                one.start()
                one.wait()
            else:
                for b in range(blocks):
                    kcur[b] = kall[gather.index(turn), b]
            for copy in state_saves(turn):
                copy.start()
            key_pre = lookup_blocks(kcur, low1.at[turn])
            pre[0] = key_pre
            khid[...] = (key_pre * sigmoid(key_pre)).astype(bf16)
            lookup.part[...] = matmul(khid[...], low2[turn]).reshape(2, chips, rows, width)
            lookup.start_pair()

            @pl.when(turn == ask_from)
            def _():
                gather.finish()

            first = per_turn * (turn - ask_from)

            @pl.when(turn >= ask_from)
            def _():
                ask(first, lax.rem(first, slots), first >= slots)

            lookup.take_pair()
            lookup.start_sends()

            @pl.when(turn >= ask_from)
            def _():
                recall(first, lax.rem(first, slots)).take_pair()
                for j in range(1, per_turn):
                    ask(first + j, lax.rem(first + j, slots), first + j >= slots)

            if paired_lanes():
                pl.when(turn == 1)(gather.stage_b)

            total = lookup.total()
            target = jnp.concatenate([vall[index * blocks + b] for b in range(blocks)], axis=1)
            error.whole[lane.colour, lane.chip] = ((total - target.astype(f32)) / span).astype(bf16)
            error.run()
            lookup.wait_sends()

            @pl.when(turn >= ask_from)
            def _():
                recall(first, lax.rem(first, slots)).start_sends()
                for j in range(1, per_turn):
                    stream = recall(first + j, lax.rem(first + j, slots))
                    stream.take_pair()
                    stream.start_sends()

            if paired_lanes():
                pl.when(turn == 0)(gather.stage_a)
                pl.when(turn == 1)(gather.stage_c)

            err = error.whole[...].reshape(span, width)
            grad_second = inner_left(khid[...], err)
            hidden_grad = inner_right(err, low2[turn])
            pre[1] = hidden_grad
            slope = (hidden_grad * silu_slope(pre[0])).astype(bf16)
            decay, moment, rate = plan.rates(turn)
            reset = plan.first(turn + 1)
            for copy in state_saves(turn):
                copy.wait()
            following = jnp.minimum(turn + 1, turns - 1)

            def update(s, m, init, low, grad, place):
                moment_new = moment * m[place] - rate * grad
                state_new = (1.0 - decay) * s[place] + moment_new
                state_new = reset * init[place].astype(f32) + (1.0 - reset) * state_new
                moment_new = (1.0 - reset) * moment_new
                m[place] = moment_new
                s[place] = state_new
                low[(following,) + place] = state_new.astype(bf16)

            gb2[...] = grad_second
            update(s2, m2, i2, low2, grad_second, (slice(None), slice(None)))
            for b in range(blocks):
                grad_first = inner_left(kcur[b], slope)
                place = (pl.ds(b * block, block), slice(None))
                gb1[place] = grad_first
                update(s1, m1, i1, low1, grad_first, place)
            saves = other_saves(turn)
            for copy in saves:
                copy.start()

            if not paired_lanes():
                pl.when(turn == 0)(gather.stage_a)
                pl.when(turn == 1)(gather.stage_b)
                pl.when(turn == 2)(gather.stage_c)

            for copy in saves:
                copy.wait()
            return carry

        lax.fori_loop(0, key_turns, turn_body, 0)
        ends = [
            pltpu.make_async_copy(low1, low1_hbm, out_sem.at[0]),
            pltpu.make_async_copy(low2, low2_hbm, out_sem.at[1]),
        ]
        for copy in ends:
            copy.start()
        left = list(range(first_left, turns))
        for q in left:
            ask(q, q % slots, q >= slots)
            if q > left[0]:
                stream = recall(q - 1, (q - 1) % slots)
                stream.take_pair()
                stream.start_sends()
        stream = recall(turns - 1, (turns - 1) % slots)
        stream.take_pair()
        stream.start_sends()
        for q in range(turns):
            rec[q] = recall(q, q % slots).total().astype(bf16)
        deliver.start([rec])
        for q in range(turns - slots, turns):
            recall(q, q % slots).wait_sends()
        for q in range(turns - slots, turns):
            for copy in query_saves(q, q % slots):
                copy.wait()
        deliver.finish(result)
        last = pltpu.make_async_copy(result.at[0], recalled_hbm, out_sem.at[2])
        last.start()
        for copy in ends + [last]:
            copy.wait()

    state = [(width, hidden), (hidden, width)]
    out_shape = (
        [jax.ShapeDtypeStruct((2, chips, rows, block), bf16)]
        + [jax.ShapeDtypeStruct((turns,) + s, bf16) for s in state]
        + [jax.ShapeDtypeStruct((key_turns,) + s, f32) for s in state * 3]
        + [
            jax.ShapeDtypeStruct((key_turns, 2, chips, rows, width), bf16),
            jax.ShapeDtypeStruct((key_turns, 2, span, hidden), f32),
            jax.ShapeDtypeStruct((turns, span, hidden), f32),
            jax.ShapeDtypeStruct((key_turns, blocks, span, block), bf16),
            jax.ShapeDtypeStruct((turns, blocks, span, block), bf16),
        ]
    )
    sem = pltpu.SemaphoreType.DMA
    scratch = (
        [pltpu.VMEM((1 if stream_keys else keys.shape[0], blocks, span, block), bf16), pltpu.VMEM(kind.shape(span, block), bf16)]
        + [pltpu.VMEM(values.shape, bf16)]
        + [pltpu.VMEM((blocks, span, block), bf16), pltpu.VMEM((slots, blocks, span, block), bf16)]
        + [pltpu.VMEM(s, bf16) for s in state]
        + [pltpu.VMEM(s, f32) for s in state * 3]
        + [pltpu.VMEM((turns,) + s, bf16) for s in state]
        + [
            pltpu.VMEM((2, span, hidden), f32),
            pltpu.VMEM((slots, span, hidden), f32),
            pltpu.VMEM((span, hidden), bf16),
            pltpu.VMEM((turns, rows, width), bf16),
            pltpu.VMEM((slots, 2, chips, rows, width), bf16),
        ]
        + [pltpu.VMEM((n, chips, rows, width), bf16) for n in (turns, slots, turns)]
        + [sem((4,)), sem((9,)), sem((slots, 2)), sem((turns,)), sem((turns,)), sem((turns, chips)), sem((turns, chips))]
        + Scatter.scratch(chips, rows, width)
        + Spread.scratch(chips, rows, width)
        + own_rows
        + Deliver.scratch(1, rows, block)
        + [pltpu.VMEM((1, 2, chips, rows, block), bf16)]
    )
    smem = pl.BlockSpec(memory_space=pltpu.SMEM)
    return pl.pallas_call(
        kernel,
        out_shape=out_shape,
        in_specs=[ANY] * 3 + [smem] * 2 + [ANY] * 2,
        out_specs=[ANY] * len(out_shape),
        scratch_shapes=scratch,
        compiler_params=pltpu.CompilerParams(
            collective_id=ident, has_side_effects=True, vmem_limit_bytes=62 * 1024 * 1024
        ),
        cost_estimate=pl.CostEstimate(
            flops=40 * turns * 2 * span * width * hidden, bytes_accessed=turns * 40 * 2**20, transcendentals=0
        ),
        name="chain_forward",
    )(keys, values, queries, lengths, gates, first_init, second_init)


def chain_backward(recall_grad, saved, lengths, gates, ident):
    low1_all, low2_all, s1_all, s2_all, m1_all, m2_all, g1_all, g2_all, err_all, pre_all, qpre_all, keys, queries = saved
    wide = lax.axis_size("wide")
    devices = wide * lax.axis_size("narrow")
    key_turns, blocks, span, block = keys.shape
    turns = key_turns + 1
    width, hidden = low1_all.shape[1:]
    chips, rows = err_all.shape[2:4]
    n_scatter = len(Scatter.scratch(1, 8, 128))
    kind = lane_gather()
    own_rows = kind.scratch(span, block)

    def kernel(*refs):
        own_hbm, q_ins, k_ins, lengths_ref, gates_ref = refs[0], refs[1:5], refs[5:14], refs[14], refs[15]
        cots_hbm, sums_out, mg1_hbm, mg2_hbm = refs[16:20]
        rest = refs[20:]
        q_bufs, k_bufs, rest = rest[:4], rest[4:13], rest[13:]
        qbuf, low1, low2, qpre = q_bufs
        kbuf, s1, s2, m1, m2, g1, g2, errs, pre = k_bufs
        rall, cf, cs, cmf, cms, w1, w2, a1, a2, c1, c2 = rest[:11]
        dh, khid, qpl, qhid, kpl, slow, sg, hk, qcots, kcots, vcots, sumrows, tile, mb1, mb2, result = rest[11:27]
        q_sem, k_sem, end_sem, tile_send, tile_recv = rest[27:32]
        rest = rest[32:]
        lane = Lane()
        grid = Grid()
        plan = Plan(lengths_ref, gates_ref, lengths.shape[0])
        lookup = Scatter.of(lane, rest[:n_scatter])
        qstream = Scatter.of(lane, rest[n_scatter : 2 * n_scatter])
        kstream = Scatter.of(lane, rest[2 * n_scatter : 3 * n_scatter])
        spread = Spread.of(lane, rest[3 * n_scatter : 3 * n_scatter + 5])
        rest = rest[3 * n_scatter + 5 :]
        gather = kind(grid, plan, own_hbm, rall, rest[: len(own_rows)])
        rest = rest[len(own_rows) :]
        deliver = Deliver(grid, plan, chips, *rest[:2], rest[2:4])

        def q_loads(turn, slot):
            return [
                pltpu.make_async_copy(source.at[turn], target.at[slot], q_sem.at[slot, i])
                for i, (source, target) in enumerate(zip(q_ins, q_bufs))
            ]

        def k_loads(turn, slot):
            return [
                pltpu.make_async_copy(source.at[turn], target.at[slot], k_sem.at[slot, i])
                for i, (source, target) in enumerate(zip(k_ins, k_bufs))
            ]

        grid.greet_all()()
        gather.begin()
        for copy in q_loads(turns - 1, 0) + q_loads(turns - 2, 1) + k_loads(turns - 2, 1):
            copy.start()
        for ref in (cf, cs, cmf, cms, a1, a2):
            ref[...] = jnp.zeros_like(ref)
        gather.middle()
        gather.finish()

        kcots[turns - 1] = jnp.zeros((rows, width), bf16)
        vcots[turns - 1] = jnp.zeros((rows, width), bf16)
        sumrows[turns - 1] = jnp.zeros((8, 128), f32)

        def finish(stream, save, turn):
            save[turn] = stream.total().astype(bf16)
            stream.wait_sends()

        def query_rows(turn, slot):
            index = gather.index(turn)
            back = inner_right(rall[index, 0], low2[slot, :, pl.ds(0, block)])
            for b in range(1, blocks):
                back = back + inner_right(rall[index, b], low2[slot, :, pl.ds(b * block, block)])
            query_pre = qpre[slot]
            qpl[...] = (plan.valid(turn) * back * silu_slope(query_pre)).astype(bf16)
            qhid[...] = (query_pre * sigmoid(query_pre)).astype(bf16)
            qstream.part[...] = inner_right(qpl[...], low1[slot]).astype(bf16).reshape(2, chips, rows, width)
            qstream.start_pair()

        def query_weights(turn, slot):
            index = gather.index(turn)
            valid = plan.valid(turn)
            for b in range(blocks):
                w1[pl.ds(b * block, block), :] = inner_left(qbuf[slot, b], qpl[...])
                w2[:, pl.ds(b * block, block)] = valid * inner_left(qhid[...], rall[index, b])

        def key_rows(slot):
            kstream.part[...] = (
                (inner_right(kpl[...], low1[slot]) + inner_right(slow[...], c1[slot]))
                .reshape(2, chips, rows, width)
            )

        for copy in q_loads(turns - 1, 0):
            copy.wait()
        query_rows(turns - 1, 0)
        query_weights(turns - 1, 0)
        reset = plan.first(turns - 1)
        for c, w, acc in ((cf, w1, a1), (cs, w2, a2)):
            acc[...] = reset * w[...]
            c[...] = (1.0 - reset) * w[...]
        qstream.take_pair()
        qstream.start_sends()

        def body(step, carry):
            turn = turns - 1 - step
            slot = lax.rem(step, 2)
            decay, moment, rate = plan.rates(turn)
            reset = plan.first(turn)
            for copy in q_loads(turn, slot) + k_loads(turn, slot):
                copy.wait()
            c1[slot] = (-rate * (cmf[...] + cf[...])).astype(bf16)
            c2[...] = (-rate * (cms[...] + cs[...])).astype(bf16)
            slope_grad = matmul(kbuf[slot, 0], c1[slot, pl.ds(0, block), :])
            for b in range(1, blocks):
                slope_grad = slope_grad + matmul(kbuf[slot, b], c1[slot, pl.ds(b * block, block), :])
            sg[...] = slope_grad
            key_pre = pre[slot, 0]
            khid[...] = (key_pre * sigmoid(key_pre)).astype(bf16)
            dh[...] = (slope_grad * silu_slope(key_pre)).astype(bf16)
            lookup.part[...] = (
                (matmul(khid[...], c2[...]) + matmul(dh[...], low2[slot])).reshape(2, chips, rows, width)
            )
            lookup.start_pair()
            finish(qstream, qcots, turn + 1)

            @pl.when(step > 2)
            def _():
                finish(kstream, kcots, turn + 2)

            lookup.take_pair()
            lookup.start_sends()
            query_rows(turn, slot)

            @pl.when(step > 1)
            def _():
                key_rows(1 - slot)
                kstream.start_pair()

            @pl.when(step + 1 < turns)
            def _():
                for copy in q_loads(turn - 1, 1 - slot) + k_loads(turn - 1, 1 - slot):
                    copy.start()

            query_weights(turn, slot)
            err = errs[slot].reshape(span, width)
            hk[...] = inner_right(err, c2[...])
            w2[...] += inner_left(dh[...], err)

            def whole_sum(first_a, first_b, second_a, second_b):
                first = jnp.sum(first_a * first_b, axis=0, keepdims=True)
                second = jnp.sum(second_a * second_b, axis=0, keepdims=True)
                return jnp.sum(first, axis=1, keepdims=True) + jnp.sum(second, axis=1, keepdims=True)

            kinds = (
                whole_sum(cf[...], s1[slot], cs[...], s2[slot]),
                whole_sum(cmf[...] + cf[...], m1[slot], cms[...] + cs[...], m2[slot]),
                whole_sum(cmf[...] + cf[...], g1[slot], cms[...] + cs[...], g2[slot]),
            )
            column = lax.broadcasted_iota(jnp.int32, (8, 128), 1)
            sumrow = jnp.zeros((8, 128), f32)
            for i, kind in enumerate(kinds):
                sumrow = jnp.where(column == i, kind, sumrow)
            sumrows[turn] = sumrow
            qstream.take_pair()
            total = lookup.total()
            mine = (total / span).astype(bf16)
            spread.whole[lane.colour, lane.chip] = mine
            vcots[turn] = mine
            spread.run()
            lookup.wait_sends()
            qstream.start_sends()

            @pl.when(step > 1)
            def _():
                kstream.take_pair()
                kstream.start_sends()

            out = spread.whole[...].reshape(span, width)
            hidden_back = hk[...] + inner_right(out, low2[slot])
            key_pre = pre[slot, 0]
            hidden_grad = pre[slot, 1]
            slope = silu_slope(key_pre)
            kpl[...] = (hidden_back * slope + sg[...] * hidden_grad * silu_curve(key_pre)).astype(bf16)
            slow[...] = (hidden_grad * slope).astype(bf16)

            def update(c, m, acc, grad_new, place):
                grad = (1.0 - decay) * c[place] + grad_new
                both = m[place] + c[place]
                acc[place] += reset * grad
                c[place] = (1.0 - reset) * grad
                m[place] = (1.0 - reset) * (moment * both)

            for b in range(blocks):
                place = (pl.ds(b * block, block), slice(None))
                update(cf, cmf, a1, w1[place] + inner_left(kbuf[slot, b], kpl[...]), place)
            place = (slice(None), slice(None))
            update(cs, cms, a2, w2[...] + inner_left(khid[...], out), place)
            return carry

        lax.fori_loop(1, turns, body, 0)
        tail = Scatter(
            lane,
            kstream.part,
            lookup.pair,
            lookup.half,
            lookup.got,
            (lookup.pair_send, lookup.pair_recv, lookup.send, lookup.recv),
            lookup.own,
        )
        key_rows((turns - 1) % 2)
        tail.start_pair()
        mb1[...] = a1[...].astype(bf16).reshape(mb1.shape)
        for owner in range(wide):
            mb2[owner] = a2[:, owner * (width // wide) : (owner + 1) * (width // wide)].astype(bf16)
        ends = [
            pltpu.make_async_copy(mb1, mg1_hbm, end_sem.at[0]),
            pltpu.make_async_copy(mb2, mg2_hbm, end_sem.at[1]),
        ]
        for copy in ends:
            copy.start()
        for span_number in range(wide):
            here = jnp.where(plan.lane_of(span_number) == plan.lane, 1.0, 0.0)
            tile[pl.ds(span_number, 1), :] = here * sumrows[plan.turn_of(span_number)][:1]

        def send_tile(step, carry):
            target = lax.rem(deliver.me + step, devices)
            where = lax.div(target, blocks), lax.rem(target, blocks)
            remote(tile, sums_out.at[deliver.me], tile_send.at[0], tile_recv.at[0], where).start()
            return carry

        lax.fori_loop(1, devices, send_tile, 0)
        sums_out[deliver.me] = tile[...]
        finish(qstream, qcots, 0)
        if turns > 2:
            finish(kstream, kcots, 1)
        tail.take_pair()
        tail.start_sends()
        finish(tail, kcots, 0)
        deliver.start([qcots, kcots, vcots])
        others = sums_out.at[pl.ds(0, devices - 1)]
        tiles = remote(others, others, tile_send.at[0], tile_recv.at[0], grid.partner)
        tiles.wait_send()
        tiles.wait_recv()
        deliver.finish(result)
        ends.append(pltpu.make_async_copy(result, cots_hbm, end_sem.at[2]))
        ends[2].start()
        for copy in ends:
            copy.wait()

    state = [(width, hidden), (hidden, width)]
    q_buffers = [((blocks, span, block), bf16)] + [(s, bf16) for s in state] + [((span, hidden), f32)]
    k_buffers = (
        [((blocks, span, block), bf16)]
        + [(s, f32) for s in state * 3]
        + [((2, chips, rows, width), bf16), ((2, span, hidden), f32)]
    )
    by_owner = [(wide, width // wide, hidden), (wide, hidden, width // wide)]
    out_shape = [
        jax.ShapeDtypeStruct((3, 2, chips, rows, block), bf16),
        jax.ShapeDtypeStruct((devices, wide, 128), f32),
    ] + [jax.ShapeDtypeStruct(s, bf16) for s in by_owner]
    sem = pltpu.SemaphoreType.DMA
    scratch = (
        [pltpu.VMEM((2,) + s, t) for s, t in q_buffers + k_buffers]
        + [pltpu.VMEM(kind.shape(span, block), bf16)]
        + [pltpu.VMEM(s, f32) for s in state * 4]
        + [pltpu.VMEM((2,) + state[0], bf16), pltpu.VMEM(state[1], bf16)]
        + [pltpu.VMEM((span, hidden), bf16)] * 6
        + [pltpu.VMEM((span, hidden), f32)] * 2
        + [pltpu.VMEM((turns, rows, width), bf16)] * 3
        + [pltpu.VMEM((turns, 8, 128), f32), pltpu.VMEM((wide, 128), f32)]
        + [pltpu.VMEM(s, bf16) for s in by_owner]
        + [pltpu.VMEM((3, 2, chips, rows, block), bf16)]
        + [sem((2, 4)), sem((2, 9)), sem((3,)), sem((1,)), sem((1,))]
        + Scatter.scratch(chips, rows, width)
        + Scatter.scratch(chips, rows, width, bf16)
        + Scatter.scratch(chips, rows, width)
        + Spread.scratch(chips, rows, width)
        + own_rows
        + Deliver.scratch(3, rows, block)
    )
    vmem = pl.BlockSpec(memory_space=pltpu.VMEM)
    smem = pl.BlockSpec(memory_space=pltpu.SMEM)
    return pl.pallas_call(
        kernel,
        out_shape=out_shape,
        in_specs=[ANY] * 14 + [smem] * 2,
        out_specs=[ANY, vmem, ANY, ANY],
        scratch_shapes=scratch,
        compiler_params=pltpu.CompilerParams(
            collective_id=ident, has_side_effects=True, vmem_limit_bytes=63 * 1024 * 1024
        ),
        cost_estimate=pl.CostEstimate(
            flops=80 * turns * 2 * span * width * hidden, bytes_accessed=turns * 60 * 2**20, transcendentals=0
        ),
        name="chain_backward",
    )(
        recall_grad, queries, low1_all, low2_all, qpre_all, keys, s1_all, s2_all, m1_all, m2_all, g1_all, g2_all, err_all, pre_all,
        lengths, gates,
    )


def from_behind(value, axis, steps):
    count = lax.axis_size(axis)
    first, last = (max(0, -steps), min(count, count - steps))
    return lax.ppermute(value, axis, [(source, source + steps) for source in range(first, last)])


def split_heads(values, head_size):
    return values.reshape(values.shape[:-1] + (values.shape[-1] // head_size, head_size))


def head_norm(values, head_size):
    shaped = split_heads(values, head_size)
    factor = lax.rsqrt(jnp.sum(shaped * shaped, axis=-1, keepdims=True) + eps_head)
    return (shaped * factor).reshape(values.shape)


def head_norm_back(values, upstream, head_size):
    shaped = split_heads(values, head_size)
    grad_shaped = split_heads(upstream, head_size)
    factor = lax.rsqrt(jnp.sum(shaped * shaped, axis=-1, keepdims=True) + eps_head)
    normed = shaped * factor
    inner_sum = jnp.sum(normed * grad_shaped, axis=-1, keepdims=True)
    return (factor * (grad_shaped - normed * inner_sum)).reshape(values.shape)


def rms_back(scaled, factor, upstream):
    return factor * (upstream - scaled * jnp.mean(upstream * scaled, axis=-1, keepdims=True))


def body(
    tokens,
    cotangent,
    seq_spans,
    w_query,
    w_key,
    w_value,
    conv_kernel,
    persistent,
    norm_gain,
    rate_proj,
    out_gate,
    out_proj,
    memory_in,
    memory_out,
    ffn_gain,
    ffn_gate,
    ffn_up,
    ffn_down,
):
    wide, narrow = lax.axis_size("wide"), lax.axis_size("narrow")
    devices = wide * narrow
    wide_pos, narrow_pos = lax.axis_index("wide"), lax.axis_index("narrow")
    span, width = tokens.shape
    taps = conv_kernel.shape[0]
    persist_count = persistent.shape[1]
    local_width = out_gate.shape[1]
    own_rows = span // narrow
    lanes = wide // LANE_WIDE
    chips = LANE_WIDE * narrow // 2
    shards = 2 * chips
    shard_rows = span // shards
    hidden = memory_in.shape[1] // LANE_WIDE
    score_scale = math.sqrt(HEAD)

    def shard_of(tw, tn):
        return lax.rem(tn, 2) * chips + lax.rem(tw, LANE_WIDE) * (narrow // 2) + lax.div(tn, 2)

    long_turns = min(6, wide * 5 // 8)
    turns = max(long_turns, wide - long_turns)
    is_first = False
    start = 0
    for i in range(seq_spans.shape[0]):
        is_first = is_first | (wide_pos == start)
        start = start + seq_spans[i]

    smalls = [conv_kernel, persistent, norm_gain, ffn_gain, rate_proj]
    small_sizes = [a.size for a in smalls]
    packed = jnp.concatenate([a.reshape(-1) for a in smalls])
    padded = -(-packed.size // 2048) * 2048
    packed = jnp.pad(packed, (0, padded - packed.size)).reshape(-1, 128)
    own_weights = jnp.concatenate(
        [a.reshape(a.shape[0], narrow, local_width) for a in (w_query, w_key, w_value)], 2
    ).transpose(1, 0, 2)
    memory_cols = memory_in.reshape(memory_in.shape[0], LANE_WIDE, hidden).transpose(1, 0, 2)
    memory_rows = memory_out.reshape(LANE_WIDE, hidden, memory_out.shape[1])
    small_all, weights_all, first_all, second_all, tail_tokens = send_parameters(
        packed, own_weights, [memory_cols, memory_rows], tokens, 1
    )
    first_init = first_all.reshape(width, hidden)
    second_init = second_all.transpose(1, 0, 2).reshape(hidden, width)
    small_all = small_all.reshape(devices, padded)
    pieces, at = [], 0
    for a, size in zip(smalls, small_sizes):
        pieces.append(small_all[:, at : at + size].reshape((devices,) + a.shape))
        at += size
    kernel_all = pieces[0].transpose(1, 0, 2).reshape(taps, 3, width)
    persist_all = pieces[1].transpose(1, 2, 0, 3).reshape(2, persist_count, width)
    gain_one = pieces[2].reshape(width).astype(f32)
    gain_two = pieces[3].reshape(width).astype(f32)
    rate_f = pieces[4].reshape(width, 3).astype(f32)
    col_offset = narrow_pos * local_width

    def own_cols(values, axis):
        return lax.dynamic_slice_in_dim(values, col_offset, local_width, axis)

    def own_part(values):
        return lax.dynamic_slice_in_dim(values, narrow_pos * own_rows, own_rows, 0)

    kernel_f = own_cols(kernel_all, 2).reshape(taps, 3 * local_width).astype(f32)
    persist_f = own_cols(persist_all, 2).astype(f32)
    qkv_weights = weights_all.reshape(width, 3 * local_width)

    key_all, value_got, gate_got, key_low, query_low, value_low, normed_low, extended, mixed_conv, span_mean, gate_tile = (
        front_step(
            tokens,
            tail_tokens,
            gain_one[None],
            qkv_weights,
            jnp.pad(kernel_f, ((0, 8 - taps), (0, 0))),
            jnp.pad(rate_f.T, ((0, 5), (0, 0))),
            seq_spans,
            shard_of,
            2,
        )
    )
    value_low = value_low.reshape(span, local_width)
    span_mean, gate_sig = span_mean[0], gate_tile[0, :3]
    gate_scale = jnp.array([decay_top, moment_top, learn_top], f32)
    later = (ffn_gate, ffn_up, ffn_down, jnp.concatenate([out_gate, out_proj.T], 1))
    key_all, *later = lax.optimization_barrier((key_all,) + later)
    out_weights = lax.all_gather(later[3], "wide", axis=0, tiled=True)
    ffn_gate_cols = lax.all_gather(later[0], "wide", axis=0, tiled=True)
    ffn_up_cols = lax.all_gather(later[1], "wide", axis=0, tiled=True)
    ffn_down_rows = lax.all_gather(later[2], "wide", axis=1, tiled=True)
    gate_cols = out_weights[:, :local_width]
    proj_cols = out_weights[:, local_width:]
    gate_rows = gate_got[::narrow, 0, :3]
    if not paired_lanes():
        long_start = (jnp.cumsum(seq_spans) - seq_spans)[jnp.argmax(seq_spans)]
        turn_order = jnp.arange(turns, dtype=jnp.int32)
        rest_order = jnp.where(turn_order < long_start, turn_order, turn_order + long_turns)
        lane_spans = jnp.where(wide_pos // LANE_WIDE == 0, long_start + turn_order, rest_order)
        key_all = key_all[jnp.clip(lane_spans, 0, wide - 1)]
    chain = chain_forward(
        key_all, value_got, query_low, seq_spans, gate_rows, turns, first_init, second_init, 3
    )
    recall_low, saved = chain[0].reshape(span, local_width), chain[1:]
    recall_own = recall_low.astype(f32)

    keys_all = jnp.concatenate(
        [head_norm(persist_f[0], HEAD).astype(bf16), head_norm(recall_own, HEAD).astype(bf16), key_low], 0
    )
    values_all = jnp.concatenate([persist_f[1].astype(bf16), recall_low, value_low], 0)
    query_heads = split_heads(query_low, HEAD)
    key_heads = split_heads(keys_all, HEAD)
    value_heads = split_heads(values_all, HEAD)
    key_total = keys_all.shape[0]
    row_index = lax.broadcasted_iota(jnp.int32, (span, key_total), 0)
    col_index = lax.broadcasted_iota(jnp.int32, (span, key_total), 1)
    allowed = (col_index < persist_count + span) | (col_index - persist_count - span <= row_index)

    def score_block():
        raw_scores = (
            jnp.einsum("thd,jhd->htj", query_heads, key_heads, preferred_element_type=f32) * score_scale
        )
        return jnp.where(allowed[None], raw_scores, masked_score)

    scores = score_block()
    row_top = jnp.max(scores, axis=-1, keepdims=True)
    exponent = jnp.exp(scores - row_top)
    total_sum = jnp.sum(exponent, axis=-1, keepdims=True)
    log_total = row_top + jnp.log(total_sum)
    weights_low = (exponent / total_sum).astype(bf16)
    attended = jnp.einsum("htj,jhd->thd", weights_low, value_heads, preferred_element_type=f32).reshape(
        span, local_width
    )
    gate_pre = matmul(normed_low, gate_cols)
    gate_sigmoid = jax.nn.sigmoid(gate_pre)
    gated_low = (attended * gate_sigmoid).astype(bf16)

    def by_rows(part):
        return part.reshape(narrow, own_rows, width)

    tokens_own, cotangent_own = own_part(tokens), own_part(cotangent)
    rows_f32, row_f32 = ((own_rows, width), f32), ((1, width), f32)

    def scaled_of(values):
        factor = lax.rsqrt(jnp.mean(values * values, axis=-1, keepdims=True) + eps_norm)
        return values * factor, factor

    def after_branch(totals, extras):
        tokens_rows, gain = extras
        middle = tokens_rows.astype(f32) + totals[0]
        return [(scaled_of(middle)[0] * gain).astype(bf16)], [middle]

    normed_two, middle = narrow_step(
        [by_rows(inner_right(gated_low, proj_cols))],
        [tokens_own, gain_two[None]],
        after_branch,
        1,
        [rows_f32],
        7,
    )
    normed_two = normed_two.reshape(span, width)
    gate_val = matmul(normed_two, ffn_gate_cols)
    up_val = matmul(normed_two, ffn_up_cols)
    gate_silu = jax.nn.silu(gate_val)
    hidden_ffn = (gate_silu * up_val).astype(bf16)
    ffn_part = matmul(hidden_ffn, ffn_down_rows)
    down_grad = inner_left(cotangent, hidden_ffn).astype(bf16)
    hidden_grad_ffn = inner_right(cotangent, ffn_down_rows)
    gate_sig_ffn = jax.nn.sigmoid(gate_val)
    gate_grad_low = (
        hidden_grad_ffn * up_val * gate_sig_ffn * (1.0 + gate_val * (1.0 - gate_sig_ffn))
    ).astype(bf16)
    up_grad_low = (hidden_grad_ffn * gate_silu).astype(bf16)
    ffn_gate_grad = inner_left(normed_two, gate_grad_low).astype(bf16)
    ffn_up_grad = inner_left(normed_two, up_grad_low).astype(bf16)
    normed_two_part = inner_right(gate_grad_low, ffn_gate_cols) + inner_right(up_grad_low, ffn_up_cols)

    def scatter_wide(grad):
        return lax.psum_scatter(grad.astype(bf16), "wide", scatter_dimension=0, tiled=True).astype(f32)

    ffn_sums = (by_rows(ffn_part), by_rows(normed_two_part))
    ffn_sums, ffn_grads = lax.optimization_barrier((ffn_sums, (ffn_gate_grad, ffn_up_grad, down_grad)))
    ffn_gate_out, ffn_up_out, ffn_down_out = [scatter_wide(a) for a in ffn_grads]

    def after_ffn(totals, extras):
        middle_rows, cotangent_rows, gain = extras
        scaled, factor = scaled_of(middle_rows)
        grad = cotangent_rows.astype(f32) + rms_back(scaled, factor, totals[1] * gain)
        gain_part = jnp.sum(totals[1] * scaled, axis=0, keepdims=True)
        return [grad.astype(bf16), (middle_rows + totals[0]).astype(bf16)], [grad, gain_part]

    branch_low, output, middle_grad, gain_two_part = narrow_step(
        list(ffn_sums), [middle, cotangent_own, gain_two[None]], after_ffn, 2, [rows_f32, row_f32], 9
    )
    branch_low, output = branch_low.reshape(span, width), output.reshape(span, width)

    gated_grad = matmul(branch_low, proj_cols)
    attended_grad_low = (gated_grad * gate_sigmoid).astype(bf16)
    gate_pre_low = (gated_grad * attended * gate_sigmoid * (1.0 - gate_sigmoid)).astype(bf16)
    early_grads = jnp.concatenate([inner_left(normed_low, gate_pre_low), inner_left(branch_low, gated_low)], 1)
    early_grads = early_grads.astype(bf16)

    weights_again = jnp.exp(score_block() - log_total)
    grad_heads = split_heads(attended_grad_low, HEAD)
    weight_grad = jnp.einsum("thd,jhd->htj", grad_heads, value_heads, preferred_element_type=f32)
    row_delta = jnp.sum(weights_again * weight_grad, axis=-1, keepdims=True)
    score_grad_low = (weights_again * (weight_grad - row_delta)).astype(bf16)
    query_att = (
        score_scale * jnp.einsum("htj,jhd->thd", score_grad_low, key_heads, preferred_element_type=f32)
    ).reshape(span, local_width)
    keys_grad = (
        score_scale * jnp.einsum("htj,thd->jhd", score_grad_low, query_heads, preferred_element_type=f32)
    ).reshape(key_total, local_width)
    values_grad = jnp.einsum(
        "htj,thd->jhd", weights_again.astype(bf16), grad_heads, preferred_element_type=f32
    ).reshape(key_total, local_width)
    recall_end = persist_count + span
    persist_part = jnp.stack(
        [head_norm_back(persist_f[0], keys_grad[:persist_count], HEAD), values_grad[:persist_count]]
    )
    recall_grad_low = (
        head_norm_back(recall_own, keys_grad[persist_count:recall_end], HEAD)
        + values_grad[persist_count:recall_end]
    ).astype(bf16)

    cots, sums_got, first_chunks, second_chunks = chain_backward(recall_grad_low, saved, seq_spans, gate_rows, 12)
    gate_sums = jnp.sum(sums_got[:, :, :3], axis=0)[wide_pos] * jnp.array([-1.0, 1.0, -1.0], f32)

    logit_grad = gate_sums * gate_scale * gate_sig * (1.0 - gate_sig)
    rate_part = span_mean[:, None] * logit_grad[None, :]
    gate_row = jnp.sum(rate_f * logit_grad[None, :], axis=1)[None, :] / span

    def after_all(totals, extras):
        tokens_rows, grad_rows, gain, row = extras
        scaled, factor = scaled_of(tokens_rows.astype(f32))
        normed_grad = totals[0] + row
        gain_part = jnp.sum(normed_grad * scaled, axis=0, keepdims=True)
        return [(grad_rows + rms_back(scaled, factor, normed_grad * gain)).astype(bf16)], [gain_part]

    def place_cols(piece, axis):
        full = piece.shape[:axis] + (width,) + piece.shape[axis + 1 :]
        return lax.dynamic_update_slice_in_dim(jnp.zeros(full, f32), piece, col_offset, axis)

    persist_full = place_cols(persist_part, 2)
    rate_part = jnp.where(narrow_pos == 0, rate_part, 0.0)
    chunks = [
        persist_full.reshape(2, persist_count, devices, -1).transpose(2, 0, 1, 3),
        gain_two_part.reshape(devices, -1),
        rate_part.reshape(devices, -1, 3),
    ]
    flat = jnp.concatenate([a.reshape(devices, -1) for a in chunks], 1)
    flat_size = -(-flat.shape[1] // 1024) * 1024
    flat = jnp.pad(flat, ((0, 0), (0, flat_size - flat.shape[1]))).reshape(devices, -1, 128)
    cots = cots.reshape(3, span, local_width)
    tokens_grad, weight_out, first_out, second_out, flat_sum, gain_sum, tap_rows, early_out = last_step(
        [cots[0], cots[1], cots[2], query_att, keys_grad[recall_end:], values_grad[recall_end:]],
        [mixed_conv, extended, jnp.pad(kernel_f, ((0, 8 - taps), (0, 0))), qkv_weights, normed_low],
        seq_spans,
        [gate_pre_low, gate_cols],
        [tokens_own, middle_grad, gain_one[None], gate_row],
        after_all,
        early_grads,
        [first_chunks, second_chunks],
        flat,
        15,
    )
    tokens_grad = tokens_grad.reshape(span, width).astype(f32)
    flat_sum = flat_sum.reshape(-1)
    own_start = (wide_pos * narrow + narrow_pos) * (width // devices)
    norm_grad = lax.dynamic_slice_in_dim(gain_sum.reshape(-1), own_start, width // devices, 0)
    small_outs, at = [], 0
    for a in chunks:
        size = a.size // devices
        small_outs.append(flat_sum[at : at + size].reshape(a.shape[1:]))
        at += size
    persist_grad, ffn_gain_grad, rate_grad = small_outs
    tap_sum = jnp.sum(tap_rows.reshape(wide, narrow, taps, 3, local_width), axis=0)
    tap_sum = tap_sum.transpose(1, 2, 0, 3).reshape(taps, 3 * width)
    kernel_grad = lax.dynamic_slice_in_dim(
        tap_sum, (wide_pos * narrow + narrow_pos) * (3 * width // devices), 3 * width // devices, 1
    )
    return (
        output,
        tokens_grad,
        weight_out[:, :local_width],
        weight_out[:, local_width : 2 * local_width],
        weight_out[:, 2 * local_width : 3 * local_width],
        kernel_grad,
        persist_grad,
        norm_grad,
        rate_grad,
        early_out[:, :local_width],
        early_out[:, local_width:].T,
        first_out,
        second_out,
        ffn_gain_grad,
        ffn_gate_out,
        ffn_up_out,
        ffn_down_out.T,
    )


def solution(mesh):
    rows, both, square, turned = P("wide", None), P(("wide", "narrow"), None), P("wide", "narrow"), P("narrow", "wide")
    flat, taps, heads = P(("wide", "narrow")), P(None, ("wide", "narrow")), P(None, None, ("wide", "narrow"))
    return jax.shard_map(
        body,
        mesh=mesh,
        in_specs=(rows, rows, P(), both, both, both, taps, heads, flat, both)
        + (square, turned, square, turned, flat, square, square, turned),
        out_specs=(rows, rows, square, square, square, taps, heads, flat, both)
        + (square, turned, square, turned, flat, square, square, turned),
        check_vma=False,
    )
```

```python
import math

import jax
import jax.numpy as jnp
from jax import lax
from jax.experimental import pallas as pl
from jax.experimental.pallas import tpu as pltpu
from jax.sharding import PartitionSpec as P

HEAD = 64
LANE_WIDE = 4
MESH = pl.DeviceIdType.MESH
ANY = pl.BlockSpec(memory_space=pl.ANY)
bf16 = jnp.bfloat16
f32 = jnp.float32

decay_top = 0.2
moment_top = 0.9
learn_top = 0.1
eps_norm = 1e-05
eps_head = 1e-06
masked_score = -1e30


def remote(src, dst, send, recv, device):
    return pltpu.make_async_remote_copy(
        src_ref=src, dst_ref=dst, send_sem=send, recv_sem=recv, device_id=device, device_id_type=MESH
    )


def sigmoid(values):
    return 1.0 / (1.0 + jnp.exp(-values))
class Grid:
    def __init__(self):
        wide, narrow = lax.axis_size("wide"), lax.axis_size("narrow")
        self.zs = 4 if wide % 4 == 0 else 1
        self.xs, self.ys = wide // self.zs, narrow // 2
        self.wide, self.narrow = lax.axis_index("wide"), lax.axis_index("narrow")
        self.z, self.x = lax.div(self.wide, self.xs), lax.rem(self.wide, self.xs)
        self.y, self.c = lax.div(self.narrow, 2), lax.rem(self.narrow, 2)
        self.partner = self.device(self.z, self.x, self.y, 1 - self.c)

    def device(self, z, x, y, c):
        return z * self.xs + x, 2 * y + c

    def z_others(self):
        if self.zs != 4:
            return [lax.rem(self.z + s, self.zs) for s in range(1, self.zs)]
        near = self.z + 1 - 2 * lax.div(self.z + 3, 4)
        far = 3 - 3 * lax.div(self.z, 2)
        return [near, 6 - self.z - near - far, far]

    def x_others(self):
        return [lax.rem(self.x + s, self.xs) for s in range(1, self.xs)]

    def y_others(self):
        return [lax.rem(self.y + s, self.ys) for s in range(1, self.ys)]

    def greet_all(self):
        wide, narrow = lax.axis_size("wide"), lax.axis_size("narrow")
        devices = wide * narrow
        me = self.wide * narrow + self.narrow
        barrier = pltpu.get_barrier_semaphore()

        def greet(step, carry):
            target = lax.rem(me + step, devices)
            where = lax.div(target, narrow), lax.rem(target, narrow)
            pl.semaphore_signal(barrier, inc=1, device_id=where, device_id_type=MESH)
            return carry

        lax.fori_loop(1, devices, greet, 0)
        return lambda: pl.semaphore_wait(barrier, devices - 1)


class Gather:
    def __init__(self, grid, source, whole, sems):
        self.grid, self.source, self.whole = grid, source, whole
        self.sent, self.got, self.sent_pair, self.got_pair = sems
        self.rows = whole.shape[2]
        self.pushes, self.pairs = 0, 0

    @staticmethod
    def counts():
        zs = 4 if lax.axis_size("wide") % 4 == 0 else 1
        xs, ys = lax.axis_size("wide") // zs, lax.axis_size("narrow") // 2
        sends = 2 * (zs - 1) + zs * 2 * (xs - 1 + ys - 1) + 2 * zs * (xs - 1) * (ys - 1)
        return zs * xs * ys, sends, 2 * zs * xs * ys

    @classmethod
    def scratch(cls):
        chips, sends, pairs = cls.counts()
        return [
            pltpu.SemaphoreType.DMA((sends,)),
            pltpu.SemaphoreType.DMA((chips, 2)),
            pltpu.SemaphoreType.DMA((pairs,)),
            pltpu.SemaphoreType.DMA((chips, 2)),
        ]

    def half(self, ref, h):
        return ref.at[pl.ds(h * (self.rows // 2), self.rows // 2)]

    def piece(self, z, x, y, c, h):
        wide, narrow = self.grid.device(z, x, y, c)
        return self.half(self.whole.at[wide, narrow], h)

    def spot(self, z, x, y):
        return (z * self.grid.xs + x) * self.grid.ys + y

    def push(self, z, x, y, h, target, own):
        here = self.piece(z, x, y, self.grid.c, h)
        copy = remote(
            self.half(self.source, h) if own else here,
            here,
            self.sent.at[self.pushes],
            self.got.at[self.spot(z, x, y), h],
            target,
        )
        self.pushes += 1
        copy.start()

    def to_partner(self, z, x, y, h, own=False):
        here = self.piece(z, x, y, self.grid.c, h)
        copy = remote(
            self.half(self.source, h) if own else here,
            here,
            self.sent_pair.at[self.pairs],
            self.got_pair.at[self.spot(z, x, y), h],
            self.grid.partner,
        )
        self.pairs += 1
        copy.start()

    def arrived(self, z, x, y, h):
        here = self.piece(z, x, y, self.grid.c, h)
        remote(here, here, self.sent.at[0], self.got.at[self.spot(z, x, y), h], self.grid.partner).wait_recv()

    def fan(self, z, own=False):
        g = self.grid
        to_y = [g.device(g.z, g.x, y, g.c) for y in g.y_others()]
        to_x = [g.device(g.z, x, g.y, g.c) for x in g.x_others()]
        for h, targets in ((0, to_y), (1, to_x), (0, to_x), (1, to_y)):
            for target in targets:
                self.push(z, g.x, g.y, h, target, own)
        for h in (0, 1):
            self.to_partner(z, g.x, g.y, h, own)

    def begin(self):
        g = self.grid
        for z in g.z_others():
            for h in (0, 1):
                self.push(g.z, g.x, g.y, h, g.device(z, g.x, g.y, g.c), True)
        self.fan(g.z, True)

    def level(self, number):
        return ([self.grid.z] + self.grid.z_others())[number]

    def along_z(self, number):
        g, z = self.grid, self.level(number)
        for h in (0, 1):
            self.arrived(z, g.x, g.y, h)
        self.fan(z)

    def across(self, number):
        g, z = self.grid, self.level(number)
        for y in g.y_others():
            self.arrived(z, g.x, y, 0)
            for x in g.x_others():
                self.push(z, g.x, y, 0, g.device(g.z, x, g.y, g.c), False)
            self.to_partner(z, g.x, y, 0)
        for x in g.x_others():
            self.arrived(z, x, g.y, 1)
            for y in g.y_others():
                self.push(z, x, g.y, 1, g.device(g.z, g.x, y, g.c), False)
            self.to_partner(z, x, g.y, 1)

    def last(self, number):
        g, z = self.grid, self.level(number)
        for x in g.x_others():
            self.arrived(z, x, g.y, 0)
            self.to_partner(z, x, g.y, 0)
            for y in g.y_others():
                self.arrived(z, x, y, 0)
                self.to_partner(z, x, y, 0)
        for y in g.y_others():
            self.arrived(z, g.x, y, 1)
            self.to_partner(z, g.x, y, 1)
            for x in g.x_others():
                self.arrived(z, x, y, 1)
                self.to_partner(z, x, y, 1)

    def middle(self):
        for number in range(1, self.grid.zs):
            self.along_z(number)
            self.across(number - 1)
            if number > 1:
                self.last(number - 2)
        self.across(self.grid.zs - 1)
        for number in range(max(0, self.grid.zs - 2), self.grid.zs):
            self.last(number)

    def finish(self):
        g = self.grid
        here = self.piece(g.z, g.x, g.y, g.c, 0)
        _, sends, pairs = self.counts()
        for sems, number in ((self.sent, sends), (self.sent_pair, pairs)):
            for i in range(number):
                remote(here, here, sems.at[i], self.got.at[0, 0], g.partner).wait_send()
        for z in range(g.zs):
            for x in range(g.xs):
                for y in range(g.ys):
                    for h in (0, 1):
                        there = self.piece(z, x, y, 1 - g.c, h)
                        remote(
                            there, there, self.sent.at[0], self.got_pair.at[self.spot(z, x, y), h], g.partner
                        ).wait_recv()


def send_parameters(smalls, weights, blocks, tokens, ident):
    wide, narrow = lax.axis_size("wide"), lax.axis_size("narrow")
    devices = wide * narrow
    count = len(blocks)

    def kernel(*refs):
        smalls_ref, weights_ref = refs[:2]
        block_refs, tokens_ref, refs = refs[2 : 2 + count], refs[2 + count], refs[3 + count :]
        smalls_out, weights_out = refs[:2]
        block_outs, tail_out, refs = refs[2 : 2 + count], refs[2 + count], refs[3 + count :]
        hold_small, hold_weight, refs = refs[0], refs[1], refs[2:]
        hold_blocks, refs = refs[:count], refs[count:]
        local_sem, all_send, all_recv, near_send, near_recv, z_send, z_recv, x_send, x_recv, b_send, b_recv, t_sem = refs
        g = Grid()
        me = g.wide * narrow + g.narrow
        wait_all = g.greet_all()
        own = [
            (smalls_ref, hold_small, smalls_out.at[me]),
            (weights_ref.at[g.narrow], hold_weight, weights_out.at[g.wide, g.narrow]),
        ] + [
            (block_refs[i].at[lax.rem(g.wide, LANE_WIDE)], hold_blocks[i], block_outs[i].at[g.wide])
            for i in range(count)
        ]
        into = [pltpu.make_async_copy(a, b, local_sem.at[i]) for i, (a, b, _) in enumerate(own)]
        back = [pltpu.make_async_copy(b, c, local_sem.at[i]) for i, (_, b, c) in enumerate(own)]
        for copy in into:
            copy.start()
        wait_all()
        near = []
        for s in range(1, narrow):
            target = lax.rem(g.narrow + s, narrow)
            copy = remote(
                weights_ref.at[target],
                weights_out.at[g.wide, g.narrow],
                near_send.at[s],
                near_recv.at[g.narrow],
                (g.wide, target),
            )
            copy.start()
            near.append(copy)
        tail = remote(
            tokens_ref.at[pl.ds(tokens_ref.shape[0] - 8, 8)],
            tail_out,
            t_sem.at[0],
            t_sem.at[1],
            (lax.rem(g.wide + 1, wide), g.narrow),
        )
        tail.start()

        def send_small(step, carry):
            target = lax.rem(me + step, devices)
            remote(
                smalls_ref,
                smalls_out.at[me],
                all_send.at[0],
                all_recv.at[0],
                (lax.div(target, narrow), lax.rem(target, narrow)),
            ).start()
            return carry

        lax.fori_loop(1, devices, send_small, 0)
        for copy in into:
            copy.wait()
        for copy in back:
            copy.start()
        for copy in back:
            copy.wait()
        for s in range(1, narrow):
            source = lax.rem(g.narrow + s, narrow)
            there = weights_out.at[g.wide, source]
            remote(there, there, near_send.at[s], near_recv.at[source], g.partner).wait_recv()

        def row(z, x):
            return weights_out.at[z * g.xs + x]

        sends = []

        def push(z, target, send, recv):
            copy = remote(row(z, g.x), row(z, g.x), send, recv, target)
            copy.start()
            sends.append(copy)

        for i, z in enumerate(g.z_others()):
            push(g.z, g.device(z, g.x, g.y, g.c), z_send.at[i], z_recv.at[g.z])
        for i, x in enumerate(g.x_others()):
            push(g.z, g.device(g.z, x, g.y, g.c), x_send.at[0, i], x_recv.at[g.z, g.x])
        for j, z in enumerate(g.z_others()):
            remote(row(z, g.x), row(z, g.x), z_send.at[0], z_recv.at[z], g.partner).wait_recv()
            for i, x in enumerate(g.x_others()):
                push(z, g.device(g.z, x, g.y, g.c), x_send.at[1 + j, i], x_recv.at[z, g.x])
        for s in range(1, wide):
            target = lax.rem(g.wide + s, wide)
            for i in range(count):
                copy = remote(
                    block_refs[i].at[lax.rem(target, LANE_WIDE)],
                    block_outs[i].at[g.wide],
                    b_send.at[i, s],
                    b_recv.at[i, g.wide],
                    (target, g.narrow),
                )
                copy.start()
                sends.append(copy)
        for x in g.x_others():
            for z in [g.z] + g.z_others():
                remote(row(z, x), row(z, x), z_send.at[0], x_recv.at[z, x], g.partner).wait_recv()
        for s in range(1, wide):
            source = lax.rem(g.wide + s, wide)
            for i in range(count):
                there = block_outs[i].at[source]
                remote(there, there, z_send.at[0], b_recv.at[i, source], g.partner).wait_recv()
        for copy in near + sends:
            copy.wait_send()
        tail.wait()
        others = smalls_out.at[pl.ds(0, devices - 1)]
        whole = remote(others, others, all_send.at[0], all_recv.at[0], g.partner)
        whole.wait_send()
        whole.wait_recv()

    zs = 4 if wide % 4 == 0 else 1
    xs = wide // zs
    sem = pltpu.SemaphoreType.DMA
    return pl.pallas_call(
        kernel,
        out_shape=[
            jax.ShapeDtypeStruct((devices,) + smalls.shape, smalls.dtype),
            jax.ShapeDtypeStruct((wide, narrow) + weights.shape[1:], weights.dtype),
        ]
        + [jax.ShapeDtypeStruct((wide,) + b.shape[1:], b.dtype) for b in blocks]
        + [jax.ShapeDtypeStruct((8, tokens.shape[1]), tokens.dtype)],
        in_specs=[ANY] * (3 + count),
        out_specs=[ANY] * (3 + count),
        scratch_shapes=[pltpu.VMEM(smalls.shape, smalls.dtype), pltpu.VMEM(weights.shape[1:], weights.dtype)]
        + [pltpu.VMEM(b.shape[1:], b.dtype) for b in blocks]
        + [sem((2 + count,)), sem((1,)), sem((1,)), sem((narrow,)), sem((narrow,)), sem((zs,)), sem((zs,))]
        + [sem((zs, xs)), sem((zs, xs)), sem((count, wide)), sem((count, wide)), sem((2,))],
        compiler_params=pltpu.CompilerParams(collective_id=ident, has_side_effects=True),
        name="send_parameters",
    )(smalls, weights, *blocks, tokens)


def narrow_step(parts, extras, work, spread_count, locals_like, ident):
    narrow, rows, width = parts[0].shape
    ys = narrow // 2
    count, extra_count, local_count = len(parts), len(extras), len(locals_like)
    parts = [p.reshape(ys, 2, rows, width) for p in parts]

    def kernel(*refs):
        part_refs, refs = refs[:count], refs[count:]
        extra_refs, refs = refs[:extra_count], refs[extra_count:]
        spread_refs, refs = refs[:spread_count], refs[spread_count:]
        local_refs, refs = refs[:local_count], refs[local_count:]
        mine, pair, half, got, rowbuf, refs = refs[0], refs[1], refs[2], refs[3], refs[4], refs[5:]
        load_sem, pair_send, pair_recv, y_send, y_recv, s_send, s_recv, p_send, p_recv, own_sem = refs
        g = Grid()
        barrier = pltpu.get_barrier_semaphore()
        friends = [g.device(g.z, g.x, y, g.c) for y in g.y_others()] + [g.partner]
        for friend in friends:
            pl.semaphore_signal(barrier, inc=1, device_id=friend, device_id_type=MESH)
        loads = [
            pltpu.make_async_copy(part_refs[i].at[:, g.c], mine.at[i], load_sem.at[i]) for i in range(count)
        ]
        for copy in loads:
            copy.start()
        pl.semaphore_wait(barrier, len(friends))
        pairs = [
            remote(part_refs[i].at[:, 1 - g.c], pair.at[i], pair_send.at[i], pair_recv.at[i], g.partner)
            for i in range(count)
        ]
        for copy in pairs:
            copy.start()
        sends = []
        for i in range(count):
            loads[i].wait()
            pairs[i].wait_recv()
            mine[i] += pair[i]
            half[i] = mine[i].astype(bf16)
            for s, y in enumerate(g.y_others()):
                copy = remote(
                    half.at[i, y], got.at[i, g.y], y_send.at[i, s], y_recv.at[i, g.y], g.device(g.z, g.x, y, g.c)
                )
                copy.start()
                sends.append(copy)
        totals = []
        for i in range(count):
            total = mine[i, g.y]
            for y in g.y_others():
                remote(got.at[i, y], got.at[i, y], y_send.at[i, 0], y_recv.at[i, y], g.partner).wait_recv()
                total = total + got[i, y].astype(f32)
            totals.append(total)
        spreads, locals_out = work(totals, [ref[...] for ref in extra_refs])
        for ref, value in zip(local_refs, locals_out):
            ref[...] = value
        own = []
        for i, value in enumerate(spreads):
            rowbuf[i] = value
            for s, y in enumerate(g.y_others()):
                copy = remote(
                    rowbuf.at[i],
                    spread_refs[i].at[g.narrow],
                    s_send.at[i, s],
                    s_recv.at[i, g.y],
                    g.device(g.z, g.x, y, g.c),
                )
                copy.start()
                sends.append(copy)
            copy = remote(
                rowbuf.at[i], spread_refs[i].at[g.narrow], p_send.at[i, g.y], p_recv.at[i, g.y], g.partner
            )
            copy.start()
            sends.append(copy)
            copy = pltpu.make_async_copy(rowbuf.at[i], spread_refs[i].at[g.narrow], own_sem.at[i])
            copy.start()
            own.append(copy)
        for i in range(spread_count):
            for y in g.y_others():
                there = spread_refs[i].at[2 * y + g.c]
                remote(there, there, s_send.at[i, 0], s_recv.at[i, y], g.partner).wait_recv()
                copy = remote(there, there, p_send.at[i, y], p_recv.at[i, y], g.partner)
                copy.start()
                sends.append(copy)
        for i in range(spread_count):
            for y in range(ys):
                there = spread_refs[i].at[2 * y + 1 - g.c]
                remote(there, there, s_send.at[i, 0], p_recv.at[i, y], g.partner).wait_recv()
        for copy in pairs + sends:
            copy.wait_send()
        for copy in own:
            copy.wait()

    sem = pltpu.SemaphoreType.DMA
    vmem = pl.BlockSpec(memory_space=pltpu.VMEM)
    return pl.pallas_call(
        kernel,
        out_shape=[jax.ShapeDtypeStruct((narrow, rows, width), bf16)] * spread_count
        + [jax.ShapeDtypeStruct(shape, dtype) for shape, dtype in locals_like],
        in_specs=[ANY] * count + [vmem] * extra_count,
        out_specs=[ANY] * spread_count + [vmem] * local_count,
        scratch_shapes=[pltpu.VMEM((count, ys, rows, width), f32)] * 2
        + [pltpu.VMEM((count, ys, rows, width), bf16)] * 2
        + [pltpu.VMEM((spread_count, rows, width), bf16)]
        + [sem((count,))] * 3
        + [sem((count, ys))] * 2
        + [sem((spread_count, ys))] * 4
        + [sem((spread_count,))],
        compiler_params=pltpu.CompilerParams(collective_id=ident, has_side_effects=True),
        cost_estimate=pl.CostEstimate(flops=30 * 10**9, bytes_accessed=100 * 2**20, transcendentals=0),
        name=f"narrow_step_{ident}",
    )(*parts, *extras)


def last_step(heads, conv, lengths, gate_back, extras, work, early, chunks, flat, ready, ident):
    span, columns = conv[0].shape
    block = columns // 3
    width = conv[3].shape[0]
    narrow = lax.axis_size("narrow")
    rows = span // narrow
    wide = lax.axis_size("wide")
    devices = wide * narrow
    ys = narrow // 2
    zs = 4 if wide % 4 == 0 else 1
    xs = wide // zs
    lanes = wide // LANE_WIDE
    extra_count = len(extras)
    own_grad, own_early = (width // wide, columns), (width // wide, early.shape[1])
    early = early.reshape((zs, xs) + own_early)
    compute = list(heads) + list(conv) + list(gate_back)
    compute_count = len(compute)
    count = 4
    first_shape, second_shape, flat_shape = chunks[0].shape[1:], chunks[1].shape[1:], flat.shape[1:]

    def kernel(*refs):
        first_ref, second_ref, flat_ref, early_ref, lengths_ref, ready_ref = refs[:6]
        compute_refs, refs = refs[6 : 6 + compute_count], refs[6 + compute_count :]
        extra_refs, refs = refs[:extra_count], refs[extra_count:]
        spread_ref, grads_out, first_out, second_out, flat_out, row_out, taps_out, early_out, ready_out = refs[:9]
        refs = refs[9:]
        part_ref, grads_ref, conv_grad, tap_rows, halo_out, halo_in, halo_sem, taps_sem, refs = refs[:8] + (refs[8:],)
        pair, half, got, rowbuf, rowtile, rowgot, refs = refs[:6] + (refs[6:],)
        gx, ghalf, gz, fgot, sgot, flatgot, refs = refs[:6] + (refs[6:],)
        load_sem, pair_sem, y_send, y_recv, s_send, s_recv, p_send, p_recv, refs = refs[:8] + (refs[8:],)
        gx_send, gx_recv, gz_send, gz_recv, c_send, c_recv, all_send, all_recv = refs[:8]
        early_own, ex, ehalf, ez, e_sems = refs[8], refs[9], refs[10], refs[11], refs[12:16]
        r_send, r_recv, rp_send, rp_recv, r_own = refs[16:21]
        g = Grid()
        me = g.wide * narrow + g.narrow
        wait_all = g.greet_all()
        plan = Plan(lengths_ref, None, lengths.shape[0])
        loads = [
            pltpu.make_async_copy(first_ref.at[g.wide], fgot.at[g.wide], load_sem.at[0]),
            pltpu.make_async_copy(second_ref.at[g.wide], sgot.at[g.wide], load_sem.at[1]),
            pltpu.make_async_copy(flat_ref.at[me], flatgot.at[me], load_sem.at[2]),
            pltpu.make_async_copy(early_ref.at[:, g.x], early_own, load_sem.at[3]),
        ]
        for copy in loads:
            copy.start()
        wait_all()
        sends = []
        order = g.z_others()[::-1] + [g.z]

        def along_x(source, place, sems):
            for z in order:
                for i, x in enumerate(g.x_others()):
                    copy = remote(
                        source.at[z, x],
                        place.at[g.x, z],
                        sems[0].at[i, z],
                        sems[1].at[g.x, z],
                        g.device(g.z, x, g.y, g.c),
                    )
                    copy.start()
                    sends.append(copy)

        def join(z, own, place, joined, sems):
            total = own.astype(f32)
            for x in g.x_others():
                there = place.at[x, z]
                remote(there, there, sems[0].at[0, 0], sems[1].at[x, z], g.partner).wait_recv()
                total = total + place[x, z].astype(f32)
            joined[z] = total.astype(bf16)

        def along_z(i, z, joined, place, sems):
            copy = remote(joined.at[z], place.at[g.z], sems[2].at[i], sems[3].at[g.z], g.device(z, g.x, g.y, g.c))
            copy.start()
            sends.append(copy)

        def whole_of(joined, place, sems):
            total = joined[g.z].astype(f32)
            for z in order[:-1]:
                there = place.at[z]
                remote(there, there, sems[2].at[0], sems[3].at[z], g.partner).wait_recv()
                total = total + place[z].astype(f32)
            return total

        g_sems = (gx_send, gx_recv, gz_send, gz_recv)
        along_x(early_ref, ex, e_sems)
        for s in range(1, wide):
            target = lax.rem(g.wide + s, wide)
            for i, (source, place) in enumerate(((first_ref, fgot), (second_ref, sgot))):
                copy = remote(
                    source.at[target],
                    place.at[g.wide],
                    c_send.at[i, s],
                    c_recv.at[i, g.wide],
                    (target, g.narrow),
                )
                copy.start()
                sends.append(copy)

        def send_flat(step, carry):
            target = lax.rem(me + step, devices)
            where = lax.div(target, narrow), lax.rem(target, narrow)
            remote(flat_ref.at[target], flatgot.at[me], all_send.at[0], all_recv.at[0], where).start()
            return carry

        lax.fori_loop(1, devices, send_flat, 0)
        ready_sends = []

        def ready_to(source, place, send, recv, target):
            copy = remote(source, ready_out.at[place], send, recv, target)
            copy.start()
            ready_sends.append(copy)

        for s, y in enumerate(g.y_others()):
            ready_to(ready_ref, g.narrow, r_send.at[s], r_recv.at[g.y], g.device(g.z, g.x, y, g.c))
        ready_to(ready_ref, g.narrow, rp_send.at[g.y], rp_recv.at[g.y], g.partner)
        ready_own = pltpu.make_async_copy(ready_ref, ready_out.at[g.narrow], r_own.at[0])
        ready_own.start()
        qmem, kmem, vmem_ref, qatt, katt, vatt = compute_refs[:6]
        mixed_ref, ext_ref, taps_ref, weights_ref, normed_ref, gate_low, gate_cols = compute_refs[6:]
        for third, (memory, attention) in enumerate(((qmem, qatt), (kmem, katt), (vmem_ref, vatt))):
            place = pl.ds(third * block, block)
            mixed = mixed_ref[:, place]
            if third < 2:
                grad = memory[...].astype(f32) + attention[...]
                act = mixed * sigmoid(mixed)
                factor = lax.rsqrt(head_sums(act * act) + eps_head)
                normed = act * factor
                grad = factor * (grad - normed * head_sums(normed * grad))
            else:
                grad = attention[...] - memory[...].astype(f32)
            grad = grad * silu_slope(mixed)
            conv_grad[pl.ds(0, span), place] = grad
            for j in range(count):
                tap_rows[pl.ds(j, 1), place] = jnp.sum(grad * ext_ref[pl.ds(8 - j, span), place], axis=0, keepdims=True)
        begins = plan.begins(g.wide)
        halo_out[...] = jnp.where(begins, 0.0, conv_grad[pl.ds(0, 8), :])
        halo = remote(
            halo_out, halo_in, halo_sem.at[0], halo_sem.at[1], (lax.rem(g.wide + wide - 1, wide), g.narrow)
        )
        halo.start()

        def send_taps(step, carry):
            target = lax.rem(me + step, devices)
            where = lax.div(target, narrow), lax.rem(target, narrow)
            remote(tap_rows, taps_out.at[me], taps_sem.at[0], taps_sem.at[1], where).start()
            return carry

        lax.fori_loop(1, devices, send_taps, 0)
        taps_out[me] = tap_rows[...]
        for copy in loads:
            copy.wait()
        for i, z in enumerate(order):
            join(z, early_own[z], ex, ehalf, e_sems)
            if i < len(order) - 1:
                along_z(i, z, ehalf, ez, e_sems)
        halo.wait()
        conv_grad[pl.ds(span, 8), :] = halo_in[...]
        projected = taps_ref[pl.ds(0, 1), :] * conv_grad[pl.ds(0, span), :]
        for j in range(1, count):
            projected = projected + taps_ref[pl.ds(j, 1), :] * conv_grad[pl.ds(j, span), :]
        projected_low = projected.astype(bf16)
        part = inner_right(projected_low, weights_ref[...]) + inner_right(gate_low[...], gate_cols[...])
        part_ref[...] = part.reshape(ys, 2, rows, width)
        pair_copy = remote(part_ref.at[:, 1 - g.c], pair, pair_sem.at[0], pair_sem.at[1], g.partner)
        pair_copy.start()
        grads_ref[...] = inner_left(normed_ref[...], projected_low).astype(bf16).reshape((zs, xs) + own_grad)
        along_x(grads_ref, gx, g_sems)
        for y in g.y_others():
            there = ready_out.at[2 * y + g.c]
            remote(there, there, r_send.at[0], r_recv.at[y], g.partner).wait_recv()
            ready_to(there, 2 * y + g.c, rp_send.at[y], rp_recv.at[y], g.partner)
        pair_copy.wait()
        pair[...] += part_ref[:, g.c]
        half[...] = pair[...].astype(bf16)
        for s, y in enumerate(g.y_others()):
            copy = remote(half.at[y], got.at[g.y], y_send.at[s], y_recv.at[g.y], g.device(g.z, g.x, y, g.c))
            copy.start()
            sends.append(copy)
        for i, z in enumerate(order[:-1]):
            join(z, grads_ref[z, g.x], gx, ghalf, g_sems)
            along_z(i, z, ghalf, gz, g_sems)
            if i == 0:
                total = pair[g.y]
                for y in g.y_others():
                    remote(got.at[y], got.at[y], y_send.at[0], y_recv.at[y], g.partner).wait_recv()
                    total = total + got[y].astype(f32)
                spreads, locals_out = work([total], [ref[...] for ref in extra_refs])
                rowbuf[...] = spreads[0]
                for j in range(8):
                    rowtile[pl.ds(j, 1), :] = locals_out[0][:, j * width // 8 : (j + 1) * width // 8]
                for s, y in enumerate(g.y_others()):
                    copy = remote(
                        rowbuf,
                        spread_ref.at[g.narrow],
                        s_send.at[s],
                        s_recv.at[g.y],
                        g.device(g.z, g.x, y, g.c),
                    )
                    copy.start()
                    sends.append(copy)
                copy = remote(rowbuf, spread_ref.at[g.narrow], p_send.at[g.y], p_recv.at[g.y], g.partner)
                copy.start()
                sends.append(copy)
                own = pltpu.make_async_copy(rowbuf, spread_ref.at[g.narrow], load_sem.at[0])
                own.start()

                def send_row(step, carry):
                    target = lax.rem(me + step, devices)
                    where = lax.div(target, narrow), lax.rem(target, narrow)
                    remote(rowtile, rowgot.at[me], all_send.at[1], all_recv.at[1], where).start()
                    return carry

                lax.fori_loop(1, devices, send_row, 0)
                rowgot[me] = rowtile[...]
        for y in g.y_others():
            there = spread_ref.at[2 * y + g.c]
            remote(there, there, s_send.at[0], s_recv.at[y], g.partner).wait_recv()
            copy = remote(there, there, p_send.at[y], p_recv.at[y], g.partner)
            copy.start()
            sends.append(copy)
        join(g.z, grads_ref[g.z, g.x], gx, ghalf, g_sems)
        early_out[...] = whole_of(ehalf, ez, e_sems)
        for s in range(1, wide):
            source = lax.rem(g.wide + s, wide)
            for i, place in enumerate((fgot, sgot)):
                there = place.at[source]
                remote(there, there, c_send.at[i, 0], c_recv.at[i, source], g.partner).wait_recv()
        for p in range(LANE_WIDE):
            first_sum, second_sum = fgot[p].astype(f32), sgot[p].astype(f32)
            for lane in range(1, lanes):
                first_sum = first_sum + fgot[lane * LANE_WIDE + p].astype(f32)
                second_sum = second_sum + sgot[lane * LANE_WIDE + p].astype(f32)
            first_out[:, p * first_shape[1] : (p + 1) * first_shape[1]] = first_sum
            second_out[p * second_shape[0] : (p + 1) * second_shape[0], :] = second_sum
        grads_out[...] = whole_of(ghalf, gz, g_sems)
        ends = ((flatgot, all_send.at[0], all_recv.at[0]), (rowgot, all_send.at[1], all_recv.at[1]))
        for place, send, recv in ends + ((taps_out, taps_sem.at[0], taps_sem.at[1]),):
            others = place.at[pl.ds(0, devices - 1)]
            whole = remote(others, others, send, recv, g.partner)
            whole.wait_send()
            whole.wait_recv()
        flat_out[...] = jnp.sum(flatgot[...], axis=0)
        row_out[...] = jnp.sum(rowgot[...], axis=0)
        for y in range(ys):
            there = spread_ref.at[2 * y + 1 - g.c]
            remote(there, there, s_send.at[0], p_recv.at[y], g.partner).wait_recv()
        for y in range(ys):
            there = ready_out.at[2 * y + 1 - g.c]
            remote(there, there, r_send.at[0], rp_recv.at[y], g.partner).wait_recv()
        for copy in sends + ready_sends:
            copy.wait_send()
        own.wait()
        ready_own.wait()

    sem = pltpu.SemaphoreType.DMA
    vmem = pl.BlockSpec(memory_space=pltpu.VMEM)
    return pl.pallas_call(
        kernel,
        out_shape=[
            jax.ShapeDtypeStruct((narrow, rows, width), bf16),
            jax.ShapeDtypeStruct(own_grad, f32),
            jax.ShapeDtypeStruct((first_shape[0], LANE_WIDE * first_shape[1]), f32),
            jax.ShapeDtypeStruct((LANE_WIDE * second_shape[0], second_shape[1]), f32),
            jax.ShapeDtypeStruct(flat_shape, f32),
            jax.ShapeDtypeStruct((8, width // 8), f32),
            jax.ShapeDtypeStruct((devices, count, columns), f32),
            jax.ShapeDtypeStruct(own_early, f32),
            jax.ShapeDtypeStruct((narrow, rows, width), bf16),
        ],
        in_specs=[ANY] * 4
        + [pl.BlockSpec(memory_space=pltpu.SMEM), vmem]
        + [vmem] * (compute_count + extra_count),
        out_specs=[ANY] + [vmem] * 7 + [ANY],
        scratch_shapes=[
            pltpu.VMEM((ys, 2, rows, width), f32),
            pltpu.VMEM((zs, xs) + own_grad, bf16),
            pltpu.VMEM((span + 8, columns), f32),
            pltpu.VMEM((count, columns), f32),
            pltpu.VMEM((8, columns), f32),
            pltpu.VMEM((8, columns), f32),
            sem((2,)),
            sem((2,)),
        ]
        + [pltpu.VMEM((ys, rows, width), f32)]
        + [pltpu.VMEM((ys, rows, width), bf16)] * 2
        + [pltpu.VMEM((rows, width), bf16)]
        + [pltpu.VMEM((8, width // 8), f32), pltpu.VMEM((devices, 8, width // 8), f32)]
        + [
            pltpu.VMEM((xs, zs) + own_grad, bf16),
            pltpu.VMEM((zs,) + own_grad, bf16),
            pltpu.VMEM((zs,) + own_grad, bf16),
            pltpu.VMEM((wide,) + first_shape, bf16),
            pltpu.VMEM((wide,) + second_shape, bf16),
            pltpu.VMEM((devices,) + flat_shape, f32),
        ]
        + [sem((4,)), sem((2,))]
        + [sem((ys,))] * 6
        + [sem((xs, zs))] * 2
        + [sem((zs,))] * 2
        + [sem((2, wide))] * 2
        + [sem((2,))] * 2
        + [
            pltpu.VMEM((zs,) + own_early, bf16),
            pltpu.VMEM((xs, zs) + own_early, bf16),
            pltpu.VMEM((zs,) + own_early, bf16),
            pltpu.VMEM((zs,) + own_early, bf16),
        ]
        + [sem((xs, zs))] * 2
        + [sem((zs,))] * 2
        + [sem((ys,))] * 4
        + [sem((1,))],
        compiler_params=pltpu.CompilerParams(
            collective_id=ident, has_side_effects=True, vmem_limit_bytes=60 * 1024 * 1024
        ),
        name="last_step",
    )(chunks[0], chunks[1], flat, early, lengths, ready, *compute, *extras)


class Plan:
    def __init__(self, spans_ref, gates_ref, count):
        self.wide = lax.axis_size("wide")
        self.long = min(6, self.wide * 5 // 8)
        self.gates = gates_ref
        lengths = [spans_ref[i] for i in range(count)]
        self.starts, at = [], 0
        for length in lengths:
            self.starts.append(at)
            at = at + length
        longest, self.start = lengths[0], 0
        for i in range(1, count):
            more = lengths[i] > longest
            longest = jnp.where(more, lengths[i], longest)
            self.start = jnp.where(more, self.starts[i], self.start)
        self.lane = lax.div(lax.axis_index("wide"), LANE_WIDE)

    def span(self, turn):
        rest = jnp.where(turn < self.start, turn, turn + self.long)
        return jnp.clip(jnp.where(self.lane == 0, self.start + turn, rest), 0, self.wide - 1)

    def valid(self, turn):
        count = jnp.where(self.lane == 0, self.long, jnp.where(self.lane == 1, self.wide - self.long, 0))
        return jnp.where(turn < count, 1.0, 0.0)

    def first(self, turn):
        span = self.span(turn)
        found = jnp.where(span == self.starts[0], 1.0, 0.0)
        for start in self.starts[1:]:
            found = jnp.maximum(found, jnp.where(span == start, 1.0, 0.0))
        return jnp.maximum(found, 1.0 - self.valid(turn))

    def begins(self, span):
        found = span == self.starts[0]
        for start in self.starts[1:]:
            found = found | (span == start)
        return found

    def rates(self, turn):
        span = self.span(turn)
        return self.gates[span, 0], self.gates[span, 1], self.gates[span, 2]

    def lane_of(self, span):
        inside = (span >= self.start) & (span < self.start + self.long)
        return jnp.where(inside, 0, 1)

    def turn_of(self, span):
        inside = (span >= self.start) & (span < self.start + self.long)
        outside = jnp.where(span < self.start, span, span - self.long)
        return jnp.where(inside, span - self.start, outside)


def paired_lanes():
    wide = lax.axis_size("wide")
    long = min(6, wide * 5 // 8)
    return wide == 2 * LANE_WIDE and long == LANE_WIDE + 1 and lax.axis_size("narrow") == 4


class LaneGather:
    def __init__(self, grid, plan, source, whole, refs):
        self.grid, self.plan, self.source, self.whole = grid, plan, source, whole
        self.own, self.taken, self.mine = refs[:3]
        self.sent, self.got, self.sent_pair, self.got_pair, self.swap_sent, self.swap_got, self.local = refs[3:]
        self.rows = whole.shape[2]
        self.quarter = self.rows // LANE_WIDE
        third = (self.rows + self.quarter) // 3 // 16 * 16
        self.cuts = [(0, third), (third, third), (2 * third, self.rows - 2 * third)]
        self.side = lax.div(grid.wide, LANE_WIDE)
        self.spot = lax.rem(grid.wide, LANE_WIDE)
        long = plan.long
        lone = jnp.where((grid.wide >= plan.wide - long) & (grid.wide < long), 1, 0)
        self.paired = lone == 0
        self.pair = (grid.wide + long - 2 * long * self.side, grid.narrow)
        self.here = (lax.div(self.spot, 2), lax.rem(self.spot, 2), grid.y)

    @staticmethod
    def scratch(rows, cols):
        sem = pltpu.SemaphoreType.DMA
        return [
            pltpu.VMEM((rows, cols), bf16),
            pltpu.VMEM((rows, cols), bf16),
            pltpu.VMEM((rows + rows // LANE_WIDE, cols), bf16),
            sem((4, 7)),
            sem((4, 8)),
            sem((4, 8)),
            sem((4, 8)),
            sem((4,)),
            sem((4,)),
            sem((5,)),
        ]

    @staticmethod
    def shape(rows, cols):
        return (LANE_WIDE + 1, lax.axis_size("narrow"), rows, cols)

    def order(self, part):
        return ((0, 1, 2), (1, 2, 0), (2, 0, 1))[part]

    def place(self, mask):
        return [1 - v if mask >> i & 1 else v for i, v in enumerate(self.here)]

    def device(self, mask, colour):
        z, x, y = self.place(mask)
        return self.side * LANE_WIDE + 2 * z + x, 2 * y + colour

    def pieces(self, part, mask, colour):
        z, x, y = self.place(mask)
        spot, narrow = 2 * z + x, 2 * y + colour
        start, size = self.cuts[part]
        result = [(part, self.whole.at[spot, narrow, pl.ds(start, size)], self.mine.at[pl.ds(start, size)])]
        if part == 2:
            there = self.whole.at[LANE_WIDE, narrow, pl.ds(spot * self.quarter, self.quarter)]
            result.append((3, there, self.mine.at[pl.ds(self.rows, self.quarter)]))
        return result

    def push(self, part, mask, axis, number):
        for i, there, own in self.pieces(part, mask, self.grid.c):
            remote(
                there if mask else own,
                there,
                self.sent.at[i, number],
                self.got.at[i, mask | 1 << axis],
                self.device(1 << axis, self.grid.c),
            ).start()

    def to_partner(self, part, mask):
        for i, there, own in self.pieces(part, mask, self.grid.c):
            remote(
                there if mask else own,
                there,
                self.sent_pair.at[i, mask],
                self.got_pair.at[i, mask],
                self.grid.partner,
            ).start()

    def arrived(self, part, mask):
        for i, there, _ in self.pieces(part, mask, self.grid.c):
            remote(there, there, self.sent.at[i, 0], self.got.at[i, mask], self.grid.partner).wait_recv()

    def swaps(self):
        return [
            remote(
                self.source.at[pl.ds(start, size)],
                self.taken.at[pl.ds(start, size)],
                self.swap_sent.at[i],
                self.swap_got.at[i],
                self.pair,
            )
            for i, (start, size) in enumerate(self.cuts)
        ]

    def quarters(self):
        return [
            remote(
                self.source.at[pl.ds(q * self.quarter, self.quarter)],
                self.mine.at[pl.ds(self.rows, self.quarter)],
                self.swap_sent.at[q],
                self.swap_got.at[3],
                (q, self.grid.narrow),
            )
            for q in range(LANE_WIDE)
        ]

    def begin(self):
        @pl.when(self.paired)
        def _():
            for copy in self.swaps():
                copy.start()

        @pl.when(self.grid.wide == LANE_WIDE)
        def _():
            for copy in self.quarters():
                copy.start()

        pltpu.make_async_copy(self.source, self.own, self.local.at[4]).start()

        @pl.when(self.side == 1)
        def _():
            self.mine[pl.ds(self.rows, self.quarter), :] = jnp.zeros((self.quarter, self.mine.shape[1]), bf16)

    def stage_a(self):
        pltpu.make_async_copy(self.source, self.own, self.local.at[4]).wait()
        keep = self.plan.lane_of(self.grid.wide) == self.side
        for part in range(3):
            start, size = self.cuts[part]
            place = (pl.ds(start, size), slice(None))

            @pl.when(self.paired)
            def _():
                self.swaps()[part].wait_recv()
                self.mine[place] = jnp.where(keep, self.own[place], self.taken[place])

            @pl.when(jnp.logical_not(self.paired))
            def _():
                self.mine[place] = self.own[place]

            if part == 2:

                @pl.when(self.side == 0)
                def _():
                    self.quarters()[0].wait_recv()

            for number, axis in enumerate(self.order(part)):
                self.push(part, 0, axis, number)
            self.to_partner(part, 0)
            for i, there, own in self.pieces(part, 0, self.grid.c):
                pltpu.make_async_copy(own, there, self.local.at[i]).start()

    def stage_b(self):
        for part in range(3):
            a, b, c = self.order(part)
            self.arrived(part, 1 << a)
            self.push(part, 1 << a, b, 3)
            self.push(part, 1 << a, c, 4)
            self.to_partner(part, 1 << a)
            self.arrived(part, 1 << b)
            self.push(part, 1 << b, c, 5)
            self.to_partner(part, 1 << b)
        for part in range(3):
            a, b, c = self.order(part)
            self.arrived(part, 1 << a | 1 << b)
            self.push(part, 1 << a | 1 << b, c, 6)
            self.to_partner(part, 1 << a | 1 << b)

    def stage_c(self):
        for part in range(3):
            a, b, c = self.order(part)
            for mask in (1 << c, 1 << a | 1 << c, 1 << b | 1 << c, 7):
                self.arrived(part, mask)
                self.to_partner(part, mask)

    def finish(self):
        for part in range(3):
            for i, there, own in self.pieces(part, 0, self.grid.c):
                for number in range(7):
                    remote(own, there, self.sent.at[i, number], self.got.at[i, 0], self.grid.partner).wait_send()
                for mask in range(8):
                    remote(own, there, self.sent_pair.at[i, mask], self.got.at[i, 0], self.grid.partner).wait_send()
                pltpu.make_async_copy(own, there, self.local.at[i]).wait()
            for mask in range(8):
                for i, there, _ in self.pieces(part, mask, 1 - self.grid.c):
                    remote(there, there, self.sent.at[i, 0], self.got_pair.at[i, mask], self.grid.partner).wait_recv()

        @pl.when(self.paired)
        def _():
            for copy in self.swaps():
                copy.wait_send()

        @pl.when(self.grid.wide == LANE_WIDE)
        def _():
            for copy in self.quarters():
                copy.wait_send()

    def middle(self):
        self.stage_a()
        self.stage_b()
        self.stage_c()

    def index(self, turn):
        start = lax.rem(self.plan.start + turn, self.plan.long)
        return jnp.where(self.plan.lane == 0, start, jnp.minimum(turn + 1, LANE_WIDE - 1))


class SpanGather(Gather):
    def __init__(self, grid, plan, source, whole, refs):
        super().__init__(grid, source, whole, refs[1:5])
        self.plan, self.own, self.local = plan, refs[0], refs[5]

    @classmethod
    def scratch(cls, rows, cols):
        return [pltpu.VMEM((rows, cols), bf16)] + Gather.scratch() + [pltpu.SemaphoreType.DMA((1,))]

    @staticmethod
    def shape(rows, cols):
        return (lax.axis_size("wide"), lax.axis_size("narrow"), rows, cols)

    def own_copies(self):
        there = self.whole.at[self.grid.wide, self.grid.narrow]
        return (
            pltpu.make_async_copy(self.source, self.own, self.local.at[0]),
            pltpu.make_async_copy(self.own, there, self.local.at[0]),
        )

    def begin(self):
        super().begin()
        self.own_copies()[0].start()

    def stage_a(self):
        self.own_copies()[0].wait()
        self.own_copies()[1].start()
        for number in range(1, self.grid.zs):
            self.along_z(number)
        self.across(0)

    def stage_b(self):
        for number in range(1, self.grid.zs):
            self.across(number)
        self.last(0)

    def stage_c(self):
        for number in range(1, self.grid.zs):
            self.last(number)

    def finish(self):
        super().finish()
        self.own_copies()[1].wait()

    def middle(self):
        self.stage_a()
        self.stage_b()
        self.stage_c()

    def index(self, turn):
        return self.plan.span(turn)


def lane_gather():
    return LaneGather if paired_lanes() else SpanGather


def head_sums(values):
    width = values.shape[1]
    row = lax.broadcasted_iota(jnp.int32, (width, width), 0) // HEAD
    column = lax.broadcasted_iota(jnp.int32, (width, width), 1) // HEAD
    same = jnp.where(row == column, 1.0, 0.0)
    return jnp.dot(values, same, precision=lax.Precision.HIGHEST, preferred_element_type=f32)


def front_step(tokens, tail, gain, weights, taps, rates, lengths, pick, ident):
    span, width = tokens.shape
    block = weights.shape[1] // 3
    wide, narrow = lax.axis_size("wide"), lax.axis_size("narrow")
    devices = wide * narrow
    shards = LANE_WIDE * narrow
    shard_rows = span // shards
    kind = lane_gather()
    count = 4

    def kernel(*refs):
        tokens_ref, tail_ref, gain_ref, weights_ref, taps_ref, rates_ref, lengths_ref = refs[:7]
        keys_out, chunks_out, tile_out, key_out, query_out, value_out = refs[7:13]
        normed_out, ext_out, mixed_out, mean_out, gate_out = refs[13:18]
        tail_low, tile, send, recv = refs[18:22]
        g = Grid()
        me = g.wide * narrow + g.narrow
        plan = Plan(lengths_ref, None, lengths.shape[0])
        wait_all = g.greet_all()
        gather = kind(g, plan, key_out, keys_out, refs[22:])

        def normed_of(rows):
            values = rows.astype(f32)
            factor = lax.rsqrt(jnp.mean(values * values, axis=-1, keepdims=True) + eps_norm)
            return values * factor * gain_ref[...]

        normed = normed_of(tokens_ref[...])
        normed_out[...] = normed.astype(bf16)
        mean_out[...] = jnp.mean(normed, axis=0, keepdims=True)
        tail_low[...] = normed_of(tail_ref[...]).astype(bf16)
        begins = plan.begins(g.wide)

        def activated(third):
            columns = pl.ds(third * block, block)
            ext_out[pl.ds(0, 8), columns] = jnp.where(begins, 0.0, matmul(tail_low[...], weights_ref[:, columns]))
            ext_out[pl.ds(8, span), columns] = matmul(normed_out[...], weights_ref[:, columns])
            mixed = taps_ref[pl.ds(0, 1), columns] * ext_out[pl.ds(8, span), columns]
            for j in range(1, count):
                mixed = mixed + taps_ref[pl.ds(j, 1), columns] * ext_out[pl.ds(8 - j, span), columns]
            mixed_out[:, columns] = mixed
            return mixed * sigmoid(mixed)

        def normed_heads(values):
            return (values * lax.rsqrt(head_sums(values * values) + eps_head)).astype(bf16)

        key_out[...] = normed_heads(activated(1))
        wait_all()
        gather.begin()
        value_out[...] = activated(2).astype(bf16).reshape(shards, shard_rows, block)
        column = lax.broadcasted_iota(jnp.int32, (8, 128), 1)
        gates = jnp.zeros((8, 128), f32)
        for i in range(3):
            logit = jnp.sum(mean_out[...] * rates_ref[pl.ds(i, 1), :], axis=1, keepdims=True)
            gates = jnp.where(column == i, sigmoid(logit), gates)
        gate_out[...] = gates
        scale = jnp.where(column == 0, decay_top, jnp.where(column == 1, moment_top, learn_top))
        tile[...] = gates * scale

        def send_chunks(step, carry):
            target = lax.rem(me + step, devices)
            where = lax.div(target, narrow), lax.rem(target, narrow)
            remote(value_out.at[pick(*where)], chunks_out.at[me], send.at[0], recv.at[0], where).start()
            remote(tile, tile_out.at[me], send.at[1], recv.at[1], where).start()
            return carry

        lax.fori_loop(1, devices, send_chunks, 0)
        chunks_out[me] = value_out[pick(g.wide, g.narrow)]
        tile_out[me] = tile[...]
        query_out[...] = normed_heads(activated(0))
        gather.middle()
        for i, out in enumerate((chunks_out, tile_out)):
            others = out.at[pl.ds(0, devices - 1)]
            whole = remote(others, others, send.at[i], recv.at[i], g.partner)
            whole.wait_send()
            whole.wait_recv()
        gather.finish()

    vmem = pl.BlockSpec(memory_space=pltpu.VMEM)
    return pl.pallas_call(
        kernel,
        out_shape=[
            jax.ShapeDtypeStruct(kind.shape(span, block), bf16),
            jax.ShapeDtypeStruct((devices, shard_rows, block), bf16),
            jax.ShapeDtypeStruct((devices, 8, 128), f32),
            jax.ShapeDtypeStruct((span, block), bf16),
            jax.ShapeDtypeStruct((span, block), bf16),
            jax.ShapeDtypeStruct((shards, shard_rows, block), bf16),
            jax.ShapeDtypeStruct((span, width), bf16),
            jax.ShapeDtypeStruct((8 + span, 3 * block), f32),
            jax.ShapeDtypeStruct((span, 3 * block), f32),
            jax.ShapeDtypeStruct((1, width), f32),
            jax.ShapeDtypeStruct((8, 128), f32),
        ],
        in_specs=[vmem] * 6 + [pl.BlockSpec(memory_space=pltpu.SMEM)],
        out_specs=[ANY] + [vmem] * 10,
        scratch_shapes=[
            pltpu.VMEM((8, width), bf16),
            pltpu.VMEM((8, 128), f32),
            pltpu.SemaphoreType.DMA((2,)),
            pltpu.SemaphoreType.DMA((2,)),
        ]
        + kind.scratch(span, block),
        compiler_params=pltpu.CompilerParams(
            collective_id=ident, has_side_effects=True, vmem_limit_bytes=40 * 1024 * 1024
        ),
        name="front_step",
    )(tokens, tail, gain, weights, taps, rates, lengths)


def matmul(left_side, right_side):
    return jnp.dot(left_side, right_side, preferred_element_type=jnp.float32)


def inner_left(left_side, right_side):
    return lax.dot_general(left_side, right_side, (((0,), (0,)), ((), ())), preferred_element_type=jnp.float32)


def inner_right(left_side, right_side):
    return lax.dot_general(left_side, right_side, (((1,), (1,)), ((), ())), preferred_element_type=jnp.float32)


def silu_slope(values):
    sigmoid_val = sigmoid(values)
    return sigmoid_val * (1.0 + values * (1.0 - sigmoid_val))


def silu_curve(values):
    sigmoid_val = sigmoid(values)
    return sigmoid_val * (1.0 - sigmoid_val) * (2.0 + values * (1.0 - 2.0 * sigmoid_val))


class Lane:
    def __init__(self):
        narrow = lax.axis_size("narrow")
        self.ys = narrow // 2
        self.chips = LANE_WIDE * self.ys
        wide_pos, narrow_pos = lax.axis_index("wide"), lax.axis_index("narrow")
        self.base = lax.div(wide_pos, LANE_WIDE) * LANE_WIDE
        self.colour = lax.rem(narrow_pos, 2)
        self.chip = lax.rem(wide_pos, LANE_WIDE) * self.ys + lax.div(narrow_pos, 2)
        self.partner = (wide_pos, narrow_pos + 1 - 2 * self.colour)

    def other(self, step):
        return lax.rem(self.chip + step, self.chips)

    def device(self, chip):
        return self.base + lax.div(chip, self.ys), 2 * lax.rem(chip, self.ys) + self.colour

    def greet(self):
        barrier = pltpu.get_barrier_semaphore()
        for step in range(1, self.chips):
            pl.semaphore_signal(barrier, inc=1, device_id=self.device(self.other(step)), device_id_type=MESH)
        pl.semaphore_signal(barrier, inc=1, device_id=self.partner, device_id_type=MESH)
        pl.semaphore_wait(barrier, self.chips)


class Scatter:
    def __init__(self, lane, part, pair, half, got, sems, own=None):
        self.lane, self.part, self.pair, self.half, self.got, self.own = lane, part, pair, half, got, own
        self.pair_send, self.pair_recv, self.send, self.recv = sems

    @staticmethod
    def scratch(chips, rows, width, pair_type=f32):
        return [
            pltpu.VMEM((rows, width), f32),
            pltpu.VMEM((2, chips, rows, width), pair_type),
            pltpu.VMEM((chips, rows, width), pair_type),
            pltpu.VMEM((chips, rows, width), bf16),
            pltpu.VMEM((chips, rows, width), bf16),
            pltpu.SemaphoreType.DMA((1,)),
            pltpu.SemaphoreType.DMA((1,)),
            pltpu.SemaphoreType.DMA((chips,)),
            pltpu.SemaphoreType.DMA((chips,)),
        ]

    @classmethod
    def of(cls, lane, refs):
        return cls(lane, *refs[1:5], refs[5:9], refs[0])

    def pair_copy(self):
        return remote(
            self.part.at[1 - self.lane.colour],
            self.pair,
            self.pair_send.at[0],
            self.pair_recv.at[0],
            self.lane.partner,
        )

    def start_pair(self):
        self.pair_copy().start()

    def take_pair(self):
        self.pair_copy().wait()
        self.half[...] = (self.part[self.lane.colour].astype(f32) + self.pair[...].astype(f32)).astype(bf16)
        if self.own is None:
            self.got[self.lane.chip] = self.half[self.lane.chip]
        else:
            chip = self.lane.chip
            self.own[...] = self.part[self.lane.colour, chip].astype(f32) + self.pair[chip].astype(f32)

    def copy_to(self, step):
        chip = self.lane.other(step)
        return remote(
            self.half.at[chip],
            self.got.at[self.lane.chip],
            self.send.at[step],
            self.recv.at[self.lane.chip],
            self.lane.device(chip),
        )

    def start_sends(self):
        for step in range(1, self.lane.chips):
            self.copy_to(step).start()

    def total(self):
        result = self.got[self.lane.chip].astype(f32) if self.own is None else self.own[...]
        for step in range(1, self.lane.chips):
            chip = self.lane.other(step)
            remote(
                self.got.at[chip], self.got.at[chip], self.send.at[step], self.recv.at[chip], self.lane.device(chip)
            ).wait_recv()
            result = result + self.got[chip].astype(f32)
        return result

    def wait_sends(self):
        for step in range(1, self.lane.chips):
            self.copy_to(step).wait_send()


class Spread:
    def __init__(self, lane, whole, sems):
        self.lane, self.whole = lane, whole
        self.send, self.recv, self.pair_send, self.pair_recv = sems

    @staticmethod
    def scratch(chips, rows, width):
        return [pltpu.VMEM((2, chips, rows, width), bf16)] + [pltpu.SemaphoreType.DMA((chips,))] * 4

    @classmethod
    def of(cls, lane, refs):
        return cls(lane, refs[0], refs[1:5])

    def mine(self):
        return self.whole.at[self.lane.colour, self.lane.chip]

    def copy_to(self, step):
        return remote(
            self.mine(),
            self.mine(),
            self.send.at[step],
            self.recv.at[self.lane.chip],
            self.lane.device(self.lane.other(step)),
        )

    def pair_copy(self, chip, colour):
        place = self.whole.at[colour, chip]
        return remote(place, place, self.pair_send.at[chip], self.pair_recv.at[chip], self.lane.partner)

    def run(self, meanwhile=None):
        lane = self.lane
        for step in range(1, lane.chips):
            self.copy_to(step).start()
        self.pair_copy(lane.chip, lane.colour).start()
        if meanwhile is not None:
            meanwhile()
        for step in range(1, lane.chips):
            chip = lane.other(step)
            place = self.whole.at[lane.colour, chip]
            remote(place, place, self.send.at[step], self.recv.at[chip], lane.device(chip)).wait_recv()
            self.pair_copy(chip, lane.colour).start()
        for chip in range(lane.chips):
            self.pair_copy(chip, 1 - lane.colour).wait_recv()
        for step in range(1, lane.chips):
            self.copy_to(step).wait_send()
        for chip in range(lane.chips):
            self.pair_copy(chip, lane.colour).wait_send()


class Deliver:
    def __init__(self, grid, plan, chips, out, got, sems):
        self.grid, self.plan, self.chips, self.out, self.got = grid, plan, chips, out, got
        self.send, self.recv = sems
        self.wide, self.narrow = lax.axis_size("wide"), lax.axis_size("narrow")
        self.me = grid.wide * self.narrow + grid.narrow

    @staticmethod
    def scratch(kinds, rows, block):
        devices = lax.axis_size("wide") * lax.axis_size("narrow")
        return [pltpu.VMEM((devices, kinds, rows, block), bf16)] * 2 + [pltpu.SemaphoreType.DMA((1,))] * 2

    def start(self, kinds):
        block = self.out.shape[3]
        for span in range(self.wide):
            turn = self.plan.turn_of(span)
            for i, kind in enumerate(kinds):
                lane_rows = kind[turn]
                for n in range(self.narrow):
                    self.out[span * self.narrow + n, i] = lane_rows[:, n * block : (n + 1) * block]

        def push(step, carry):
            target = lax.rem(self.me + step, self.wide * self.narrow)
            where = lax.div(target, self.narrow), lax.rem(target, self.narrow)
            remote(self.out.at[target], self.got.at[self.me], self.send.at[0], self.recv.at[0], where).start()
            return carry

        lax.fori_loop(1, self.wide * self.narrow, push, 0)
        self.got[self.me] = self.out[self.me]

    def finish(self, result):
        others = self.got.at[pl.ds(0, self.wide * self.narrow - 1)]
        whole = remote(others, others, self.send.at[0], self.recv.at[0], self.grid.partner)
        whole.wait_send()
        whole.wait_recv()
        base = self.plan.lane_of(self.grid.wide) * LANE_WIDE
        ys = self.narrow // 2
        for p in range(LANE_WIDE):
            for y in range(ys):
                for colour in range(2):
                    source = (base + p) * self.narrow + 2 * y + colour
                    for i in range(result.shape[0]):
                        result[i, colour, p * ys + y] = self.got[source, i]


def chain_forward(keys, values, queries, lengths, gates, turns, first_init, second_init, ident):
    wide = lax.axis_size("wide")
    blocks, span, block = keys.shape[1:]
    width, hidden = first_init.shape
    rows = values.shape[1]
    sequences = lengths.shape[0]
    key_turns = turns - 1
    kind = lane_gather()
    own_rows = kind.scratch(span, block)
    per_turn, ask_from = (2, 2) if paired_lanes() else (1, 3)
    first_left = per_turn * (key_turns - ask_from)
    slots = 3
    stream_keys = not paired_lanes()
    chips = LANE_WIDE * (lax.axis_size("narrow") // 2)
    n_scatter = len(Scatter.scratch(1, 8, 128))

    def kernel(*refs):
        keys_hbm, values_hbm, own_hbm, lengths_ref, gates_ref, first_hbm, second_hbm = refs[:7]
        recalled_hbm, low1_hbm, low2_hbm, s1_hbm, s2_hbm, m1_hbm, m2_hbm, g1_hbm, g2_hbm = refs[7:16]
        err_hbm, pre_hbm, qpre_hbm, klane_hbm, qlane_hbm = refs[16:21]
        rest = refs[21:]
        kall, qall, vall, kcur, qcur, i1, i2, s1, s2, m1, m2, gb1, gb2, low1, low2 = rest[:15]
        pre, qpre, khid, rec, qpart, qpair, qhalf, qgot = rest[15:23]
        in_sem, out_sem, q_sem, q_pair_send, q_pair_recv, q_send, q_recv = rest[23:30]
        rest = rest[30:]
        lane = Lane()
        grid = Grid()
        plan = Plan(lengths_ref, gates_ref, sequences)
        lookup = Scatter.of(lane, rest[:n_scatter])
        error = Spread.of(lane, rest[n_scatter : n_scatter + 5])
        rest = rest[n_scatter + 5 :]
        gather = kind(grid, plan, own_hbm, qall, rest[: len(own_rows)])
        rest = rest[len(own_rows) :]
        deliver = Deliver(grid, plan, chips, *rest[:2], rest[2:4])
        result = rest[4]

        def recall(q, slot):
            sems = q_pair_send.at[pl.ds(q, 1)], q_pair_recv.at[pl.ds(q, 1)], q_send.at[q], q_recv.at[q]
            return Scatter(lane, qpart.at[slot], qpair.at[q], qhalf.at[slot], qgot.at[q], sems)

        def state_saves(turn):
            return [
                pltpu.make_async_copy(source, target.at[turn], out_sem.at[i])
                for i, (source, target) in enumerate(((m1, m1_hbm), (m2, m2_hbm), (kcur, klane_hbm), (s1, s1_hbm), (s2, s2_hbm)))
            ]

        def other_saves(turn):
            return [
                pltpu.make_async_copy(source, target.at[turn], out_sem.at[5 + i])
                for i, (source, target) in enumerate(
                    ((gb1, g1_hbm), (gb2, g2_hbm), (error.whole, err_hbm), (pre, pre_hbm))
                )
            ]

        def query_saves(q, slot):
            return [
                pltpu.make_async_copy(source.at[slot], target.at[q], q_sem.at[slot, i])
                for i, (source, target) in enumerate(((qcur, qlane_hbm), (qpre, qpre_hbm)))
            ]

        inputs = [
            pltpu.make_async_copy(source, target, in_sem.at[i])
            for i, (source, target) in enumerate(
                ((first_hbm, i1), (second_hbm, i2), (keys_hbm, kall), (values_hbm, vall))
            )
            if not (stream_keys and i == 2)
        ]
        for copy in inputs:
            copy.start()
        grid.greet_all()()
        gather.begin()
        for copy in inputs:
            copy.wait()
        low1[0] = i1[...]
        low2[0] = i2[...]
        s1[...] = i1[...].astype(f32)
        s2[...] = i2[...].astype(f32)
        for ref in (m1, m2):
            ref[...] = jnp.zeros_like(ref)

        def lookup_blocks(buf, first):
            total = matmul(buf[0], first[pl.ds(0, block), :])
            for b in range(1, blocks):
                total = total + matmul(buf[b], first[pl.ds(b * block, block), :])
            return total

        def ask(q, slot, waits):
            def settle():
                recall(q - slots, slot).wait_sends()
                for copy in query_saves(q - slots, slot):
                    copy.wait()

            if waits is True:
                settle()
            elif waits is not False:
                pl.when(waits)(settle)
            index = gather.index(q)
            for b in range(blocks):
                qcur[slot, b] = qall[index, b]
            query_pre = lookup_blocks(qcur.at[slot], low1.at[q])
            qpre[slot] = query_pre
            for copy in query_saves(q, slot):
                copy.start()
            query_hidden = (query_pre * sigmoid(query_pre)).astype(bf16)
            qpart[slot] = matmul(query_hidden, low2[q]).astype(bf16).reshape(2, chips, rows, width)
            recall(q, slot).start_pair()

        def turn_body(turn, carry):
            index = plan.span(turn)
            if stream_keys:
                one = pltpu.make_async_copy(keys_hbm.at[turn], kcur, in_sem.at[2])
                one.start()
                one.wait()
            else:
                for b in range(blocks):
                    kcur[b] = kall[gather.index(turn), b]
            for copy in state_saves(turn):
                copy.start()
            key_pre = lookup_blocks(kcur, low1.at[turn])
            pre[0] = key_pre
            khid[...] = (key_pre * sigmoid(key_pre)).astype(bf16)
            lookup.part[...] = matmul(khid[...], low2[turn]).reshape(2, chips, rows, width)
            lookup.start_pair()

            @pl.when(turn == ask_from)
            def _():
                gather.finish()

            first = per_turn * (turn - ask_from)

            @pl.when(turn >= ask_from)
            def _():
                ask(first, lax.rem(first, slots), first >= slots)

            lookup.take_pair()
            lookup.start_sends()

            @pl.when(turn >= ask_from)
            def _():
                recall(first, lax.rem(first, slots)).take_pair()
                for j in range(1, per_turn):
                    ask(first + j, lax.rem(first + j, slots), first + j >= slots)

            if paired_lanes():
                pl.when(turn == 1)(gather.stage_b)

            total = lookup.total()
            target = jnp.concatenate([vall[index * blocks + b] for b in range(blocks)], axis=1)
            error.whole[lane.colour, lane.chip] = ((total - target.astype(f32)) / span).astype(bf16)
            error.run()
            lookup.wait_sends()

            @pl.when(turn >= ask_from)
            def _():
                recall(first, lax.rem(first, slots)).start_sends()
                for j in range(1, per_turn):
                    stream = recall(first + j, lax.rem(first + j, slots))
                    stream.take_pair()
                    stream.start_sends()

            if paired_lanes():
                pl.when(turn == 0)(gather.stage_a)
                pl.when(turn == 1)(gather.stage_c)

            err = error.whole[...].reshape(span, width)
            grad_second = inner_left(khid[...], err)
            hidden_grad = inner_right(err, low2[turn])
            pre[1] = hidden_grad
            slope = (hidden_grad * silu_slope(pre[0])).astype(bf16)
            decay, moment, rate = plan.rates(turn)
            reset = plan.first(turn + 1)
            for copy in state_saves(turn):
                copy.wait()
            following = jnp.minimum(turn + 1, turns - 1)

            def update(s, m, init, low, grad, place):
                moment_new = moment * m[place] - rate * grad
                state_new = (1.0 - decay) * s[place] + moment_new
                state_new = reset * init[place].astype(f32) + (1.0 - reset) * state_new
                moment_new = (1.0 - reset) * moment_new
                m[place] = moment_new
                s[place] = state_new
                low[(following,) + place] = state_new.astype(bf16)

            gb2[...] = grad_second
            update(s2, m2, i2, low2, grad_second, (slice(None), slice(None)))
            for b in range(blocks):
                grad_first = inner_left(kcur[b], slope)
                place = (pl.ds(b * block, block), slice(None))
                gb1[place] = grad_first
                update(s1, m1, i1, low1, grad_first, place)
            saves = other_saves(turn)
            for copy in saves:
                copy.start()

            if not paired_lanes():
                pl.when(turn == 0)(gather.stage_a)
                pl.when(turn == 1)(gather.stage_b)
                pl.when(turn == 2)(gather.stage_c)

            for copy in saves:
                copy.wait()
            return carry

        lax.fori_loop(0, key_turns, turn_body, 0)
        ends = [
            pltpu.make_async_copy(low1, low1_hbm, out_sem.at[0]),
            pltpu.make_async_copy(low2, low2_hbm, out_sem.at[1]),
        ]
        for copy in ends:
            copy.start()
        left = list(range(first_left, turns))
        for q in left:
            ask(q, q % slots, q >= slots)
            if q > left[0]:
                stream = recall(q - 1, (q - 1) % slots)
                stream.take_pair()
                stream.start_sends()
        stream = recall(turns - 1, (turns - 1) % slots)
        stream.take_pair()
        stream.start_sends()
        for q in range(turns):
            rec[q] = recall(q, q % slots).total().astype(bf16)
        deliver.start([rec])
        for q in range(turns - slots, turns):
            recall(q, q % slots).wait_sends()
        for q in range(turns - slots, turns):
            for copy in query_saves(q, q % slots):
                copy.wait()
        deliver.finish(result)
        last = pltpu.make_async_copy(result.at[0], recalled_hbm, out_sem.at[2])
        last.start()
        for copy in ends + [last]:
            copy.wait()

    state = [(width, hidden), (hidden, width)]
    out_shape = (
        [jax.ShapeDtypeStruct((2, chips, rows, block), bf16)]
        + [jax.ShapeDtypeStruct((turns,) + s, bf16) for s in state]
        + [jax.ShapeDtypeStruct((key_turns,) + s, f32) for s in state * 3]
        + [
            jax.ShapeDtypeStruct((key_turns, 2, chips, rows, width), bf16),
            jax.ShapeDtypeStruct((key_turns, 2, span, hidden), f32),
            jax.ShapeDtypeStruct((turns, span, hidden), f32),
            jax.ShapeDtypeStruct((key_turns, blocks, span, block), bf16),
            jax.ShapeDtypeStruct((turns, blocks, span, block), bf16),
        ]
    )
    sem = pltpu.SemaphoreType.DMA
    scratch = (
        [pltpu.VMEM((1 if stream_keys else keys.shape[0], blocks, span, block), bf16), pltpu.VMEM(kind.shape(span, block), bf16)]
        + [pltpu.VMEM(values.shape, bf16)]
        + [pltpu.VMEM((blocks, span, block), bf16), pltpu.VMEM((slots, blocks, span, block), bf16)]
        + [pltpu.VMEM(s, bf16) for s in state]
        + [pltpu.VMEM(s, f32) for s in state * 3]
        + [pltpu.VMEM((turns,) + s, bf16) for s in state]
        + [
            pltpu.VMEM((2, span, hidden), f32),
            pltpu.VMEM((slots, span, hidden), f32),
            pltpu.VMEM((span, hidden), bf16),
            pltpu.VMEM((turns, rows, width), bf16),
            pltpu.VMEM((slots, 2, chips, rows, width), bf16),
        ]
        + [pltpu.VMEM((n, chips, rows, width), bf16) for n in (turns, slots, turns)]
        + [sem((4,)), sem((9,)), sem((slots, 2)), sem((turns,)), sem((turns,)), sem((turns, chips)), sem((turns, chips))]
        + Scatter.scratch(chips, rows, width)
        + Spread.scratch(chips, rows, width)
        + own_rows
        + Deliver.scratch(1, rows, block)
        + [pltpu.VMEM((1, 2, chips, rows, block), bf16)]
    )
    smem = pl.BlockSpec(memory_space=pltpu.SMEM)
    return pl.pallas_call(
        kernel,
        out_shape=out_shape,
        in_specs=[ANY] * 3 + [smem] * 2 + [ANY] * 2,
        out_specs=[ANY] * len(out_shape),
        scratch_shapes=scratch,
        compiler_params=pltpu.CompilerParams(
            collective_id=ident, has_side_effects=True, vmem_limit_bytes=62 * 1024 * 1024
        ),
        cost_estimate=pl.CostEstimate(
            flops=40 * turns * 2 * span * width * hidden, bytes_accessed=turns * 40 * 2**20, transcendentals=0
        ),
        name="chain_forward",
    )(keys, values, queries, lengths, gates, first_init, second_init)


def chain_backward(recall_grad, saved, lengths, gates, ident):
    low1_all, low2_all, s1_all, s2_all, m1_all, m2_all, g1_all, g2_all, err_all, pre_all, qpre_all, keys, queries = saved
    wide = lax.axis_size("wide")
    devices = wide * lax.axis_size("narrow")
    key_turns, blocks, span, block = keys.shape
    turns = key_turns + 1
    width, hidden = low1_all.shape[1:]
    chips, rows = err_all.shape[2:4]
    n_scatter = len(Scatter.scratch(1, 8, 128))
    kind = lane_gather()
    own_rows = kind.scratch(span, block)

    def kernel(*refs):
        own_hbm, q_ins, k_ins, lengths_ref, gates_ref = refs[0], refs[1:5], refs[5:14], refs[14], refs[15]
        cots_hbm, sums_out, mg1_hbm, mg2_hbm = refs[16:20]
        rest = refs[20:]
        q_bufs, k_bufs, rest = rest[:4], rest[4:13], rest[13:]
        qbuf, low1, low2, qpre = q_bufs
        kbuf, s1, s2, m1, m2, g1, g2, errs, pre = k_bufs
        rall, cf, cs, cmf, cms, w1, w2, a1, a2, c1, c2 = rest[:11]
        dh, khid, qpl, qhid, kpl, slow, sg, hk, qcots, kcots, vcots, sumrows, tile, mb1, mb2, result = rest[11:27]
        q_sem, k_sem, end_sem, tile_send, tile_recv = rest[27:32]
        rest = rest[32:]
        lane = Lane()
        grid = Grid()
        plan = Plan(lengths_ref, gates_ref, lengths.shape[0])
        lookup = Scatter.of(lane, rest[:n_scatter])
        qstream = Scatter.of(lane, rest[n_scatter : 2 * n_scatter])
        kstream = Scatter.of(lane, rest[2 * n_scatter : 3 * n_scatter])
        spread = Spread.of(lane, rest[3 * n_scatter : 3 * n_scatter + 5])
        rest = rest[3 * n_scatter + 5 :]
        gather = kind(grid, plan, own_hbm, rall, rest[: len(own_rows)])
        rest = rest[len(own_rows) :]
        deliver = Deliver(grid, plan, chips, *rest[:2], rest[2:4])

        def q_loads(turn, slot):
            return [
                pltpu.make_async_copy(source.at[turn], target.at[slot], q_sem.at[slot, i])
                for i, (source, target) in enumerate(zip(q_ins, q_bufs))
            ]

        def k_loads(turn, slot):
            return [
                pltpu.make_async_copy(source.at[turn], target.at[slot], k_sem.at[slot, i])
                for i, (source, target) in enumerate(zip(k_ins, k_bufs))
            ]

        grid.greet_all()()
        gather.begin()
        for copy in q_loads(turns - 1, 0) + q_loads(turns - 2, 1) + k_loads(turns - 2, 1):
            copy.start()
        for ref in (cf, cs, cmf, cms, a1, a2):
            ref[...] = jnp.zeros_like(ref)
        gather.middle()
        gather.finish()

        kcots[turns - 1] = jnp.zeros((rows, width), bf16)
        vcots[turns - 1] = jnp.zeros((rows, width), bf16)
        sumrows[turns - 1] = jnp.zeros((8, 128), f32)

        def finish(stream, save, turn):
            save[turn] = stream.total().astype(bf16)
            stream.wait_sends()

        def query_rows(turn, slot):
            index = gather.index(turn)
            back = inner_right(rall[index, 0], low2[slot, :, pl.ds(0, block)])
            for b in range(1, blocks):
                back = back + inner_right(rall[index, b], low2[slot, :, pl.ds(b * block, block)])
            query_pre = qpre[slot]
            qpl[...] = (plan.valid(turn) * back * silu_slope(query_pre)).astype(bf16)
            qhid[...] = (query_pre * sigmoid(query_pre)).astype(bf16)
            qstream.part[...] = inner_right(qpl[...], low1[slot]).astype(bf16).reshape(2, chips, rows, width)
            qstream.start_pair()

        def query_weights(turn, slot):
            index = gather.index(turn)
            valid = plan.valid(turn)
            for b in range(blocks):
                w1[pl.ds(b * block, block), :] = inner_left(qbuf[slot, b], qpl[...])
                w2[:, pl.ds(b * block, block)] = valid * inner_left(qhid[...], rall[index, b])

        def key_rows(slot):
            kstream.part[...] = (
                (inner_right(kpl[...], low1[slot]) + inner_right(slow[...], c1[slot]))
                .reshape(2, chips, rows, width)
            )

        for copy in q_loads(turns - 1, 0):
            copy.wait()
        query_rows(turns - 1, 0)
        query_weights(turns - 1, 0)
        reset = plan.first(turns - 1)
        for c, w, acc in ((cf, w1, a1), (cs, w2, a2)):
            acc[...] = reset * w[...]
            c[...] = (1.0 - reset) * w[...]
        qstream.take_pair()
        qstream.start_sends()

        def body(step, carry):
            turn = turns - 1 - step
            slot = lax.rem(step, 2)
            decay, moment, rate = plan.rates(turn)
            reset = plan.first(turn)
            for copy in q_loads(turn, slot) + k_loads(turn, slot):
                copy.wait()
            c1[slot] = (-rate * (cmf[...] + cf[...])).astype(bf16)
            c2[...] = (-rate * (cms[...] + cs[...])).astype(bf16)
            slope_grad = matmul(kbuf[slot, 0], c1[slot, pl.ds(0, block), :])
            for b in range(1, blocks):
                slope_grad = slope_grad + matmul(kbuf[slot, b], c1[slot, pl.ds(b * block, block), :])
            sg[...] = slope_grad
            key_pre = pre[slot, 0]
            khid[...] = (key_pre * sigmoid(key_pre)).astype(bf16)
            dh[...] = (slope_grad * silu_slope(key_pre)).astype(bf16)
            lookup.part[...] = (
                (matmul(khid[...], c2[...]) + matmul(dh[...], low2[slot])).reshape(2, chips, rows, width)
            )
            lookup.start_pair()
            finish(qstream, qcots, turn + 1)

            @pl.when(step > 2)
            def _():
                finish(kstream, kcots, turn + 2)

            lookup.take_pair()
            lookup.start_sends()
            query_rows(turn, slot)

            @pl.when(step > 1)
            def _():
                key_rows(1 - slot)
                kstream.start_pair()

            @pl.when(step + 1 < turns)
            def _():
                for copy in q_loads(turn - 1, 1 - slot) + k_loads(turn - 1, 1 - slot):
                    copy.start()

            query_weights(turn, slot)
            err = errs[slot].reshape(span, width)
            hk[...] = inner_right(err, c2[...])
            w2[...] += inner_left(dh[...], err)

            def whole_sum(first_a, first_b, second_a, second_b):
                first = jnp.sum(first_a * first_b, axis=0, keepdims=True)
                second = jnp.sum(second_a * second_b, axis=0, keepdims=True)
                return jnp.sum(first, axis=1, keepdims=True) + jnp.sum(second, axis=1, keepdims=True)

            def gate_sums():
                kinds = (
                    whole_sum(cf[...], s1[slot], cs[...], s2[slot]),
                    whole_sum(cmf[...] + cf[...], m1[slot], cms[...] + cs[...], m2[slot]),
                    whole_sum(cmf[...] + cf[...], g1[slot], cms[...] + cs[...], g2[slot]),
                )
                column = lax.broadcasted_iota(jnp.int32, (8, 128), 1)
                sumrow = jnp.zeros((8, 128), f32)
                for i, kind in enumerate(kinds):
                    sumrow = jnp.where(column == i, kind, sumrow)
                sumrows[turn] = sumrow

            qstream.take_pair()
            total = lookup.total()
            mine = (total / span).astype(bf16)
            spread.whole[lane.colour, lane.chip] = mine
            vcots[turn] = mine
            spread.run(gate_sums)
            lookup.wait_sends()
            qstream.start_sends()

            @pl.when(step > 1)
            def _():
                kstream.take_pair()
                kstream.start_sends()

            out = spread.whole[...].reshape(span, width)
            hidden_back = hk[...] + inner_right(out, low2[slot])
            key_pre = pre[slot, 0]
            hidden_grad = pre[slot, 1]
            slope = silu_slope(key_pre)
            kpl[...] = (hidden_back * slope + sg[...] * hidden_grad * silu_curve(key_pre)).astype(bf16)
            slow[...] = (hidden_grad * slope).astype(bf16)

            def update(c, m, acc, grad_new, place):
                grad = (1.0 - decay) * c[place] + grad_new
                both = m[place] + c[place]
                acc[place] += reset * grad
                c[place] = (1.0 - reset) * grad
                m[place] = (1.0 - reset) * (moment * both)

            for b in range(blocks):
                place = (pl.ds(b * block, block), slice(None))
                update(cf, cmf, a1, w1[place] + inner_left(kbuf[slot, b], kpl[...]), place)
            place = (slice(None), slice(None))
            update(cs, cms, a2, w2[...] + inner_left(khid[...], out), place)
            return carry

        lax.fori_loop(1, turns, body, 0)
        tail = Scatter(
            lane,
            kstream.part,
            lookup.pair,
            lookup.half,
            lookup.got,
            (lookup.pair_send, lookup.pair_recv, lookup.send, lookup.recv),
            lookup.own,
        )
        key_rows((turns - 1) % 2)
        tail.start_pair()
        mb1[...] = a1[...].astype(bf16).reshape(mb1.shape)
        for owner in range(wide):
            mb2[owner] = a2[:, owner * (width // wide) : (owner + 1) * (width // wide)].astype(bf16)
        ends = [
            pltpu.make_async_copy(mb1, mg1_hbm, end_sem.at[0]),
            pltpu.make_async_copy(mb2, mg2_hbm, end_sem.at[1]),
        ]
        for copy in ends:
            copy.start()
        for span_number in range(wide):
            here = jnp.where(plan.lane_of(span_number) == plan.lane, 1.0, 0.0)
            tile[pl.ds(span_number, 1), :] = here * sumrows[plan.turn_of(span_number)][:1]

        def send_tile(step, carry):
            target = lax.rem(deliver.me + step, devices)
            where = lax.div(target, blocks), lax.rem(target, blocks)
            remote(tile, sums_out.at[deliver.me], tile_send.at[0], tile_recv.at[0], where).start()
            return carry

        lax.fori_loop(1, devices, send_tile, 0)
        sums_out[deliver.me] = tile[...]
        finish(qstream, qcots, 0)
        if turns > 2:
            finish(kstream, kcots, 1)
        tail.take_pair()
        tail.start_sends()
        finish(tail, kcots, 0)
        deliver.start([qcots, kcots, vcots])
        others = sums_out.at[pl.ds(0, devices - 1)]
        tiles = remote(others, others, tile_send.at[0], tile_recv.at[0], grid.partner)
        tiles.wait_send()
        tiles.wait_recv()
        deliver.finish(result)
        ends.append(pltpu.make_async_copy(result, cots_hbm, end_sem.at[2]))
        ends[2].start()
        for copy in ends:
            copy.wait()

    state = [(width, hidden), (hidden, width)]
    q_buffers = [((blocks, span, block), bf16)] + [(s, bf16) for s in state] + [((span, hidden), f32)]
    k_buffers = (
        [((blocks, span, block), bf16)]
        + [(s, f32) for s in state * 3]
        + [((2, chips, rows, width), bf16), ((2, span, hidden), f32)]
    )
    by_owner = [(wide, width // wide, hidden), (wide, hidden, width // wide)]
    out_shape = [
        jax.ShapeDtypeStruct((3, 2, chips, rows, block), bf16),
        jax.ShapeDtypeStruct((devices, wide, 128), f32),
    ] + [jax.ShapeDtypeStruct(s, bf16) for s in by_owner]
    sem = pltpu.SemaphoreType.DMA
    scratch = (
        [pltpu.VMEM((2,) + s, t) for s, t in q_buffers + k_buffers]
        + [pltpu.VMEM(kind.shape(span, block), bf16)]
        + [pltpu.VMEM(s, f32) for s in state * 4]
        + [pltpu.VMEM((2,) + state[0], bf16), pltpu.VMEM(state[1], bf16)]
        + [pltpu.VMEM((span, hidden), bf16)] * 6
        + [pltpu.VMEM((span, hidden), f32)] * 2
        + [pltpu.VMEM((turns, rows, width), bf16)] * 3
        + [pltpu.VMEM((turns, 8, 128), f32), pltpu.VMEM((wide, 128), f32)]
        + [pltpu.VMEM(s, bf16) for s in by_owner]
        + [pltpu.VMEM((3, 2, chips, rows, block), bf16)]
        + [sem((2, 4)), sem((2, 9)), sem((3,)), sem((1,)), sem((1,))]
        + Scatter.scratch(chips, rows, width)
        + Scatter.scratch(chips, rows, width, bf16)
        + Scatter.scratch(chips, rows, width)
        + Spread.scratch(chips, rows, width)
        + own_rows
        + Deliver.scratch(3, rows, block)
    )
    vmem = pl.BlockSpec(memory_space=pltpu.VMEM)
    smem = pl.BlockSpec(memory_space=pltpu.SMEM)
    return pl.pallas_call(
        kernel,
        out_shape=out_shape,
        in_specs=[ANY] * 14 + [smem] * 2,
        out_specs=[ANY, vmem, ANY, ANY],
        scratch_shapes=scratch,
        compiler_params=pltpu.CompilerParams(
            collective_id=ident, has_side_effects=True, vmem_limit_bytes=63 * 1024 * 1024
        ),
        cost_estimate=pl.CostEstimate(
            flops=80 * turns * 2 * span * width * hidden, bytes_accessed=turns * 60 * 2**20, transcendentals=0
        ),
        name="chain_backward",
    )(
        recall_grad, queries, low1_all, low2_all, qpre_all, keys, s1_all, s2_all, m1_all, m2_all, g1_all, g2_all, err_all, pre_all,
        lengths, gates,
    )


def from_behind(value, axis, steps):
    count = lax.axis_size(axis)
    first, last = (max(0, -steps), min(count, count - steps))
    return lax.ppermute(value, axis, [(source, source + steps) for source in range(first, last)])


def split_heads(values, head_size):
    return values.reshape(values.shape[:-1] + (values.shape[-1] // head_size, head_size))


def head_norm(values, head_size):
    shaped = split_heads(values, head_size)
    factor = lax.rsqrt(jnp.sum(shaped * shaped, axis=-1, keepdims=True) + eps_head)
    return (shaped * factor).reshape(values.shape)


def head_norm_back(values, upstream, head_size):
    shaped = split_heads(values, head_size)
    grad_shaped = split_heads(upstream, head_size)
    factor = lax.rsqrt(jnp.sum(shaped * shaped, axis=-1, keepdims=True) + eps_head)
    normed = shaped * factor
    inner_sum = jnp.sum(normed * grad_shaped, axis=-1, keepdims=True)
    return (factor * (grad_shaped - normed * inner_sum)).reshape(values.shape)


def rms_back(scaled, factor, upstream):
    return factor * (upstream - scaled * jnp.mean(upstream * scaled, axis=-1, keepdims=True))


def body(
    tokens,
    cotangent,
    seq_spans,
    w_query,
    w_key,
    w_value,
    conv_kernel,
    persistent,
    norm_gain,
    rate_proj,
    out_gate,
    out_proj,
    memory_in,
    memory_out,
    ffn_gain,
    ffn_gate,
    ffn_up,
    ffn_down,
):
    wide, narrow = lax.axis_size("wide"), lax.axis_size("narrow")
    devices = wide * narrow
    wide_pos, narrow_pos = lax.axis_index("wide"), lax.axis_index("narrow")
    span, width = tokens.shape
    taps = conv_kernel.shape[0]
    persist_count = persistent.shape[1]
    local_width = out_gate.shape[1]
    own_rows = span // narrow
    lanes = wide // LANE_WIDE
    chips = LANE_WIDE * narrow // 2
    shards = 2 * chips
    shard_rows = span // shards
    hidden = memory_in.shape[1] // LANE_WIDE
    score_scale = math.sqrt(HEAD)

    def shard_of(tw, tn):
        return lax.rem(tn, 2) * chips + lax.rem(tw, LANE_WIDE) * (narrow // 2) + lax.div(tn, 2)

    long_turns = min(6, wide * 5 // 8)
    turns = max(long_turns, wide - long_turns)
    is_first = False
    start = 0
    for i in range(seq_spans.shape[0]):
        is_first = is_first | (wide_pos == start)
        start = start + seq_spans[i]

    smalls = [conv_kernel, persistent, norm_gain, ffn_gain, rate_proj]
    small_sizes = [a.size for a in smalls]
    packed = jnp.concatenate([a.reshape(-1) for a in smalls])
    padded = -(-packed.size // 2048) * 2048
    packed = jnp.pad(packed, (0, padded - packed.size)).reshape(-1, 128)
    own_weights = jnp.concatenate(
        [a.reshape(a.shape[0], narrow, local_width) for a in (w_query, w_key, w_value)], 2
    ).transpose(1, 0, 2)
    memory_cols = memory_in.reshape(memory_in.shape[0], LANE_WIDE, hidden).transpose(1, 0, 2)
    memory_rows = memory_out.reshape(LANE_WIDE, hidden, memory_out.shape[1])
    small_all, weights_all, first_all, second_all, tail_tokens = send_parameters(
        packed, own_weights, [memory_cols, memory_rows], tokens, 1
    )
    first_init = first_all.reshape(width, hidden)
    second_init = second_all.transpose(1, 0, 2).reshape(hidden, width)
    small_all = small_all.reshape(devices, padded)
    pieces, at = [], 0
    for a, size in zip(smalls, small_sizes):
        pieces.append(small_all[:, at : at + size].reshape((devices,) + a.shape))
        at += size
    kernel_all = pieces[0].transpose(1, 0, 2).reshape(taps, 3, width)
    persist_all = pieces[1].transpose(1, 2, 0, 3).reshape(2, persist_count, width)
    gain_one = pieces[2].reshape(width).astype(f32)
    gain_two = pieces[3].reshape(width).astype(f32)
    rate_f = pieces[4].reshape(width, 3).astype(f32)
    col_offset = narrow_pos * local_width

    def own_cols(values, axis):
        return lax.dynamic_slice_in_dim(values, col_offset, local_width, axis)

    def own_part(values):
        return lax.dynamic_slice_in_dim(values, narrow_pos * own_rows, own_rows, 0)

    kernel_f = own_cols(kernel_all, 2).reshape(taps, 3 * local_width).astype(f32)
    persist_f = own_cols(persist_all, 2).astype(f32)
    qkv_weights = weights_all.reshape(width, 3 * local_width)

    key_all, value_got, gate_got, key_low, query_low, value_low, normed_low, extended, mixed_conv, span_mean, gate_tile = (
        front_step(
            tokens,
            tail_tokens,
            gain_one[None],
            qkv_weights,
            jnp.pad(kernel_f, ((0, 8 - taps), (0, 0))),
            jnp.pad(rate_f.T, ((0, 5), (0, 0))),
            seq_spans,
            shard_of,
            2,
        )
    )
    value_low = value_low.reshape(span, local_width)
    span_mean, gate_sig = span_mean[0], gate_tile[0, :3]
    gate_scale = jnp.array([decay_top, moment_top, learn_top], f32)
    later = (ffn_gate, ffn_up, ffn_down, jnp.concatenate([out_gate, out_proj.T], 1))
    key_all, *later = lax.optimization_barrier((key_all,) + later)
    out_weights = lax.all_gather(later[3], "wide", axis=0, tiled=True)
    ffn_gate_cols = lax.all_gather(later[0], "wide", axis=0, tiled=True)
    ffn_up_cols = lax.all_gather(later[1], "wide", axis=0, tiled=True)
    ffn_down_rows = lax.all_gather(later[2], "wide", axis=1, tiled=True)
    gate_cols = out_weights[:, :local_width]
    proj_cols = out_weights[:, local_width:]
    gate_rows = gate_got[::narrow, 0, :3]
    if not paired_lanes():
        long_start = (jnp.cumsum(seq_spans) - seq_spans)[jnp.argmax(seq_spans)]
        turn_order = jnp.arange(turns, dtype=jnp.int32)
        rest_order = jnp.where(turn_order < long_start, turn_order, turn_order + long_turns)
        lane_spans = jnp.where(wide_pos // LANE_WIDE == 0, long_start + turn_order, rest_order)
        key_all = key_all[jnp.clip(lane_spans, 0, wide - 1)]
    chain = chain_forward(
        key_all, value_got, query_low, seq_spans, gate_rows, turns, first_init, second_init, 3
    )
    recall_low, saved = chain[0].reshape(span, local_width), chain[1:]
    recall_own = recall_low.astype(f32)

    keys_all = jnp.concatenate(
        [head_norm(persist_f[0], HEAD).astype(bf16), head_norm(recall_own, HEAD).astype(bf16), key_low], 0
    )
    values_all = jnp.concatenate([persist_f[1].astype(bf16), recall_low, value_low], 0)
    query_heads = split_heads(query_low, HEAD)
    key_heads = split_heads(keys_all, HEAD)
    value_heads = split_heads(values_all, HEAD)
    key_total = keys_all.shape[0]
    row_index = lax.broadcasted_iota(jnp.int32, (span, key_total), 0)
    col_index = lax.broadcasted_iota(jnp.int32, (span, key_total), 1)
    allowed = (col_index < persist_count + span) | (col_index - persist_count - span <= row_index)

    def score_block():
        raw_scores = (
            jnp.einsum("thd,jhd->htj", query_heads, key_heads, preferred_element_type=f32) * score_scale
        )
        return jnp.where(allowed[None], raw_scores, masked_score)

    scores = score_block()
    row_top = jnp.max(scores, axis=-1, keepdims=True)
    exponent = jnp.exp(scores - row_top)
    total_sum = jnp.sum(exponent, axis=-1, keepdims=True)
    log_total = row_top + jnp.log(total_sum)
    weights_low = (exponent / total_sum).astype(bf16)
    attended = jnp.einsum("htj,jhd->thd", weights_low, value_heads, preferred_element_type=f32).reshape(
        span, local_width
    )
    gate_pre = matmul(normed_low, gate_cols)
    gate_sigmoid = jax.nn.sigmoid(gate_pre)
    gated_low = (attended * gate_sigmoid).astype(bf16)

    def by_rows(part):
        return part.reshape(narrow, own_rows, width)

    tokens_own, cotangent_own = own_part(tokens), own_part(cotangent)
    rows_f32, row_f32 = ((own_rows, width), f32), ((1, width), f32)

    def scaled_of(values):
        factor = lax.rsqrt(jnp.mean(values * values, axis=-1, keepdims=True) + eps_norm)
        return values * factor, factor

    def after_branch(totals, extras):
        tokens_rows, gain = extras
        middle = tokens_rows.astype(f32) + totals[0]
        return [(scaled_of(middle)[0] * gain).astype(bf16)], [middle]

    normed_two, middle = narrow_step(
        [by_rows(inner_right(gated_low, proj_cols))],
        [tokens_own, gain_two[None]],
        after_branch,
        1,
        [rows_f32],
        7,
    )
    normed_two = normed_two.reshape(span, width)
    gate_val = matmul(normed_two, ffn_gate_cols)
    up_val = matmul(normed_two, ffn_up_cols)
    gate_silu = jax.nn.silu(gate_val)
    hidden_ffn = (gate_silu * up_val).astype(bf16)
    ffn_part = matmul(hidden_ffn, ffn_down_rows)
    down_grad = inner_left(cotangent, hidden_ffn).astype(bf16)
    hidden_grad_ffn = inner_right(cotangent, ffn_down_rows)
    gate_sig_ffn = jax.nn.sigmoid(gate_val)
    gate_grad_low = (
        hidden_grad_ffn * up_val * gate_sig_ffn * (1.0 + gate_val * (1.0 - gate_sig_ffn))
    ).astype(bf16)
    up_grad_low = (hidden_grad_ffn * gate_silu).astype(bf16)
    ffn_gate_grad = inner_left(normed_two, gate_grad_low).astype(bf16)
    ffn_up_grad = inner_left(normed_two, up_grad_low).astype(bf16)
    normed_two_part = inner_right(gate_grad_low, ffn_gate_cols) + inner_right(up_grad_low, ffn_up_cols)

    def scatter_wide(grad):
        return lax.psum_scatter(grad.astype(bf16), "wide", scatter_dimension=0, tiled=True).astype(f32)

    ffn_sums = (by_rows(ffn_part), by_rows(normed_two_part))
    ffn_sums, ffn_grads = lax.optimization_barrier((ffn_sums, (ffn_gate_grad, ffn_up_grad, down_grad)))
    ffn_gate_out, ffn_up_out, ffn_down_out = [scatter_wide(a) for a in ffn_grads]

    def after_ffn(totals, extras):
        middle_rows, cotangent_rows, gain = extras
        scaled, factor = scaled_of(middle_rows)
        grad = cotangent_rows.astype(f32) + rms_back(scaled, factor, totals[1] * gain)
        gain_part = jnp.sum(totals[1] * scaled, axis=0, keepdims=True)
        return [grad.astype(bf16)], [grad, gain_part, (middle_rows + totals[0]).astype(bf16)]

    branch_low, middle_grad, gain_two_part, output_own = narrow_step(
        list(ffn_sums),
        [middle, cotangent_own, gain_two[None]],
        after_ffn,
        1,
        [rows_f32, row_f32, ((own_rows, width), bf16)],
        9,
    )
    branch_low = branch_low.reshape(span, width)

    gated_grad = matmul(branch_low, proj_cols)
    attended_grad_low = (gated_grad * gate_sigmoid).astype(bf16)
    gate_pre_low = (gated_grad * attended * gate_sigmoid * (1.0 - gate_sigmoid)).astype(bf16)
    early_grads = jnp.concatenate([inner_left(normed_low, gate_pre_low), inner_left(branch_low, gated_low)], 1)
    early_grads = early_grads.astype(bf16)

    weights_again = jnp.exp(score_block() - log_total)
    grad_heads = split_heads(attended_grad_low, HEAD)
    weight_grad = jnp.einsum("thd,jhd->htj", grad_heads, value_heads, preferred_element_type=f32)
    row_delta = jnp.sum(weights_again * weight_grad, axis=-1, keepdims=True)
    score_grad_low = (weights_again * (weight_grad - row_delta)).astype(bf16)
    query_att = (
        score_scale * jnp.einsum("htj,jhd->thd", score_grad_low, key_heads, preferred_element_type=f32)
    ).reshape(span, local_width)
    keys_grad = (
        score_scale * jnp.einsum("htj,thd->jhd", score_grad_low, query_heads, preferred_element_type=f32)
    ).reshape(key_total, local_width)
    values_grad = jnp.einsum(
        "htj,thd->jhd", weights_again.astype(bf16), grad_heads, preferred_element_type=f32
    ).reshape(key_total, local_width)
    recall_end = persist_count + span
    persist_part = jnp.stack(
        [head_norm_back(persist_f[0], keys_grad[:persist_count], HEAD), values_grad[:persist_count]]
    )
    recall_grad_low = (
        head_norm_back(recall_own, keys_grad[persist_count:recall_end], HEAD)
        + values_grad[persist_count:recall_end]
    ).astype(bf16)

    cots, sums_got, first_chunks, second_chunks = chain_backward(recall_grad_low, saved, seq_spans, gate_rows, 12)
    gate_sums = jnp.sum(sums_got[:, :, :3], axis=0)[wide_pos] * jnp.array([-1.0, 1.0, -1.0], f32)

    logit_grad = gate_sums * gate_scale * gate_sig * (1.0 - gate_sig)
    rate_part = span_mean[:, None] * logit_grad[None, :]
    gate_row = jnp.sum(rate_f * logit_grad[None, :], axis=1)[None, :] / span

    def after_all(totals, extras):
        tokens_rows, grad_rows, gain, row = extras
        scaled, factor = scaled_of(tokens_rows.astype(f32))
        normed_grad = totals[0] + row
        gain_part = jnp.sum(normed_grad * scaled, axis=0, keepdims=True)
        return [(grad_rows + rms_back(scaled, factor, normed_grad * gain)).astype(bf16)], [gain_part]

    def place_cols(piece, axis):
        full = piece.shape[:axis] + (width,) + piece.shape[axis + 1 :]
        return lax.dynamic_update_slice_in_dim(jnp.zeros(full, f32), piece, col_offset, axis)

    persist_full = place_cols(persist_part, 2)
    rate_part = jnp.where(narrow_pos == 0, rate_part, 0.0)
    chunks = [
        persist_full.reshape(2, persist_count, devices, -1).transpose(2, 0, 1, 3),
        gain_two_part.reshape(devices, -1),
        rate_part.reshape(devices, -1, 3),
    ]
    flat = jnp.concatenate([a.reshape(devices, -1) for a in chunks], 1)
    flat_size = -(-flat.shape[1] // 1024) * 1024
    flat = jnp.pad(flat, ((0, 0), (0, flat_size - flat.shape[1]))).reshape(devices, -1, 128)
    cots = cots.reshape(3, span, local_width)
    tokens_grad, weight_out, first_out, second_out, flat_sum, gain_sum, tap_rows, early_out, output = last_step(
        [cots[0], cots[1], cots[2], query_att, keys_grad[recall_end:], values_grad[recall_end:]],
        [mixed_conv, extended, jnp.pad(kernel_f, ((0, 8 - taps), (0, 0))), qkv_weights, normed_low],
        seq_spans,
        [gate_pre_low, gate_cols],
        [tokens_own, middle_grad, gain_one[None], gate_row],
        after_all,
        early_grads,
        [first_chunks, second_chunks],
        flat,
        output_own,
        15,
    )
    output = output.reshape(span, width)
    tokens_grad = tokens_grad.reshape(span, width).astype(f32)
    flat_sum = flat_sum.reshape(-1)
    own_start = (wide_pos * narrow + narrow_pos) * (width // devices)
    norm_grad = lax.dynamic_slice_in_dim(gain_sum.reshape(-1), own_start, width // devices, 0)
    small_outs, at = [], 0
    for a in chunks:
        size = a.size // devices
        small_outs.append(flat_sum[at : at + size].reshape(a.shape[1:]))
        at += size
    persist_grad, ffn_gain_grad, rate_grad = small_outs
    tap_sum = jnp.sum(tap_rows.reshape(wide, narrow, taps, 3, local_width), axis=0)
    tap_sum = tap_sum.transpose(1, 2, 0, 3).reshape(taps, 3 * width)
    kernel_grad = lax.dynamic_slice_in_dim(
        tap_sum, (wide_pos * narrow + narrow_pos) * (3 * width // devices), 3 * width // devices, 1
    )
    return (
        output,
        tokens_grad,
        weight_out[:, :local_width],
        weight_out[:, local_width : 2 * local_width],
        weight_out[:, 2 * local_width : 3 * local_width],
        kernel_grad,
        persist_grad,
        norm_grad,
        rate_grad,
        early_out[:, :local_width],
        early_out[:, local_width:].T,
        first_out,
        second_out,
        ffn_gain_grad,
        ffn_gate_out,
        ffn_up_out,
        ffn_down_out.T,
    )


def solution(mesh):
    rows, both, square, turned = P("wide", None), P(("wide", "narrow"), None), P("wide", "narrow"), P("narrow", "wide")
    flat, taps, heads = P(("wide", "narrow")), P(None, ("wide", "narrow")), P(None, None, ("wide", "narrow"))
    return jax.shard_map(
        body,
        mesh=mesh,
        in_specs=(rows, rows, P(), both, both, both, taps, heads, flat, both)
        + (square, turned, square, turned, flat, square, square, turned),
        out_specs=(rows, rows, square, square, square, taps, heads, flat, both)
        + (square, turned, square, turned, flat, square, square, turned),
        check_vma=False,
    )
```
